32 devices in a mesh: seq: 8 (over z, x), tensor: 4 (over y, core).
Axes of the slice: x: 2, y: 2, z: 4, core: 2. Of those that a mesh axis runs over, the one named last changes fastest.
Arguments:
- inputs: bfloat16 [2, 2048, 2048], P(None, 'seq'), may hold values from -6 to 6
- segment: int32 [2, 2048], P(None, 'seq'), may hold values from 0 to 2, as said below
- position: int32 [2, 2048], P(None, 'seq'), may hold values from 0 to 1535, as said below
- w_query: float32 [2048, 2048], P('seq', 'tensor'), may hold values from -0.125 to 0.125
- w_keyval: float32 [2048, 256], P(('seq', 'tensor')), may hold values from -0.125 to 0.125
- w_out: float32 [2048, 2048], P('tensor', 'seq'), may hold values from -3 to 3
- w_fc: float32 [2048, 8192], P('seq', 'tensor'), may hold values from -0.125 to 0.125
- w_proj: float32 [8192, 2048], P('tensor', 'seq'), may hold values from -0.0625 to 0.0625
- vectors: float32 [7, 2048], P(None, ('seq', 'tensor'))
- fc_bias: float32 [8192], P(('seq', 'tensor')), may hold values from -1.5 to 1.5
- value_bias: float32 [128], replicated, may hold values from -0.1 to 0.1
- grad_out: bfloat16 [2, 2048, 2048], P(None, 'seq'), may hold values from -6 to 6
Outputs:
- output: bfloat16 [2, 2048, 2048], P(None, 'seq')
- grad_input: bfloat16 [2, 2048, 2048], P(None, 'seq')
- grad_w_query: float32 [2048, 2048], P('seq', 'tensor')
- grad_w_keyval: float32 [2048, 256], P(('seq', 'tensor'))
- grad_w_out: float32 [2048, 2048], P('tensor', 'seq')
- grad_w_fc: float32 [2048, 8192], P('seq', 'tensor')
- grad_w_proj: float32 [8192, 2048], P('tensor', 'seq')
- grad_vectors: float32 [7, 2048], P(None, ('seq', 'tensor'))
- grad_fc_bias: float32 [8192], P(('seq', 'tensor'))
- grad_value_bias: float32 [128], replicated
- grad_shift_two: float32 [2048], P(('seq', 'tensor'))
The draws below stay inside these ranges and needn't reach their ends.
Inputs may be any that keep to these rules, and one draw needn't show every extreme that they name: The rows of a micro-batch form blocks of 256 rows in an arbitrary order; each block holds 256 consecutive positions of one sequence. Segment 0 is the prompt of 1024 tokens with positions 0 to 1023; each segment of 1 to 2 is a continuation of 512 tokens with positions 1024 to 1535. `position`: positions of each sequence are distinct and as stated under segment.
All inputs are finite; a program needn't handle non-finite values.
Results may differ from the reference program's by a relative error of at most 0.02.
Values may be sent and summed in bfloat16 or wider, within the bound.
A program may use at most 192 MiB of HBM per device.

```python
import math
import jax
import jax.numpy as jnp
from jax import lax

D = 2048
HD = 128
FF = 8192
UNIT = 256
MICRO = 2
TOKENS = 2048
PROMPT = 1024
N_TENSOR = 4


def unit_layout(key):
    unit_count = TOKENS // UNIT
    half_count = unit_count // 2
    micro_keys = jax.random.split(jax.random.fold_in(key, 11), MICRO)
    orders = jax.vmap(lambda micro_key: jax.random.permutation(micro_key, unit_count))(micro_keys).astype(jnp.int32)
    offsets = jnp.arange(UNIT, dtype=jnp.int32)
    in_prompt = orders < half_count
    later = orders - half_count
    segment_ids = jnp.where(in_prompt, 0, later // 2 + 1).astype(jnp.int32)
    positions = jnp.where(in_prompt[:, :, None], orders[:, :, None] * UNIT + offsets, PROMPT + (later % 2)[:, :, None] * UNIT + offsets)
    segment_full = jnp.broadcast_to(segment_ids[:, :, None], (MICRO, unit_count, UNIT)).reshape(MICRO, TOKENS)
    return (segment_full.astype(jnp.int32), positions.reshape(MICRO, TOKENS).astype(jnp.int32))


def draw_segment(key, part):
    return unit_layout(key)[0]


def draw_position(key, part):
    return unit_layout(key)[1]


def draw_vectors(key, part):
    gain_key, shift_key = jax.random.split(jax.random.fold_in(key, 5))
    gains = jax.random.uniform(gain_key, (7, D), jnp.float32, 0.6, 1.4)
    shifts = 0.2 * jax.random.normal(shift_key, (7, D), jnp.float32)
    row_ids = jnp.arange(7)[:, None]
    is_gain = (row_ids == 0) | (row_ids == 4)
    return jnp.where(is_gain, gains, shifts).astype(jnp.float32)


def level_of(key, shape, cuts, low, largest):
    factor_of = 1.0
    for dim, parts in cuts:
        heights = jax.random.uniform(jax.random.fold_in(jax.random.fold_in(key, 6), dim), (parts,), jnp.float32, low / len(cuts), largest / len(cuts))
        factor_of = factor_of * jnp.repeat(jnp.exp(heights), shape[dim] // parts).reshape((-1,) + (1,) * (len(shape) - 1 - dim))
    return factor_of


def scatter_about(stream_key, extent, deviation, bound, cuts=(), held_as=jnp.bfloat16):
    array = deviation * jax.random.normal(stream_key, extent, jnp.float32)
    if cuts:
        array = array * level_of(stream_key, extent, cuts, -0.22, 0.18)
    return jnp.clip(array, -bound, bound).astype(held_as)


def setup_inputs(seed: int = 0) -> dict:
    arg_keys = jax.random.split(jax.random.key(seed), 13)
    inputs = scatter_about(arg_keys[0], (MICRO, TOKENS, D), 1.0, 6.0, ((1, 8),))
    segment = draw_segment(jax.random.fold_in(arg_keys[12], 71), 0)
    position = draw_position(jax.random.fold_in(arg_keys[12], 71), 0)
    w_query = scatter_about(arg_keys[3], (D, D), D ** -0.5, 0.125, ((0, 8), (1, 4)), jnp.float32)
    w_keyval = scatter_about(arg_keys[4], (D, 2 * HD), D ** -0.5, 0.125, ((0, 32),), jnp.float32)
    w_out = scatter_about(arg_keys[5], (D, D), 0.5, 3.0, ((0, 4), (1, 8)), jnp.float32)
    w_fc = scatter_about(arg_keys[6], (D, FF), D ** -0.5, 0.125, ((0, 8), (1, 4)), jnp.float32)
    w_proj = scatter_about(arg_keys[7], (FF, D), FF ** -0.5, 0.0625, ((0, 4), (1, 8)), jnp.float32)
    vectors = draw_vectors(jax.random.fold_in(arg_keys[12], 71), 0)
    fc_bias = scatter_about(arg_keys[9], (FF,), 0.3, 1.5, ((0, 32),), jnp.float32)
    value_bias = scatter_about(arg_keys[10], (HD,), 0.02, 0.1, (), jnp.float32)
    grad_out = scatter_about(arg_keys[11], (MICRO, TOKENS, D), 1.0, 6.0, ((1, 8),))
    return dict(inputs=inputs, segment=segment, position=position, w_query=w_query, w_keyval=w_keyval, w_out=w_out, w_fc=w_fc, w_proj=w_proj, vectors=vectors, fc_bias=fc_bias, value_bias=value_bias, grad_out=grad_out)


EPS = 1e-05
NEG = -1e+30
HIGH = lax.Precision.HIGHEST

@jax.custom_vjp
def low(v):
    return lax.optimization_barrier(v.astype(jnp.bfloat16)).astype(jnp.float32)

@jax.custom_vjp
def low_back(v):
    return v

def low_keep(v):
    return (low(v), None)

def low_pass(kept, grad):
    return (grad,)

def back_keep(v):
    return (v, None)

def back_low(kept, grad):
    return (low(grad),)
low.defvjp(low_keep, low_pass)
low_back.defvjp(back_keep, back_low)

def matmul(left, right):
    return jnp.dot(left, right, precision=HIGH, preferred_element_type=jnp.float32)

def layer_norm(values, gain_vec, shift_vec):
    average = lax.optimization_barrier(jnp.mean(values, axis=-1, keepdims=True))
    centred = values - average
    spread = lax.optimization_barrier(jnp.mean(centred * centred, axis=-1, keepdims=True))
    return centred * lax.rsqrt(spread + EPS) * gain_vec + shift_vec

def attention(queries, keyval, segment_row, position_row):
    total_rows = queries.shape[0]
    head_count = queries.shape[1] // HD
    block_rows = math.gcd(256, total_rows)
    num_blocks = total_rows // block_rows
    key_rows = keyval[:, :HD]
    values = keyval[:, HD:]
    query_blocks = queries.reshape(num_blocks, block_rows, head_count, HD)
    seg_blocks = segment_row.reshape(num_blocks, block_rows)
    pos_blocks = position_row.reshape(num_blocks, block_rows)

    def one_block(packed):
        query_part, seg_query, pos_query = packed
        scores = jnp.einsum('qhd,kd->hqk', query_part, key_rows, precision=HIGH) * HD ** (-0.5)
        visible = ((segment_row[None, :] == 0) | (segment_row[None, :] == seg_query[:, None])) & (position_row[None, :] <= pos_query[:, None])
        scores = low_back(jnp.where(visible[None], scores, NEG))
        attn_probs = low(jax.nn.softmax(scores, axis=-1))
        return jnp.einsum('hqk,kd->qhd', attn_probs, values, precision=HIGH)
    blocks_out = lax.map(jax.checkpoint(one_block), (query_blocks, seg_blocks, pos_blocks))
    return blocks_out.reshape(total_rows, head_count * HD)

def forward(inputs_f, segment_row, position_row, w_query, w_keyval, w_out, w_fc, w_proj, vectors, fc_bias, value_bias):
    w_query, w_keyval, w_out, w_fc, w_proj = (low(w_query), low(w_keyval), low(w_out), low(w_fc), low(w_proj))
    vectors, fc_bias, value_bias = (low(vectors), low(fc_bias), low(value_bias))
    gain_one, shift_one, query_bias, out_bias, gain_two, shift_two, proj_bias = [vectors[row_index] for row_index in range(7)]
    normed = low(layer_norm(inputs_f, gain_one, shift_one))
    queries = low(low_back(matmul(normed, w_query) + query_bias))
    keyval = matmul(normed, w_keyval)
    keyval = keyval + jnp.concatenate([jnp.zeros((HD,), keyval.dtype), value_bias])
    group_width = D // N_TENSOR
    pieces = []
    for head_group in range(N_TENSOR):
        shared = low(low_back(keyval))
        pieces.append(attention(queries[:, head_group * group_width:(head_group + 1) * group_width], shared, segment_row, position_row))
    mixed_heads = low(low_back(jnp.concatenate(pieces, axis=1)))
    middle = inputs_f + low_back(matmul(mixed_heads, w_out)) + out_bias
    normed_two = low(layer_norm(middle, gain_two, shift_two))
    hidden = low_back(matmul(normed_two, w_fc) + fc_bias)
    active = low(jax.nn.gelu(hidden, approximate=True))
    return middle + low_back(matmul(active, w_proj)) + proj_bias

def reference(inputs, segment, position, w_query, w_keyval, w_out, w_fc, w_proj, vectors, fc_bias, value_bias, grad_out):
    params = (w_query, w_keyval, w_out, w_fc, w_proj, vectors, fc_bias, value_bias)
    totals = tuple((jnp.zeros_like(param) for param in params))
    results = []
    input_grads = []
    for batch_index in range(MICRO):
        seg_row = segment[batch_index]
        pos_row = position[batch_index]

        def local_fn(inputs_f, *weights):
            return forward(inputs_f, seg_row, pos_row, *weights)
        result, pullback = jax.vjp(local_fn, inputs[batch_index].astype(jnp.float32), *params)
        gradients = pullback(grad_out[batch_index].astype(jnp.float32))
        results.append(result.astype(jnp.bfloat16))
        input_grads.append(gradients[0].astype(jnp.bfloat16))
        totals = tuple((total + extra for total, extra in zip(totals, gradients[1:])))
    return (jnp.stack(results), jnp.stack(input_grads), totals[0], totals[1], totals[2], totals[3], totals[4], totals[5], totals[6], totals[7], totals[5][5])
```

```python
from functools import partial

import jax
import jax.numpy as jnp
from jax import lax
from jax.experimental import pallas as pl
from jax.experimental.pallas import tpu as pltpu
from jax.sharding import PartitionSpec as P

EPS = 1e-05
NEG = -1e30
LOW = jnp.bfloat16
F32 = jnp.float32


def bits_of(count):
    return count.bit_length() - 1


def swap(value, axis, bit):
    count = lax.axis_size(axis)
    return lax.ppermute(value, axis, [(i, i ^ (1 << bit)) for i in range(count)])


def after(value, *others):
    return lax.optimization_barrier((value,) + others)[0]


def dot(left, right):
    return jnp.dot(left, right, preferred_element_type=F32)


def dot_tn(left, right):
    return lax.dot_general(left, right, (((0,), (0,)), ((), ())), preferred_element_type=F32)


def dot_nt(left, right):
    return lax.dot_general(left, right, (((1,), (1,)), ((), ())), preferred_element_type=F32)


def offsets_in_order(count):
    width = bits_of(count)
    return [int(format(p, "0%db" % width)[::-1], 2) if width else 0 for p in range(count)]


def gather_blocks(own):
    count = lax.axis_size("seq")
    blocks = {0: own}
    for bit in reversed(range(bits_of(count))):
        for r in list(blocks):
            blocks[r | (1 << bit)] = swap(blocks[r], "seq", bit)
    return blocks


def scatter_blocks(blocks):
    count = lax.axis_size("seq")
    blocks = dict(blocks)
    for bit in range(bits_of(count)):
        for r in sorted(blocks):
            if r & (1 << bit):
                arrived = swap(blocks.pop(r).astype(LOW), "seq", bit)
                blocks[r ^ (1 << bit)] = blocks[r ^ (1 << bit)] + arrived.astype(F32)
    return blocks[0]


def tensor_gather(own, axis):
    count = lax.axis_size("tensor")
    out = jnp.expand_dims(own, axis)
    for bit in reversed(range(bits_of(count))):
        out_other = swap(out, "tensor", bit)
        mine = (lax.axis_index("tensor") >> bit) & 1
        low_part = jnp.where(mine == 0, out, out_other)
        high_part = jnp.where(mine == 0, out_other, out)
        size = out.shape[axis]
        shape = out.shape
        low_part = jnp.expand_dims(low_part, axis)
        high_part = jnp.expand_dims(high_part, axis)
        out = jnp.concatenate([low_part, high_part], axis=axis)
        out = jnp.swapaxes(out, axis, axis + 1) if size > 1 else out
        out = out.reshape(shape[:axis] + (2 * size,) + shape[axis + 1 :])
    return out


def tensor_scatter(parts, axis):
    count = lax.axis_size("tensor")
    index = lax.axis_index("tensor")
    for bit in range(bits_of(count)):
        shape = parts.shape
        split = parts.reshape(shape[:axis] + (shape[axis] // 2, 2) + shape[axis + 1 :])
        mine = (index >> bit) & 1
        keep = lax.dynamic_index_in_dim(split, mine, axis + 1, keepdims=False)
        give = lax.dynamic_index_in_dim(split, 1 - mine, axis + 1, keepdims=False)
        parts = keep.astype(F32) + swap(give.astype(LOW), "tensor", bit).astype(F32)
    return lax.squeeze(parts, (axis,))


def visible(meta_q, meta_k):
    seg_q, pos_q = meta_q[:, 0:1], meta_q[:, 1:2]
    seg_k, pos_k = meta_k[0:1, :], meta_k[1:2, :]
    return ((seg_k == 0) | (seg_k == seg_q)) & (pos_k <= pos_q)


def forward_kernel(live_ref, q_ref, kv_ref, mq_ref, mk_ref, o_ref, lse_ref, top, total, acc):
    batch = pl.program_id(0)
    hd = kv_ref.shape[-1] // 2
    heads = q_ref.shape[-1] // hd
    blocks = kv_ref.shape[1]
    scale = float(hd) ** (-0.5)
    top[...] = jnp.full_like(top, NEG)
    total[...] = jnp.zeros_like(total)
    acc[...] = jnp.zeros_like(acc)

    def step(index, carry):
        @pl.when(live_ref[batch, index] > 0)
        def _():
            mask = visible(mq_ref[0], mk_ref[0, index])
            keys = kv_ref[0, index, :, :hd]
            values = kv_ref[0, index, :, hd:]
            for head in range(heads):
                cols = slice(head * hd, (head + 1) * hd)
                scores = jnp.where(mask, dot_nt(q_ref[0, :, cols], keys) * scale, NEG)
                before = top[head]
                now = jnp.maximum(before, jnp.max(scores, axis=-1, keepdims=True))
                shrink = jnp.exp(before - now)
                probs = jnp.exp(scores - now)
                total[head] = total[head] * shrink + jnp.sum(probs, axis=-1, keepdims=True)
                acc[:, cols] = acc[:, cols] * shrink + dot(probs.astype(LOW), values)
                top[head] = now

        return carry

    lax.fori_loop(0, blocks, step, 0)
    for head in range(heads):
        cols = slice(head * hd, (head + 1) * hd)
        o_ref[0, :, cols] = (acc[:, cols] / total[head]).astype(LOW)
        lse_ref[0, head] = top[head] + jnp.log(total[head])


def attend_forward(queries, keyval, meta_q, meta_k, live):
    batches, rows, width = queries.shape
    _, blocks, keys, two = keyval.shape
    hd = two // 2
    heads = width // hd
    flops = 4 * batches * rows * width * blocks * keys
    return pl.pallas_call(
        forward_kernel,
        grid_spec=pltpu.PrefetchScalarGridSpec(
            num_scalar_prefetch=1,
            grid=(batches,),
            in_specs=[
                pl.BlockSpec((1, rows, width), lambda b, live: (b, 0, 0)),
                pl.BlockSpec((1, blocks, keys, two), lambda b, live: (b, 0, 0, 0)),
                pl.BlockSpec((1, rows, 128), lambda b, live: (b, 0, 0)),
                pl.BlockSpec((1, blocks, 8, keys), lambda b, live: (b, 0, 0, 0)),
            ],
            out_specs=[
                pl.BlockSpec((1, rows, width), lambda b, live: (b, 0, 0)),
                pl.BlockSpec((1, heads, rows, 1), lambda b, live: (b, 0, 0, 0)),
            ],
            scratch_shapes=[
                pltpu.VMEM((heads, rows, 1), F32),
                pltpu.VMEM((heads, rows, 1), F32),
                pltpu.VMEM((rows, width), F32),
            ],
        ),
        out_shape=[
            jax.ShapeDtypeStruct((batches, rows, width), LOW),
            jax.ShapeDtypeStruct((batches, heads, rows, 1), F32),
        ],
        name="attend_forward",
        cost_estimate=pl.CostEstimate(
            flops=flops, transcendentals=0, bytes_accessed=2 * keyval.size
        ),
    )(live, queries, keyval, meta_q, meta_k)


def backward_kernel(
    live_ref, q_ref, kv_ref, mq_ref, mk_ref, o_ref, lse_ref, do_ref, dq_ref, dkv_ref, delta, acc
):
    batch = pl.program_id(0)
    hd = kv_ref.shape[-1] // 2
    heads = q_ref.shape[-1] // hd
    blocks = kv_ref.shape[1]
    scale = float(hd) ** (-0.5)
    acc[...] = jnp.zeros_like(acc)
    for head in range(heads):
        cols = slice(head * hd, (head + 1) * hd)
        delta[head] = jnp.sum(
            do_ref[0, :, cols].astype(F32) * o_ref[0, :, cols].astype(F32), axis=-1, keepdims=True
        )

    def step(index, carry):
        @pl.when(live_ref[batch, index] > 0)
        def _():
            mask = visible(mq_ref[0], mk_ref[0, index])
            keys = kv_ref[0, index, :, :hd]
            values = kv_ref[0, index, :, hd:]
            grad_k = jnp.zeros((keys.shape[0], hd), F32)
            grad_v = jnp.zeros((keys.shape[0], hd), F32)
            for head in range(heads):
                cols = slice(head * hd, (head + 1) * hd)
                query = q_ref[0, :, cols]
                grad_o = do_ref[0, :, cols]
                scores = dot_nt(query, keys) * scale
                probs = jnp.where(mask, jnp.exp(scores - lse_ref[0, head]), 0.0)
                grad_p = dot_nt(grad_o, values)
                grad_s = (probs * (grad_p - delta[head])).astype(LOW)
                acc[:, cols] += dot(grad_s, keys)
                grad_k = grad_k + dot_tn(grad_s, query)
                grad_v = grad_v + dot_tn(probs.astype(LOW), grad_o)
            dkv_ref[0, index, :, :hd] = (grad_k * scale).astype(LOW)
            dkv_ref[0, index, :, hd:] = grad_v.astype(LOW)

        @pl.when(live_ref[batch, index] == 0)
        def _():
            dkv_ref[0, index] = jnp.zeros(dkv_ref.shape[2:], LOW)

        return carry

    lax.fori_loop(0, blocks, step, 0)
    dq_ref[0] = (acc[...] * scale).astype(LOW)


def attend_backward(queries, keyval, meta_q, meta_k, live, mixed, lse, grad_mixed):
    batches, rows, width = queries.shape
    _, blocks, keys, two = keyval.shape
    hd = two // 2
    heads = width // hd
    flops = 10 * batches * rows * width * blocks * keys
    row_spec = pl.BlockSpec((1, rows, width), lambda b, live: (b, 0, 0))
    kv_spec = pl.BlockSpec((1, blocks, keys, two), lambda b, live: (b, 0, 0, 0))
    return pl.pallas_call(
        backward_kernel,
        grid_spec=pltpu.PrefetchScalarGridSpec(
            num_scalar_prefetch=1,
            grid=(batches,),
            in_specs=[
                row_spec,
                kv_spec,
                pl.BlockSpec((1, rows, 128), lambda b, live: (b, 0, 0)),
                pl.BlockSpec((1, blocks, 8, keys), lambda b, live: (b, 0, 0, 0)),
                row_spec,
                pl.BlockSpec((1, heads, rows, 1), lambda b, live: (b, 0, 0, 0)),
                row_spec,
            ],
            out_specs=[row_spec, kv_spec],
            scratch_shapes=[
                pltpu.VMEM((heads, rows, 1), F32),
                pltpu.VMEM((rows, width), F32),
            ],
        ),
        out_shape=[
            jax.ShapeDtypeStruct((batches, rows, width), LOW),
            jax.ShapeDtypeStruct((batches, blocks, keys, two), LOW),
        ],
        name="attend_backward",
        cost_estimate=pl.CostEstimate(
            flops=flops, transcendentals=0, bytes_accessed=4 * keyval.size
        ),
    )(live, queries, keyval, meta_q, meta_k, mixed, lse, grad_mixed)


def norm_parts(values):
    average = jnp.mean(values, axis=-1, keepdims=True)
    centred = values - average
    spread = jnp.mean(centred * centred, axis=-1, keepdims=True)
    return centred, lax.rsqrt(spread + EPS)


def norm_back(values, gain, grad):
    centred, inverse = norm_parts(values)
    unit = centred * inverse
    scaled = grad * gain
    inner = (
        scaled
        - jnp.mean(scaled, axis=-1, keepdims=True)
        - unit * jnp.mean(scaled * unit, axis=-1, keepdims=True)
    )
    return inverse * inner, grad * unit


def gelu_pair(values):
    const = 0.7978845608028654
    square = values * values
    inner = jnp.tanh(const * (values + 0.044715 * (values * square)))
    half = 0.5 * (1.0 + inner)
    slope = half + 0.5 * values * (1.0 - inner * inner) * const * (1.0 + 3 * 0.044715 * square)
    return values * half, slope


def local(
    inputs,
    segment,
    position,
    w_query,
    w_keyval,
    w_out,
    w_fc,
    w_proj,
    vectors,
    fc_bias,
    value_bias,
    grad_out,
):
    seq_size, tensor_size = lax.axis_size("seq"), lax.axis_size("tensor")
    seq_index, tensor_index = lax.axis_index("seq"), lax.axis_index("tensor")
    batches, rows, full_width = inputs.shape
    width_block = w_query.shape[0]
    group_width = w_query.shape[1]
    hidden_width = w_fc.shape[1]
    hd = value_bias.shape[0]
    quarter = rows // tensor_size
    order = offsets_in_order(seq_size)
    shard = vectors.shape[1]
    bias_shard = fc_bias.shape[0]

    def to_order(array):
        starts = [jnp.bitwise_xor(seq_index, r) * width_block for r in order]
        last = array.ndim - 1
        return jnp.concatenate(
            [lax.dynamic_slice_in_dim(array, start, width_block, last) for start in starts], last
        )

    def from_order(array):
        place = {r: p for p, r in enumerate(order)}
        table = jnp.array([place[r] for r in range(seq_size)], jnp.int32)
        last = array.ndim - 1
        return jnp.concatenate(
            [
                lax.dynamic_slice_in_dim(
                    array, table[jnp.bitwise_xor(seq_index, b)] * width_block, width_block, last
                )
                for b in range(seq_size)
            ],
            last,
        )

    pieces = [
        vectors.reshape(-1).astype(LOW),
        fc_bias.astype(LOW),
        segment.reshape(-1).astype(LOW),
        (position // 128).reshape(-1).astype(LOW),
        (position % 128).reshape(-1).astype(LOW),
    ]
    sizes = [piece.shape[0] for piece in pieces]
    packed = jnp.concatenate(pieces)
    pad = -packed.shape[0] % 1024
    packed = jnp.pad(packed, (0, pad)).reshape(-1, 128)
    small = lax.all_gather(packed, ("seq", "tensor"), axis=0, tiled=False)
    small = small.reshape(seq_size, tensor_size, -1).astype(F32)
    cuts = [0]
    for size in sizes:
        cuts.append(cuts[-1] + size)
    vec_all = small[:, :, cuts[0] : cuts[1]].reshape(seq_size * tensor_size, 7, shard)
    vec_all = jnp.swapaxes(vec_all, 0, 1).reshape(7, full_width)
    fc_all = small[:, :, cuts[1] : cuts[2]].reshape(-1)
    seg_all = small[:, 0, cuts[2] : cuts[3]].reshape(seq_size, batches, rows)
    pos_all = 128.0 * small[:, 0, cuts[3] : cuts[4]] + small[:, 0, cuts[4] : cuts[5]]
    pos_all = pos_all.reshape(seq_size, batches, rows)
    offset_ids = jnp.bitwise_xor(seq_index, jnp.array(order, jnp.int32))
    seg_keys = jnp.swapaxes(seg_all[offset_ids], 0, 1).astype(jnp.int32)
    pos_keys = jnp.swapaxes(pos_all[offset_ids], 0, 1).astype(jnp.int32)
    meta_k = jnp.pad(jnp.stack([seg_keys, pos_keys], axis=2), ((0, 0), (0, 0), (0, 6), (0, 0)))
    meta_q = jnp.pad(jnp.stack([segment, position], axis=2), ((0, 0), (0, 0), (0, 126)))
    seg_lo, seg_hi = jnp.min(seg_keys, axis=2), jnp.max(seg_keys, axis=2)
    own_lo = jnp.min(segment, axis=1, keepdims=True)
    own_hi = jnp.max(segment, axis=1, keepdims=True)
    live = (
        ((seg_lo == 0) | ((seg_lo <= own_hi) & (own_lo <= seg_hi)))
        & (jnp.min(pos_keys, axis=2) <= jnp.max(position, axis=1, keepdims=True))
    ).astype(jnp.int32)

    vec_rows = to_order(vec_all)
    gain_one, shift_one, _, out_bias, gain_two, shift_two, proj_bias = [
        vec_rows[i] for i in range(7)
    ]
    query_bias = lax.dynamic_slice_in_dim(vec_all[2], tensor_index * group_width, group_width, 0)
    fc_local = lax.dynamic_slice_in_dim(fc_all, tensor_index * hidden_width, hidden_width, 0)
    bias_value = value_bias.astype(LOW).astype(F32)
    kv_bias = jnp.concatenate([jnp.zeros((hd,), F32), bias_value])

    kv_rows = tensor_gather(w_keyval.astype(LOW), 0).reshape(width_block, 2 * hd)
    first_own = jnp.concatenate([w_query.astype(LOW), kv_rows], axis=1)
    first_blocks = gather_blocks(first_own)
    first_mat = jnp.concatenate([first_blocks[r] for r in order], axis=0)
    out_blocks = gather_blocks(after(w_out.T.astype(LOW), first_blocks[seq_size - 1]))
    out_t = jnp.concatenate([out_blocks[r] for r in order], axis=0)
    fc_blocks = gather_blocks(after(w_fc.astype(LOW), out_blocks[seq_size // 2 - 1]))
    fc_mat = jnp.concatenate([fc_blocks[r] for r in order], axis=0)
    proj_blocks = gather_blocks(after(w_proj.T.astype(LOW), fc_blocks[seq_size // 2 - 1]))
    proj_t = jnp.concatenate([proj_blocks[r] for r in order], axis=0)

    hidden_in = to_order(inputs)
    residual = hidden_in.astype(F32)
    centred, inverse = norm_parts(residual)
    normed = (centred * inverse * gain_one + shift_one).astype(LOW).reshape(-1, full_width)
    first_out = dot(normed, first_mat)
    queries = (first_out[:, :group_width] + query_bias).astype(LOW)
    queries = queries.reshape(batches, rows, group_width)
    keyval = (first_out[:, group_width:] + kv_bias).astype(LOW).reshape(batches, rows, 2 * hd)
    kv_blocks = gather_blocks(keyval)
    kv_all = jnp.stack([kv_blocks[r] for r in order], axis=1)
    mixed, lse = attend_forward(queries, kv_all, meta_q, meta_k, live)
    mixed_rows = mixed.reshape(-1, group_width)

    def quarters(array):
        return array.reshape(batches, tensor_size, quarter, array.shape[-1])

    def my_quarter(array):
        split = quarters(array)
        return lax.dynamic_index_in_dim(split, tensor_index, 1, keepdims=False)

    attn_part = quarters(dot_nt(mixed_rows, out_t))
    attn_sum = tensor_scatter(attn_part, 1)
    middle = my_quarter(hidden_in).astype(F32) + attn_sum + out_bias
    centred, inverse = norm_parts(middle)
    normed_q = (centred * inverse * gain_two + shift_two).astype(LOW)
    normed_two = tensor_gather(normed_q, 1).reshape(-1, full_width)
    hidden = dot(normed_two, fc_mat) + fc_local
    active_f, slope = gelu_pair(hidden)
    active = active_f.astype(LOW)

    grad_rows = to_order(grad_out)
    grad_flat = grad_rows.reshape(-1, full_width)
    grad_hidden = (slope * dot(grad_flat, proj_t)).astype(LOW)
    fcbias_local = jnp.sum(grad_hidden.astype(F32), axis=0)
    grad_normed_two = quarters(dot_nt(grad_hidden, fc_mat))
    back_sum = tensor_scatter(grad_normed_two, 1)
    grad_q = my_quarter(grad_rows).astype(F32)
    norm_part, gain_part = norm_back(middle, gain_two, back_sum)
    grad_middle = grad_q + norm_part
    grad_gain_two = jnp.sum(gain_part, axis=(0, 1))
    grad_shift_two = jnp.sum(back_sum, axis=(0, 1))
    grad_out_bias = jnp.sum(grad_middle, axis=(0, 1))
    grad_proj_bias = jnp.sum(grad_q, axis=(0, 1))
    grad_middle_low = tensor_gather(grad_middle.astype(LOW), 1).reshape(-1, full_width)

    def grads_by_block(left, right):
        return {
            r: dot_tn(left[:, p * width_block : (p + 1) * width_block], right)
            for p, r in enumerate(order)
        }

    proj_sum = scatter_blocks(grads_by_block(grad_flat, active))
    fc_sum = scatter_blocks(grads_by_block(normed_two, grad_hidden))

    ff_sum = tensor_scatter(quarters(dot_nt(active, proj_t)), 1)
    result_q = (middle + ff_sum + proj_bias).astype(LOW)
    result = from_order(tensor_gather(result_q, 1).reshape(batches, rows, full_width))

    grad_mixed = dot(grad_middle_low, out_t).astype(LOW).reshape(batches, rows, group_width)
    out_sum = scatter_blocks(grads_by_block(grad_middle_low, mixed_rows))
    grad_queries, grad_kv_all = attend_backward(
        queries, kv_all, meta_q, meta_k, live, mixed, lse, grad_mixed
    )
    grad_keyval = scatter_blocks({r: grad_kv_all[:, p].astype(F32) for p, r in enumerate(order)})
    grad_keyval = grad_keyval.astype(LOW).reshape(-1, 2 * hd)
    grad_queries = grad_queries.reshape(-1, group_width)
    grad_first = jnp.concatenate([grad_queries, grad_keyval], axis=1)
    first_sum = scatter_blocks(grads_by_block(normed, grad_first))
    grad_normed = quarters(dot_nt(grad_first, first_mat))
    in_sum = tensor_scatter(grad_normed, 1)
    residual_q = my_quarter(hidden_in).astype(F32)
    norm_part, gain_part = norm_back(residual_q, gain_one, in_sum)
    grad_in_q = (grad_middle + norm_part).astype(LOW)
    input_grad = from_order(tensor_gather(grad_in_q, 1).reshape(batches, rows, full_width))
    grad_gain_one = jnp.sum(gain_part, axis=(0, 1))
    grad_shift_one = jnp.sum(in_sum, axis=(0, 1))
    qbias_local = jnp.sum(grad_queries.astype(F32), axis=0)
    vbias_local = jnp.sum(grad_keyval[:, hd:].astype(F32), axis=0)

    qbias_full = lax.dynamic_update_slice_in_dim(
        jnp.zeros((full_width,), F32), qbias_local, tensor_index * group_width, 0
    )
    full_hidden = bias_shard * seq_size * tensor_size
    fcbias_full = lax.dynamic_update_slice_in_dim(
        jnp.zeros((full_hidden,), F32), fcbias_local, tensor_index * hidden_width, 0
    )
    grads_rel = jnp.stack(
        [
            grad_gain_one,
            grad_shift_one,
            to_order(qbias_full),
            grad_out_bias,
            grad_gain_two,
            grad_shift_two,
            grad_proj_bias,
        ]
    )
    chunk = full_hidden // seq_size
    small_rows = {}
    for p, r in enumerate(order):
        part = lax.dynamic_slice_in_dim(
            fcbias_full, jnp.bitwise_xor(seq_index, r) * chunk, chunk, 0
        )
        vec_part = grads_rel[:, p * width_block : (p + 1) * width_block].reshape(-1)
        row = jnp.concatenate([vec_part, part, vbias_local])
        small_rows[r] = jnp.pad(row, (0, -row.shape[0] % 1024)).reshape(-1, 128)
    for bit in range(bits_of(seq_size)):
        for r in sorted(small_rows):
            if r & (1 << bit):
                got = swap(small_rows.pop(r), "seq", bit)
                small_rows[r ^ (1 << bit)] = small_rows[r ^ (1 << bit)] + got
    small_sum = small_rows[0]
    for bit in range(bits_of(tensor_size)):
        small_sum = small_sum + swap(small_sum, "tensor", bit)
    small_sum = small_sum.reshape(-1)
    vec_cut = 7 * width_block
    vec_grad = lax.dynamic_slice_in_dim(
        small_sum[:vec_cut].reshape(7, width_block), tensor_index * shard, shard, 1
    )
    fcbias_grad = lax.dynamic_slice_in_dim(
        small_sum[vec_cut : vec_cut + chunk], tensor_index * bias_shard, bias_shard, 0
    )
    vbias_grad = small_sum[vec_cut + chunk : vec_cut + chunk + hd]

    query_grad = first_sum[:, :group_width]
    kv_part = first_sum[:, group_width:].reshape(tensor_size, -1, 2 * hd)
    keyval_grad = tensor_scatter(kv_part, 0)
    return (
        result,
        input_grad,
        query_grad,
        keyval_grad,
        out_sum.T,
        fc_sum,
        proj_sum.T,
        vec_grad,
        fcbias_grad,
        vbias_grad,
        vec_grad[5],
    )


def solution(mesh):
    in_specs = (
        P(None, "seq", None),
        P(None, "seq"),
        P(None, "seq"),
        P("seq", "tensor"),
        P(("seq", "tensor"), None),
        P("tensor", "seq"),
        P("seq", "tensor"),
        P("tensor", "seq"),
        P(None, ("seq", "tensor")),
        P(("seq", "tensor")),
        P(),
        P(None, "seq", None),
    )
    out_specs = (
        P(None, "seq", None),
        P(None, "seq", None),
        P("seq", "tensor"),
        P(("seq", "tensor"), None),
        P("tensor", "seq"),
        P("seq", "tensor"),
        P("tensor", "seq"),
        P(None, ("seq", "tensor")),
        P(("seq", "tensor")),
        P(),
        P(("seq", "tensor")),
    )
    return jax.shard_map(local, mesh=mesh, in_specs=in_specs, out_specs=out_specs, check_vma=False)
```

```python
from functools import partial

import jax
import jax.numpy as jnp
from jax import lax
from jax.experimental import pallas as pl
from jax.experimental.pallas import tpu as pltpu
from jax.sharding import PartitionSpec as P

EPS = 1e-05
NEG = -1e30
LOW = jnp.bfloat16
F32 = jnp.float32


def bits_of(count):
    return count.bit_length() - 1


def swap(value, axis, bit):
    count = lax.axis_size(axis)
    return lax.ppermute(value, axis, [(i, i ^ (1 << bit)) for i in range(count)])


def after(value, *others):
    return lax.optimization_barrier((value,) + others)[0]


def dot(left, right):
    return jnp.dot(left, right, preferred_element_type=F32)


def dot_tn(left, right):
    return lax.dot_general(left, right, (((0,), (0,)), ((), ())), preferred_element_type=F32)


def dot_nt(left, right):
    return lax.dot_general(left, right, (((1,), (1,)), ((), ())), preferred_element_type=F32)


MESH = pl.DeviceIdType.MESH


def flip(index, mask):
    bit = 1
    out = index
    while bit <= mask:
        if mask & bit:
            out = out + bit * (1 - 2 * lax.rem(lax.div(index, bit), 2))
        bit *= 2
    return out


class Wire:
    def __init__(self, send_sem, recv_sem):
        self.send_sem, self.recv_sem = send_sem, recv_sem
        self.started = []
        self.landed = set()

    def copy(self, src, dst, peer):
        place = len(self.started)
        item = pltpu.make_async_remote_copy(
            src_ref=src,
            dst_ref=dst,
            send_sem=self.send_sem.at[place],
            recv_sem=self.recv_sem.at[place],
            device_id=peer,
            device_id_type=MESH,
        )
        item.start()
        self.started.append(item)
        return place

    def arrived(self, place):
        if place not in self.landed:
            self.landed.add(place)
            self.started[place].wait_recv()

    def finish(self):
        for place in range(len(self.started)):
            self.arrived(place)
        for item in self.started:
            item.wait_send()


def greet(peers):
    barrier = pltpu.get_barrier_semaphore()
    for peer in peers:
        pl.semaphore_signal(barrier, inc=1, device_id=peer, device_id_type=MESH)
    pl.semaphore_wait(barrier, len(peers))


def seq_peers(index, count):
    return [{"seq": flip(index, 2 * d)} for d in range(1, count // 2)] + [
        {"seq": flip(index, 1)}
    ]


def weights_kernel(count, tensor, *refs):
    small_in, kv_in, q_in, o_in, fc_in, pj_in = refs[:6]
    small_out, kv_out, q_out, o_out, fc_out, pj_out = refs[6:12]
    send_sem, recv_sem, local_sem = refs[12:]
    index = lax.axis_index("seq")
    place = lax.axis_index("tensor")
    half = lax.rem(lax.div(index, 2), 2)
    over = [{"tensor": flip(place, d)} for d in range(1, tensor)]
    along = seq_peers(index, count)
    far, near = along[:-1], along[-1]
    greet(over + along)
    wire = Wire(send_sem, recv_sem)
    own = []

    def keep(src, dst):
        item = pltpu.make_async_copy(src, dst, local_sem.at[len(own)])
        item.start()
        own.append(item)

    first = [wire.copy(kv_in, kv_out.at[index, place], peer) for peer in over]
    first += [wire.copy(small_in, small_out.at[index, place], peer) for peer in over]
    keep(kv_in, kv_out.at[index, place])
    keep(small_in, small_out.at[index, place])
    hops = []

    def spread(source, out):
        handles = [wire.copy(source(d), out.at[index], far[d - 1]) for d in range(1, count // 2)]
        wire.copy(source(0), out.at[index], near)
        hops.append((out, handles))

    spread(lambda d: q_in, q_out)
    for item in first:
        wire.arrived(item)
    for item in own:
        item.wait()
    spread(lambda d: kv_out.at[index], kv_out)
    spread(lambda d: small_out.at[index], small_out)
    spread(lambda d: o_in, o_out)
    spread(lambda d: fc_in.at[flip(half, d & 1)], fc_out)
    spread(lambda d: pj_in.at[flip(half, d & 1)], pj_out)
    held = len(own)
    keep(q_in, q_out.at[index])
    keep(o_in, o_out.at[index])
    keep(fc_in.at[half], fc_out.at[index])
    keep(pj_in.at[half], pj_out.at[index])
    for out, handles in hops:
        for d, handle in enumerate(handles, 1):
            wire.arrived(handle)
            block = out.at[flip(index, 2 * d)]
            wire.copy(block, block, near)
    for item in own[held:]:
        item.wait()
    wire.finish()


def gather_weights(small, keyval, query, out, fc, proj):
    count, tensor = lax.axis_size("seq"), lax.axis_size("tensor")
    arrays = (small, keyval, query, out, fc, proj)
    shapes = [
        (count, tensor) + small.shape,
        (count, tensor) + keyval.shape,
        (count,) + query.shape,
        (count,) + out.shape,
        (count,) + fc.shape[1:],
        (count,) + proj.shape[1:],
    ]
    copies = 2 * (tensor - 1) + 6 * (count - 1)
    return pl.pallas_call(
        partial(weights_kernel, count, tensor),
        out_shape=[jax.ShapeDtypeStruct(shape, LOW) for shape in shapes],
        in_specs=[pl.BlockSpec(memory_space=pl.ANY)] * 6,
        out_specs=[pl.BlockSpec(memory_space=pl.ANY)] * 6,
        scratch_shapes=[
            pltpu.SemaphoreType.DMA((copies,)),
            pltpu.SemaphoreType.DMA((copies,)),
            pltpu.SemaphoreType.DMA((6,)),
        ],
        compiler_params=pltpu.CompilerParams(collective_id=0, has_side_effects=True),
        name="gather_weights",
    )(*arrays)


def keyval_kernel(count, kv_in, kv_out, send_sem, recv_sem, local_sem):
    index = lax.axis_index("seq")
    place = lax.axis_index("tensor")
    core = lax.rem(place, 2)
    other = {"tensor": flip(place, 1)}
    along = seq_peers(index, count)
    far, near = along[:-1], along[-1]
    greet([other] + along)
    wire = Wire(send_sem, recv_sem)
    handles = [
        wire.copy(kv_in.at[core], kv_out.at[core, index], far[d - 1]) for d in range(1, count // 2)
    ]
    own_near = wire.copy(kv_in.at[core], kv_out.at[core, index], near)
    own = []
    for batch in range(2):
        item = pltpu.make_async_copy(kv_in.at[batch], kv_out.at[batch, index], local_sem.at[batch])
        item.start()
        own.append(item)
    relays = [(1, own_near)]
    for d, handle in enumerate(handles, 1):
        wire.arrived(handle)
        block = kv_out.at[core, flip(index, 2 * d)]
        relays.append((2 * d + 1, wire.copy(block, block, near)))
        wire.copy(block, block, other)
    for r, handle in relays:
        wire.arrived(handle)
        block = kv_out.at[core, flip(index, r)]
        wire.copy(block, block, other)
    for item in own:
        item.wait()
    wire.finish()


def gather_keyval(keyval):
    count = lax.axis_size("seq")
    copies = 2 * (count - 1)
    batches, rows, two = keyval.shape
    return pl.pallas_call(
        partial(keyval_kernel, count),
        out_shape=jax.ShapeDtypeStruct((batches, count, rows, two), LOW),
        in_specs=[pl.BlockSpec(memory_space=pltpu.VMEM)],
        out_specs=pl.BlockSpec(memory_space=pltpu.VMEM),
        scratch_shapes=[
            pltpu.SemaphoreType.DMA((copies,)),
            pltpu.SemaphoreType.DMA((copies,)),
            pltpu.SemaphoreType.DMA((2,)),
        ],
        compiler_params=pltpu.CompilerParams(collective_id=1, has_side_effects=True),
        name="gather_keyval",
    )(keyval)


def scatter_kernel(count, split, arrays, *refs):
    parts = refs[:arrays]
    outs = refs[arrays : 2 * arrays]
    from_near = refs[2 * arrays : 3 * arrays]
    to_far = refs[3 * arrays : 4 * arrays]
    from_far = refs[4 * arrays : 5 * arrays]
    send_sem, recv_sem = refs[5 * arrays :]
    index = lax.axis_index("seq")
    half = lax.rem(lax.div(index, 2), 2)
    along = seq_peers(index, count)
    far, near = along[:-1], along[-1]
    lines = count // 2
    greet(along)
    wire = Wire(send_sem, recv_sem)
    turn = list(range(1, lines)) + [0]
    near_handles, far_handles = {}, {}
    for a in range(arrays):
        for d in turn:
            block = parts[a].at[flip(index, 2 * d + 1)]
            near_handles[a, d] = wire.copy(block, from_near[a].at[d], near)
    rows = parts[0].shape[1]
    step = min(64, rows)

    def by_rows(body):
        def run(i, carry):
            body(pl.ds(pl.multiple_of(i * step, step), step))
            return carry

        lax.fori_loop(0, rows // step, run, 0)

    for a in range(arrays):
        for d in range(1, lines):
            wire.arrived(near_handles[a, d])

            def join(at, a=a, d=d):
                total = parts[a][flip(index, 2 * d), at].astype(F32)
                total = total + from_near[a][d, at].astype(F32)
                to_far[a][d - 1, at] = total.astype(LOW)

            by_rows(join)
            far_handles[a, d] = wire.copy(to_far[a].at[d - 1], from_far[a].at[d - 1], far[d - 1])
    for a in range(arrays):
        wire.arrived(near_handles[a, 0])
        for d in range(1, lines):
            wire.arrived(far_handles[a, d])
        width = parts[a].shape[2]

        def total(at, a=a, width=width):
            same = parts[a][index, at].astype(F32) + from_near[a][0, at].astype(F32)
            other = None
            for d in range(1, lines):
                got = from_far[a][d - 1, at].astype(F32)
                if split and d % 2:
                    other = got if other is None else other + got
                else:
                    same = same + got
            if split:
                outs[a][at, pl.ds(pl.multiple_of(half * width, width), width)] = same
                outs[a][at, pl.ds(pl.multiple_of((1 - half) * width, width), width)] = other
            else:
                outs[a][at, :] = same

        by_rows(total)
    wire.finish()


def scatter_grads(parts, split, collective_id):
    count = lax.axis_size("seq")
    lines = count // 2
    arrays = len(parts)
    copies = arrays * (count - 1)
    scratch = []
    for depth in (lines, lines - 1, lines - 1):
        scratch += [pltpu.VMEM((depth,) + part.shape[1:], LOW) for part in parts]
    return pl.pallas_call(
        partial(scatter_kernel, count, split, arrays),
        out_shape=[
            jax.ShapeDtypeStruct((part.shape[1], part.shape[2] * (2 if split else 1)), F32)
            for part in parts
        ],
        in_specs=[pl.BlockSpec(memory_space=pltpu.VMEM)] * arrays,
        out_specs=[pl.BlockSpec(memory_space=pltpu.VMEM)] * arrays,
        scratch_shapes=scratch
        + [pltpu.SemaphoreType.DMA((copies,)), pltpu.SemaphoreType.DMA((copies,))],
        compiler_params=pltpu.CompilerParams(
            collective_id=collective_id, has_side_effects=True, vmem_limit_bytes=60 << 20
        ),
        name="scatter_grads",
    )(*parts)


def scatter_blocks(blocks):
    count = lax.axis_size("seq")
    blocks = dict(blocks)
    for bit in range(bits_of(count)):
        for r in sorted(blocks):
            if r & (1 << bit):
                arrived = swap(blocks.pop(r).astype(LOW), "seq", bit)
                blocks[r ^ (1 << bit)] = blocks[r ^ (1 << bit)] + arrived.astype(F32)
    return blocks[0]


def tensor_gather(own, axis):
    count = lax.axis_size("tensor")
    out = jnp.expand_dims(own, axis)
    for bit in reversed(range(bits_of(count))):
        out_other = swap(out, "tensor", bit)
        mine = (lax.axis_index("tensor") >> bit) & 1
        low_part = jnp.where(mine == 0, out, out_other)
        high_part = jnp.where(mine == 0, out_other, out)
        size = out.shape[axis]
        shape = out.shape
        low_part = jnp.expand_dims(low_part, axis)
        high_part = jnp.expand_dims(high_part, axis)
        out = jnp.concatenate([low_part, high_part], axis=axis)
        out = jnp.swapaxes(out, axis, axis + 1) if size > 1 else out
        out = out.reshape(shape[:axis] + (2 * size,) + shape[axis + 1 :])
    return out


def tensor_scatter(parts, axis):
    count = lax.axis_size("tensor")
    index = lax.axis_index("tensor")
    for bit in range(bits_of(count)):
        shape = parts.shape
        split = parts.reshape(shape[:axis] + (shape[axis] // 2, 2) + shape[axis + 1 :])
        mine = (index >> bit) & 1
        keep = lax.dynamic_index_in_dim(split, mine, axis + 1, keepdims=False)
        give = lax.dynamic_index_in_dim(split, 1 - mine, axis + 1, keepdims=False)
        parts = keep.astype(F32) + swap(give.astype(LOW), "tensor", bit).astype(F32)
    return lax.squeeze(parts, (axis,))


def visible(meta_q, meta_k):
    seg_q, pos_q = meta_q[:, 0:1], meta_q[:, 1:2]
    seg_k, pos_k = meta_k[0:1, :], meta_k[1:2, :]
    return ((seg_k == 0) | (seg_k == seg_q)) & (pos_k <= pos_q)


def forward_kernel(live_ref, q_ref, kv_ref, mq_ref, mk_ref, o_ref, lse_ref, top, total, acc):
    batch = pl.program_id(0)
    hd = kv_ref.shape[-1] // 2
    heads = q_ref.shape[-1] // hd
    blocks = kv_ref.shape[1]
    scale = float(hd) ** (-0.5)
    top[...] = jnp.full_like(top, NEG)
    total[...] = jnp.zeros_like(total)
    acc[...] = jnp.zeros_like(acc)

    def step(index, carry):
        @pl.when(live_ref[batch, index] > 0)
        def _():
            mask = visible(mq_ref[0], mk_ref[0, index])
            keys = kv_ref[0, index, :, :hd]
            values = kv_ref[0, index, :, hd:]
            for head in range(heads):
                cols = slice(head * hd, (head + 1) * hd)
                scores = jnp.where(mask, dot_nt(q_ref[0, :, cols], keys) * scale, NEG)
                before = top[head]
                now = jnp.maximum(before, jnp.max(scores, axis=-1, keepdims=True))
                shrink = jnp.exp(before - now)
                probs = jnp.exp(scores - now)
                total[head] = total[head] * shrink + jnp.sum(probs, axis=-1, keepdims=True)
                acc[:, cols] = acc[:, cols] * shrink + dot(probs.astype(LOW), values)
                top[head] = now

        return carry

    lax.fori_loop(0, blocks, step, 0)
    for head in range(heads):
        cols = slice(head * hd, (head + 1) * hd)
        o_ref[0, :, cols] = (acc[:, cols] / total[head]).astype(LOW)
        lse_ref[0, head] = top[head] + jnp.log(total[head])


def attend_forward(queries, keyval, meta_q, meta_k, live):
    batches, rows, width = queries.shape
    _, blocks, keys, two = keyval.shape
    hd = two // 2
    heads = width // hd
    flops = 4 * batches * rows * width * blocks * keys
    return pl.pallas_call(
        forward_kernel,
        grid_spec=pltpu.PrefetchScalarGridSpec(
            num_scalar_prefetch=1,
            grid=(batches,),
            in_specs=[
                pl.BlockSpec((1, rows, width), lambda b, live: (b, 0, 0)),
                pl.BlockSpec((1, blocks, keys, two), lambda b, live: (b, 0, 0, 0)),
                pl.BlockSpec((1, rows, 128), lambda b, live: (b, 0, 0)),
                pl.BlockSpec((1, blocks, 8, keys), lambda b, live: (b, 0, 0, 0)),
            ],
            out_specs=[
                pl.BlockSpec((1, rows, width), lambda b, live: (b, 0, 0)),
                pl.BlockSpec((1, heads, rows, 1), lambda b, live: (b, 0, 0, 0)),
            ],
            scratch_shapes=[
                pltpu.VMEM((heads, rows, 1), F32),
                pltpu.VMEM((heads, rows, 1), F32),
                pltpu.VMEM((rows, width), F32),
            ],
        ),
        out_shape=[
            jax.ShapeDtypeStruct((batches, rows, width), LOW),
            jax.ShapeDtypeStruct((batches, heads, rows, 1), F32),
        ],
        name="attend_forward",
        cost_estimate=pl.CostEstimate(
            flops=flops, transcendentals=0, bytes_accessed=2 * keyval.size
        ),
    )(live, queries, keyval, meta_q, meta_k)


def backward_kernel(
    live_ref, q_ref, kv_ref, mq_ref, mk_ref, o_ref, lse_ref, do_ref, dq_ref, dkv_ref, delta, acc
):
    batch = pl.program_id(0)
    hd = kv_ref.shape[-1] // 2
    heads = q_ref.shape[-1] // hd
    blocks = kv_ref.shape[1]
    scale = float(hd) ** (-0.5)
    acc[...] = jnp.zeros_like(acc)
    for head in range(heads):
        cols = slice(head * hd, (head + 1) * hd)
        delta[head] = jnp.sum(
            do_ref[0, :, cols].astype(F32) * o_ref[0, :, cols].astype(F32), axis=-1, keepdims=True
        )

    def step(index, carry):
        @pl.when(live_ref[batch, index] > 0)
        def _():
            mask = visible(mq_ref[0], mk_ref[0, index])
            keys = kv_ref[0, index, :, :hd]
            values = kv_ref[0, index, :, hd:]
            grad_k = jnp.zeros((keys.shape[0], hd), F32)
            grad_v = jnp.zeros((keys.shape[0], hd), F32)
            for head in range(heads):
                cols = slice(head * hd, (head + 1) * hd)
                query = q_ref[0, :, cols]
                grad_o = do_ref[0, :, cols]
                scores = dot_nt(query, keys) * scale
                probs = jnp.where(mask, jnp.exp(scores - lse_ref[0, head]), 0.0)
                grad_p = dot_nt(grad_o, values)
                grad_s = (probs * (grad_p - delta[head])).astype(LOW)
                acc[:, cols] += dot(grad_s, keys)
                grad_k = grad_k + dot_tn(grad_s, query)
                grad_v = grad_v + dot_tn(probs.astype(LOW), grad_o)
            dkv_ref[0, index, :, :hd] = (grad_k * scale).astype(LOW)
            dkv_ref[0, index, :, hd:] = grad_v.astype(LOW)

        @pl.when(live_ref[batch, index] == 0)
        def _():
            dkv_ref[0, index] = jnp.zeros(dkv_ref.shape[2:], LOW)

        return carry

    lax.fori_loop(0, blocks, step, 0)
    dq_ref[0] = (acc[...] * scale).astype(LOW)


def attend_backward(queries, keyval, meta_q, meta_k, live, mixed, lse, grad_mixed):
    batches, rows, width = queries.shape
    _, blocks, keys, two = keyval.shape
    hd = two // 2
    heads = width // hd
    flops = 10 * batches * rows * width * blocks * keys
    row_spec = pl.BlockSpec((1, rows, width), lambda b, live: (b, 0, 0))
    kv_spec = pl.BlockSpec((1, blocks, keys, two), lambda b, live: (b, 0, 0, 0))
    return pl.pallas_call(
        backward_kernel,
        grid_spec=pltpu.PrefetchScalarGridSpec(
            num_scalar_prefetch=1,
            grid=(batches,),
            in_specs=[
                row_spec,
                kv_spec,
                pl.BlockSpec((1, rows, 128), lambda b, live: (b, 0, 0)),
                pl.BlockSpec((1, blocks, 8, keys), lambda b, live: (b, 0, 0, 0)),
                row_spec,
                pl.BlockSpec((1, heads, rows, 1), lambda b, live: (b, 0, 0, 0)),
                row_spec,
            ],
            out_specs=[row_spec, kv_spec],
            scratch_shapes=[
                pltpu.VMEM((heads, rows, 1), F32),
                pltpu.VMEM((rows, width), F32),
            ],
        ),
        out_shape=[
            jax.ShapeDtypeStruct((batches, rows, width), LOW),
            jax.ShapeDtypeStruct((batches, blocks, keys, two), LOW),
        ],
        name="attend_backward",
        cost_estimate=pl.CostEstimate(
            flops=flops, transcendentals=0, bytes_accessed=4 * keyval.size
        ),
    )(live, queries, keyval, meta_q, meta_k, mixed, lse, grad_mixed)


def norm_parts(values):
    average = jnp.mean(values, axis=-1, keepdims=True)
    centred = values - average
    spread = jnp.mean(centred * centred, axis=-1, keepdims=True)
    return centred, lax.rsqrt(spread + EPS)


def norm_back(values, gain, grad):
    centred, inverse = norm_parts(values)
    unit = centred * inverse
    scaled = grad * gain
    inner = (
        scaled
        - jnp.mean(scaled, axis=-1, keepdims=True)
        - unit * jnp.mean(scaled * unit, axis=-1, keepdims=True)
    )
    return inverse * inner, grad * unit


def gelu_pair(values):
    const = 0.7978845608028654
    square = values * values
    inner = jnp.tanh(const * (values + 0.044715 * (values * square)))
    half = 0.5 * (1.0 + inner)
    slope = half + 0.5 * values * (1.0 - inner * inner) * const * (1.0 + 3 * 0.044715 * square)
    return values * half, slope


def local(
    inputs,
    segment,
    position,
    w_query,
    w_keyval,
    w_out,
    w_fc,
    w_proj,
    vectors,
    fc_bias,
    value_bias,
    grad_out,
):
    seq_size, tensor_size = lax.axis_size("seq"), lax.axis_size("tensor")
    seq_index, tensor_index = lax.axis_index("seq"), lax.axis_index("tensor")
    batches, rows, full_width = inputs.shape
    width_block = w_query.shape[0]
    group_width = w_query.shape[1]
    hidden_width = w_fc.shape[1]
    unit_width = hidden_width // 2
    unit_half = (seq_index >> 1) & 1
    hd = value_bias.shape[0]
    quarter = rows // tensor_size
    shard = vectors.shape[1]
    bias_shard = fc_bias.shape[0]

    pieces = [
        vectors.reshape(-1).astype(LOW),
        fc_bias.astype(LOW),
        segment.reshape(-1).astype(LOW),
        (position // 128).reshape(-1).astype(LOW),
        (position % 128).reshape(-1).astype(LOW),
    ]
    cuts = [0]
    for piece in pieces:
        cuts.append(cuts[-1] + piece.shape[0])
    packed = jnp.concatenate(pieces)
    packed = jnp.pad(packed, (0, -packed.shape[0] % 2048)).reshape(-1, 128)

    def halves(array):
        return jnp.swapaxes(array.astype(LOW).reshape(width_block, 2, unit_width), 0, 1)

    small, kv_mat, q_mat, out_t, fc_mat, proj_t = gather_weights(
        packed,
        w_keyval.astype(LOW),
        w_query.astype(LOW),
        w_out.T.astype(LOW),
        halves(w_fc),
        halves(w_proj.T),
    )
    kv_mat = kv_mat.reshape(full_width, 2 * hd)
    q_mat = q_mat.reshape(full_width, group_width)
    out_t = out_t.reshape(full_width, group_width)
    fc_mat = fc_mat.reshape(full_width, unit_width)
    proj_t = proj_t.reshape(full_width, unit_width)

    small = small.reshape(seq_size, tensor_size, -1).astype(F32)
    vec_all = small[:, :, cuts[0] : cuts[1]].reshape(seq_size * tensor_size, 7, shard)
    vec_all = jnp.swapaxes(vec_all, 0, 1).reshape(7, full_width)
    fc_all = small[:, :, cuts[1] : cuts[2]].reshape(-1)
    seg_keys = small[:, 0, cuts[2] : cuts[3]].reshape(seq_size, batches, rows)
    pos_keys = 128.0 * small[:, 0, cuts[3] : cuts[4]] + small[:, 0, cuts[4] : cuts[5]]
    seg_keys = jnp.swapaxes(seg_keys, 0, 1).astype(jnp.int32)
    pos_keys = jnp.swapaxes(pos_keys.reshape(seq_size, batches, rows), 0, 1).astype(jnp.int32)
    meta_k = jnp.pad(jnp.stack([seg_keys, pos_keys], axis=2), ((0, 0), (0, 0), (0, 6), (0, 0)))
    meta_q = jnp.pad(jnp.stack([segment, position], axis=2), ((0, 0), (0, 0), (0, 126)))
    seg_lo, seg_hi = jnp.min(seg_keys, axis=2), jnp.max(seg_keys, axis=2)
    own_lo = jnp.min(segment, axis=1, keepdims=True)
    own_hi = jnp.max(segment, axis=1, keepdims=True)
    live = (
        ((seg_lo == 0) | ((seg_lo <= own_hi) & (own_lo <= seg_hi)))
        & (jnp.min(pos_keys, axis=2) <= jnp.max(position, axis=1, keepdims=True))
    ).astype(jnp.int32)

    gain_one, shift_one, _, out_bias, gain_two, shift_two, proj_bias = [
        vec_all[i] for i in range(7)
    ]
    query_bias = lax.dynamic_slice_in_dim(vec_all[2], tensor_index * group_width, group_width, 0)
    fc_local = lax.dynamic_slice_in_dim(
        fc_all, tensor_index * hidden_width + unit_half * unit_width, unit_width, 0
    )
    bias_value = value_bias.astype(LOW).astype(F32)
    kv_bias = jnp.concatenate([jnp.zeros((hd,), F32), bias_value])

    residual = inputs.astype(F32)
    centred, inverse = norm_parts(residual)
    normed = (centred * inverse * gain_one + shift_one).astype(LOW).reshape(-1, full_width)
    keyval = (dot(normed, kv_mat) + kv_bias).astype(LOW).reshape(batches, rows, 2 * hd)
    kv_all = gather_keyval(keyval)
    queries = (dot(normed, q_mat) + query_bias).astype(LOW)
    queries = queries.reshape(batches, rows, group_width)
    mixed, lse = attend_forward(queries, kv_all, meta_q, meta_k, live)
    mixed_rows = mixed.reshape(-1, group_width)

    def quarters(array):
        return array.reshape(-1, batches, tensor_size, quarter, array.shape[-1])

    def my_quarter(array):
        split = array.reshape(batches, tensor_size, quarter, full_width)
        return lax.dynamic_index_in_dim(split, tensor_index, 1, keepdims=False)

    def pair_gather(own):
        both = jnp.stack([own, swap(own, "seq", 1)])
        return tensor_gather(both, 2).reshape(-1, full_width)

    def pair_scatter(part):
        split = quarters(part)
        got = tensor_scatter(split, 2)
        return got[0] + swap(got[1].astype(LOW), "seq", 1).astype(F32)

    attn_sum = tensor_scatter(quarters(dot_nt(mixed_rows, out_t)), 2)[0]
    middle = my_quarter(inputs).astype(F32) + attn_sum + out_bias
    centred, inverse = norm_parts(middle)
    normed_q = (centred * inverse * gain_two + shift_two).astype(LOW)
    normed_two = pair_gather(normed_q)
    hidden = dot(normed_two, fc_mat) + fc_local
    active_f, slope = gelu_pair(hidden)
    active = active_f.astype(LOW)

    grad_q_low = my_quarter(grad_out)
    grad_flat = jnp.concatenate(
        [grad_out.reshape(-1, full_width), swap(grad_out.reshape(-1, full_width), "seq", 1)]
    )
    grad_hidden = (slope * dot(grad_flat, proj_t)).astype(LOW)
    fcbias_local = jnp.sum(grad_hidden.astype(F32), axis=0)
    back_sum = pair_scatter(dot_nt(grad_hidden, fc_mat))
    grad_q = grad_q_low.astype(F32)
    norm_part, gain_part = norm_back(middle, gain_two, back_sum)
    grad_middle = grad_q + norm_part
    grad_gain_two = jnp.sum(gain_part, axis=(0, 1))
    grad_shift_two = jnp.sum(back_sum, axis=(0, 1))
    grad_out_bias = jnp.sum(grad_middle, axis=(0, 1))
    grad_proj_bias = jnp.sum(grad_q, axis=(0, 1))
    grad_middle_low = tensor_gather(grad_middle.astype(LOW), 1).reshape(-1, full_width)

    def blocked(array):
        return array.astype(LOW).reshape(seq_size, width_block, array.shape[-1])

    proj_sum, fc_sum = scatter_grads(
        [blocked(dot_tn(grad_flat, active)), blocked(dot_tn(normed_two, grad_hidden))], True, 2
    )

    ff_sum = pair_scatter(dot_nt(active, proj_t))
    result_q = (middle + ff_sum + proj_bias).astype(LOW)
    result = tensor_gather(result_q, 1).reshape(batches, rows, full_width)

    grad_mixed = dot(grad_middle_low, out_t).astype(LOW).reshape(batches, rows, group_width)
    grad_queries, grad_kv_all = attend_backward(
        queries, kv_all, meta_q, meta_k, live, mixed, lse, grad_mixed
    )
    grad_keyval = scatter_blocks(
        {
            r: lax.dynamic_index_in_dim(
                grad_kv_all, jnp.bitwise_xor(seq_index, r), 1, keepdims=False
            ).astype(F32)
            for r in range(seq_size)
        }
    )
    grad_keyval = grad_keyval.astype(LOW).reshape(-1, 2 * hd)
    grad_queries = grad_queries.reshape(-1, group_width)
    out_sum, query_sum, kv_sum = scatter_grads(
        [
            blocked(dot_tn(grad_middle_low, mixed_rows)),
            blocked(dot_tn(normed, grad_queries)),
            blocked(dot_tn(normed, grad_keyval)),
        ],
        False,
        3,
    )
    grad_normed = dot_nt(grad_queries, q_mat) + dot_nt(grad_keyval, kv_mat)
    in_sum = tensor_scatter(quarters(grad_normed), 2)[0]
    residual_q = my_quarter(inputs).astype(F32)
    norm_part, gain_part = norm_back(residual_q, gain_one, in_sum)
    grad_in_q = (grad_middle + norm_part).astype(LOW)
    input_grad = tensor_gather(grad_in_q, 1).reshape(batches, rows, full_width)
    grad_gain_one = jnp.sum(gain_part, axis=(0, 1))
    grad_shift_one = jnp.sum(in_sum, axis=(0, 1))
    qbias_local = jnp.sum(grad_queries.astype(F32), axis=0)
    vbias_local = jnp.sum(grad_keyval[:, hd:].astype(F32), axis=0)

    qbias_full = lax.dynamic_update_slice_in_dim(
        jnp.zeros((full_width,), F32), qbias_local, tensor_index * group_width, 0
    )
    full_hidden = bias_shard * seq_size * tensor_size
    fcbias_full = lax.dynamic_update_slice_in_dim(
        jnp.zeros((full_hidden,), F32),
        fcbias_local,
        tensor_index * hidden_width + unit_half * unit_width,
        0,
    )
    vec_grads = jnp.stack(
        [
            grad_gain_one,
            grad_shift_one,
            qbias_full,
            grad_out_bias,
            grad_gain_two,
            grad_shift_two,
            grad_proj_bias,
        ]
    )
    chunk = full_hidden // seq_size
    vec_cut = 7 * width_block
    rows_all = jnp.concatenate(
        [
            jnp.swapaxes(vec_grads.reshape(7, seq_size, width_block), 0, 1).reshape(seq_size, -1),
            fcbias_full.reshape(seq_size, chunk),
            jnp.broadcast_to(vbias_local, (seq_size, hd)),
        ],
        axis=1,
    )
    rows_all = jnp.pad(rows_all, ((0, 0), (0, -rows_all.shape[1] % 1024)))
    rows_all = rows_all.reshape(seq_size, -1, 128)
    for bit in reversed(range(bits_of(seq_size))):
        size = rows_all.shape[0] // 2
        mine = (seq_index >> bit) & 1
        keep = lax.dynamic_slice_in_dim(rows_all, mine * size, size, 0)
        give = lax.dynamic_slice_in_dim(rows_all, (1 - mine) * size, size, 0)
        rows_all = keep + swap(give, "seq", bit)
    small_sum = rows_all[0]
    for bit in range(bits_of(tensor_size)):
        small_sum = small_sum + swap(small_sum, "tensor", bit)
    small_sum = small_sum.reshape(-1)
    vec_grad = lax.dynamic_slice_in_dim(
        small_sum[:vec_cut].reshape(7, width_block), tensor_index * shard, shard, 1
    )
    fcbias_grad = lax.dynamic_slice_in_dim(
        small_sum[vec_cut : vec_cut + chunk], tensor_index * bias_shard, bias_shard, 0
    )
    vbias_grad = small_sum[vec_cut + chunk : vec_cut + chunk + hd]
    keyval_grad = tensor_scatter(kv_sum.reshape(tensor_size, -1, 2 * hd), 0)
    return (
        result,
        input_grad,
        query_sum,
        keyval_grad,
        out_sum.T,
        fc_sum,
        proj_sum.T,
        vec_grad,
        fcbias_grad,
        vbias_grad,
        vec_grad[5],
    )


def solution(mesh):
    in_specs = (
        P(None, "seq", None),
        P(None, "seq"),
        P(None, "seq"),
        P("seq", "tensor"),
        P(("seq", "tensor"), None),
        P("tensor", "seq"),
        P("seq", "tensor"),
        P("tensor", "seq"),
        P(None, ("seq", "tensor")),
        P(("seq", "tensor")),
        P(),
        P(None, "seq", None),
    )
    out_specs = (
        P(None, "seq", None),
        P(None, "seq", None),
        P("seq", "tensor"),
        P(("seq", "tensor"), None),
        P("tensor", "seq"),
        P("seq", "tensor"),
        P("tensor", "seq"),
        P(None, ("seq", "tensor")),
        P(("seq", "tensor")),
        P(),
        P(("seq", "tensor")),
    )
    return jax.shard_map(local, mesh=mesh, in_specs=in_specs, out_specs=out_specs, check_vma=False)
```

```python
from functools import partial

import jax
import jax.numpy as jnp
from jax import lax
from jax.experimental import pallas as pl
from jax.experimental.pallas import tpu as pltpu
from jax.sharding import PartitionSpec as P

EPS = 1e-05
NEG = -1e30
LOG2E = 1.4426950408889634
LOW = jnp.bfloat16
F32 = jnp.float32


def bits_of(count):
    return count.bit_length() - 1


def swap(value, axis, bit):
    count = lax.axis_size(axis)
    return lax.ppermute(value, axis, [(i, i ^ (1 << bit)) for i in range(count)])


def after(value, *others):
    return lax.optimization_barrier((value,) + others)[0]


def dot(left, right):
    return jnp.dot(left, right, preferred_element_type=F32)


def dot_tn(left, right):
    return lax.dot_general(left, right, (((0,), (0,)), ((), ())), preferred_element_type=F32)


def dot_nt(left, right):
    return lax.dot_general(left, right, (((1,), (1,)), ((), ())), preferred_element_type=F32)


MESH = pl.DeviceIdType.MESH


def flip(index, mask):
    bit = 1
    out = index
    while bit <= mask:
        if mask & bit:
            out = out + bit * (1 - 2 * lax.rem(lax.div(index, bit), 2))
        bit *= 2
    return out


class Wire:
    def __init__(self, send_sem, recv_sem):
        self.send_sem, self.recv_sem = send_sem, recv_sem
        self.started = []
        self.landed = set()

    def copy(self, src, dst, peer):
        place = len(self.started)
        item = pltpu.make_async_remote_copy(
            src_ref=src,
            dst_ref=dst,
            send_sem=self.send_sem.at[place],
            recv_sem=self.recv_sem.at[place],
            device_id=peer,
            device_id_type=MESH,
        )
        item.start()
        self.started.append(item)
        return place

    def arrived(self, place):
        if place not in self.landed:
            self.landed.add(place)
            self.started[place].wait_recv()

    def finish(self):
        for place in range(len(self.started)):
            self.arrived(place)
        for item in self.started:
            item.wait_send()


def greet(peers):
    barrier = pltpu.get_barrier_semaphore()
    for peer in peers:
        pl.semaphore_signal(barrier, inc=1, device_id=peer, device_id_type=MESH)
    pl.semaphore_wait(barrier, len(peers))


def seq_peers(index, count):
    return [{"seq": flip(index, 2 * d)} for d in range(1, count // 2)] + [
        {"seq": flip(index, 1)}
    ]


def first_kernel(count, tensor, *refs):
    ins, outs = refs[:3], refs[3:6]
    send_sem, recv_sem, local_sem = refs[6:]
    index = lax.axis_index("seq")
    place = lax.axis_index("tensor")
    across = [{"tensor": flip(place, tensor >> (i + 1))} for i in range(bits_of(tensor))]
    along = seq_peers(index, count)
    far, near = along[:-1], along[-1]
    greet(across + along)
    wire = Wire(send_sem, recv_sem)
    own = []
    targets = [(lambda at, out=out: out.at[at, place]) for out in outs[:2]]
    targets.append(lambda at: outs[2].at[at])
    handles = []
    for source, target in zip(ins, targets):
        handles.append([wire.copy(source, target(index), peer) for peer in far])
        handles[-1].append(wire.copy(source, target(index), near))
        item = pltpu.make_async_copy(source, target(index), local_sem.at[len(own)])
        item.start()
        own.append(item)
    relays = []
    for a, target in enumerate(targets):
        for d in range(1, count // 2):
            wire.arrived(handles[a][d - 1])
            block = target(flip(index, 2 * d))
            relays.append(wire.copy(block, block, near))
        if a == 1:
            for handle in [handles[0][-1], handles[1][-1]] + relays:
                wire.arrived(handle)
            own[0].wait()
            own[1].wait()
            masks = [0]
            for i, peer in enumerate(across):
                step = tensor >> (i + 1)
                sent = [
                    wire.copy(out.at[:, flip(place, mask)], out.at[:, flip(place, mask)], peer)
                    for mask in masks
                    for out in outs[:2]
                ]
                masks = masks + [mask | step for mask in masks]
                if i + 1 < len(across):
                    for handle in sent:
                        wire.arrived(handle)
    own[2].wait()
    wire.finish()


def gather_first(small, keyval, query):
    count, tensor = lax.axis_size("seq"), lax.axis_size("tensor")
    arrays = (small, keyval, query)
    shapes = [
        (count, tensor) + small.shape,
        (count, tensor) + keyval.shape,
        (count,) + query.shape,
    ]
    copies = 3 * (count - 1) + 2 * (tensor - 1)
    return pl.pallas_call(
        partial(first_kernel, count, tensor),
        out_shape=[jax.ShapeDtypeStruct(shape, LOW) for shape in shapes],
        in_specs=[pl.BlockSpec(memory_space=pltpu.VMEM)] * 3,
        out_specs=[pl.BlockSpec(memory_space=pltpu.VMEM)] * 3,
        scratch_shapes=[
            pltpu.SemaphoreType.DMA((copies,)),
            pltpu.SemaphoreType.DMA((copies,)),
            pltpu.SemaphoreType.DMA((3,)),
        ],
        compiler_params=pltpu.CompilerParams(collective_id=0, has_side_effects=True),
        name="gather_first",
    )(*arrays)


def front_kernel(count, *refs):
    q_in, kv_in, mq_in, mk_in, x_in, vec_in, o_in, fc_in, pj_in, dy_in = refs[:10]
    mixed, lse, kv_all, out_t, middle, rows_two, fc_out, pj_out, dy_out = refs[10:19]
    (
        top,
        total,
        acc,
        core_keep,
        core_send,
        core_got,
        y_send,
        y_got,
        send_sem,
        recv_sem,
        local_sem,
    ) = refs[19:]
    index = lax.axis_index("seq")
    place = lax.axis_index("tensor")
    core = lax.rem(place, 2)
    side = lax.div(place, 2)
    half = lax.rem(lax.div(index, 2), 2)
    other_core = {"tensor": flip(place, 1)}
    other_side = {"tensor": flip(place, 2)}
    across = {"tensor": flip(place, 3)}
    along = seq_peers(index, count)
    far, near = along[:-1], along[-1]
    pair = far[0]
    lines = count // 2
    greet(along + [other_core, other_side, across])
    wire = Wire(send_sem, recv_sem)
    own = []

    def keep(src, dst):
        item = pltpu.make_async_copy(src, dst, local_sem.at[len(own)])
        item.start()
        own.append(item)

    kv_far = [wire.copy(kv_in.at[core], kv_all.at[core, index], peer) for peer in far]
    kv_near = wire.copy(kv_in.at[core], kv_all.at[core, index], near)
    for batch in range(2):
        keep(kv_in.at[batch], kv_all.at[batch, index])
    o_far = [wire.copy(o_in, out_t.at[index], peer) for peer in far]
    o_near = [wire.copy(o_in, out_t.at[index], near)]
    keep(o_in, out_t.at[index])
    dy_pair = wire.copy(dy_in.at[place], dy_out.at[place], pair)

    def send_far(source, out):
        return [
            wire.copy(source.at[flip(half, d & 1)], out.at[index], far[d - 1])
            for d in range(1, lines)
        ]

    fc_far = send_far(fc_in, fc_out)
    kv_near = [(1, kv_near)]
    kv_core = []
    for d in range(1, lines):
        wire.arrived(kv_far[d - 1])
        block = kv_all.at[core, flip(index, 2 * d)]
        kv_near.append((2 * d + 1, wire.copy(block, block, near)))
        kv_core.append(wire.copy(block, block, other_core))
    wire.copy(fc_in.at[half], fc_out.at[index], near)
    wire.copy(pj_in.at[half], pj_out.at[index], near)
    keep(fc_in.at[half], fc_out.at[index])
    keep(pj_in.at[half], pj_out.at[index])
    for r, handle in kv_near:
        wire.arrived(handle)
        block = kv_all.at[core, flip(index, r)]
        kv_core.append(wire.copy(block, block, other_core))
    own[0].wait()
    own[1].wait()

    jobs = [(o_far, out_t, d) for d in range(1, lines)]
    jobs += [(fc_far, fc_out, d) for d in range(1, lines)]

    def tick(number):
        for _ in range(min(number, len(jobs))):
            handles, out, d = jobs.pop(0)
            wire.arrived(handles[d - 1])
            block = out.at[flip(index, 2 * d)]
            handle = wire.copy(block, block, near)
            if out is out_t:
                o_near.append(handle)

    hd = kv_in.shape[-1] // 2
    heads = q_in.shape[-1] // hd
    scale = float(hd) ** (-0.5) * LOG2E

    def attend(batch, block):
        mask = visible(mq_in[batch], mk_in[batch, block])
        keys = kv_all[batch, block, :, :hd]
        values = kv_all[batch, block, :, hd:]
        for head in range(heads):
            cols = slice(head * hd, (head + 1) * hd)
            scores = jnp.where(mask, dot_nt(q_in[batch, :, cols], keys) * scale, NEG)
            before = top[head]
            now = jnp.maximum(before, jnp.max(scores, axis=-1, keepdims=True))
            shrink = jnp.exp2(before - now)
            probs = jnp.exp2(scores - now)
            total[head] = total[head] * shrink + jnp.sum(probs, axis=-1, keepdims=True)
            acc[:, cols] = acc[:, cols] * shrink + dot(probs.astype(LOW), values)
            top[head] = now

    def attend_batch(batch, ticks):
        top[...] = jnp.full_like(top, NEG)
        total[...] = jnp.zeros_like(total)
        acc[...] = jnp.zeros_like(acc)

        def block_body(block, carry):
            attend(batch, block)
            return carry

        parts = len(ticks)
        for i in range(parts):
            lax.fori_loop(i * count // parts, (i + 1) * count // parts, block_body, 0)
            tick(ticks[i])
        for head in range(heads):
            cols = slice(head * hd, (head + 1) * hd)
            mixed[batch, :, cols] = (acc[:, cols] / total[head]).astype(LOW)
            lse[batch, head] = top[head] + jnp.log2(total[head])

    spread = lines - 1
    attend_batch(core, [spread // 3, spread - spread // 3])
    for handle in kv_core:
        wire.arrived(handle)
    attend_batch(1 - core, [0, spread // 3])
    wire.arrived(dy_pair)
    for peer in (other_core, other_side, across):
        wire.copy(dy_out.at[place], dy_out.at[place], peer)

    quarter = x_in.shape[0] // 2
    for handle in o_near:
        wire.arrived(handle)
    own[2].wait()
    width = out_t.shape[1]
    group = max(1, 256 // width)
    for which, target in ((1 - core, core_send), (core, core_keep)):
        rows = [
            mixed[batch, pl.ds(pl.multiple_of((2 * s + which) * quarter, quarter), quarter), :]
            for s in range(2)
            for batch in range(2)
        ]
        rows = jnp.concatenate(rows, axis=0)

        def project(i, carry, rows=rows, target=target):
            cols = pl.ds(pl.multiple_of(i * group * width, group * width), group * width)
            block = out_t[pl.ds(i * group, group)].reshape(group * width, -1)
            target[:, cols] = dot_nt(rows, block).astype(target.dtype)
            return carry

        lax.fori_loop(0, count // group, project, 0)
        if target is core_send:
            core_handle = wire.copy(core_send, core_got, other_core)
    wire.arrived(core_handle)
    part = 2 * quarter
    step = 16

    def to_side(i, carry):
        at = pl.ds(pl.multiple_of((1 - side) * part + i * step, step), step)
        y_send[pl.ds(pl.multiple_of(i * step, step), step), :] = (
            core_keep[at, :] + core_got[at, :].astype(F32)
        ).astype(LOW)
        return carry

    lax.fori_loop(0, part // step, to_side, 0)
    y_handle = wire.copy(y_send, y_got, other_side)
    tick(spread - spread // 3 - 1)
    wire.arrived(y_handle)
    out_bias, gain_two, shift_two = vec_in[0:1, :], vec_in[1:2, :], vec_in[2:3, :]

    def norm(i, carry):
        at = pl.ds(pl.multiple_of(i * step, step), step)
        far_at = pl.ds(pl.multiple_of(side * part + i * step, step), step)
        value = core_keep[far_at, :] + core_got[far_at, :].astype(F32)
        value = value + y_got[at, :].astype(F32)
        value = x_in[at, :].astype(F32) + value + out_bias
        middle[at, :] = value
        centred, inverse = norm_parts(value)
        rows_two[0, place, at, :] = (centred * inverse * gain_two + shift_two).astype(LOW)
        return carry

    lax.fori_loop(0, part // step, norm, 0)
    mine = rows_two.at[0, place]
    pair_handle = wire.copy(mine, rows_two.at[1, place], pair)
    side_handle = wire.copy(mine, mine, other_side)
    wire.copy(mine, mine, other_core)
    pj_far = send_far(pj_in, pj_out)
    tick(len(jobs))
    jobs.extend((pj_far, pj_out, d) for d in range(1, lines))
    wire.arrived(pair_handle)
    theirs = rows_two.at[1, place]
    side_two = wire.copy(theirs, theirs, other_side)
    wire.copy(theirs, theirs, other_core)
    wire.arrived(side_handle)
    block = rows_two.at[0, flip(place, 2)]
    wire.copy(block, block, other_core)
    wire.arrived(side_two)
    block = rows_two.at[1, flip(place, 2)]
    wire.copy(block, block, other_core)
    tick(len(jobs))
    for item in own[3:]:
        item.wait()
    wire.finish()


def front(queries, keyval, meta_q, meta_k, own_rows, vecs, out, fc, proj, grad_rows):
    count = lax.axis_size("seq")
    tensor = lax.axis_size("tensor")
    batches, rows, width = queries.shape
    two = keyval.shape[2]
    heads = 2 * width // two
    part, full = own_rows.shape
    shapes = [
        ((batches, rows, width), LOW),
        ((batches, heads, rows, 1), F32),
        ((batches, count, rows, two), LOW),
        ((count,) + out.shape, LOW),
        ((part, full), F32),
        ((2, tensor, part, full), LOW),
        ((count,) + fc.shape[1:], LOW),
        ((count,) + proj.shape[1:], LOW),
        ((tensor, part, full), LOW),
    ]
    copies = 2 * (count - 1) + 3 * (count - 1) + 4 + 2 + 7
    vmem, hbm = pl.BlockSpec(memory_space=pltpu.VMEM), pl.BlockSpec(memory_space=pl.ANY)
    return pl.pallas_call(
        partial(front_kernel, count),
        out_shape=[jax.ShapeDtypeStruct(shape, dtype) for shape, dtype in shapes],
        in_specs=[vmem] * 6 + [hbm] * 4,
        out_specs=[vmem] * 6 + [hbm] * 3,
        scratch_shapes=[
            pltpu.VMEM((heads, rows, 1), F32),
            pltpu.VMEM((heads, rows, 1), F32),
            pltpu.VMEM((rows, width), F32),
            pltpu.VMEM((2 * part, full), F32),
            pltpu.VMEM((2 * part, full), LOW),
            pltpu.VMEM((2 * part, full), LOW),
            pltpu.VMEM((part, full), LOW),
            pltpu.VMEM((part, full), LOW),
            pltpu.SemaphoreType.DMA((copies,)),
            pltpu.SemaphoreType.DMA((copies,)),
            pltpu.SemaphoreType.DMA((5,)),
        ],
        compiler_params=pltpu.CompilerParams(
            collective_id=1, has_side_effects=True, vmem_limit_bytes=56 << 20
        ),
        name="front",
    )(queries, keyval, meta_q, meta_k, own_rows, vecs, out, fc, proj, grad_rows)


def scatter_kernel(count, split, arrays, *refs):
    parts = refs[:arrays]
    outs = refs[arrays : 2 * arrays]
    from_near = refs[2 * arrays : 3 * arrays]
    to_far = refs[3 * arrays : 4 * arrays]
    from_far = refs[4 * arrays : 5 * arrays]
    send_sem, recv_sem = refs[5 * arrays :]
    index = lax.axis_index("seq")
    half = lax.rem(lax.div(index, 2), 2)
    along = seq_peers(index, count)
    far, near = along[:-1], along[-1]
    lines = count // 2
    greet(along)
    wire = Wire(send_sem, recv_sem)
    turn = list(range(1, lines)) + [0]
    near_handles, far_handles = {}, {}
    for a in range(arrays):
        for d in turn:
            block = parts[a].at[flip(index, 2 * d + 1)]
            near_handles[a, d] = wire.copy(block, from_near[a].at[d], near)
    rows = parts[0].shape[1]
    step = min(64, rows)

    def by_rows(body):
        def run(i, carry):
            body(pl.ds(pl.multiple_of(i * step, step), step))
            return carry

        lax.fori_loop(0, rows // step, run, 0)

    for a in range(arrays):
        for d in range(1, lines):
            wire.arrived(near_handles[a, d])

            def join(at, a=a, d=d):
                total = parts[a][flip(index, 2 * d), at].astype(F32)
                total = total + from_near[a][d, at].astype(F32)
                to_far[a][d - 1, at] = total.astype(LOW)

            by_rows(join)
            far_handles[a, d] = wire.copy(to_far[a].at[d - 1], from_far[a].at[d - 1], far[d - 1])
    for a in range(arrays):
        wire.arrived(near_handles[a, 0])
        for d in range(1, lines):
            wire.arrived(far_handles[a, d])
        width = parts[a].shape[2]

        def total(at, a=a, width=width):
            same = parts[a][index, at].astype(F32) + from_near[a][0, at].astype(F32)
            other = None
            for d in range(1, lines):
                got = from_far[a][d - 1, at].astype(F32)
                if split and d % 2:
                    other = got if other is None else other + got
                else:
                    same = same + got
            if split:
                outs[a][at, pl.ds(pl.multiple_of(half * width, width), width)] = same
                outs[a][at, pl.ds(pl.multiple_of((1 - half) * width, width), width)] = other
            else:
                outs[a][at, :] = same

        by_rows(total)
    wire.finish()


def scatter_grads(parts, split, collective_id):
    count = lax.axis_size("seq")
    lines = count // 2
    arrays = len(parts)
    copies = arrays * (count - 1)
    scratch = []
    for depth in (lines, lines - 1, lines - 1):
        scratch += [pltpu.VMEM((depth,) + part.shape[1:], LOW) for part in parts]
    return pl.pallas_call(
        partial(scatter_kernel, count, split, arrays),
        out_shape=[
            jax.ShapeDtypeStruct((part.shape[1], part.shape[2] * (2 if split else 1)), F32)
            for part in parts
        ],
        in_specs=[pl.BlockSpec(memory_space=pltpu.VMEM)] * arrays,
        out_specs=[pl.BlockSpec(memory_space=pltpu.VMEM)] * arrays,
        scratch_shapes=scratch
        + [pltpu.SemaphoreType.DMA((copies,)), pltpu.SemaphoreType.DMA((copies,))],
        compiler_params=pltpu.CompilerParams(
            collective_id=collective_id, has_side_effects=True, vmem_limit_bytes=60 << 20
        ),
        name="scatter_grads",
    )(*parts)


def scatter_blocks(blocks):
    count = lax.axis_size("seq")
    blocks = dict(blocks)
    for bit in range(bits_of(count)):
        for r in sorted(blocks):
            if r & (1 << bit):
                arrived = swap(blocks.pop(r).astype(LOW), "seq", bit)
                blocks[r ^ (1 << bit)] = blocks[r ^ (1 << bit)] + arrived.astype(F32)
    return blocks[0]


def tensor_gather(own, axis):
    count = lax.axis_size("tensor")
    out = jnp.expand_dims(own, axis)
    for bit in reversed(range(bits_of(count))):
        out_other = swap(out, "tensor", bit)
        mine = (lax.axis_index("tensor") >> bit) & 1
        low_part = jnp.where(mine == 0, out, out_other)
        high_part = jnp.where(mine == 0, out_other, out)
        size = out.shape[axis]
        shape = out.shape
        low_part = jnp.expand_dims(low_part, axis)
        high_part = jnp.expand_dims(high_part, axis)
        out = jnp.concatenate([low_part, high_part], axis=axis)
        out = jnp.swapaxes(out, axis, axis + 1) if size > 1 else out
        out = out.reshape(shape[:axis] + (2 * size,) + shape[axis + 1 :])
    return out


def tensor_scatter(parts, axis):
    count = lax.axis_size("tensor")
    index = lax.axis_index("tensor")
    for bit in range(bits_of(count)):
        shape = parts.shape
        split = parts.reshape(shape[:axis] + (shape[axis] // 2, 2) + shape[axis + 1 :])
        mine = (index >> bit) & 1
        keep = lax.dynamic_index_in_dim(split, mine, axis + 1, keepdims=False)
        give = lax.dynamic_index_in_dim(split, 1 - mine, axis + 1, keepdims=False)
        parts = keep.astype(F32) + swap(give.astype(LOW), "tensor", bit).astype(F32)
    return lax.squeeze(parts, (axis,))


def visible(meta_q, meta_k):
    seg_q, pos_q = meta_q[:, 0:1], meta_q[:, 1:2]
    seg_k, pos_k = meta_k[0:1, :], meta_k[1:2, :]
    return ((seg_k == 0) | (seg_k == seg_q)) & (pos_k <= pos_q)


def backward_kernel(
    live_ref, q_ref, kv_ref, mq_ref, mk_ref, o_ref, lse_ref, do_ref, dq_ref, dkv_ref, delta, acc
):
    batch = pl.program_id(0)
    hd = kv_ref.shape[-1] // 2
    heads = q_ref.shape[-1] // hd
    blocks = kv_ref.shape[1]
    scale = float(hd) ** (-0.5)
    scale_two = scale * LOG2E
    acc[...] = jnp.zeros_like(acc)
    for head in range(heads):
        cols = slice(head * hd, (head + 1) * hd)
        delta[head] = jnp.sum(
            do_ref[0, :, cols].astype(F32) * o_ref[0, :, cols].astype(F32), axis=-1, keepdims=True
        )

    def step(index, carry):
        @pl.when(live_ref[batch, index] > 0)
        def _():
            mask = visible(mq_ref[0], mk_ref[0, index])
            keys = kv_ref[0, index, :, :hd]
            values = kv_ref[0, index, :, hd:]
            grad_k = jnp.zeros((keys.shape[0], hd), F32)
            grad_v = jnp.zeros((keys.shape[0], hd), F32)
            for head in range(heads):
                cols = slice(head * hd, (head + 1) * hd)
                query = q_ref[0, :, cols]
                grad_o = do_ref[0, :, cols]
                scores = dot_nt(query, keys) * scale_two
                probs = jnp.where(mask, jnp.exp2(scores - lse_ref[0, head]), 0.0)
                grad_p = dot_nt(grad_o, values)
                grad_s = (probs * (grad_p - delta[head])).astype(LOW)
                acc[:, cols] += dot(grad_s, keys)
                grad_k = grad_k + dot_tn(grad_s, query)
                grad_v = grad_v + dot_tn(probs.astype(LOW), grad_o)
            dkv_ref[0, index, :, :hd] = (grad_k * scale).astype(LOW)
            dkv_ref[0, index, :, hd:] = grad_v.astype(LOW)

        @pl.when(live_ref[batch, index] == 0)
        def _():
            dkv_ref[0, index] = jnp.zeros(dkv_ref.shape[2:], LOW)

        return carry

    lax.fori_loop(0, blocks, step, 0)
    dq_ref[0] = (acc[...] * scale).astype(LOW)


def attend_backward(queries, keyval, meta_q, meta_k, live, mixed, lse, grad_mixed):
    batches, rows, width = queries.shape
    _, blocks, keys, two = keyval.shape
    hd = two // 2
    heads = width // hd
    flops = 10 * batches * rows * width * blocks * keys
    row_spec = pl.BlockSpec((1, rows, width), lambda b, live: (b, 0, 0))
    kv_spec = pl.BlockSpec((1, blocks, keys, two), lambda b, live: (b, 0, 0, 0))
    return pl.pallas_call(
        backward_kernel,
        grid_spec=pltpu.PrefetchScalarGridSpec(
            num_scalar_prefetch=1,
            grid=(batches,),
            in_specs=[
                row_spec,
                kv_spec,
                pl.BlockSpec((1, rows, 128), lambda b, live: (b, 0, 0)),
                pl.BlockSpec((1, blocks, 8, keys), lambda b, live: (b, 0, 0, 0)),
                row_spec,
                pl.BlockSpec((1, heads, rows, 1), lambda b, live: (b, 0, 0, 0)),
                row_spec,
            ],
            out_specs=[row_spec, kv_spec],
            scratch_shapes=[
                pltpu.VMEM((heads, rows, 1), F32),
                pltpu.VMEM((rows, width), F32),
            ],
        ),
        out_shape=[
            jax.ShapeDtypeStruct((batches, rows, width), LOW),
            jax.ShapeDtypeStruct((batches, blocks, keys, two), LOW),
        ],
        name="attend_backward",
        cost_estimate=pl.CostEstimate(
            flops=flops, transcendentals=0, bytes_accessed=4 * keyval.size
        ),
    )(live, queries, keyval, meta_q, meta_k, mixed, lse, grad_mixed)


def norm_parts(values):
    average = jnp.mean(values, axis=-1, keepdims=True)
    centred = values - average
    spread = jnp.mean(centred * centred, axis=-1, keepdims=True)
    return centred, lax.rsqrt(spread + EPS)


def norm_back(values, gain, grad):
    centred, inverse = norm_parts(values)
    unit = centred * inverse
    scaled = grad * gain
    inner = (
        scaled
        - jnp.mean(scaled, axis=-1, keepdims=True)
        - unit * jnp.mean(scaled * unit, axis=-1, keepdims=True)
    )
    return inverse * inner, grad * unit


def gelu_pair(values):
    const = 0.7978845608028654
    square = values * values
    inner = jnp.tanh(const * (values + 0.044715 * (values * square)))
    half = 0.5 * (1.0 + inner)
    slope = half + 0.5 * values * (1.0 - inner * inner) * const * (1.0 + 3 * 0.044715 * square)
    return values * half, slope


def local(
    inputs,
    segment,
    position,
    w_query,
    w_keyval,
    w_out,
    w_fc,
    w_proj,
    vectors,
    fc_bias,
    value_bias,
    grad_out,
):
    seq_size, tensor_size = lax.axis_size("seq"), lax.axis_size("tensor")
    seq_index, tensor_index = lax.axis_index("seq"), lax.axis_index("tensor")
    batches, rows, full_width = inputs.shape
    width_block = w_query.shape[0]
    group_width = w_query.shape[1]
    hidden_width = w_fc.shape[1]
    unit_width = hidden_width // 2
    unit_half = (seq_index >> 1) & 1
    hd = value_bias.shape[0]
    quarter = rows // tensor_size
    shard = vectors.shape[1]
    bias_shard = fc_bias.shape[0]

    pieces = [
        vectors.reshape(-1).astype(LOW),
        fc_bias.astype(LOW),
        segment.reshape(-1).astype(LOW),
        (position // 128).reshape(-1).astype(LOW),
        (position % 128).reshape(-1).astype(LOW),
    ]
    cuts = [0]
    for piece in pieces:
        cuts.append(cuts[-1] + piece.shape[0])
    packed = jnp.concatenate(pieces)
    packed = jnp.pad(packed, (0, -packed.shape[0] % 2048)).reshape(-1, 128)

    def halves(array):
        return jnp.swapaxes(array.astype(LOW).reshape(width_block, 2, unit_width), 0, 1)

    small, kv_mat, q_mat = gather_first(packed, w_keyval.astype(LOW), w_query.astype(LOW))
    kv_mat = kv_mat.reshape(full_width, 2 * hd)
    q_mat = q_mat.reshape(full_width, group_width)

    small = small.reshape(seq_size, tensor_size, -1).astype(F32)
    vec_all = small[:, :, cuts[0] : cuts[1]].reshape(seq_size * tensor_size, 7, shard)
    vec_all = jnp.swapaxes(vec_all, 0, 1).reshape(7, full_width)
    fc_all = small[:, :, cuts[1] : cuts[2]].reshape(-1)
    seg_keys = small[:, 0, cuts[2] : cuts[3]].reshape(seq_size, batches, rows)
    pos_keys = 128.0 * small[:, 0, cuts[3] : cuts[4]] + small[:, 0, cuts[4] : cuts[5]]
    seg_keys = jnp.swapaxes(seg_keys, 0, 1).astype(jnp.int32)
    pos_keys = jnp.swapaxes(pos_keys.reshape(seq_size, batches, rows), 0, 1).astype(jnp.int32)
    meta_k = jnp.pad(jnp.stack([seg_keys, pos_keys], axis=2), ((0, 0), (0, 0), (0, 6), (0, 0)))
    meta_q = jnp.pad(jnp.stack([segment, position], axis=2), ((0, 0), (0, 0), (0, 126)))
    seg_lo, seg_hi = jnp.min(seg_keys, axis=2), jnp.max(seg_keys, axis=2)
    own_lo = jnp.min(segment, axis=1, keepdims=True)
    own_hi = jnp.max(segment, axis=1, keepdims=True)
    live = (
        ((seg_lo == 0) | ((seg_lo <= own_hi) & (own_lo <= seg_hi)))
        & (jnp.min(pos_keys, axis=2) <= jnp.max(position, axis=1, keepdims=True))
    ).astype(jnp.int32)

    gain_one, shift_one, _, out_bias, gain_two, shift_two, proj_bias = [
        vec_all[i] for i in range(7)
    ]
    query_bias = lax.dynamic_slice_in_dim(vec_all[2], tensor_index * group_width, group_width, 0)
    fc_local = lax.dynamic_slice_in_dim(
        fc_all, tensor_index * hidden_width + unit_half * unit_width, unit_width, 0
    )
    bias_value = value_bias.astype(LOW).astype(F32)
    kv_bias = jnp.concatenate([jnp.zeros((hd,), F32), bias_value])

    residual = inputs.astype(F32)
    centred, inverse = norm_parts(residual)
    normed = (centred * inverse * gain_one + shift_one).astype(LOW).reshape(-1, full_width)
    keyval = (dot(normed, kv_mat) + kv_bias).astype(LOW).reshape(batches, rows, 2 * hd)
    queries = (dot(normed, q_mat) + query_bias).astype(LOW)
    queries = queries.reshape(batches, rows, group_width)

    def by_quarter(array):
        split = array.reshape(batches, tensor_size, quarter, array.shape[-1])
        return jnp.swapaxes(split, 0, 1).reshape(tensor_size, batches * quarter, -1)

    def by_batch(array):
        split = array.reshape(tensor_size, batches, quarter, array.shape[-1])
        return jnp.swapaxes(split, 0, 1).reshape(batches, rows, -1)

    def my_quarter(array):
        split = array.reshape(batches, tensor_size, quarter, full_width)
        own = lax.dynamic_index_in_dim(split, tensor_index, 1, keepdims=False)
        return own.reshape(batches * quarter, full_width)

    def pair_scatter(part):
        got = tensor_scatter(part.reshape(2, tensor_size, batches * quarter, full_width), 1)
        return got[0] + swap(got[1].astype(LOW), "seq", 1).astype(F32)

    vecs = jnp.pad(jnp.stack([out_bias, gain_two, shift_two]), ((0, 5), (0, 0)))
    grad_split = by_quarter(grad_out)
    mixed, lse, kv_all, out_t, middle, rows_two, fc_mat, proj_t, grad_other = front(
        queries,
        keyval,
        meta_q,
        meta_k,
        my_quarter(inputs),
        vecs,
        w_out.T.astype(LOW),
        halves(w_fc),
        halves(w_proj.T),
        grad_split,
    )
    out_t = out_t.reshape(full_width, group_width)
    fc_mat = fc_mat.reshape(full_width, unit_width)
    proj_t = proj_t.reshape(full_width, unit_width)
    mixed_rows = by_quarter(mixed).reshape(-1, group_width)
    normed_two = rows_two.reshape(-1, full_width)
    hidden = dot(normed_two, fc_mat) + fc_local
    active_f, slope = gelu_pair(hidden)
    active = active_f.astype(LOW)

    grad_q_low = my_quarter(grad_out)
    grad_flat = jnp.concatenate([grad_split, grad_other]).reshape(-1, full_width)
    grad_hidden = (slope * dot(grad_flat, proj_t)).astype(LOW)
    fcbias_local = jnp.sum(grad_hidden.astype(F32), axis=0)
    back_sum = pair_scatter(dot_nt(grad_hidden, fc_mat))
    grad_q = grad_q_low.astype(F32)
    norm_part, gain_part = norm_back(middle, gain_two, back_sum)
    grad_middle = grad_q + norm_part
    grad_gain_two = jnp.sum(gain_part, axis=0)
    grad_shift_two = jnp.sum(back_sum, axis=0)
    grad_out_bias = jnp.sum(grad_middle, axis=0)
    grad_proj_bias = jnp.sum(grad_q, axis=0)
    grad_middle_low = tensor_gather(grad_middle.astype(LOW), 0).reshape(-1, full_width)

    def blocked(array):
        return array.astype(LOW).reshape(seq_size, width_block, array.shape[-1])

    proj_sum, fc_sum = scatter_grads(
        [blocked(dot_tn(grad_flat, active)), blocked(dot_tn(normed_two, grad_hidden))], True, 2
    )

    ff_sum = pair_scatter(dot_nt(active, proj_t))
    result_q = (middle + ff_sum + proj_bias).astype(LOW)
    result = by_batch(tensor_gather(result_q, 0))

    grad_mixed = by_batch(dot(grad_middle_low, out_t).astype(LOW))
    grad_queries, grad_kv_all = attend_backward(
        queries, kv_all, meta_q, meta_k, live, mixed, lse, grad_mixed
    )
    grad_keyval = scatter_blocks(
        {
            r: lax.dynamic_index_in_dim(
                grad_kv_all, jnp.bitwise_xor(seq_index, r), 1, keepdims=False
            ).astype(F32)
            for r in range(seq_size)
        }
    )
    grad_keyval = grad_keyval.astype(LOW).reshape(-1, 2 * hd)
    grad_queries = grad_queries.reshape(-1, group_width)
    out_sum, query_sum, kv_sum = scatter_grads(
        [
            blocked(dot_tn(grad_middle_low, mixed_rows)),
            blocked(dot_tn(normed, grad_queries)),
            blocked(dot_tn(normed, grad_keyval)),
        ],
        False,
        3,
    )
    grad_normed = dot_nt(grad_queries, q_mat) + dot_nt(grad_keyval, kv_mat)
    in_sum = tensor_scatter(by_quarter(grad_normed), 0)
    residual_q = my_quarter(inputs).astype(F32)
    norm_part, gain_part = norm_back(residual_q, gain_one, in_sum)
    grad_in_q = (grad_middle + norm_part).astype(LOW)
    input_grad = by_batch(tensor_gather(grad_in_q, 0))
    grad_gain_one = jnp.sum(gain_part, axis=0)
    grad_shift_one = jnp.sum(in_sum, axis=0)
    qbias_local = jnp.sum(grad_queries.astype(F32), axis=0)
    vbias_local = jnp.sum(grad_keyval[:, hd:].astype(F32), axis=0)

    qbias_full = lax.dynamic_update_slice_in_dim(
        jnp.zeros((full_width,), F32), qbias_local, tensor_index * group_width, 0
    )
    full_hidden = bias_shard * seq_size * tensor_size
    fcbias_full = lax.dynamic_update_slice_in_dim(
        jnp.zeros((full_hidden,), F32),
        fcbias_local,
        tensor_index * hidden_width + unit_half * unit_width,
        0,
    )
    vec_grads = jnp.stack(
        [
            grad_gain_one,
            grad_shift_one,
            qbias_full,
            grad_out_bias,
            grad_gain_two,
            grad_shift_two,
            grad_proj_bias,
        ]
    )
    chunk = full_hidden // seq_size
    vec_cut = 7 * width_block
    rows_all = jnp.concatenate(
        [
            jnp.swapaxes(vec_grads.reshape(7, seq_size, width_block), 0, 1).reshape(seq_size, -1),
            fcbias_full.reshape(seq_size, chunk),
            jnp.broadcast_to(vbias_local, (seq_size, hd)),
        ],
        axis=1,
    )
    rows_all = jnp.pad(rows_all, ((0, 0), (0, -rows_all.shape[1] % 1024)))
    rows_all = rows_all.reshape(seq_size, -1, 128)
    for bit in reversed(range(bits_of(seq_size))):
        size = rows_all.shape[0] // 2
        mine = (seq_index >> bit) & 1
        keep = lax.dynamic_slice_in_dim(rows_all, mine * size, size, 0)
        give = lax.dynamic_slice_in_dim(rows_all, (1 - mine) * size, size, 0)
        rows_all = keep + swap(give, "seq", bit)
    small_sum = rows_all[0]
    for bit in range(bits_of(tensor_size)):
        small_sum = small_sum + swap(small_sum, "tensor", bit)
    small_sum = small_sum.reshape(-1)
    vec_grad = lax.dynamic_slice_in_dim(
        small_sum[:vec_cut].reshape(7, width_block), tensor_index * shard, shard, 1
    )
    fcbias_grad = lax.dynamic_slice_in_dim(
        small_sum[vec_cut : vec_cut + chunk], tensor_index * bias_shard, bias_shard, 0
    )
    vbias_grad = small_sum[vec_cut + chunk : vec_cut + chunk + hd]
    keyval_grad = tensor_scatter(kv_sum.reshape(tensor_size, -1, 2 * hd), 0)
    return (
        result,
        input_grad,
        query_sum,
        keyval_grad,
        out_sum.T,
        fc_sum,
        proj_sum.T,
        vec_grad,
        fcbias_grad,
        vbias_grad,
        vec_grad[5],
    )


def solution(mesh):
    in_specs = (
        P(None, "seq", None),
        P(None, "seq"),
        P(None, "seq"),
        P("seq", "tensor"),
        P(("seq", "tensor"), None),
        P("tensor", "seq"),
        P("seq", "tensor"),
        P("tensor", "seq"),
        P(None, ("seq", "tensor")),
        P(("seq", "tensor")),
        P(),
        P(None, "seq", None),
    )
    out_specs = (
        P(None, "seq", None),
        P(None, "seq", None),
        P("seq", "tensor"),
        P(("seq", "tensor"), None),
        P("tensor", "seq"),
        P("seq", "tensor"),
        P("tensor", "seq"),
        P(None, ("seq", "tensor")),
        P(("seq", "tensor")),
        P(),
        P(("seq", "tensor")),
    )
    return jax.shard_map(local, mesh=mesh, in_specs=in_specs, out_specs=out_specs, check_vma=False)
```

```python
from functools import partial

import jax
import jax.numpy as jnp
from jax import lax
from jax.experimental import pallas as pl
from jax.experimental.pallas import tpu as pltpu
from jax.sharding import PartitionSpec as P

EPS = 1e-05
NEG = -1e30
LOG2E = 1.4426950408889634
LOW = jnp.bfloat16
F32 = jnp.float32


def bits_of(count):
    return count.bit_length() - 1


def swap(value, axis, bit):
    count = lax.axis_size(axis)
    return lax.ppermute(value, axis, [(i, i ^ (1 << bit)) for i in range(count)])


def after(value, *others):
    return lax.optimization_barrier((value,) + others)[0]


def dot(left, right):
    return jnp.dot(left, right, preferred_element_type=F32)


def dot_tn(left, right):
    return lax.dot_general(left, right, (((0,), (0,)), ((), ())), preferred_element_type=F32)


def dot_nt(left, right):
    return lax.dot_general(left, right, (((1,), (1,)), ((), ())), preferred_element_type=F32)


MESH = pl.DeviceIdType.MESH


def flip(index, mask):
    bit = 1
    out = index
    while bit <= mask:
        if mask & bit:
            out = out + bit * (1 - 2 * lax.rem(lax.div(index, bit), 2))
        bit *= 2
    return out


class Wire:
    def __init__(self, send_sem, recv_sem):
        self.send_sem, self.recv_sem = send_sem, recv_sem
        self.started = []
        self.landed = set()

    def copy(self, src, dst, peer):
        place = len(self.started)
        item = pltpu.make_async_remote_copy(
            src_ref=src,
            dst_ref=dst,
            send_sem=self.send_sem.at[place],
            recv_sem=self.recv_sem.at[place],
            device_id=peer,
            device_id_type=MESH,
        )
        item.start()
        self.started.append(item)
        return place

    def arrived(self, place):
        if place not in self.landed:
            self.landed.add(place)
            self.started[place].wait_recv()

    def finish(self):
        for place in range(len(self.started)):
            self.arrived(place)
        for item in self.started:
            item.wait_send()


def greet(peers):
    barrier = pltpu.get_barrier_semaphore()
    for peer in peers:
        pl.semaphore_signal(barrier, inc=1, device_id=peer, device_id_type=MESH)
    pl.semaphore_wait(barrier, len(peers))


def seq_peers(index, count):
    return [{"seq": flip(index, 2 * d)} for d in range(1, count // 2)] + [
        {"seq": flip(index, 1)}
    ]


def first_kernel(count, tensor, *refs):
    ins, outs = refs[:3], refs[3:6]
    send_sem, recv_sem, local_sem = refs[6:]
    index = lax.axis_index("seq")
    place = lax.axis_index("tensor")
    across = [{"tensor": flip(place, tensor >> (i + 1))} for i in range(bits_of(tensor))]
    along = seq_peers(index, count)
    far, near = along[:-1], along[-1]
    greet(across + along)
    wire = Wire(send_sem, recv_sem)
    own = []
    targets = [(lambda at, out=out: out.at[at, place]) for out in outs[:2]]
    targets.append(lambda at: outs[2].at[at])
    handles = []
    for source, target in zip(ins, targets):
        handles.append([wire.copy(source, target(index), peer) for peer in far])
        handles[-1].append(wire.copy(source, target(index), near))
        item = pltpu.make_async_copy(source, target(index), local_sem.at[len(own)])
        item.start()
        own.append(item)
    relays = []
    for a, target in enumerate(targets):
        for d in range(1, count // 2):
            wire.arrived(handles[a][d - 1])
            block = target(flip(index, 2 * d))
            relays.append(wire.copy(block, block, near))
        if a == 1:
            for handle in [handles[0][-1], handles[1][-1]] + relays:
                wire.arrived(handle)
            own[0].wait()
            own[1].wait()
            masks = [0]
            for i, peer in enumerate(across):
                step = tensor >> (i + 1)
                sent = [
                    wire.copy(out.at[:, flip(place, mask)], out.at[:, flip(place, mask)], peer)
                    for mask in masks
                    for out in outs[:2]
                ]
                masks = masks + [mask | step for mask in masks]
                if i + 1 < len(across):
                    for handle in sent:
                        wire.arrived(handle)
    own[2].wait()
    wire.finish()


def gather_first(small, keyval, query):
    count, tensor = lax.axis_size("seq"), lax.axis_size("tensor")
    arrays = (small, keyval, query)
    shapes = [
        (count, tensor) + small.shape,
        (count, tensor) + keyval.shape,
        (count,) + query.shape,
    ]
    copies = 3 * (count - 1) + 2 * (tensor - 1)
    return pl.pallas_call(
        partial(first_kernel, count, tensor),
        out_shape=[jax.ShapeDtypeStruct(shape, LOW) for shape in shapes],
        in_specs=[pl.BlockSpec(memory_space=pltpu.VMEM)] * 3,
        out_specs=[pl.BlockSpec(memory_space=pltpu.VMEM)] * 3,
        scratch_shapes=[
            pltpu.SemaphoreType.DMA((copies,)),
            pltpu.SemaphoreType.DMA((copies,)),
            pltpu.SemaphoreType.DMA((3,)),
        ],
        compiler_params=pltpu.CompilerParams(collective_id=0, has_side_effects=True),
        name="gather_first",
    )(*arrays)


def front_kernel(count, *refs):
    q_in, kv_in, mq_in, mk_in, x_in, vec_in, o_in, fc_in, pj_in, dy_in = refs[:10]
    mixed, lse, kv_all, out_t, middle, rows_two, fc_out, pj_out, dy_out = refs[10:19]
    (
        top,
        total,
        acc,
        core_keep,
        core_send,
        core_got,
        y_send,
        y_got,
        send_sem,
        recv_sem,
        local_sem,
    ) = refs[19:]
    index = lax.axis_index("seq")
    place = lax.axis_index("tensor")
    core = lax.rem(place, 2)
    side = lax.div(place, 2)
    half = lax.rem(lax.div(index, 2), 2)
    other_core = {"tensor": flip(place, 1)}
    other_side = {"tensor": flip(place, 2)}
    across = {"tensor": flip(place, 3)}
    along = seq_peers(index, count)
    far, near = along[:-1], along[-1]
    pair = far[0]
    lines = count // 2
    greet(along + [other_core, other_side, across])
    wire = Wire(send_sem, recv_sem)
    own = []

    def keep(src, dst):
        item = pltpu.make_async_copy(src, dst, local_sem.at[len(own)])
        item.start()
        own.append(item)

    kv_far = [wire.copy(kv_in.at[core], kv_all.at[core, index], peer) for peer in far]
    kv_near = wire.copy(kv_in.at[core], kv_all.at[core, index], near)
    for batch in range(2):
        keep(kv_in.at[batch], kv_all.at[batch, index])
    o_far = [wire.copy(o_in, out_t.at[index], peer) for peer in far]
    o_near = [wire.copy(o_in, out_t.at[index], near)]
    keep(o_in, out_t.at[index])
    dy_pair = wire.copy(dy_in.at[place], dy_out.at[place], pair)

    def send_far(source, out):
        return [
            wire.copy(source.at[flip(half, d & 1)], out.at[index], far[d - 1])
            for d in range(1, lines)
        ]

    fc_far = send_far(fc_in, fc_out)
    kv_near = [(1, kv_near)]
    kv_core = []
    for d in range(1, lines):
        wire.arrived(kv_far[d - 1])
        block = kv_all.at[core, flip(index, 2 * d)]
        kv_near.append((2 * d + 1, wire.copy(block, block, near)))
        kv_core.append(wire.copy(block, block, other_core))
    wire.copy(fc_in.at[half], fc_out.at[index], near)
    wire.copy(pj_in.at[half], pj_out.at[index], near)
    keep(fc_in.at[half], fc_out.at[index])
    keep(pj_in.at[half], pj_out.at[index])
    for r, handle in kv_near:
        wire.arrived(handle)
        block = kv_all.at[core, flip(index, r)]
        kv_core.append(wire.copy(block, block, other_core))
    own[0].wait()
    own[1].wait()

    jobs = [(o_far, out_t, d) for d in range(1, lines)]
    jobs += [(fc_far, fc_out, d) for d in range(1, lines)]

    def tick(number):
        for _ in range(min(number, len(jobs))):
            handles, out, d = jobs.pop(0)
            wire.arrived(handles[d - 1])
            block = out.at[flip(index, 2 * d)]
            handle = wire.copy(block, block, near)
            if out is out_t:
                o_near.append(handle)

    hd = kv_in.shape[-1] // 2
    heads = q_in.shape[-1] // hd
    scale = float(hd) ** (-0.5) * LOG2E

    def attend(batch, block):
        mask = visible(mq_in[batch], mk_in[batch, block])
        keys = kv_all[batch, block, :, :hd]
        values = kv_all[batch, block, :, hd:]
        for head in range(heads):
            cols = slice(head * hd, (head + 1) * hd)
            scores = jnp.where(mask, dot_nt(q_in[batch, :, cols], keys) * scale, NEG)
            before = top[head]
            now = jnp.maximum(before, jnp.max(scores, axis=-1, keepdims=True))
            shrink = jnp.exp2(before - now)
            probs = jnp.exp2(scores - now)
            total[head] = total[head] * shrink + jnp.sum(probs, axis=-1, keepdims=True)
            acc[:, cols] = acc[:, cols] * shrink + dot(probs.astype(LOW), values)
            top[head] = now

    def attend_batch(batch, ticks):
        top[...] = jnp.full_like(top, NEG)
        total[...] = jnp.zeros_like(total)
        acc[...] = jnp.zeros_like(acc)

        def block_body(block, carry):
            attend(batch, block)
            return carry

        parts = len(ticks)
        for i in range(parts):
            lax.fori_loop(i * count // parts, (i + 1) * count // parts, block_body, 0)
            tick(ticks[i])
        for head in range(heads):
            cols = slice(head * hd, (head + 1) * hd)
            mixed[batch, :, cols] = (acc[:, cols] / total[head]).astype(LOW)
            lse[batch, head] = top[head] + jnp.log2(total[head])

    spread = lines - 1
    attend_batch(core, [spread // 3, spread - spread // 3])
    for handle in kv_core:
        wire.arrived(handle)
    attend_batch(1 - core, [0, spread // 3])
    wire.arrived(dy_pair)
    for peer in (other_core, other_side, across):
        wire.copy(dy_out.at[place], dy_out.at[place], peer)

    quarter = x_in.shape[0] // 2
    for handle in o_near:
        wire.arrived(handle)
    own[2].wait()
    width = out_t.shape[1]
    group = max(1, 256 // width)
    for which, target in ((1 - core, core_send), (core, core_keep)):
        rows = [
            mixed[batch, pl.ds(pl.multiple_of((2 * s + which) * quarter, quarter), quarter), :]
            for s in range(2)
            for batch in range(2)
        ]
        rows = jnp.concatenate(rows, axis=0)

        def project(i, carry, rows=rows, target=target):
            cols = pl.ds(pl.multiple_of(i * group * width, group * width), group * width)
            block = out_t[pl.ds(i * group, group)].reshape(group * width, -1)
            target[:, cols] = dot_nt(rows, block).astype(target.dtype)
            return carry

        lax.fori_loop(0, count // group, project, 0)
        if target is core_send:
            core_handle = wire.copy(core_send, core_got, other_core)
    wire.arrived(core_handle)
    part = 2 * quarter
    step = 16

    def to_side(i, carry):
        at = pl.ds(pl.multiple_of((1 - side) * part + i * step, step), step)
        y_send[pl.ds(pl.multiple_of(i * step, step), step), :] = (
            core_keep[at, :] + core_got[at, :].astype(F32)
        ).astype(LOW)
        return carry

    lax.fori_loop(0, part // step, to_side, 0)
    y_handle = wire.copy(y_send, y_got, other_side)
    tick(spread - spread // 3 - 1)
    wire.arrived(y_handle)
    out_bias, gain_two, shift_two = vec_in[0:1, :], vec_in[1:2, :], vec_in[2:3, :]

    def norm(i, carry):
        at = pl.ds(pl.multiple_of(i * step, step), step)
        far_at = pl.ds(pl.multiple_of(side * part + i * step, step), step)
        value = core_keep[far_at, :] + core_got[far_at, :].astype(F32)
        value = value + y_got[at, :].astype(F32)
        value = x_in[at, :].astype(F32) + value + out_bias
        middle[at, :] = value
        centred, inverse = norm_parts(value)
        rows_two[0, place, at, :] = (centred * inverse * gain_two + shift_two).astype(LOW)
        return carry

    lax.fori_loop(0, part // step, norm, 0)
    mine = rows_two.at[0, place]
    pair_handle = wire.copy(mine, rows_two.at[1, place], pair)
    side_handle = wire.copy(mine, mine, other_side)
    wire.copy(mine, mine, other_core)
    pj_far = send_far(pj_in, pj_out)
    tick(len(jobs))
    jobs.extend((pj_far, pj_out, d) for d in range(1, lines))
    wire.arrived(pair_handle)
    theirs = rows_two.at[1, place]
    side_two = wire.copy(theirs, theirs, other_side)
    wire.copy(theirs, theirs, other_core)
    wire.arrived(side_handle)
    block = rows_two.at[0, flip(place, 2)]
    wire.copy(block, block, other_core)
    wire.arrived(side_two)
    block = rows_two.at[1, flip(place, 2)]
    wire.copy(block, block, other_core)
    tick(len(jobs))
    for item in own[3:]:
        item.wait()
    wire.finish()


def front(queries, keyval, meta_q, meta_k, own_rows, vecs, out, fc, proj, grad_rows):
    count = lax.axis_size("seq")
    tensor = lax.axis_size("tensor")
    batches, rows, width = queries.shape
    two = keyval.shape[2]
    heads = 2 * width // two
    part, full = own_rows.shape
    shapes = [
        ((batches, rows, width), LOW),
        ((batches, heads, rows, 1), F32),
        ((batches, count, rows, two), LOW),
        ((count,) + out.shape, LOW),
        ((part, full), F32),
        ((2, tensor, part, full), LOW),
        ((count,) + fc.shape[1:], LOW),
        ((count,) + proj.shape[1:], LOW),
        ((tensor, part, full), LOW),
    ]
    copies = 2 * (count - 1) + 3 * (count - 1) + 4 + 2 + 7
    vmem, hbm = pl.BlockSpec(memory_space=pltpu.VMEM), pl.BlockSpec(memory_space=pl.ANY)
    return pl.pallas_call(
        partial(front_kernel, count),
        out_shape=[jax.ShapeDtypeStruct(shape, dtype) for shape, dtype in shapes],
        in_specs=[vmem] * 6 + [hbm] * 4,
        out_specs=[vmem] * 6 + [hbm] * 3,
        scratch_shapes=[
            pltpu.VMEM((heads, rows, 1), F32),
            pltpu.VMEM((heads, rows, 1), F32),
            pltpu.VMEM((rows, width), F32),
            pltpu.VMEM((2 * part, full), F32),
            pltpu.VMEM((2 * part, full), LOW),
            pltpu.VMEM((2 * part, full), LOW),
            pltpu.VMEM((part, full), LOW),
            pltpu.VMEM((part, full), LOW),
            pltpu.SemaphoreType.DMA((copies,)),
            pltpu.SemaphoreType.DMA((copies,)),
            pltpu.SemaphoreType.DMA((5,)),
        ],
        compiler_params=pltpu.CompilerParams(
            collective_id=1, has_side_effects=True, vmem_limit_bytes=56 << 20
        ),
        name="front",
    )(queries, keyval, meta_q, meta_k, own_rows, vecs, out, fc, proj, grad_rows)


def by_rows(rows, step, body):
    def run(i, carry):
        body(pl.ds(pl.multiple_of(i * step, step), step))
        return carry

    lax.fori_loop(0, rows // step, run, 0)


class SeqSum:
    def __init__(self, wire, index, peers, part, from_near, to_far, from_far, out, split):
        self.wire, self.index = wire, index
        self.far, self.near = peers[:-1], peers[-1]
        self.lines = len(peers)
        self.part, self.out, self.split = part, out, split
        self.from_near, self.to_far, self.from_far = from_near, to_far, from_far
        self.rows = part.shape[1]
        self.step = min(64, self.rows)
        self.near_handles, self.far_handles = {}, {}
        self.next = 1

    def start(self):
        for d in list(range(1, self.lines)) + [0]:
            block = self.part.at[flip(self.index, 2 * d + 1)]
            self.near_handles[d] = self.wire.copy(block, self.from_near.at[d], self.near)

    def relay(self, number):
        for _ in range(number):
            d = self.next
            self.next += 1
            self.wire.arrived(self.near_handles[d])

            def join(at, d=d):
                total = self.part[flip(self.index, 2 * d), at].astype(F32)
                total = total + self.from_near[d, at].astype(F32)
                self.to_far[d - 1, at] = total.astype(LOW)

            by_rows(self.rows, self.step, join)
            self.far_handles[d] = self.wire.copy(
                self.to_far.at[d - 1], self.from_far.at[d - 1], self.far[d - 1]
            )

    def close(self):
        self.wire.arrived(self.near_handles[0])
        for d in range(1, self.lines):
            self.wire.arrived(self.far_handles[d])
        width = self.part.shape[2]
        half = lax.rem(lax.div(self.index, 2), 2)

        def total(at):
            same = self.part[self.index, at].astype(F32) + self.from_near[0, at].astype(F32)
            other = None
            for d in range(1, self.lines):
                got = self.from_far[d - 1, at].astype(F32)
                if self.split and d % 2:
                    other = got if other is None else other + got
                else:
                    same = same + got
            if self.split:
                out = self.out
                out[at, pl.ds(pl.multiple_of(half * width, width), width)] = same
                out[at, pl.ds(pl.multiple_of((1 - half) * width, width), width)] = other
            else:
                self.out[at, :] = same

        by_rows(self.rows, self.step, total)


def seq_sum_scratch(part):
    lines = part.shape[0] // 2
    return [
        pltpu.VMEM((depth,) + part.shape[1:], LOW) for depth in (lines, lines - 1, lines - 1)
    ]


class RowSum:
    def __init__(self, wire, place, pair, part, core_got, y_send, y_got, pair_send, pair_got):
        self.wire, self.place, self.pair = wire, place, pair
        self.core, self.side = lax.rem(place, 2), lax.div(place, 2)
        self.part, self.core_got, self.y_send, self.y_got = part, core_got, y_send, y_got
        self.pair_send, self.pair_got = pair_send, pair_got
        self.sides = (1 - self.side, self.side)
        self.rows = part.shape[2]
        self.core_handles, self.y_handles = {}, {}

    def start(self):
        peer = {"tensor": flip(self.place, 1)}
        for which in range(2):
            for p in reversed(range(self.part.shape[0])):
                at = self.sides[which]
                block = self.part.at[p, 2 * at + 1 - self.core]
                self.core_handles[p, which] = self.wire.copy(block, self.core_got.at[p, at], peer)

    def both(self, p, which, at):
        side = self.sides[which]
        mine = self.part[p, 2 * side + self.core, at, :].astype(F32)
        return mine + self.core_got[p, side, at, :].astype(F32)

    def to_side(self, p):
        self.wire.arrived(self.core_handles[p, 0])

        def body(at):
            self.y_send[p, at, :] = self.both(p, 0, at).astype(LOW)

        by_rows(self.rows, 16, body)
        peer = {"tensor": flip(self.place, 2)}
        self.y_handles[p] = self.wire.copy(self.y_send.at[p], self.y_got.at[p], peer)

    def to_pair(self):
        self.wire.arrived(self.core_handles[1, 1])
        self.wire.arrived(self.y_handles[1])

        def body(at):
            total = self.both(1, 1, at) + self.y_got[1, at, :].astype(F32)
            self.pair_send[at, :] = total.astype(LOW)

        by_rows(self.rows, 16, body)
        self.pair_handle = self.wire.copy(self.pair_send, self.pair_got, self.pair)

    def ready(self):
        self.wire.arrived(self.core_handles[0, 1])
        self.wire.arrived(self.y_handles[0])
        if self.pair is not None:
            self.wire.arrived(self.pair_handle)

    def total(self, at):
        total = self.both(0, 1, at) + self.y_got[0, at, :].astype(F32)
        if self.pair is not None:
            total = total + self.pair_got[at, :].astype(F32)
        return total


def row_sum_scratch(part):
    pairs, _, rows, width = part.shape
    scratch = [pltpu.VMEM((pairs, 2, rows, width), LOW)]
    scratch += [pltpu.VMEM((pairs, rows, width), LOW)] * 2
    if pairs == 2:
        scratch += [pltpu.VMEM((rows, width), LOW)] * 2
    return scratch


class RowGather:
    def __init__(self, wire, place, rows):
        self.wire, self.place, self.rows = wire, place, rows

    def start(self):
        mine = self.rows.at[self.place]
        self.side_handle = self.wire.copy(mine, mine, {"tensor": flip(self.place, 2)})
        self.wire.copy(mine, mine, {"tensor": flip(self.place, 1)})

    def forward(self):
        self.wire.arrived(self.side_handle)
        block = self.rows.at[flip(self.place, 2)]
        self.wire.copy(block, block, {"tensor": flip(self.place, 1)})


def sem_scratch(copies):
    return [pltpu.SemaphoreType.DMA((copies,)), pltpu.SemaphoreType.DMA((copies,))]


def middle_kernel(count, *refs):
    back, proj, centre, dy, vec = refs[:5]
    proj_sum, grad, rows, sums = refs[5:9]
    row_refs, seq_refs, (send_sem, recv_sem) = refs[9:14], refs[14:17], refs[17:]
    index, place = lax.axis_index("seq"), lax.axis_index("tensor")
    along = seq_peers(index, count)
    greet(along + [{"tensor": flip(place, 1)}, {"tensor": flip(place, 2)}])
    wire = Wire(send_sem, recv_sem)
    reduce = RowSum(wire, place, along[0], back, *row_refs)
    bulk = SeqSum(wire, index, along, proj, *seq_refs, proj_sum, True)
    gather = RowGather(wire, place, rows)
    lines = count // 2
    reduce.start()
    bulk.start()
    reduce.to_side(1)
    reduce.to_side(0)
    bulk.relay(1)
    reduce.to_pair()
    bulk.relay((lines - 1) // 3)
    reduce.ready()
    sums[...] = jnp.zeros_like(sums)
    gain = vec[0:1, :]

    def body(at):
        over = reduce.total(at)
        inner, product = norm_back(centre[at, :], gain, over)
        value = dy[at, :].astype(F32) + inner
        grad[at, :] = value
        rows[place, at, :] = value.astype(LOW)
        sums[0] += product
        sums[1] += over
        sums[2] += value

    by_rows(centre.shape[0], 16, body)
    gather.start()
    bulk.relay(lines - 1 - 1 - (lines - 1) // 3)
    gather.forward()
    bulk.close()
    wire.finish()


def middle_stage(back, proj, centre, dy, vec):
    count = lax.axis_size("seq")
    tensor = lax.axis_size("tensor")
    part, full = centre.shape
    vmem = pl.BlockSpec(memory_space=pltpu.VMEM)
    copies = 2 * count + 12
    return pl.pallas_call(
        partial(middle_kernel, count),
        out_shape=[
            jax.ShapeDtypeStruct((proj.shape[1], 2 * proj.shape[2]), F32),
            jax.ShapeDtypeStruct((part, full), F32),
            jax.ShapeDtypeStruct((tensor, part, full), LOW),
            jax.ShapeDtypeStruct((3, 16, full), F32),
        ],
        in_specs=[vmem] * 5,
        out_specs=[vmem] * 4,
        scratch_shapes=row_sum_scratch(back) + seq_sum_scratch(proj) + sem_scratch(copies),
        compiler_params=pltpu.CompilerParams(
            collective_id=2, has_side_effects=True, vmem_limit_bytes=60 << 20
        ),
        name="middle",
    )(back, proj, centre, dy, vec)


def scatter_kernel(count, split, arrays, *refs):
    parts = refs[:arrays]
    outs = refs[arrays : 2 * arrays]
    from_near = refs[2 * arrays : 3 * arrays]
    to_far = refs[3 * arrays : 4 * arrays]
    from_far = refs[4 * arrays : 5 * arrays]
    send_sem, recv_sem = refs[5 * arrays :]
    index = lax.axis_index("seq")
    half = lax.rem(lax.div(index, 2), 2)
    along = seq_peers(index, count)
    far, near = along[:-1], along[-1]
    lines = count // 2
    greet(along)
    wire = Wire(send_sem, recv_sem)
    turn = list(range(1, lines)) + [0]
    near_handles, far_handles = {}, {}
    for a in range(arrays):
        for d in turn:
            block = parts[a].at[flip(index, 2 * d + 1)]
            near_handles[a, d] = wire.copy(block, from_near[a].at[d], near)
    rows = parts[0].shape[1]
    step = min(64, rows)

    def by_rows(body):
        def run(i, carry):
            body(pl.ds(pl.multiple_of(i * step, step), step))
            return carry

        lax.fori_loop(0, rows // step, run, 0)

    for a in range(arrays):
        for d in range(1, lines):
            wire.arrived(near_handles[a, d])

            def join(at, a=a, d=d):
                total = parts[a][flip(index, 2 * d), at].astype(F32)
                total = total + from_near[a][d, at].astype(F32)
                to_far[a][d - 1, at] = total.astype(LOW)

            by_rows(join)
            far_handles[a, d] = wire.copy(to_far[a].at[d - 1], from_far[a].at[d - 1], far[d - 1])
    for a in range(arrays):
        wire.arrived(near_handles[a, 0])
        for d in range(1, lines):
            wire.arrived(far_handles[a, d])
        width = parts[a].shape[2]

        def total(at, a=a, width=width):
            same = parts[a][index, at].astype(F32) + from_near[a][0, at].astype(F32)
            other = None
            for d in range(1, lines):
                got = from_far[a][d - 1, at].astype(F32)
                if split and d % 2:
                    other = got if other is None else other + got
                else:
                    same = same + got
            if split:
                outs[a][at, pl.ds(pl.multiple_of(half * width, width), width)] = same
                outs[a][at, pl.ds(pl.multiple_of((1 - half) * width, width), width)] = other
            else:
                outs[a][at, :] = same

        by_rows(total)
    wire.finish()


def scatter_grads(parts, split, collective_id):
    count = lax.axis_size("seq")
    lines = count // 2
    arrays = len(parts)
    copies = arrays * (count - 1)
    scratch = []
    for depth in (lines, lines - 1, lines - 1):
        scratch += [pltpu.VMEM((depth,) + part.shape[1:], LOW) for part in parts]
    return pl.pallas_call(
        partial(scatter_kernel, count, split, arrays),
        out_shape=[
            jax.ShapeDtypeStruct((part.shape[1], part.shape[2] * (2 if split else 1)), F32)
            for part in parts
        ],
        in_specs=[pl.BlockSpec(memory_space=pltpu.VMEM)] * arrays,
        out_specs=[pl.BlockSpec(memory_space=pltpu.VMEM)] * arrays,
        scratch_shapes=scratch
        + [pltpu.SemaphoreType.DMA((copies,)), pltpu.SemaphoreType.DMA((copies,))],
        compiler_params=pltpu.CompilerParams(
            collective_id=collective_id, has_side_effects=True, vmem_limit_bytes=60 << 20
        ),
        name="scatter_grads",
    )(*parts)


def scatter_blocks(blocks):
    count = lax.axis_size("seq")
    blocks = dict(blocks)
    for bit in range(bits_of(count)):
        for r in sorted(blocks):
            if r & (1 << bit):
                arrived = swap(blocks.pop(r).astype(LOW), "seq", bit)
                blocks[r ^ (1 << bit)] = blocks[r ^ (1 << bit)] + arrived.astype(F32)
    return blocks[0]


def tensor_gather(own, axis):
    count = lax.axis_size("tensor")
    out = jnp.expand_dims(own, axis)
    for bit in reversed(range(bits_of(count))):
        out_other = swap(out, "tensor", bit)
        mine = (lax.axis_index("tensor") >> bit) & 1
        low_part = jnp.where(mine == 0, out, out_other)
        high_part = jnp.where(mine == 0, out_other, out)
        size = out.shape[axis]
        shape = out.shape
        low_part = jnp.expand_dims(low_part, axis)
        high_part = jnp.expand_dims(high_part, axis)
        out = jnp.concatenate([low_part, high_part], axis=axis)
        out = jnp.swapaxes(out, axis, axis + 1) if size > 1 else out
        out = out.reshape(shape[:axis] + (2 * size,) + shape[axis + 1 :])
    return out


def tensor_scatter(parts, axis):
    count = lax.axis_size("tensor")
    index = lax.axis_index("tensor")
    for bit in range(bits_of(count)):
        shape = parts.shape
        split = parts.reshape(shape[:axis] + (shape[axis] // 2, 2) + shape[axis + 1 :])
        mine = (index >> bit) & 1
        keep = lax.dynamic_index_in_dim(split, mine, axis + 1, keepdims=False)
        give = lax.dynamic_index_in_dim(split, 1 - mine, axis + 1, keepdims=False)
        parts = keep.astype(F32) + swap(give.astype(LOW), "tensor", bit).astype(F32)
    return lax.squeeze(parts, (axis,))


def visible(meta_q, meta_k):
    seg_q, pos_q = meta_q[:, 0:1], meta_q[:, 1:2]
    seg_k, pos_k = meta_k[0:1, :], meta_k[1:2, :]
    return ((seg_k == 0) | (seg_k == seg_q)) & (pos_k <= pos_q)


def backward_kernel(
    live_ref, q_ref, kv_ref, mq_ref, mk_ref, o_ref, lse_ref, do_ref, dq_ref, dkv_ref, delta, acc
):
    batch = pl.program_id(0)
    hd = kv_ref.shape[-1] // 2
    heads = q_ref.shape[-1] // hd
    blocks = kv_ref.shape[1]
    scale = float(hd) ** (-0.5)
    scale_two = scale * LOG2E
    acc[...] = jnp.zeros_like(acc)
    for head in range(heads):
        cols = slice(head * hd, (head + 1) * hd)
        delta[head] = jnp.sum(
            do_ref[0, :, cols].astype(F32) * o_ref[0, :, cols].astype(F32), axis=-1, keepdims=True
        )

    def step(index, carry):
        @pl.when(live_ref[batch, index] > 0)
        def _():
            mask = visible(mq_ref[0], mk_ref[0, index])
            keys = kv_ref[0, index, :, :hd]
            values = kv_ref[0, index, :, hd:]
            grad_k = jnp.zeros((keys.shape[0], hd), F32)
            grad_v = jnp.zeros((keys.shape[0], hd), F32)
            for head in range(heads):
                cols = slice(head * hd, (head + 1) * hd)
                query = q_ref[0, :, cols]
                grad_o = do_ref[0, :, cols]
                scores = dot_nt(query, keys) * scale_two
                probs = jnp.where(mask, jnp.exp2(scores - lse_ref[0, head]), 0.0)
                grad_p = dot_nt(grad_o, values)
                grad_s = (probs * (grad_p - delta[head])).astype(LOW)
                acc[:, cols] += dot(grad_s, keys)
                grad_k = grad_k + dot_tn(grad_s, query)
                grad_v = grad_v + dot_tn(probs.astype(LOW), grad_o)
            dkv_ref[0, index, :, :hd] = (grad_k * scale).astype(LOW)
            dkv_ref[0, index, :, hd:] = grad_v.astype(LOW)

        @pl.when(live_ref[batch, index] == 0)
        def _():
            dkv_ref[0, index] = jnp.zeros(dkv_ref.shape[2:], LOW)

        return carry

    lax.fori_loop(0, blocks, step, 0)
    dq_ref[0] = (acc[...] * scale).astype(LOW)


def attend_backward(queries, keyval, meta_q, meta_k, live, mixed, lse, grad_mixed):
    batches, rows, width = queries.shape
    _, blocks, keys, two = keyval.shape
    hd = two // 2
    heads = width // hd
    flops = 10 * batches * rows * width * blocks * keys
    row_spec = pl.BlockSpec((1, rows, width), lambda b, live: (b, 0, 0))
    kv_spec = pl.BlockSpec((1, blocks, keys, two), lambda b, live: (b, 0, 0, 0))
    return pl.pallas_call(
        backward_kernel,
        grid_spec=pltpu.PrefetchScalarGridSpec(
            num_scalar_prefetch=1,
            grid=(batches,),
            in_specs=[
                row_spec,
                kv_spec,
                pl.BlockSpec((1, rows, 128), lambda b, live: (b, 0, 0)),
                pl.BlockSpec((1, blocks, 8, keys), lambda b, live: (b, 0, 0, 0)),
                row_spec,
                pl.BlockSpec((1, heads, rows, 1), lambda b, live: (b, 0, 0, 0)),
                row_spec,
            ],
            out_specs=[row_spec, kv_spec],
            scratch_shapes=[
                pltpu.VMEM((heads, rows, 1), F32),
                pltpu.VMEM((rows, width), F32),
            ],
        ),
        out_shape=[
            jax.ShapeDtypeStruct((batches, rows, width), LOW),
            jax.ShapeDtypeStruct((batches, blocks, keys, two), LOW),
        ],
        name="attend_backward",
        cost_estimate=pl.CostEstimate(
            flops=flops, transcendentals=0, bytes_accessed=4 * keyval.size
        ),
    )(live, queries, keyval, meta_q, meta_k, mixed, lse, grad_mixed)


def norm_parts(values):
    average = jnp.mean(values, axis=-1, keepdims=True)
    centred = values - average
    spread = jnp.mean(centred * centred, axis=-1, keepdims=True)
    return centred, lax.rsqrt(spread + EPS)


def norm_back(values, gain, grad):
    centred, inverse = norm_parts(values)
    unit = centred * inverse
    scaled = grad * gain
    inner = (
        scaled
        - jnp.mean(scaled, axis=-1, keepdims=True)
        - unit * jnp.mean(scaled * unit, axis=-1, keepdims=True)
    )
    return inverse * inner, grad * unit


def gelu_pair(values):
    const = 0.7978845608028654
    square = values * values
    inner = jnp.tanh(const * (values + 0.044715 * (values * square)))
    half = 0.5 * (1.0 + inner)
    slope = half + 0.5 * values * (1.0 - inner * inner) * const * (1.0 + 3 * 0.044715 * square)
    return values * half, slope


def local(
    inputs,
    segment,
    position,
    w_query,
    w_keyval,
    w_out,
    w_fc,
    w_proj,
    vectors,
    fc_bias,
    value_bias,
    grad_out,
):
    seq_size, tensor_size = lax.axis_size("seq"), lax.axis_size("tensor")
    seq_index, tensor_index = lax.axis_index("seq"), lax.axis_index("tensor")
    batches, rows, full_width = inputs.shape
    width_block = w_query.shape[0]
    group_width = w_query.shape[1]
    hidden_width = w_fc.shape[1]
    unit_width = hidden_width // 2
    unit_half = (seq_index >> 1) & 1
    hd = value_bias.shape[0]
    quarter = rows // tensor_size
    shard = vectors.shape[1]
    bias_shard = fc_bias.shape[0]

    pieces = [
        vectors.reshape(-1).astype(LOW),
        fc_bias.astype(LOW),
        segment.reshape(-1).astype(LOW),
        (position // 128).reshape(-1).astype(LOW),
        (position % 128).reshape(-1).astype(LOW),
    ]
    cuts = [0]
    for piece in pieces:
        cuts.append(cuts[-1] + piece.shape[0])
    packed = jnp.concatenate(pieces)
    packed = jnp.pad(packed, (0, -packed.shape[0] % 2048)).reshape(-1, 128)

    def halves(array):
        return jnp.swapaxes(array.astype(LOW).reshape(width_block, 2, unit_width), 0, 1)

    small, kv_mat, q_mat = gather_first(packed, w_keyval.astype(LOW), w_query.astype(LOW))
    kv_mat = kv_mat.reshape(full_width, 2 * hd)
    q_mat = q_mat.reshape(full_width, group_width)

    small = small.reshape(seq_size, tensor_size, -1).astype(F32)
    vec_all = small[:, :, cuts[0] : cuts[1]].reshape(seq_size * tensor_size, 7, shard)
    vec_all = jnp.swapaxes(vec_all, 0, 1).reshape(7, full_width)
    fc_all = small[:, :, cuts[1] : cuts[2]].reshape(-1)
    seg_keys = small[:, 0, cuts[2] : cuts[3]].reshape(seq_size, batches, rows)
    pos_keys = 128.0 * small[:, 0, cuts[3] : cuts[4]] + small[:, 0, cuts[4] : cuts[5]]
    seg_keys = jnp.swapaxes(seg_keys, 0, 1).astype(jnp.int32)
    pos_keys = jnp.swapaxes(pos_keys.reshape(seq_size, batches, rows), 0, 1).astype(jnp.int32)
    meta_k = jnp.pad(jnp.stack([seg_keys, pos_keys], axis=2), ((0, 0), (0, 0), (0, 6), (0, 0)))
    meta_q = jnp.pad(jnp.stack([segment, position], axis=2), ((0, 0), (0, 0), (0, 126)))
    seg_lo, seg_hi = jnp.min(seg_keys, axis=2), jnp.max(seg_keys, axis=2)
    own_lo = jnp.min(segment, axis=1, keepdims=True)
    own_hi = jnp.max(segment, axis=1, keepdims=True)
    live = (
        ((seg_lo == 0) | ((seg_lo <= own_hi) & (own_lo <= seg_hi)))
        & (jnp.min(pos_keys, axis=2) <= jnp.max(position, axis=1, keepdims=True))
    ).astype(jnp.int32)

    gain_one, shift_one, _, out_bias, gain_two, shift_two, proj_bias = [
        vec_all[i] for i in range(7)
    ]
    query_bias = lax.dynamic_slice_in_dim(vec_all[2], tensor_index * group_width, group_width, 0)
    fc_local = lax.dynamic_slice_in_dim(
        fc_all, tensor_index * hidden_width + unit_half * unit_width, unit_width, 0
    )
    bias_value = value_bias.astype(LOW).astype(F32)
    kv_bias = jnp.concatenate([jnp.zeros((hd,), F32), bias_value])

    residual = inputs.astype(F32)
    centred, inverse = norm_parts(residual)
    normed = (centred * inverse * gain_one + shift_one).astype(LOW).reshape(-1, full_width)
    keyval = (dot(normed, kv_mat) + kv_bias).astype(LOW).reshape(batches, rows, 2 * hd)
    queries = (dot(normed, q_mat) + query_bias).astype(LOW)
    queries = queries.reshape(batches, rows, group_width)

    def by_quarter(array):
        split = array.reshape(batches, tensor_size, quarter, array.shape[-1])
        return jnp.swapaxes(split, 0, 1).reshape(tensor_size, batches * quarter, -1)

    def by_batch(array):
        split = array.reshape(tensor_size, batches, quarter, array.shape[-1])
        return jnp.swapaxes(split, 0, 1).reshape(batches, rows, -1)

    def my_quarter(array):
        split = array.reshape(batches, tensor_size, quarter, full_width)
        own = lax.dynamic_index_in_dim(split, tensor_index, 1, keepdims=False)
        return own.reshape(batches * quarter, full_width)

    def pair_scatter(part):
        got = tensor_scatter(part.reshape(2, tensor_size, batches * quarter, full_width), 1)
        return got[0] + swap(got[1].astype(LOW), "seq", 1).astype(F32)

    vecs = jnp.pad(jnp.stack([out_bias, gain_two, shift_two]), ((0, 5), (0, 0)))
    grad_split = by_quarter(grad_out)
    mixed, lse, kv_all, out_t, middle, rows_two, fc_mat, proj_t, grad_other = front(
        queries,
        keyval,
        meta_q,
        meta_k,
        my_quarter(inputs),
        vecs,
        w_out.T.astype(LOW),
        halves(w_fc),
        halves(w_proj.T),
        grad_split,
    )
    out_t = out_t.reshape(full_width, group_width)
    fc_mat = fc_mat.reshape(full_width, unit_width)
    proj_t = proj_t.reshape(full_width, unit_width)
    mixed_rows = by_quarter(mixed).reshape(-1, group_width)
    normed_two = rows_two.reshape(-1, full_width)
    hidden = dot(normed_two, fc_mat) + fc_local
    active_f, slope = gelu_pair(hidden)
    active = active_f.astype(LOW)

    grad_q_low = my_quarter(grad_out)
    grad_flat = jnp.concatenate([grad_split, grad_other]).reshape(-1, full_width)
    grad_hidden = (slope * dot(grad_flat, proj_t)).astype(LOW)
    fcbias_local = jnp.sum(grad_hidden.astype(F32), axis=0)
    back_part = dot_nt(grad_hidden, fc_mat).astype(LOW)
    back_part = back_part.reshape(2, tensor_size, batches * quarter, full_width)

    def blocked(array):
        return array.astype(LOW).reshape(seq_size, width_block, array.shape[-1])

    proj_sum, grad_middle, rows_middle, sums = middle_stage(
        back_part,
        blocked(dot_tn(grad_flat, active)),
        middle,
        grad_q_low,
        jnp.pad(gain_two[None], ((0, 7), (0, 0))),
    )
    grad_gain_two, grad_shift_two, grad_out_bias = jnp.sum(sums, axis=1)
    grad_proj_bias = jnp.sum(grad_q_low.astype(F32), axis=0)
    grad_middle_low = rows_middle.reshape(-1, full_width)
    (fc_sum,) = scatter_grads([blocked(dot_tn(normed_two, grad_hidden))], True, 4)

    ff_sum = pair_scatter(dot_nt(active, proj_t))
    result_q = (middle + ff_sum + proj_bias).astype(LOW)
    result = by_batch(tensor_gather(result_q, 0))

    grad_mixed = by_batch(dot(grad_middle_low, out_t).astype(LOW))
    grad_queries, grad_kv_all = attend_backward(
        queries, kv_all, meta_q, meta_k, live, mixed, lse, grad_mixed
    )
    grad_keyval = scatter_blocks(
        {
            r: lax.dynamic_index_in_dim(
                grad_kv_all, jnp.bitwise_xor(seq_index, r), 1, keepdims=False
            ).astype(F32)
            for r in range(seq_size)
        }
    )
    grad_keyval = grad_keyval.astype(LOW).reshape(-1, 2 * hd)
    grad_queries = grad_queries.reshape(-1, group_width)
    out_sum, query_sum, kv_sum = scatter_grads(
        [
            blocked(dot_tn(grad_middle_low, mixed_rows)),
            blocked(dot_tn(normed, grad_queries)),
            blocked(dot_tn(normed, grad_keyval)),
        ],
        False,
        3,
    )
    grad_normed = dot_nt(grad_queries, q_mat) + dot_nt(grad_keyval, kv_mat)
    in_sum = tensor_scatter(by_quarter(grad_normed), 0)
    residual_q = my_quarter(inputs).astype(F32)
    norm_part, gain_part = norm_back(residual_q, gain_one, in_sum)
    grad_in_q = (grad_middle + norm_part).astype(LOW)
    input_grad = by_batch(tensor_gather(grad_in_q, 0))
    grad_gain_one = jnp.sum(gain_part, axis=0)
    grad_shift_one = jnp.sum(in_sum, axis=0)
    qbias_local = jnp.sum(grad_queries.astype(F32), axis=0)
    vbias_local = jnp.sum(grad_keyval[:, hd:].astype(F32), axis=0)

    qbias_full = lax.dynamic_update_slice_in_dim(
        jnp.zeros((full_width,), F32), qbias_local, tensor_index * group_width, 0
    )
    full_hidden = bias_shard * seq_size * tensor_size
    fcbias_full = lax.dynamic_update_slice_in_dim(
        jnp.zeros((full_hidden,), F32),
        fcbias_local,
        tensor_index * hidden_width + unit_half * unit_width,
        0,
    )
    vec_grads = jnp.stack(
        [
            grad_gain_one,
            grad_shift_one,
            qbias_full,
            grad_out_bias,
            grad_gain_two,
            grad_shift_two,
            grad_proj_bias,
        ]
    )
    chunk = full_hidden // seq_size
    vec_cut = 7 * width_block
    rows_all = jnp.concatenate(
        [
            jnp.swapaxes(vec_grads.reshape(7, seq_size, width_block), 0, 1).reshape(seq_size, -1),
            fcbias_full.reshape(seq_size, chunk),
            jnp.broadcast_to(vbias_local, (seq_size, hd)),
        ],
        axis=1,
    )
    rows_all = jnp.pad(rows_all, ((0, 0), (0, -rows_all.shape[1] % 1024)))
    rows_all = rows_all.reshape(seq_size, -1, 128)
    for bit in reversed(range(bits_of(seq_size))):
        size = rows_all.shape[0] // 2
        mine = (seq_index >> bit) & 1
        keep = lax.dynamic_slice_in_dim(rows_all, mine * size, size, 0)
        give = lax.dynamic_slice_in_dim(rows_all, (1 - mine) * size, size, 0)
        rows_all = keep + swap(give, "seq", bit)
    small_sum = rows_all[0]
    for bit in range(bits_of(tensor_size)):
        small_sum = small_sum + swap(small_sum, "tensor", bit)
    small_sum = small_sum.reshape(-1)
    vec_grad = lax.dynamic_slice_in_dim(
        small_sum[:vec_cut].reshape(7, width_block), tensor_index * shard, shard, 1
    )
    fcbias_grad = lax.dynamic_slice_in_dim(
        small_sum[vec_cut : vec_cut + chunk], tensor_index * bias_shard, bias_shard, 0
    )
    vbias_grad = small_sum[vec_cut + chunk : vec_cut + chunk + hd]
    keyval_grad = tensor_scatter(kv_sum.reshape(tensor_size, -1, 2 * hd), 0)
    return (
        result,
        input_grad,
        query_sum,
        keyval_grad,
        out_sum.T,
        fc_sum,
        proj_sum.T,
        vec_grad,
        fcbias_grad,
        vbias_grad,
        vec_grad[5],
    )


def solution(mesh):
    in_specs = (
        P(None, "seq", None),
        P(None, "seq"),
        P(None, "seq"),
        P("seq", "tensor"),
        P(("seq", "tensor"), None),
        P("tensor", "seq"),
        P("seq", "tensor"),
        P("tensor", "seq"),
        P(None, ("seq", "tensor")),
        P(("seq", "tensor")),
        P(),
        P(None, "seq", None),
    )
    out_specs = (
        P(None, "seq", None),
        P(None, "seq", None),
        P("seq", "tensor"),
        P(("seq", "tensor"), None),
        P("tensor", "seq"),
        P("seq", "tensor"),
        P("tensor", "seq"),
        P(None, ("seq", "tensor")),
        P(("seq", "tensor")),
        P(),
        P(("seq", "tensor")),
    )
    return jax.shard_map(local, mesh=mesh, in_specs=in_specs, out_specs=out_specs, check_vma=False)
```

```python
from functools import partial

import jax
import jax.numpy as jnp
from jax import lax
from jax.experimental import pallas as pl
from jax.experimental.pallas import tpu as pltpu
from jax.sharding import PartitionSpec as P

EPS = 1e-05
NEG = -1e30
LOG2E = 1.4426950408889634
LOW = jnp.bfloat16
F32 = jnp.float32


def bits_of(count):
    return count.bit_length() - 1


def swap(value, axis, bit):
    count = lax.axis_size(axis)
    return lax.ppermute(value, axis, [(i, i ^ (1 << bit)) for i in range(count)])


def after(value, *others):
    return lax.optimization_barrier((value,) + others)[0]


def dot(left, right):
    return jnp.dot(left, right, preferred_element_type=F32)


def dot_tn(left, right):
    return lax.dot_general(left, right, (((0,), (0,)), ((), ())), preferred_element_type=F32)


def dot_nt(left, right):
    return lax.dot_general(left, right, (((1,), (1,)), ((), ())), preferred_element_type=F32)


MESH = pl.DeviceIdType.MESH


def flip(index, mask):
    bit = 1
    out = index
    while bit <= mask:
        if mask & bit:
            out = out + bit * (1 - 2 * lax.rem(lax.div(index, bit), 2))
        bit *= 2
    return out


class Wire:
    def __init__(self, send_sem, recv_sem):
        self.send_sem, self.recv_sem = send_sem, recv_sem
        self.started = []
        self.landed = set()

    def copy(self, src, dst, peer):
        place = len(self.started)
        item = pltpu.make_async_remote_copy(
            src_ref=src,
            dst_ref=dst,
            send_sem=self.send_sem.at[place],
            recv_sem=self.recv_sem.at[place],
            device_id=peer,
            device_id_type=MESH,
        )
        item.start()
        self.started.append(item)
        return place

    def arrived(self, place):
        if place not in self.landed:
            self.landed.add(place)
            self.started[place].wait_recv()

    def finish(self):
        for place in range(len(self.started)):
            self.arrived(place)
        for item in self.started:
            item.wait_send()


def greet(peers):
    barrier = pltpu.get_barrier_semaphore()
    for peer in peers:
        pl.semaphore_signal(barrier, inc=1, device_id=peer, device_id_type=MESH)
    pl.semaphore_wait(barrier, len(peers))


def seq_peers(index, count):
    return [{"seq": flip(index, 2 * d)} for d in range(1, count // 2)] + [
        {"seq": flip(index, 1)}
    ]


def first_kernel(count, tensor, *refs):
    ins, outs = refs[:3], refs[3:6]
    send_sem, recv_sem, local_sem = refs[6:]
    index = lax.axis_index("seq")
    place = lax.axis_index("tensor")
    across = [{"tensor": flip(place, tensor >> (i + 1))} for i in range(bits_of(tensor))]
    along = seq_peers(index, count)
    far, near = along[:-1], along[-1]
    greet(across + along)
    wire = Wire(send_sem, recv_sem)
    own = []
    targets = [(lambda at, out=out: out.at[at, place]) for out in outs[:2]]
    targets.append(lambda at: outs[2].at[at])
    handles = []
    for source, target in zip(ins, targets):
        handles.append([wire.copy(source, target(index), peer) for peer in far])
        handles[-1].append(wire.copy(source, target(index), near))
        item = pltpu.make_async_copy(source, target(index), local_sem.at[len(own)])
        item.start()
        own.append(item)
    relays = []
    for a, target in enumerate(targets):
        for d in range(1, count // 2):
            wire.arrived(handles[a][d - 1])
            block = target(flip(index, 2 * d))
            relays.append(wire.copy(block, block, near))
        if a == 1:
            for handle in [handles[0][-1], handles[1][-1]] + relays:
                wire.arrived(handle)
            own[0].wait()
            own[1].wait()
            masks = [0]
            for i, peer in enumerate(across):
                step = tensor >> (i + 1)
                sent = [
                    wire.copy(out.at[:, flip(place, mask)], out.at[:, flip(place, mask)], peer)
                    for mask in masks
                    for out in outs[:2]
                ]
                masks = masks + [mask | step for mask in masks]
                if i + 1 < len(across):
                    for handle in sent:
                        wire.arrived(handle)
    own[2].wait()
    wire.finish()


def gather_first(small, keyval, query):
    count, tensor = lax.axis_size("seq"), lax.axis_size("tensor")
    arrays = (small, keyval, query)
    shapes = [
        (count, tensor) + small.shape,
        (count, tensor) + keyval.shape,
        (count,) + query.shape,
    ]
    copies = 3 * (count - 1) + 2 * (tensor - 1)
    return pl.pallas_call(
        partial(first_kernel, count, tensor),
        out_shape=[jax.ShapeDtypeStruct(shape, LOW) for shape in shapes],
        in_specs=[pl.BlockSpec(memory_space=pltpu.VMEM)] * 3,
        out_specs=[pl.BlockSpec(memory_space=pltpu.VMEM)] * 3,
        scratch_shapes=[
            pltpu.SemaphoreType.DMA((copies,)),
            pltpu.SemaphoreType.DMA((copies,)),
            pltpu.SemaphoreType.DMA((3,)),
        ],
        compiler_params=pltpu.CompilerParams(collective_id=0, has_side_effects=True),
        name="gather_first",
    )(*arrays)


def front_kernel(count, *refs):
    q_in, kv_in, mq_in, mk_in, x_in, vec_in, o_in, fc_in, pj_in, dy_in = refs[:10]
    mixed, lse, kv_all, out_t, middle, rows_two, fc_out, pj_out, dy_out = refs[10:19]
    (
        top,
        total,
        acc,
        core_keep,
        core_send,
        core_got,
        y_send,
        y_got,
        send_sem,
        recv_sem,
        local_sem,
    ) = refs[19:]
    index = lax.axis_index("seq")
    place = lax.axis_index("tensor")
    core = lax.rem(place, 2)
    side = lax.div(place, 2)
    half = lax.rem(lax.div(index, 2), 2)
    other_core = {"tensor": flip(place, 1)}
    other_side = {"tensor": flip(place, 2)}
    across = {"tensor": flip(place, 3)}
    along = seq_peers(index, count)
    far, near = along[:-1], along[-1]
    pair = far[0]
    lines = count // 2
    greet(along + [other_core, other_side, across])
    wire = Wire(send_sem, recv_sem)
    own = []

    def keep(src, dst):
        item = pltpu.make_async_copy(src, dst, local_sem.at[len(own)])
        item.start()
        own.append(item)

    kv_far = [wire.copy(kv_in.at[core], kv_all.at[core, index], peer) for peer in far]
    kv_near = wire.copy(kv_in.at[core], kv_all.at[core, index], near)
    for batch in range(2):
        keep(kv_in.at[batch], kv_all.at[batch, index])
    o_far = [wire.copy(o_in, out_t.at[index], peer) for peer in far]
    o_near = [wire.copy(o_in, out_t.at[index], near)]
    keep(o_in, out_t.at[index])
    dy_pair = wire.copy(dy_in.at[place], dy_out.at[place], pair)

    def send_far(source, out):
        return [
            wire.copy(source.at[flip(half, d & 1)], out.at[index], far[d - 1])
            for d in range(1, lines)
        ]

    fc_far = send_far(fc_in, fc_out)
    kv_near = [(1, kv_near)]
    kv_core = []
    for d in range(1, lines):
        wire.arrived(kv_far[d - 1])
        block = kv_all.at[core, flip(index, 2 * d)]
        kv_near.append((2 * d + 1, wire.copy(block, block, near)))
        kv_core.append(wire.copy(block, block, other_core))
    wire.copy(fc_in.at[half], fc_out.at[index], near)
    wire.copy(pj_in.at[half], pj_out.at[index], near)
    keep(fc_in.at[half], fc_out.at[index])
    keep(pj_in.at[half], pj_out.at[index])
    for r, handle in kv_near:
        wire.arrived(handle)
        block = kv_all.at[core, flip(index, r)]
        kv_core.append(wire.copy(block, block, other_core))
    own[0].wait()
    own[1].wait()

    jobs = [(o_far, out_t, d) for d in range(1, lines)]
    jobs += [(fc_far, fc_out, d) for d in range(1, lines)]

    def tick(number):
        for _ in range(min(number, len(jobs))):
            handles, out, d = jobs.pop(0)
            wire.arrived(handles[d - 1])
            block = out.at[flip(index, 2 * d)]
            handle = wire.copy(block, block, near)
            if out is out_t:
                o_near.append(handle)

    hd = kv_in.shape[-1] // 2
    heads = q_in.shape[-1] // hd
    scale = float(hd) ** (-0.5) * LOG2E

    def attend(batch, block):
        mask = visible(mq_in[batch], mk_in[batch, block])
        keys = kv_all[batch, block, :, :hd]
        values = kv_all[batch, block, :, hd:]
        for head in range(heads):
            cols = slice(head * hd, (head + 1) * hd)
            scores = jnp.where(mask, dot_nt(q_in[batch, :, cols], keys) * scale, NEG)
            before = top[head]
            now = jnp.maximum(before, jnp.max(scores, axis=-1, keepdims=True))
            shrink = jnp.exp2(before - now)
            probs = jnp.exp2(scores - now)
            total[head] = total[head] * shrink + jnp.sum(probs, axis=-1, keepdims=True)
            acc[:, cols] = acc[:, cols] * shrink + dot(probs.astype(LOW), values)
            top[head] = now

    def attend_batch(batch, ticks):
        top[...] = jnp.full_like(top, NEG)
        total[...] = jnp.zeros_like(total)
        acc[...] = jnp.zeros_like(acc)

        def block_body(block, carry):
            attend(batch, block)
            return carry

        parts = len(ticks)
        for i in range(parts):
            lax.fori_loop(i * count // parts, (i + 1) * count // parts, block_body, 0)
            tick(ticks[i])
        for head in range(heads):
            cols = slice(head * hd, (head + 1) * hd)
            mixed[batch, :, cols] = (acc[:, cols] / total[head]).astype(LOW)
            lse[batch, head] = top[head] + jnp.log2(total[head])

    spread = lines - 1
    attend_batch(core, [spread // 3, spread - spread // 3])
    for handle in kv_core:
        wire.arrived(handle)
    attend_batch(1 - core, [0, spread // 3])
    wire.arrived(dy_pair)
    for peer in (other_core, other_side, across):
        wire.copy(dy_out.at[place], dy_out.at[place], peer)

    quarter = x_in.shape[0] // 2
    for handle in o_near:
        wire.arrived(handle)
    own[2].wait()
    width = out_t.shape[1]
    group = max(1, 256 // width)
    for which, target in ((1 - core, core_send), (core, core_keep)):
        rows = [
            mixed[batch, pl.ds(pl.multiple_of((2 * s + which) * quarter, quarter), quarter), :]
            for s in range(2)
            for batch in range(2)
        ]
        rows = jnp.concatenate(rows, axis=0)

        def project(i, carry, rows=rows, target=target):
            cols = pl.ds(pl.multiple_of(i * group * width, group * width), group * width)
            block = out_t[pl.ds(i * group, group)].reshape(group * width, -1)
            target[:, cols] = dot_nt(rows, block).astype(target.dtype)
            return carry

        lax.fori_loop(0, count // group, project, 0)
        if target is core_send:
            core_handle = wire.copy(core_send, core_got, other_core)
    wire.arrived(core_handle)
    part = 2 * quarter
    step = 16

    def to_side(i, carry):
        at = pl.ds(pl.multiple_of((1 - side) * part + i * step, step), step)
        y_send[pl.ds(pl.multiple_of(i * step, step), step), :] = (
            core_keep[at, :] + core_got[at, :].astype(F32)
        ).astype(LOW)
        return carry

    lax.fori_loop(0, part // step, to_side, 0)
    y_handle = wire.copy(y_send, y_got, other_side)
    tick(spread - spread // 3 - 1)
    wire.arrived(y_handle)
    out_bias, gain_two, shift_two = vec_in[0:1, :], vec_in[1:2, :], vec_in[2:3, :]

    def norm(i, carry):
        at = pl.ds(pl.multiple_of(i * step, step), step)
        far_at = pl.ds(pl.multiple_of(side * part + i * step, step), step)
        value = core_keep[far_at, :] + core_got[far_at, :].astype(F32)
        value = value + y_got[at, :].astype(F32)
        value = x_in[at, :].astype(F32) + value + out_bias
        middle[at, :] = value
        centred, inverse = norm_parts(value)
        rows_two[0, place, at, :] = (centred * inverse * gain_two + shift_two).astype(LOW)
        return carry

    lax.fori_loop(0, part // step, norm, 0)
    mine = rows_two.at[0, place]
    pair_handle = wire.copy(mine, rows_two.at[1, place], pair)
    side_handle = wire.copy(mine, mine, other_side)
    wire.copy(mine, mine, other_core)
    pj_far = send_far(pj_in, pj_out)
    tick(len(jobs))
    jobs.extend((pj_far, pj_out, d) for d in range(1, lines))
    wire.arrived(pair_handle)
    theirs = rows_two.at[1, place]
    side_two = wire.copy(theirs, theirs, other_side)
    wire.copy(theirs, theirs, other_core)
    wire.arrived(side_handle)
    block = rows_two.at[0, flip(place, 2)]
    wire.copy(block, block, other_core)
    wire.arrived(side_two)
    block = rows_two.at[1, flip(place, 2)]
    wire.copy(block, block, other_core)
    tick(len(jobs))
    for item in own[3:]:
        item.wait()
    wire.finish()


def front(queries, keyval, meta_q, meta_k, own_rows, vecs, out, fc, proj, grad_rows):
    count = lax.axis_size("seq")
    tensor = lax.axis_size("tensor")
    batches, rows, width = queries.shape
    two = keyval.shape[2]
    heads = 2 * width // two
    part, full = own_rows.shape
    shapes = [
        ((batches, rows, width), LOW),
        ((batches, heads, rows, 1), F32),
        ((batches, count, rows, two), LOW),
        ((count,) + out.shape, LOW),
        ((part, full), F32),
        ((2, tensor, part, full), LOW),
        ((count,) + fc.shape[1:], LOW),
        ((count,) + proj.shape[1:], LOW),
        ((tensor, part, full), LOW),
    ]
    copies = 2 * (count - 1) + 3 * (count - 1) + 4 + 2 + 7
    vmem, hbm = pl.BlockSpec(memory_space=pltpu.VMEM), pl.BlockSpec(memory_space=pl.ANY)
    return pl.pallas_call(
        partial(front_kernel, count),
        out_shape=[jax.ShapeDtypeStruct(shape, dtype) for shape, dtype in shapes],
        in_specs=[vmem] * 6 + [hbm] * 4,
        out_specs=[vmem] * 6 + [hbm] * 3,
        scratch_shapes=[
            pltpu.VMEM((heads, rows, 1), F32),
            pltpu.VMEM((heads, rows, 1), F32),
            pltpu.VMEM((rows, width), F32),
            pltpu.VMEM((2 * part, full), F32),
            pltpu.VMEM((2 * part, full), LOW),
            pltpu.VMEM((2 * part, full), LOW),
            pltpu.VMEM((part, full), LOW),
            pltpu.VMEM((part, full), LOW),
            pltpu.SemaphoreType.DMA((copies,)),
            pltpu.SemaphoreType.DMA((copies,)),
            pltpu.SemaphoreType.DMA((5,)),
        ],
        compiler_params=pltpu.CompilerParams(
            collective_id=1, has_side_effects=True, vmem_limit_bytes=56 << 20
        ),
        name="front",
    )(queries, keyval, meta_q, meta_k, own_rows, vecs, out, fc, proj, grad_rows)


def by_rows(rows, step, body):
    def run(i, carry):
        body(pl.ds(pl.multiple_of(i * step, step), step))
        return carry

    lax.fori_loop(0, rows // step, run, 0)


class SeqSum:
    def __init__(self, wire, index, peers, part, from_near, to_far, from_far, out, split):
        self.wire, self.index = wire, index
        self.far, self.near = peers[:-1], peers[-1]
        self.lines = len(peers)
        self.part, self.out, self.split = part, out, split
        self.from_near, self.to_far, self.from_far = from_near, to_far, from_far
        self.rows = part.shape[1]
        self.step = min(64, self.rows)
        self.near_handles, self.far_handles = {}, {}
        self.next = 1

    def start(self, order=None):
        for d in order or list(range(1, self.lines)) + [0]:
            block = self.part.at[flip(self.index, 2 * d + 1)]
            self.near_handles[d] = self.wire.copy(block, self.from_near.at[d], self.near)

    def relay(self, number):
        for _ in range(number):
            d = self.next
            self.next += 1
            self.wire.arrived(self.near_handles[d])

            def join(at, d=d):
                total = self.part[flip(self.index, 2 * d), at].astype(F32)
                total = total + self.from_near[d, at].astype(F32)
                self.to_far[d - 1, at] = total.astype(LOW)

            by_rows(self.rows, self.step, join)
            self.far_handles[d] = self.wire.copy(
                self.to_far.at[d - 1], self.from_far.at[d - 1], self.far[d - 1]
            )

    def close(self):
        self.wire.arrived(self.near_handles[0])
        for d in range(1, self.lines):
            self.wire.arrived(self.far_handles[d])
        width = self.part.shape[2]
        half = lax.rem(lax.div(self.index, 2), 2)

        def total(at):
            same = self.part[self.index, at].astype(F32) + self.from_near[0, at].astype(F32)
            other = None
            for d in range(1, self.lines):
                got = self.from_far[d - 1, at].astype(F32)
                if self.split and d % 2:
                    other = got if other is None else other + got
                else:
                    same = same + got
            if self.split:
                out = self.out
                out[at, pl.ds(pl.multiple_of(half * width, width), width)] = same
                out[at, pl.ds(pl.multiple_of((1 - half) * width, width), width)] = other
            else:
                self.out[at, :] = same

        by_rows(self.rows, self.step, total)


def seq_sum_scratch(part):
    lines = part.shape[0] // 2
    return [
        pltpu.VMEM((depth,) + part.shape[1:], LOW) for depth in (lines, lines - 1, lines - 1)
    ]


class RowSum:
    def __init__(self, wire, place, pair, part, core_got, y_send, y_got, pair_send, pair_got):
        self.wire, self.place, self.pair = wire, place, pair
        self.core, self.side = lax.rem(place, 2), lax.div(place, 2)
        self.part, self.core_got, self.y_send, self.y_got = part, core_got, y_send, y_got
        self.pair_send, self.pair_got = pair_send, pair_got
        self.sides = (1 - self.side, self.side)
        self.rows = part.shape[2]
        self.core_handles, self.y_handles = {}, {}

    def start(self):
        peer = {"tensor": flip(self.place, 1)}
        for which in range(2):
            for p in reversed(range(self.part.shape[0])):
                at = self.sides[which]
                block = self.part.at[p, 2 * at + 1 - self.core]
                self.core_handles[p, which] = self.wire.copy(block, self.core_got.at[p, at], peer)

    def both(self, p, which, at):
        side = self.sides[which]
        mine = self.part[p, 2 * side + self.core, at, :].astype(F32)
        return mine + self.core_got[p, side, at, :].astype(F32)

    def to_side(self, p):
        self.wire.arrived(self.core_handles[p, 0])

        def body(at):
            self.y_send[p, at, :] = self.both(p, 0, at).astype(LOW)

        by_rows(self.rows, 16, body)
        peer = {"tensor": flip(self.place, 2)}
        self.y_handles[p] = self.wire.copy(self.y_send.at[p], self.y_got.at[p], peer)

    def to_pair(self):
        self.wire.arrived(self.core_handles[1, 1])
        self.wire.arrived(self.y_handles[1])

        def body(at):
            total = self.both(1, 1, at) + self.y_got[1, at, :].astype(F32)
            self.pair_send[at, :] = total.astype(LOW)

        by_rows(self.rows, 16, body)
        self.pair_handle = self.wire.copy(self.pair_send, self.pair_got, self.pair)

    def ready(self):
        self.wire.arrived(self.core_handles[0, 1])
        self.wire.arrived(self.y_handles[0])
        if self.pair is not None:
            self.wire.arrived(self.pair_handle)

    def total(self, at):
        total = self.both(0, 1, at) + self.y_got[0, at, :].astype(F32)
        if self.pair is not None:
            total = total + self.pair_got[at, :].astype(F32)
        return total


def row_sum_scratch(part):
    pairs, _, rows, width = part.shape
    scratch = [pltpu.VMEM((pairs, 2, rows, width), LOW)]
    scratch += [pltpu.VMEM((pairs, rows, width), LOW)] * 2
    if pairs == 2:
        scratch += [pltpu.VMEM((rows, width), LOW)] * 2
    return scratch


class RowGather:
    def __init__(self, wire, place, rows):
        self.wire, self.place, self.rows = wire, place, rows

    def start(self):
        mine = self.rows.at[self.place]
        self.side_handle = self.wire.copy(mine, mine, {"tensor": flip(self.place, 2)})
        self.wire.copy(mine, mine, {"tensor": flip(self.place, 1)})

    def forward(self):
        self.wire.arrived(self.side_handle)
        block = self.rows.at[flip(self.place, 2)]
        self.wire.copy(block, block, {"tensor": flip(self.place, 1)})


def sem_scratch(copies):
    return [pltpu.SemaphoreType.DMA((copies,)), pltpu.SemaphoreType.DMA((copies,))]


def middle_kernel(count, *refs):
    back, proj, centre, dy, vec = refs[:5]
    proj_sum, grad, rows, sums = refs[5:9]
    row_refs, seq_refs, (send_sem, recv_sem) = refs[9:14], refs[14:17], refs[17:]
    index, place = lax.axis_index("seq"), lax.axis_index("tensor")
    along = seq_peers(index, count)
    greet(along + [{"tensor": flip(place, 1)}, {"tensor": flip(place, 2)}])
    wire = Wire(send_sem, recv_sem)
    reduce = RowSum(wire, place, along[0], back, *row_refs)
    bulk = SeqSum(wire, index, along, proj, *seq_refs, proj_sum, True)
    gather = RowGather(wire, place, rows)
    lines = count // 2
    reduce.start()
    bulk.start()
    reduce.to_side(1)
    reduce.to_side(0)
    bulk.relay(1)
    reduce.to_pair()
    bulk.relay((lines - 1) // 3)
    reduce.ready()
    sums[...] = jnp.zeros_like(sums)
    gain = vec[0:1, :]

    def body(at):
        over = reduce.total(at)
        inner, product = norm_back(centre[at, :], gain, over)
        value = dy[at, :].astype(F32) + inner
        grad[at, :] = value
        rows[place, at, :] = value.astype(LOW)
        sums[0] += product
        sums[1] += over
        sums[2] += value

    by_rows(centre.shape[0], 16, body)
    gather.start()
    bulk.relay(lines - 1 - 1 - (lines - 1) // 3)
    gather.forward()
    bulk.close()
    wire.finish()


def middle_stage(back, proj, centre, dy, vec):
    count = lax.axis_size("seq")
    tensor = lax.axis_size("tensor")
    part, full = centre.shape
    vmem = pl.BlockSpec(memory_space=pltpu.VMEM)
    copies = 2 * count + 12
    return pl.pallas_call(
        partial(middle_kernel, count),
        out_shape=[
            jax.ShapeDtypeStruct((proj.shape[1], 2 * proj.shape[2]), F32),
            jax.ShapeDtypeStruct((part, full), F32),
            jax.ShapeDtypeStruct((tensor, part, full), LOW),
            jax.ShapeDtypeStruct((3, 16, full), F32),
        ],
        in_specs=[vmem] * 5,
        out_specs=[vmem] * 4,
        scratch_shapes=row_sum_scratch(back) + seq_sum_scratch(proj) + sem_scratch(copies),
        compiler_params=pltpu.CompilerParams(
            collective_id=2, has_side_effects=True, vmem_limit_bytes=60 << 20
        ),
        name="middle",
    )(back, proj, centre, dy, vec)


def back_kernel(count, *refs):
    feed, fc, q_in, kv_in, mq_in, mk_in, mixed, lse, grad_o_in, centre, vec = refs[:11]
    fc_sum, dq, dkv, result = refs[11:15]
    row_refs, seq_refs, kv_refs = refs[15:20], refs[20:23], refs[23:26]
    kv_send, kv_got, kv_part, kv_total, delta, acc, send_sem, recv_sem = refs[26:]
    index, place = lax.axis_index("seq"), lax.axis_index("tensor")
    core = lax.rem(place, 2)
    other_core = {"tensor": flip(place, 1)}
    along = seq_peers(index, count)
    lines = count // 2
    spread = lines - 1
    greet(along + [other_core, {"tensor": flip(place, 2)}])
    wire = Wire(send_sem, recv_sem)
    reduce = RowSum(wire, place, along[0], feed, *row_refs)
    bulk = SeqSum(wire, index, along, fc, *seq_refs, fc_sum, True)
    keys_sum = SeqSum(wire, index, along, kv_part, *kv_refs, kv_total, False)
    gather = RowGather(wire, place, result)
    hd = kv_in.shape[-1] // 2
    heads = q_in.shape[-1] // hd
    scale = float(hd) ** (-0.5)
    scale_two = scale * LOG2E
    near_x = 1 - lax.rem(index, 2)

    def open_batch(batch):
        acc[...] = jnp.zeros_like(acc)
        for head in range(heads):
            cols = slice(head * hd, (head + 1) * hd)
            product = grad_o_in[batch, :, cols].astype(F32) * mixed[batch, :, cols].astype(F32)
            delta[head] = jnp.sum(product, axis=-1, keepdims=True)

    def blocks_of(batch, which, target, extra):
        def body(line, carry):
            block = 2 * line + which
            mask = visible(mq_in[batch], mk_in[batch, block])
            keys = kv_in[batch, block, :, :hd]
            values = kv_in[batch, block, :, hd:]
            grad_k = jnp.zeros((keys.shape[0], hd), F32)
            grad_v = jnp.zeros((keys.shape[0], hd), F32)
            for head in range(heads):
                cols = slice(head * hd, (head + 1) * hd)
                query = q_in[batch, :, cols]
                grad_o = grad_o_in[batch, :, cols]
                scores = dot_nt(query, keys) * scale_two
                probs = jnp.where(mask, jnp.exp2(scores - lse[batch, head]), 0.0)
                grad_p = dot_nt(grad_o, values)
                grad_s = (probs * (grad_p - delta[head])).astype(LOW)
                acc[:, cols] += dot(grad_s, keys)
                grad_k = grad_k + dot_tn(grad_s, query)
                grad_v = grad_v + dot_tn(probs.astype(LOW), grad_o)
            grad_k = grad_k * scale
            if extra is not None:
                grad_k = grad_k + extra[block, :, :hd].astype(F32)
                grad_v = grad_v + extra[block, :, hd:].astype(F32)
            target[block, :, :hd] = grad_k.astype(LOW)
            target[block, :, hd:] = grad_v.astype(LOW)
            return carry

        lax.fori_loop(0, lines, body, 0)

    def close_batch(batch):
        dq[batch] = (acc[...] * scale).astype(LOW)

    def to_core(which):
        return [
            wire.copy(kv_send.at[2 * line + which], kv_got.at[2 * line + which], other_core)
            for line in range(lines)
        ]

    reduce.start()
    bulk.start(list(range(1, lines)))
    open_batch(1 - core)
    blocks_of(1 - core, near_x, kv_send, None)
    near_handles = to_core(near_x)
    reduce.to_side(1)
    reduce.to_side(0)
    blocks_of(1 - core, 1 - near_x, kv_send, None)
    own_handles = to_core(1 - near_x)
    close_batch(1 - core)
    bulk.relay(spread // 3)
    for handle in near_handles:
        wire.arrived(handle)
    open_batch(core)
    blocks_of(core, near_x, kv_part, kv_got)
    keys_sum.start()
    bulk.start([0])
    reduce.to_pair()
    bulk.relay(spread // 3)
    for handle in own_handles:
        wire.arrived(handle)
    blocks_of(core, 1 - near_x, kv_part, kv_got)
    close_batch(core)
    reduce.ready()
    bias = vec[0:1, :]

    def body(at):
        total = centre[at, :] + reduce.total(at) + bias
        result[place, at, :] = total.astype(LOW)

    by_rows(centre.shape[0], 16, body)
    gather.start()
    keys_sum.relay(spread)
    bulk.relay(spread - 2 * (spread // 3))
    gather.forward()
    keys_sum.close()
    dkv[1 - core] = jnp.zeros(dkv.shape[1:], LOW)
    dkv[core] = kv_total[...].astype(LOW)
    bulk.close()
    wire.finish()


def back_stage(feed, fc, queries, keyval, meta_q, meta_k, mixed, lse, grad_mixed, centre, vec):
    count = lax.axis_size("seq")
    tensor = lax.axis_size("tensor")
    part, full = centre.shape
    batches, rows, width = queries.shape
    blocks, two = keyval.shape[1], keyval.shape[3]
    heads = 2 * width // two
    vmem = pl.BlockSpec(memory_space=pltpu.VMEM)
    kv_part = jax.ShapeDtypeStruct((blocks, rows, two), LOW)
    copies = 3 * count + 14
    return pl.pallas_call(
        partial(back_kernel, count),
        out_shape=[
            jax.ShapeDtypeStruct((fc.shape[1], 2 * fc.shape[2]), F32),
            jax.ShapeDtypeStruct((batches, rows, width), LOW),
            jax.ShapeDtypeStruct((batches, rows, two), LOW),
            jax.ShapeDtypeStruct((tensor, part, full), LOW),
        ],
        in_specs=[vmem] * 11,
        out_specs=[vmem] * 4,
        scratch_shapes=row_sum_scratch(feed)
        + seq_sum_scratch(fc)
        + seq_sum_scratch(kv_part)
        + [pltpu.VMEM(kv_part.shape, LOW)] * 3
        + [
            pltpu.VMEM((rows, two), F32),
            pltpu.VMEM((heads, rows, 1), F32),
            pltpu.VMEM((rows, width), F32),
        ]
        + sem_scratch(copies),
        compiler_params=pltpu.CompilerParams(
            collective_id=3, has_side_effects=True, vmem_limit_bytes=60 << 20
        ),
        name="back",
    )(feed, fc, queries, keyval, meta_q, meta_k, mixed, lse, grad_mixed, centre, vec)


def last_kernel(count, *refs):
    back, out, query, keyval, own, dy, vec = refs[:7]
    out_sum, query_sum, keyval_sum, rows, sums = refs[7:12]
    row_refs = list(refs[12:15]) + [None, None]
    out_refs, query_refs, keyval_refs = refs[15:18], refs[18:21], refs[21:24]
    send_sem, recv_sem = refs[24:]
    index, place = lax.axis_index("seq"), lax.axis_index("tensor")
    along = seq_peers(index, count)
    greet(along + [{"tensor": flip(place, 1)}, {"tensor": flip(place, 2)}])
    wire = Wire(send_sem, recv_sem)
    reduce = RowSum(wire, place, None, back, *row_refs)
    out_bulk = SeqSum(wire, index, along, out, *out_refs, out_sum, False)
    query_bulk = SeqSum(wire, index, along, query, *query_refs, query_sum, False)
    keyval_bulk = SeqSum(wire, index, along, keyval, *keyval_refs, keyval_sum, False)
    gather = RowGather(wire, place, rows)
    spread = count // 2 - 1
    first = 2 * spread // 3
    reduce.start()
    for bulk in (out_bulk, query_bulk, keyval_bulk):
        bulk.start()
    reduce.to_side(0)
    out_bulk.relay(first)
    reduce.ready()
    sums[...] = jnp.zeros_like(sums)
    gain = vec[0:1, :]

    def body(at):
        over = reduce.total(at)
        inner, product = norm_back(own[at, :].astype(F32), gain, over)
        rows[place, at, :] = (dy[at, :] + inner).astype(LOW)
        sums[0] += product
        sums[1] += over

    by_rows(own.shape[0], 16, body)
    gather.start()
    out_bulk.relay(spread - first)
    gather.forward()
    query_bulk.relay(spread)
    keyval_bulk.relay(spread)
    for bulk in (out_bulk, query_bulk, keyval_bulk):
        bulk.close()
    wire.finish()


def last_stage(back, out, query, keyval, own, dy, vec):
    count = lax.axis_size("seq")
    tensor = lax.axis_size("tensor")
    part, full = own.shape
    vmem = pl.BlockSpec(memory_space=pltpu.VMEM)
    bulk = (out, query, keyval)
    copies = 3 * count + 8
    scratch = row_sum_scratch(back)
    for array in bulk:
        scratch += seq_sum_scratch(array)
    return pl.pallas_call(
        partial(last_kernel, count),
        out_shape=[jax.ShapeDtypeStruct(array.shape[1:], F32) for array in bulk]
        + [
            jax.ShapeDtypeStruct((tensor, part, full), LOW),
            jax.ShapeDtypeStruct((2, 16, full), F32),
        ],
        in_specs=[vmem] * 7,
        out_specs=[vmem] * 5,
        scratch_shapes=scratch + sem_scratch(copies),
        compiler_params=pltpu.CompilerParams(
            collective_id=4, has_side_effects=True, vmem_limit_bytes=60 << 20
        ),
        name="last",
    )(back, out, query, keyval, own, dy, vec)


def visible(meta_q, meta_k):
    seg_q, pos_q = meta_q[:, 0:1], meta_q[:, 1:2]
    seg_k, pos_k = meta_k[0:1, :], meta_k[1:2, :]
    return ((seg_k == 0) | (seg_k == seg_q)) & (pos_k <= pos_q)


def tensor_scatter(parts, axis):
    count = lax.axis_size("tensor")
    index = lax.axis_index("tensor")
    for bit in range(bits_of(count)):
        shape = parts.shape
        split = parts.reshape(shape[:axis] + (shape[axis] // 2, 2) + shape[axis + 1 :])
        mine = (index >> bit) & 1
        keep = lax.dynamic_index_in_dim(split, mine, axis + 1, keepdims=False)
        give = lax.dynamic_index_in_dim(split, 1 - mine, axis + 1, keepdims=False)
        parts = keep.astype(F32) + swap(give.astype(LOW), "tensor", bit).astype(F32)
    return lax.squeeze(parts, (axis,))


def norm_parts(values):
    average = jnp.mean(values, axis=-1, keepdims=True)
    centred = values - average
    spread = jnp.mean(centred * centred, axis=-1, keepdims=True)
    return centred, lax.rsqrt(spread + EPS)


def norm_back(values, gain, grad):
    centred, inverse = norm_parts(values)
    unit = centred * inverse
    scaled = grad * gain
    inner = (
        scaled
        - jnp.mean(scaled, axis=-1, keepdims=True)
        - unit * jnp.mean(scaled * unit, axis=-1, keepdims=True)
    )
    return inverse * inner, grad * unit


def gelu_pair(values):
    const = 0.7978845608028654
    square = values * values
    inner = jnp.tanh(const * (values + 0.044715 * (values * square)))
    half = 0.5 * (1.0 + inner)
    slope = half + 0.5 * values * (1.0 - inner * inner) * const * (1.0 + 3 * 0.044715 * square)
    return values * half, slope


def local(
    inputs,
    segment,
    position,
    w_query,
    w_keyval,
    w_out,
    w_fc,
    w_proj,
    vectors,
    fc_bias,
    value_bias,
    grad_out,
):
    seq_size, tensor_size = lax.axis_size("seq"), lax.axis_size("tensor")
    seq_index, tensor_index = lax.axis_index("seq"), lax.axis_index("tensor")
    batches, rows, full_width = inputs.shape
    width_block = w_query.shape[0]
    group_width = w_query.shape[1]
    hidden_width = w_fc.shape[1]
    unit_width = hidden_width // 2
    unit_half = (seq_index >> 1) & 1
    hd = value_bias.shape[0]
    quarter = rows // tensor_size
    shard = vectors.shape[1]
    bias_shard = fc_bias.shape[0]

    pieces = [
        vectors.reshape(-1).astype(LOW),
        fc_bias.astype(LOW),
        segment.reshape(-1).astype(LOW),
        (position // 128).reshape(-1).astype(LOW),
        (position % 128).reshape(-1).astype(LOW),
    ]
    cuts = [0]
    for piece in pieces:
        cuts.append(cuts[-1] + piece.shape[0])
    packed = jnp.concatenate(pieces)
    packed = jnp.pad(packed, (0, -packed.shape[0] % 2048)).reshape(-1, 128)

    def halves(array):
        return jnp.swapaxes(array.astype(LOW).reshape(width_block, 2, unit_width), 0, 1)

    small, kv_mat, q_mat = gather_first(packed, w_keyval.astype(LOW), w_query.astype(LOW))
    kv_mat = kv_mat.reshape(full_width, 2 * hd)
    q_mat = q_mat.reshape(full_width, group_width)

    small = small.reshape(seq_size, tensor_size, -1).astype(F32)
    vec_all = small[:, :, cuts[0] : cuts[1]].reshape(seq_size * tensor_size, 7, shard)
    vec_all = jnp.swapaxes(vec_all, 0, 1).reshape(7, full_width)
    fc_all = small[:, :, cuts[1] : cuts[2]].reshape(-1)
    seg_keys = small[:, 0, cuts[2] : cuts[3]].reshape(seq_size, batches, rows)
    pos_keys = 128.0 * small[:, 0, cuts[3] : cuts[4]] + small[:, 0, cuts[4] : cuts[5]]
    seg_keys = jnp.swapaxes(seg_keys, 0, 1).astype(jnp.int32)
    pos_keys = jnp.swapaxes(pos_keys.reshape(seq_size, batches, rows), 0, 1).astype(jnp.int32)
    meta_k = jnp.pad(jnp.stack([seg_keys, pos_keys], axis=2), ((0, 0), (0, 0), (0, 6), (0, 0)))
    meta_q = jnp.pad(jnp.stack([segment, position], axis=2), ((0, 0), (0, 0), (0, 126)))

    gain_one, shift_one, _, out_bias, gain_two, shift_two, proj_bias = [
        vec_all[i] for i in range(7)
    ]
    query_bias = lax.dynamic_slice_in_dim(vec_all[2], tensor_index * group_width, group_width, 0)
    fc_local = lax.dynamic_slice_in_dim(
        fc_all, tensor_index * hidden_width + unit_half * unit_width, unit_width, 0
    )
    bias_value = value_bias.astype(LOW).astype(F32)
    kv_bias = jnp.concatenate([jnp.zeros((hd,), F32), bias_value])

    residual = inputs.astype(F32)
    centred, inverse = norm_parts(residual)
    normed = (centred * inverse * gain_one + shift_one).astype(LOW).reshape(-1, full_width)
    keyval = (dot(normed, kv_mat) + kv_bias).astype(LOW).reshape(batches, rows, 2 * hd)
    queries = (dot(normed, q_mat) + query_bias).astype(LOW)
    queries = queries.reshape(batches, rows, group_width)

    def by_quarter(array):
        split = array.reshape(batches, tensor_size, quarter, array.shape[-1])
        return jnp.swapaxes(split, 0, 1).reshape(tensor_size, batches * quarter, -1)

    def by_batch(array):
        split = array.reshape(tensor_size, batches, quarter, array.shape[-1])
        return jnp.swapaxes(split, 0, 1).reshape(batches, rows, -1)

    def my_quarter(array):
        split = array.reshape(batches, tensor_size, quarter, full_width)
        own = lax.dynamic_index_in_dim(split, tensor_index, 1, keepdims=False)
        return own.reshape(batches * quarter, full_width)

    vecs = jnp.pad(jnp.stack([out_bias, gain_two, shift_two]), ((0, 5), (0, 0)))
    grad_split = by_quarter(grad_out)
    mixed, lse, kv_all, out_t, middle, rows_two, fc_mat, proj_t, grad_other = front(
        queries,
        keyval,
        meta_q,
        meta_k,
        my_quarter(inputs),
        vecs,
        w_out.T.astype(LOW),
        halves(w_fc),
        halves(w_proj.T),
        grad_split,
    )
    out_t = out_t.reshape(full_width, group_width)
    fc_mat = fc_mat.reshape(full_width, unit_width)
    proj_t = proj_t.reshape(full_width, unit_width)
    mixed_rows = by_quarter(mixed).reshape(-1, group_width)
    normed_two = rows_two.reshape(-1, full_width)
    hidden = dot(normed_two, fc_mat) + fc_local
    active_f, slope = gelu_pair(hidden)
    active = active_f.astype(LOW)

    grad_q_low = my_quarter(grad_out)
    grad_flat = jnp.concatenate([grad_split, grad_other]).reshape(-1, full_width)
    grad_hidden = (slope * dot(grad_flat, proj_t)).astype(LOW)
    fcbias_local = jnp.sum(grad_hidden.astype(F32), axis=0)
    back_part = dot_nt(grad_hidden, fc_mat).astype(LOW)
    back_part = back_part.reshape(2, tensor_size, batches * quarter, full_width)

    def blocked(array):
        return array.astype(LOW).reshape(seq_size, width_block, array.shape[-1])

    proj_sum, grad_middle, rows_middle, sums = middle_stage(
        back_part,
        blocked(dot_tn(grad_flat, active)),
        middle,
        grad_q_low,
        jnp.pad(gain_two[None], ((0, 7), (0, 0))),
    )
    grad_gain_two, grad_shift_two, grad_out_bias = jnp.sum(sums, axis=1)
    grad_proj_bias = jnp.sum(grad_q_low.astype(F32), axis=0)
    grad_middle_low = rows_middle.reshape(-1, full_width)
    def one_row(row):
        return jnp.pad(row[None], ((0, 7), (0, 0)))

    grad_mixed = by_batch(dot(grad_middle_low, out_t).astype(LOW))
    feed_part = dot_nt(active, proj_t).astype(LOW)
    fc_sum, grad_queries, grad_keyval, result_rows = back_stage(
        feed_part.reshape(2, tensor_size, batches * quarter, full_width),
        blocked(dot_tn(normed_two, grad_hidden)),
        queries,
        kv_all,
        meta_q,
        meta_k,
        mixed,
        lse,
        grad_mixed,
        middle,
        one_row(proj_bias),
    )
    result = by_batch(result_rows)
    grad_keyval = grad_keyval.reshape(-1, 2 * hd)
    grad_queries = grad_queries.reshape(-1, group_width)
    grad_normed = dot_nt(grad_queries, q_mat) + dot_nt(grad_keyval, kv_mat)
    out_sum, query_sum, kv_sum, input_rows, sums_one = last_stage(
        by_quarter(grad_normed.astype(LOW))[None],
        blocked(dot_tn(grad_middle_low, mixed_rows)),
        blocked(dot_tn(normed, grad_queries)),
        blocked(dot_tn(normed, grad_keyval)),
        my_quarter(inputs),
        grad_middle,
        one_row(gain_one),
    )
    input_grad = by_batch(input_rows)
    grad_gain_one, grad_shift_one = jnp.sum(sums_one, axis=1)
    qbias_local = jnp.sum(grad_queries.astype(F32), axis=0)
    vbias_local = jnp.sum(grad_keyval[:, hd:].astype(F32), axis=0)

    qbias_full = lax.dynamic_update_slice_in_dim(
        jnp.zeros((full_width,), F32), qbias_local, tensor_index * group_width, 0
    )
    full_hidden = bias_shard * seq_size * tensor_size
    fcbias_full = lax.dynamic_update_slice_in_dim(
        jnp.zeros((full_hidden,), F32),
        fcbias_local,
        tensor_index * hidden_width + unit_half * unit_width,
        0,
    )
    vec_grads = jnp.stack(
        [
            grad_gain_one,
            grad_shift_one,
            qbias_full,
            grad_out_bias,
            grad_gain_two,
            grad_shift_two,
            grad_proj_bias,
        ]
    )
    chunk = full_hidden // seq_size
    vec_cut = 7 * width_block
    rows_all = jnp.concatenate(
        [
            jnp.swapaxes(vec_grads.reshape(7, seq_size, width_block), 0, 1).reshape(seq_size, -1),
            fcbias_full.reshape(seq_size, chunk),
            jnp.broadcast_to(vbias_local, (seq_size, hd)),
        ],
        axis=1,
    )
    rows_all = jnp.pad(rows_all, ((0, 0), (0, -rows_all.shape[1] % 1024)))
    rows_all = rows_all.reshape(seq_size, -1, 128)
    for bit in reversed(range(bits_of(seq_size))):
        size = rows_all.shape[0] // 2
        mine = (seq_index >> bit) & 1
        keep = lax.dynamic_slice_in_dim(rows_all, mine * size, size, 0)
        give = lax.dynamic_slice_in_dim(rows_all, (1 - mine) * size, size, 0)
        rows_all = keep + swap(give, "seq", bit)
    small_sum = rows_all[0]
    for bit in range(bits_of(tensor_size)):
        small_sum = small_sum + swap(small_sum, "tensor", bit)
    small_sum = small_sum.reshape(-1)
    vec_grad = lax.dynamic_slice_in_dim(
        small_sum[:vec_cut].reshape(7, width_block), tensor_index * shard, shard, 1
    )
    fcbias_grad = lax.dynamic_slice_in_dim(
        small_sum[vec_cut : vec_cut + chunk], tensor_index * bias_shard, bias_shard, 0
    )
    vbias_grad = small_sum[vec_cut + chunk : vec_cut + chunk + hd]
    keyval_grad = tensor_scatter(kv_sum.reshape(tensor_size, -1, 2 * hd), 0)
    return (
        result,
        input_grad,
        query_sum,
        keyval_grad,
        out_sum.T,
        fc_sum,
        proj_sum.T,
        vec_grad,
        fcbias_grad,
        vbias_grad,
        vec_grad[5],
    )


def solution(mesh):
    in_specs = (
        P(None, "seq", None),
        P(None, "seq"),
        P(None, "seq"),
        P("seq", "tensor"),
        P(("seq", "tensor"), None),
        P("tensor", "seq"),
        P("seq", "tensor"),
        P("tensor", "seq"),
        P(None, ("seq", "tensor")),
        P(("seq", "tensor")),
        P(),
        P(None, "seq", None),
    )
    out_specs = (
        P(None, "seq", None),
        P(None, "seq", None),
        P("seq", "tensor"),
        P(("seq", "tensor"), None),
        P("tensor", "seq"),
        P("seq", "tensor"),
        P("tensor", "seq"),
        P(None, ("seq", "tensor")),
        P(("seq", "tensor")),
        P(),
        P(("seq", "tensor")),
    )
    return jax.shard_map(local, mesh=mesh, in_specs=in_specs, out_specs=out_specs, check_vma=False)
```

```python
from functools import partial

import jax
import jax.numpy as jnp
from jax import lax
from jax.experimental import pallas as pl
from jax.experimental.pallas import tpu as pltpu
from jax.sharding import PartitionSpec as P

EPS = 1e-05
NEG = -1e30
LOG2E = 1.4426950408889634
LOW = jnp.bfloat16
F32 = jnp.float32


def bits_of(count):
    return count.bit_length() - 1


def swap(value, axis, bit):
    count = lax.axis_size(axis)
    return lax.ppermute(value, axis, [(i, i ^ (1 << bit)) for i in range(count)])


def after(value, *others):
    return lax.optimization_barrier((value,) + others)[0]


def dot(left, right):
    return jnp.dot(left, right, preferred_element_type=F32)


def dot_tn(left, right):
    return lax.dot_general(left, right, (((0,), (0,)), ((), ())), preferred_element_type=F32)


def dot_nt(left, right):
    return lax.dot_general(left, right, (((1,), (1,)), ((), ())), preferred_element_type=F32)


MESH = pl.DeviceIdType.MESH


def flip(index, mask):
    bit = 1
    out = index
    while bit <= mask:
        if mask & bit:
            out = out + bit * (1 - 2 * lax.rem(lax.div(index, bit), 2))
        bit *= 2
    return out


class Wire:
    def __init__(self, send_sem, recv_sem):
        self.send_sem, self.recv_sem = send_sem, recv_sem
        self.started = []
        self.landed = set()

    def copy(self, src, dst, peer):
        place = len(self.started)
        item = pltpu.make_async_remote_copy(
            src_ref=src,
            dst_ref=dst,
            send_sem=self.send_sem.at[place],
            recv_sem=self.recv_sem.at[place],
            device_id=peer,
            device_id_type=MESH,
        )
        item.start()
        self.started.append(item)
        return place

    def arrived(self, place):
        if place not in self.landed:
            self.landed.add(place)
            self.started[place].wait_recv()

    def finish(self):
        for place in range(len(self.started)):
            self.arrived(place)
        for item in self.started:
            item.wait_send()


def greet(peers):
    barrier = pltpu.get_barrier_semaphore()
    for peer in peers:
        pl.semaphore_signal(barrier, inc=1, device_id=peer, device_id_type=MESH)
    pl.semaphore_wait(barrier, len(peers))


def seq_peers(index, count):
    return [{"seq": flip(index, 2 * d)} for d in range(1, count // 2)] + [
        {"seq": flip(index, 1)}
    ]


def first_kernel(count, tensor, *refs):
    ins, outs = refs[:3], refs[3:6]
    send_sem, recv_sem, local_sem = refs[6:]
    index = lax.axis_index("seq")
    place = lax.axis_index("tensor")
    across = [{"tensor": flip(place, tensor >> (i + 1))} for i in range(bits_of(tensor))]
    along = seq_peers(index, count)
    far, near = along[:-1], along[-1]
    greet(across + along)
    wire = Wire(send_sem, recv_sem)
    own = []
    targets = [(lambda at, out=out: out.at[at, place]) for out in outs[:2]]
    targets.append(lambda at: outs[2].at[at])
    handles = []
    for source, target in zip(ins, targets):
        handles.append([wire.copy(source, target(index), peer) for peer in far])
        handles[-1].append(wire.copy(source, target(index), near))
        item = pltpu.make_async_copy(source, target(index), local_sem.at[len(own)])
        item.start()
        own.append(item)
    relays = []
    for a, target in enumerate(targets):
        for d in range(1, count // 2):
            wire.arrived(handles[a][d - 1])
            block = target(flip(index, 2 * d))
            relays.append(wire.copy(block, block, near))
        if a == 1:
            for handle in [handles[0][-1], handles[1][-1]] + relays:
                wire.arrived(handle)
            own[0].wait()
            own[1].wait()
            masks = [0]
            for i, peer in enumerate(across):
                step = tensor >> (i + 1)
                sent = [
                    wire.copy(out.at[:, flip(place, mask)], out.at[:, flip(place, mask)], peer)
                    for mask in masks
                    for out in outs[:2]
                ]
                masks = masks + [mask | step for mask in masks]
                if i + 1 < len(across):
                    for handle in sent:
                        wire.arrived(handle)
    own[2].wait()
    wire.finish()


def gather_first(small, keyval, query):
    count, tensor = lax.axis_size("seq"), lax.axis_size("tensor")
    arrays = (small, keyval, query)
    shapes = [
        (count, tensor) + small.shape,
        (count, tensor) + keyval.shape,
        (count,) + query.shape,
    ]
    copies = 3 * (count - 1) + 2 * (tensor - 1)
    return pl.pallas_call(
        partial(first_kernel, count, tensor),
        out_shape=[jax.ShapeDtypeStruct(shape, LOW) for shape in shapes],
        in_specs=[pl.BlockSpec(memory_space=pltpu.VMEM)] * 3,
        out_specs=[pl.BlockSpec(memory_space=pltpu.VMEM)] * 3,
        scratch_shapes=[
            pltpu.SemaphoreType.DMA((copies,)),
            pltpu.SemaphoreType.DMA((copies,)),
            pltpu.SemaphoreType.DMA((3,)),
        ],
        compiler_params=pltpu.CompilerParams(collective_id=0, has_side_effects=True),
        name="gather_first",
    )(*arrays)


def front_kernel(count, *refs):
    q_in, kv_in, mq_in, mk_in, x_in, vec_in, o_in, fc_in, pj_in, dy_in = refs[:10]
    mixed, lse, kv_all, out_t, middle, rows_two, fc_out, pj_out, dy_out = refs[10:19]
    (
        top,
        total,
        acc,
        core_keep,
        core_send,
        core_got,
        y_send,
        y_got,
        send_sem,
        recv_sem,
        local_sem,
    ) = refs[19:]
    index = lax.axis_index("seq")
    place = lax.axis_index("tensor")
    core = lax.rem(place, 2)
    side = lax.div(place, 2)
    half = lax.rem(lax.div(index, 2), 2)
    other_core = {"tensor": flip(place, 1)}
    other_side = {"tensor": flip(place, 2)}
    across = {"tensor": flip(place, 3)}
    along = seq_peers(index, count)
    far, near = along[:-1], along[-1]
    pair = far[0]
    lines = count // 2
    greet(along + [other_core, other_side, across])
    wire = Wire(send_sem, recv_sem)
    own = []

    def keep(src, dst):
        item = pltpu.make_async_copy(src, dst, local_sem.at[len(own)])
        item.start()
        own.append(item)

    kv_far = [wire.copy(kv_in.at[core], kv_all.at[core, index], peer) for peer in far]
    kv_near = wire.copy(kv_in.at[core], kv_all.at[core, index], near)
    for batch in range(2):
        keep(kv_in.at[batch], kv_all.at[batch, index])
    o_far = [wire.copy(o_in, out_t.at[index], peer) for peer in far]
    o_near = [wire.copy(o_in, out_t.at[index], near)]
    keep(o_in, out_t.at[index])
    dy_pair = wire.copy(dy_in.at[place], dy_out.at[place], pair)

    def send_far(source, out):
        return [
            wire.copy(source.at[flip(half, d & 1)], out.at[index], far[d - 1])
            for d in range(1, lines)
        ]

    fc_far = send_far(fc_in, fc_out)
    kv_near = [(1, kv_near)]
    kv_core = []
    for d in range(1, lines):
        wire.arrived(kv_far[d - 1])
        block = kv_all.at[core, flip(index, 2 * d)]
        kv_near.append((2 * d + 1, wire.copy(block, block, near)))
        kv_core.append(wire.copy(block, block, other_core))
    wire.copy(fc_in.at[half], fc_out.at[index], near)
    wire.copy(pj_in.at[half], pj_out.at[index], near)
    keep(fc_in.at[half], fc_out.at[index])
    keep(pj_in.at[half], pj_out.at[index])
    for r, handle in kv_near:
        wire.arrived(handle)
        block = kv_all.at[core, flip(index, r)]
        kv_core.append(wire.copy(block, block, other_core))
    own[0].wait()
    own[1].wait()

    jobs = [(o_far, out_t, d) for d in range(1, lines)]
    jobs += [(fc_far, fc_out, d) for d in range(1, lines)]

    def tick(number):
        for _ in range(min(number, len(jobs))):
            handles, out, d = jobs.pop(0)
            wire.arrived(handles[d - 1])
            block = out.at[flip(index, 2 * d)]
            handle = wire.copy(block, block, near)
            if out is out_t:
                o_near.append(handle)

    hd = kv_in.shape[-1] // 2
    heads = q_in.shape[-1] // hd
    scale = float(hd) ** (-0.5) * LOG2E

    def attend(batch, block):
        mask = visible(mq_in[batch], mk_in[batch, block])
        keys = kv_all[batch, block, :, :hd]
        values = kv_all[batch, block, :, hd:]
        for head in range(heads):
            cols = slice(head * hd, (head + 1) * hd)
            scores = jnp.where(mask, dot_nt(q_in[batch, :, cols], keys) * scale, NEG)
            before = top[head]
            now = jnp.maximum(before, jnp.max(scores, axis=-1, keepdims=True))
            shrink = jnp.exp2(before - now)
            probs = jnp.exp2(scores - now)
            total[head] = total[head] * shrink + jnp.sum(probs, axis=-1, keepdims=True)
            acc[:, cols] = acc[:, cols] * shrink + dot(probs.astype(LOW), values)
            top[head] = now

    def attend_batch(batch, ticks):
        top[...] = jnp.full_like(top, NEG)
        total[...] = jnp.zeros_like(total)
        acc[...] = jnp.zeros_like(acc)

        def block_body(block, carry):
            attend(batch, block)
            return carry

        parts = len(ticks)
        for i in range(parts):
            lax.fori_loop(i * count // parts, (i + 1) * count // parts, block_body, 0)
            tick(ticks[i])
        for head in range(heads):
            cols = slice(head * hd, (head + 1) * hd)
            mixed[batch, :, cols] = (acc[:, cols] / total[head]).astype(LOW)
            lse[batch, head] = top[head] + jnp.log2(total[head])

    spread = lines - 1
    attend_batch(core, [spread // 3, spread - spread // 3])
    for handle in kv_core:
        wire.arrived(handle)
    attend_batch(1 - core, [0, spread // 3])
    wire.arrived(dy_pair)
    for peer in (other_core, other_side, across):
        wire.copy(dy_out.at[place], dy_out.at[place], peer)

    quarter = x_in.shape[0] // 2
    for handle in o_near:
        wire.arrived(handle)
    own[2].wait()
    width = out_t.shape[1]
    group = max(1, 256 // width)
    for which, target in ((1 - core, core_send), (core, core_keep)):
        rows = [
            mixed[batch, pl.ds(pl.multiple_of((2 * s + which) * quarter, quarter), quarter), :]
            for s in range(2)
            for batch in range(2)
        ]
        rows = jnp.concatenate(rows, axis=0)

        def project(i, carry, rows=rows, target=target):
            cols = pl.ds(pl.multiple_of(i * group * width, group * width), group * width)
            block = out_t[pl.ds(i * group, group)].reshape(group * width, -1)
            target[:, cols] = dot_nt(rows, block).astype(target.dtype)
            return carry

        lax.fori_loop(0, count // group, project, 0)
        if target is core_send:
            core_handle = wire.copy(core_send, core_got, other_core)
    wire.arrived(core_handle)
    part = 2 * quarter
    step = 16

    def to_side(i, carry):
        at = pl.ds(pl.multiple_of((1 - side) * part + i * step, step), step)
        y_send[pl.ds(pl.multiple_of(i * step, step), step), :] = (
            core_keep[at, :] + core_got[at, :].astype(F32)
        ).astype(LOW)
        return carry

    lax.fori_loop(0, part // step, to_side, 0)
    y_handle = wire.copy(y_send, y_got, other_side)
    tick(spread - spread // 3 - 1)
    wire.arrived(y_handle)
    out_bias, gain_two, shift_two = vec_in[0:1, :], vec_in[1:2, :], vec_in[2:3, :]

    def norm(i, carry):
        at = pl.ds(pl.multiple_of(i * step, step), step)
        far_at = pl.ds(pl.multiple_of(side * part + i * step, step), step)
        value = core_keep[far_at, :] + core_got[far_at, :].astype(F32)
        value = value + y_got[at, :].astype(F32)
        value = x_in[at, :].astype(F32) + value + out_bias
        middle[at, :] = value
        centred, inverse = norm_parts(value)
        rows_two[0, place, at, :] = (centred * inverse * gain_two + shift_two).astype(LOW)
        return carry

    lax.fori_loop(0, part // step, norm, 0)
    mine = rows_two.at[0, place]
    pair_handle = wire.copy(mine, rows_two.at[1, place], pair)
    side_handle = wire.copy(mine, mine, other_side)
    wire.copy(mine, mine, other_core)
    pj_far = send_far(pj_in, pj_out)
    tick(len(jobs))
    jobs.extend((pj_far, pj_out, d) for d in range(1, lines))
    wire.arrived(pair_handle)
    theirs = rows_two.at[1, place]
    side_two = wire.copy(theirs, theirs, other_side)
    wire.copy(theirs, theirs, other_core)
    wire.arrived(side_handle)
    block = rows_two.at[0, flip(place, 2)]
    wire.copy(block, block, other_core)
    wire.arrived(side_two)
    block = rows_two.at[1, flip(place, 2)]
    wire.copy(block, block, other_core)
    tick(len(jobs))
    for item in own[3:]:
        item.wait()
    wire.finish()


def front(queries, keyval, meta_q, meta_k, own_rows, vecs, out, fc, proj, grad_rows):
    count = lax.axis_size("seq")
    tensor = lax.axis_size("tensor")
    batches, rows, width = queries.shape
    two = keyval.shape[2]
    heads = 2 * width // two
    part, full = own_rows.shape
    shapes = [
        ((batches, rows, width), LOW),
        ((batches, heads, rows, 1), F32),
        ((batches, count, rows, two), LOW),
        ((count,) + out.shape, LOW),
        ((part, full), F32),
        ((2, tensor, part, full), LOW),
        ((count,) + fc.shape[1:], LOW),
        ((count,) + proj.shape[1:], LOW),
        ((tensor, part, full), LOW),
    ]
    copies = 2 * (count - 1) + 3 * (count - 1) + 4 + 2 + 7
    vmem, hbm = pl.BlockSpec(memory_space=pltpu.VMEM), pl.BlockSpec(memory_space=pl.ANY)
    return pl.pallas_call(
        partial(front_kernel, count),
        out_shape=[jax.ShapeDtypeStruct(shape, dtype) for shape, dtype in shapes],
        in_specs=[vmem] * 6 + [hbm] * 4,
        out_specs=[vmem] * 6 + [hbm] * 3,
        scratch_shapes=[
            pltpu.VMEM((heads, rows, 1), F32),
            pltpu.VMEM((heads, rows, 1), F32),
            pltpu.VMEM((rows, width), F32),
            pltpu.VMEM((2 * part, full), F32),
            pltpu.VMEM((2 * part, full), LOW),
            pltpu.VMEM((2 * part, full), LOW),
            pltpu.VMEM((part, full), LOW),
            pltpu.VMEM((part, full), LOW),
            pltpu.SemaphoreType.DMA((copies,)),
            pltpu.SemaphoreType.DMA((copies,)),
            pltpu.SemaphoreType.DMA((5,)),
        ],
        compiler_params=pltpu.CompilerParams(
            collective_id=1, has_side_effects=True, vmem_limit_bytes=56 << 20
        ),
        name="front",
    )(queries, keyval, meta_q, meta_k, own_rows, vecs, out, fc, proj, grad_rows)


def by_rows(rows, step, body):
    def run(i, carry):
        body(pl.ds(pl.multiple_of(i * step, step), step))
        return carry

    lax.fori_loop(0, rows // step, run, 0)


class SeqSum:
    def __init__(self, wire, index, peers, part, from_near, to_far, from_far, out, split):
        self.wire, self.index = wire, index
        self.far, self.near = peers[:-1], peers[-1]
        self.lines = len(peers)
        self.part, self.out, self.split = part, out, split
        self.from_near, self.to_far, self.from_far = from_near, to_far, from_far
        self.rows = part.shape[1]
        self.step = min(64, self.rows)
        self.near_handles, self.far_handles = {}, {}
        self.next = 1

    def start(self, order=None):
        for d in order or list(range(1, self.lines)) + [0]:
            block = self.part.at[flip(self.index, 2 * d + 1)]
            self.near_handles[d] = self.wire.copy(block, self.from_near.at[d], self.near)

    def relay(self, number):
        for _ in range(number):
            d = self.next
            self.next += 1
            self.wire.arrived(self.near_handles[d])

            def join(at, d=d):
                total = self.part[flip(self.index, 2 * d), at].astype(F32)
                total = total + self.from_near[d, at].astype(F32)
                self.to_far[d - 1, at] = total.astype(self.to_far.dtype)

            by_rows(self.rows, self.step, join)
            self.far_handles[d] = self.wire.copy(
                self.to_far.at[d - 1], self.from_far.at[d - 1], self.far[d - 1]
            )

    def close(self):
        self.wire.arrived(self.near_handles[0])
        for d in range(1, self.lines):
            self.wire.arrived(self.far_handles[d])
        width = self.part.shape[2]
        half = lax.rem(lax.div(self.index, 2), 2)

        def total(at):
            same = self.part[self.index, at].astype(F32) + self.from_near[0, at].astype(F32)
            other = None
            for d in range(1, self.lines):
                got = self.from_far[d - 1, at].astype(F32)
                if self.split and d % 2:
                    other = got if other is None else other + got
                else:
                    same = same + got
            if self.split:
                out = self.out
                out[at, pl.ds(pl.multiple_of(half * width, width), width)] = same
                out[at, pl.ds(pl.multiple_of((1 - half) * width, width), width)] = other
            else:
                self.out[at, :] = same

        by_rows(self.rows, self.step, total)


def seq_sum_scratch(part, dtype=LOW):
    lines = part.shape[0] // 2
    return [
        pltpu.VMEM((depth,) + part.shape[1:], dtype) for depth in (lines, lines - 1, lines - 1)
    ]


class RowSum:
    def __init__(self, wire, place, pair, part, core_got, y_send, y_got, pair_send, pair_got):
        self.wire, self.place, self.pair = wire, place, pair
        self.core, self.side = lax.rem(place, 2), lax.div(place, 2)
        self.part, self.core_got, self.y_send, self.y_got = part, core_got, y_send, y_got
        self.pair_send, self.pair_got = pair_send, pair_got
        self.sides = (1 - self.side, self.side)
        self.rows = part.shape[2]
        self.core_handles, self.y_handles = {}, {}

    def start(self):
        peer = {"tensor": flip(self.place, 1)}
        for which in range(2):
            for p in reversed(range(self.part.shape[0])):
                at = self.sides[which]
                block = self.part.at[p, 2 * at + 1 - self.core]
                self.core_handles[p, which] = self.wire.copy(block, self.core_got.at[p, at], peer)

    def both(self, p, which, at):
        side = self.sides[which]
        mine = self.part[p, 2 * side + self.core, at, :].astype(F32)
        return mine + self.core_got[p, side, at, :].astype(F32)

    def to_side(self, p):
        self.wire.arrived(self.core_handles[p, 0])

        def body(at):
            self.y_send[p, at, :] = self.both(p, 0, at).astype(LOW)

        by_rows(self.rows, 16, body)
        peer = {"tensor": flip(self.place, 2)}
        self.y_handles[p] = self.wire.copy(self.y_send.at[p], self.y_got.at[p], peer)

    def to_pair(self):
        self.wire.arrived(self.core_handles[1, 1])
        self.wire.arrived(self.y_handles[1])

        def body(at):
            total = self.both(1, 1, at) + self.y_got[1, at, :].astype(F32)
            self.pair_send[at, :] = total.astype(LOW)

        by_rows(self.rows, 16, body)
        self.pair_handle = self.wire.copy(self.pair_send, self.pair_got, self.pair)

    def ready(self):
        self.wire.arrived(self.core_handles[0, 1])
        self.wire.arrived(self.y_handles[0])
        if self.pair is not None:
            self.wire.arrived(self.pair_handle)

    def total(self, at):
        total = self.both(0, 1, at) + self.y_got[0, at, :].astype(F32)
        if self.pair is not None:
            total = total + self.pair_got[at, :].astype(F32)
        return total


def row_sum_scratch(part):
    pairs, _, rows, width = part.shape
    scratch = [pltpu.VMEM((pairs, 2, rows, width), LOW)]
    scratch += [pltpu.VMEM((pairs, rows, width), LOW)] * 2
    if pairs == 2:
        scratch += [pltpu.VMEM((rows, width), LOW)] * 2
    return scratch


class RowGather:
    def __init__(self, wire, place, rows):
        self.wire, self.place, self.rows = wire, place, rows

    def start(self):
        mine = self.rows.at[self.place]
        self.side_handle = self.wire.copy(mine, mine, {"tensor": flip(self.place, 2)})
        self.wire.copy(mine, mine, {"tensor": flip(self.place, 1)})

    def forward(self):
        self.wire.arrived(self.side_handle)
        block = self.rows.at[flip(self.place, 2)]
        self.wire.copy(block, block, {"tensor": flip(self.place, 1)})


def sem_scratch(copies):
    return [pltpu.SemaphoreType.DMA((copies,)), pltpu.SemaphoreType.DMA((copies,))]


def middle_kernel(count, *refs):
    back, proj, centre, dy, vec = refs[:5]
    proj_sum, grad, rows, sums = refs[5:9]
    row_refs, seq_refs, (send_sem, recv_sem) = refs[9:14], refs[14:17], refs[17:]
    index, place = lax.axis_index("seq"), lax.axis_index("tensor")
    along = seq_peers(index, count)
    greet(along + [{"tensor": flip(place, 1)}, {"tensor": flip(place, 2)}])
    wire = Wire(send_sem, recv_sem)
    reduce = RowSum(wire, place, along[0], back, *row_refs)
    bulk = SeqSum(wire, index, along, proj, *seq_refs, proj_sum, True)
    gather = RowGather(wire, place, rows)
    lines = count // 2
    reduce.start()
    bulk.start()
    reduce.to_side(1)
    reduce.to_side(0)
    bulk.relay(1)
    reduce.to_pair()
    bulk.relay((lines - 1) // 3)
    reduce.ready()
    sums[...] = jnp.zeros_like(sums)
    gain = vec[0:1, :]

    def body(at):
        over = reduce.total(at)
        inner, product = norm_back(centre[at, :], gain, over)
        value = dy[at, :].astype(F32) + inner
        grad[at, :] = value
        rows[place, at, :] = value.astype(LOW)
        sums[0] += product
        sums[1] += over
        sums[2] += value

    by_rows(centre.shape[0], 16, body)
    gather.start()
    bulk.relay(lines - 1 - 1 - (lines - 1) // 3)
    gather.forward()
    bulk.close()
    wire.finish()


def middle_stage(back, proj, centre, dy, vec):
    count = lax.axis_size("seq")
    tensor = lax.axis_size("tensor")
    part, full = centre.shape
    vmem = pl.BlockSpec(memory_space=pltpu.VMEM)
    copies = 2 * count + 12
    return pl.pallas_call(
        partial(middle_kernel, count),
        out_shape=[
            jax.ShapeDtypeStruct((proj.shape[1], 2 * proj.shape[2]), F32),
            jax.ShapeDtypeStruct((part, full), F32),
            jax.ShapeDtypeStruct((tensor, part, full), LOW),
            jax.ShapeDtypeStruct((3, 16, full), F32),
        ],
        in_specs=[vmem] * 5,
        out_specs=[vmem] * 4,
        scratch_shapes=row_sum_scratch(back) + seq_sum_scratch(proj) + sem_scratch(copies),
        compiler_params=pltpu.CompilerParams(
            collective_id=2, has_side_effects=True, vmem_limit_bytes=60 << 20
        ),
        name="middle",
    )(back, proj, centre, dy, vec)


def back_kernel(count, *refs):
    feed, fc, out, q_in, kv_in, mq_in, mk_in, mixed, lse, grad_o_in, centre, vec = refs[:12]
    fc_sum, out_sum, dq, dkv, result = refs[12:17]
    row_refs, seq_refs, out_refs, kv_refs = refs[17:22], refs[22:25], refs[25:28], refs[28:31]
    kv_send, kv_got, kv_part, kv_total, delta, acc, send_sem, recv_sem = refs[31:]
    index, place = lax.axis_index("seq"), lax.axis_index("tensor")
    core = lax.rem(place, 2)
    other_core = {"tensor": flip(place, 1)}
    along = seq_peers(index, count)
    lines = count // 2
    spread = lines - 1
    greet(along + [other_core, {"tensor": flip(place, 2)}])
    wire = Wire(send_sem, recv_sem)
    reduce = RowSum(wire, place, along[0], feed, *row_refs)
    bulk = SeqSum(wire, index, along, fc, *seq_refs, fc_sum, True)
    out_bulk = SeqSum(wire, index, along, out, *out_refs, out_sum, False)
    keys_sum = SeqSum(wire, index, along, kv_part, *kv_refs, kv_total, False)
    gather = RowGather(wire, place, result)
    hd = kv_in.shape[-1] // 2
    heads = q_in.shape[-1] // hd
    scale = float(hd) ** (-0.5)
    scale_two = scale * LOG2E
    near_x = 1 - lax.rem(index, 2)

    def open_batch(batch):
        acc[...] = jnp.zeros_like(acc)
        for head in range(heads):
            cols = slice(head * hd, (head + 1) * hd)
            product = grad_o_in[batch, :, cols].astype(F32) * mixed[batch, :, cols].astype(F32)
            delta[head] = jnp.sum(product, axis=-1, keepdims=True)

    def blocks_of(batch, which, target, extra):
        def body(line, carry):
            block = 2 * line + which
            mask = visible(mq_in[batch], mk_in[batch, block])
            keys = kv_in[batch, block, :, :hd]
            values = kv_in[batch, block, :, hd:]
            grad_k = jnp.zeros((keys.shape[0], hd), F32)
            grad_v = jnp.zeros((keys.shape[0], hd), F32)
            for head in range(heads):
                cols = slice(head * hd, (head + 1) * hd)
                query = q_in[batch, :, cols]
                grad_o = grad_o_in[batch, :, cols]
                scores = dot_nt(query, keys) * scale_two
                probs = jnp.where(mask, jnp.exp2(scores - lse[batch, head]), 0.0)
                grad_p = dot_nt(grad_o, values)
                grad_s = (probs * (grad_p - delta[head])).astype(LOW)
                acc[:, cols] += dot(grad_s, keys)
                grad_k = grad_k + dot_tn(grad_s, query)
                grad_v = grad_v + dot_tn(probs.astype(LOW), grad_o)
            grad_k = grad_k * scale
            if extra is not None:
                grad_k = grad_k + extra[block, :, :hd].astype(F32)
                grad_v = grad_v + extra[block, :, hd:].astype(F32)
            target[block, :, :hd] = grad_k.astype(LOW)
            target[block, :, hd:] = grad_v.astype(LOW)
            return carry

        lax.fori_loop(0, lines, body, 0)

    def close_batch(batch):
        dq[batch] = (acc[...] * scale).astype(LOW)

    def to_core(which):
        return [
            wire.copy(kv_send.at[2 * line + which], kv_got.at[2 * line + which], other_core)
            for line in range(lines)
        ]

    reduce.start()
    bulk.start(list(range(1, lines)))
    open_batch(1 - core)
    blocks_of(1 - core, near_x, kv_send, None)
    near_handles = to_core(near_x)
    reduce.to_side(1)
    reduce.to_side(0)
    blocks_of(1 - core, 1 - near_x, kv_send, None)
    own_handles = to_core(1 - near_x)
    close_batch(1 - core)
    bulk.relay(spread // 3)
    for handle in near_handles:
        wire.arrived(handle)
    open_batch(core)
    blocks_of(core, near_x, kv_part, kv_got)
    keys_sum.start()
    bulk.start([0])
    out_bulk.start()
    reduce.to_pair()
    bulk.relay(spread // 3)
    for handle in own_handles:
        wire.arrived(handle)
    blocks_of(core, 1 - near_x, kv_part, kv_got)
    close_batch(core)
    reduce.ready()
    bias = vec[0:1, :]

    def body(at):
        total = centre[at, :] + reduce.total(at) + bias
        result[place, at, :] = total.astype(LOW)

    by_rows(centre.shape[0], 16, body)
    gather.start()
    keys_sum.relay(spread)
    bulk.relay(spread - 2 * (spread // 3))
    gather.forward()
    out_bulk.relay(spread)
    keys_sum.close()
    dkv[1 - core] = jnp.zeros(dkv.shape[1:], LOW)
    dkv[core] = kv_total[...].astype(LOW)
    bulk.close()
    out_bulk.close()
    wire.finish()


def back_stage(feed, fc, out, queries, keyval, meta_q, meta_k, mixed, lse, grad_mixed, centre, vec):
    count = lax.axis_size("seq")
    tensor = lax.axis_size("tensor")
    part, full = centre.shape
    batches, rows, width = queries.shape
    blocks, two = keyval.shape[1], keyval.shape[3]
    heads = 2 * width // two
    vmem = pl.BlockSpec(memory_space=pltpu.VMEM)
    kv_part = jax.ShapeDtypeStruct((blocks, rows, two), LOW)
    copies = 4 * count + 14
    return pl.pallas_call(
        partial(back_kernel, count),
        out_shape=[
            jax.ShapeDtypeStruct((fc.shape[1], 2 * fc.shape[2]), F32),
            jax.ShapeDtypeStruct(out.shape[1:], F32),
            jax.ShapeDtypeStruct((batches, rows, width), LOW),
            jax.ShapeDtypeStruct((batches, rows, two), LOW),
            jax.ShapeDtypeStruct((tensor, part, full), LOW),
        ],
        in_specs=[vmem] * 12,
        out_specs=[vmem] * 5,
        scratch_shapes=row_sum_scratch(feed)
        + seq_sum_scratch(fc)
        + seq_sum_scratch(out)
        + seq_sum_scratch(kv_part)
        + [pltpu.VMEM(kv_part.shape, LOW)] * 3
        + [
            pltpu.VMEM((rows, two), F32),
            pltpu.VMEM((heads, rows, 1), F32),
            pltpu.VMEM((rows, width), F32),
        ]
        + sem_scratch(copies),
        compiler_params=pltpu.CompilerParams(
            collective_id=3, has_side_effects=True, vmem_limit_bytes=60 << 20
        ),
        name="back",
    )(feed, fc, out, queries, keyval, meta_q, meta_k, mixed, lse, grad_mixed, centre, vec)


def last_kernel(count, *refs):
    back, query, keyval, small, own, dy, vec = refs[:7]
    query_sum, keyval_sum, rows, small_sum = refs[7:11]
    row_refs, key_row_refs = refs[11:14], refs[14:17]
    query_refs, key_refs, small_refs = refs[17:20], refs[20:23], refs[23:26]
    key_part, small_part, small_own, small_got, sums, send_sem, recv_sem = refs[26:]
    index, place = lax.axis_index("seq"), lax.axis_index("tensor")
    along = seq_peers(index, count)
    other_core, other_side = {"tensor": flip(place, 1)}, {"tensor": flip(place, 2)}
    greet(along + [other_core, other_side])
    wire = Wire(send_sem, recv_sem)
    reduce = RowSum(wire, place, None, back, *row_refs, None, None)
    key_reduce = RowSum(wire, place, None, keyval, *key_row_refs, None, None)
    query_bulk = SeqSum(wire, index, along, query, *query_refs, query_sum, False)
    key_bulk = SeqSum(wire, index, along, key_part, *key_refs, keyval_sum, False)
    small_bulk = SeqSum(wire, index, along, small_part, *small_refs, small_own.at[0], False)
    gather = RowGather(wire, place, rows)
    spread = count // 2 - 1
    reduce.start()
    query_bulk.start()
    key_reduce.start()
    reduce.to_side(0)
    key_reduce.to_side(0)
    query_bulk.relay(spread // 3)
    reduce.ready()
    sums[...] = jnp.zeros_like(sums)
    gain = vec[0:1, :]

    def body(at):
        over = reduce.total(at)
        inner, product = norm_back(own[at, :].astype(F32), gain, over)
        rows[place, at, :] = (dy[at, :] + inner).astype(LOW)
        sums[0] += product
        sums[1] += over

    by_rows(own.shape[0], 16, body)
    gather.start()
    small_part[...] = small[...]
    width = own.shape[1] // count
    for row in range(2):
        line = jnp.sum(sums[row], axis=0, keepdims=True)
        for block in range(count):
            part = line[:, block * width : (block + 1) * width]
            small_part[block, row : row + 1, 0:width] = part
    small_bulk.start()
    key_reduce.ready()
    step = key_part.shape[1]
    for block in range(count):
        key_part[block] = key_reduce.total(slice(block * step, (block + 1) * step)).astype(LOW)
    key_bulk.start()
    query_bulk.relay(spread // 3)
    gather.forward()
    small_bulk.relay(spread)
    query_bulk.relay(spread - 2 * (spread // 3))
    key_bulk.relay(spread)
    small_bulk.close()
    for turn, peer in enumerate((other_core, other_side)):
        handle = wire.copy(small_own.at[turn], small_got.at[turn], peer)
        wire.arrived(handle)
        total = small_own[turn] + small_got[turn]
        if turn:
            small_sum[...] = total
        else:
            small_own[1] = total
    query_bulk.close()
    key_bulk.close()
    wire.finish()


def last_stage(back, query, keyval, small, own, dy, vec):
    count = lax.axis_size("seq")
    tensor = lax.axis_size("tensor")
    part, full = own.shape
    vmem = pl.BlockSpec(memory_space=pltpu.VMEM)
    key_part = jax.ShapeDtypeStruct((count, keyval.shape[2] // count, keyval.shape[3]), LOW)
    copies = 3 * count + 12
    return pl.pallas_call(
        partial(last_kernel, count),
        out_shape=[
            jax.ShapeDtypeStruct(query.shape[1:], F32),
            jax.ShapeDtypeStruct(key_part.shape[1:], F32),
            jax.ShapeDtypeStruct((tensor, part, full), LOW),
            jax.ShapeDtypeStruct(small.shape[1:], F32),
        ],
        in_specs=[vmem] * 7,
        out_specs=[vmem] * 4,
        scratch_shapes=row_sum_scratch(back)
        + row_sum_scratch(keyval)
        + seq_sum_scratch(query)
        + seq_sum_scratch(key_part)
        + seq_sum_scratch(small, F32)
        + [
            pltpu.VMEM(key_part.shape, LOW),
            pltpu.VMEM(small.shape, F32),
            pltpu.VMEM((2,) + small.shape[1:], F32),
            pltpu.VMEM((2,) + small.shape[1:], F32),
            pltpu.VMEM((2, 16, full), F32),
        ]
        + sem_scratch(copies),
        compiler_params=pltpu.CompilerParams(
            collective_id=4, has_side_effects=True, vmem_limit_bytes=60 << 20
        ),
        name="last",
    )(back, query, keyval, small, own, dy, vec)


def visible(meta_q, meta_k):
    seg_q, pos_q = meta_q[:, 0:1], meta_q[:, 1:2]
    seg_k, pos_k = meta_k[0:1, :], meta_k[1:2, :]
    return ((seg_k == 0) | (seg_k == seg_q)) & (pos_k <= pos_q)


def norm_parts(values):
    average = jnp.mean(values, axis=-1, keepdims=True)
    centred = values - average
    spread = jnp.mean(centred * centred, axis=-1, keepdims=True)
    return centred, lax.rsqrt(spread + EPS)


def norm_back(values, gain, grad):
    centred, inverse = norm_parts(values)
    unit = centred * inverse
    scaled = grad * gain
    inner = (
        scaled
        - jnp.mean(scaled, axis=-1, keepdims=True)
        - unit * jnp.mean(scaled * unit, axis=-1, keepdims=True)
    )
    return inverse * inner, grad * unit


def gelu_pair(values):
    const = 0.7978845608028654
    square = values * values
    inner = jnp.tanh(const * (values + 0.044715 * (values * square)))
    half = 0.5 * (1.0 + inner)
    slope = half + 0.5 * values * (1.0 - inner * inner) * const * (1.0 + 3 * 0.044715 * square)
    return values * half, slope


def local(
    inputs,
    segment,
    position,
    w_query,
    w_keyval,
    w_out,
    w_fc,
    w_proj,
    vectors,
    fc_bias,
    value_bias,
    grad_out,
):
    seq_size, tensor_size = lax.axis_size("seq"), lax.axis_size("tensor")
    seq_index, tensor_index = lax.axis_index("seq"), lax.axis_index("tensor")
    batches, rows, full_width = inputs.shape
    width_block = w_query.shape[0]
    group_width = w_query.shape[1]
    hidden_width = w_fc.shape[1]
    unit_width = hidden_width // 2
    unit_half = (seq_index >> 1) & 1
    hd = value_bias.shape[0]
    quarter = rows // tensor_size
    shard = vectors.shape[1]
    bias_shard = fc_bias.shape[0]

    pieces = [
        vectors.reshape(-1).astype(LOW),
        fc_bias.astype(LOW),
        segment.reshape(-1).astype(LOW),
        (position // 128).reshape(-1).astype(LOW),
        (position % 128).reshape(-1).astype(LOW),
    ]
    cuts = [0]
    for piece in pieces:
        cuts.append(cuts[-1] + piece.shape[0])
    packed = jnp.concatenate(pieces)
    packed = jnp.pad(packed, (0, -packed.shape[0] % 2048)).reshape(-1, 128)

    def halves(array):
        return jnp.swapaxes(array.astype(LOW).reshape(width_block, 2, unit_width), 0, 1)

    small, kv_mat, q_mat = gather_first(packed, w_keyval.astype(LOW), w_query.astype(LOW))
    kv_mat = kv_mat.reshape(full_width, 2 * hd)
    q_mat = q_mat.reshape(full_width, group_width)

    small = small.reshape(seq_size, tensor_size, -1).astype(F32)
    vec_all = small[:, :, cuts[0] : cuts[1]].reshape(seq_size * tensor_size, 7, shard)
    vec_all = jnp.swapaxes(vec_all, 0, 1).reshape(7, full_width)
    fc_all = small[:, :, cuts[1] : cuts[2]].reshape(-1)
    seg_keys = small[:, 0, cuts[2] : cuts[3]].reshape(seq_size, batches, rows)
    pos_keys = 128.0 * small[:, 0, cuts[3] : cuts[4]] + small[:, 0, cuts[4] : cuts[5]]
    seg_keys = jnp.swapaxes(seg_keys, 0, 1).astype(jnp.int32)
    pos_keys = jnp.swapaxes(pos_keys.reshape(seq_size, batches, rows), 0, 1).astype(jnp.int32)
    meta_k = jnp.pad(jnp.stack([seg_keys, pos_keys], axis=2), ((0, 0), (0, 0), (0, 6), (0, 0)))
    meta_q = jnp.pad(jnp.stack([segment, position], axis=2), ((0, 0), (0, 0), (0, 126)))

    gain_one, shift_one, _, out_bias, gain_two, shift_two, proj_bias = [
        vec_all[i] for i in range(7)
    ]
    query_bias = lax.dynamic_slice_in_dim(vec_all[2], tensor_index * group_width, group_width, 0)
    fc_local = lax.dynamic_slice_in_dim(
        fc_all, tensor_index * hidden_width + unit_half * unit_width, unit_width, 0
    )
    bias_value = value_bias.astype(LOW).astype(F32)
    kv_bias = jnp.concatenate([jnp.zeros((hd,), F32), bias_value])

    residual = inputs.astype(F32)
    centred, inverse = norm_parts(residual)
    normed = (centred * inverse * gain_one + shift_one).astype(LOW).reshape(-1, full_width)
    keyval = (dot(normed, kv_mat) + kv_bias).astype(LOW).reshape(batches, rows, 2 * hd)
    queries = (dot(normed, q_mat) + query_bias).astype(LOW)
    queries = queries.reshape(batches, rows, group_width)

    def by_quarter(array):
        split = array.reshape(batches, tensor_size, quarter, array.shape[-1])
        return jnp.swapaxes(split, 0, 1).reshape(tensor_size, batches * quarter, -1)

    def by_batch(array):
        split = array.reshape(tensor_size, batches, quarter, array.shape[-1])
        return jnp.swapaxes(split, 0, 1).reshape(batches, rows, -1)

    def my_quarter(array):
        split = array.reshape(batches, tensor_size, quarter, full_width)
        own = lax.dynamic_index_in_dim(split, tensor_index, 1, keepdims=False)
        return own.reshape(batches * quarter, full_width)

    vecs = jnp.pad(jnp.stack([out_bias, gain_two, shift_two]), ((0, 5), (0, 0)))
    grad_split = by_quarter(grad_out)
    mixed, lse, kv_all, out_t, middle, rows_two, fc_mat, proj_t, grad_other = front(
        queries,
        keyval,
        meta_q,
        meta_k,
        my_quarter(inputs),
        vecs,
        w_out.T.astype(LOW),
        halves(w_fc),
        halves(w_proj.T),
        grad_split,
    )
    out_t = out_t.reshape(full_width, group_width)
    fc_mat = fc_mat.reshape(full_width, unit_width)
    proj_t = proj_t.reshape(full_width, unit_width)
    mixed_rows = by_quarter(mixed).reshape(-1, group_width)
    normed_two = rows_two.reshape(-1, full_width)
    hidden = dot(normed_two, fc_mat) + fc_local
    active_f, slope = gelu_pair(hidden)
    active = active_f.astype(LOW)

    grad_q_low = my_quarter(grad_out)
    grad_flat = jnp.concatenate([grad_split, grad_other]).reshape(-1, full_width)
    grad_hidden = (slope * dot(grad_flat, proj_t)).astype(LOW)
    fcbias_local = jnp.sum(grad_hidden.astype(F32), axis=0)
    back_part = dot_nt(grad_hidden, fc_mat).astype(LOW)
    back_part = back_part.reshape(2, tensor_size, batches * quarter, full_width)

    def blocked(array):
        return array.astype(LOW).reshape(seq_size, width_block, array.shape[-1])

    proj_sum, grad_middle, rows_middle, sums = middle_stage(
        back_part,
        blocked(dot_tn(grad_flat, active)),
        middle,
        grad_q_low,
        jnp.pad(gain_two[None], ((0, 7), (0, 0))),
    )
    grad_gain_two, grad_shift_two, grad_out_bias = jnp.sum(sums, axis=1)
    grad_proj_bias = jnp.sum(grad_q_low.astype(F32), axis=0)
    grad_middle_low = rows_middle.reshape(-1, full_width)
    def one_row(row):
        return jnp.pad(row[None], ((0, 7), (0, 0)))

    grad_mixed = by_batch(dot(grad_middle_low, out_t).astype(LOW))
    feed_part = dot_nt(active, proj_t).astype(LOW)
    fc_sum, out_sum, grad_queries, grad_keyval, result_rows = back_stage(
        feed_part.reshape(2, tensor_size, batches * quarter, full_width),
        blocked(dot_tn(normed_two, grad_hidden)),
        blocked(dot_tn(grad_middle_low, mixed_rows)),
        queries,
        kv_all,
        meta_q,
        meta_k,
        mixed,
        lse,
        grad_mixed,
        middle,
        one_row(proj_bias),
    )
    result = by_batch(result_rows)
    grad_keyval = grad_keyval.reshape(-1, 2 * hd)
    grad_queries = grad_queries.reshape(-1, group_width)
    grad_normed = dot_nt(grad_queries, q_mat) + dot_nt(grad_keyval, kv_mat)
    qbias_local = jnp.sum(grad_queries.astype(F32), axis=0)
    vbias_local = jnp.sum(grad_keyval[:, hd:].astype(F32), axis=0)

    qbias_full = lax.dynamic_update_slice_in_dim(
        jnp.zeros((full_width,), F32), qbias_local, tensor_index * group_width, 0
    )
    full_hidden = bias_shard * seq_size * tensor_size
    fcbias_full = lax.dynamic_update_slice_in_dim(
        jnp.zeros((full_hidden,), F32),
        fcbias_local,
        tensor_index * hidden_width + unit_half * unit_width,
        0,
    )
    chunk = full_hidden // seq_size
    blank = jnp.zeros((full_width,), F32)
    vec_grads = jnp.stack(
        [blank, blank, qbias_full, grad_out_bias, grad_gain_two, grad_shift_two, grad_proj_bias]
    )

    def in_rows(array):
        array = jnp.pad(array, ((0, 0), (0, -array.shape[1] % width_block)))
        return array.reshape(seq_size, -1, width_block)

    vec_rows = 7
    bias_rows = chunk // width_block
    small_rows = jnp.concatenate(
        [
            jnp.swapaxes(vec_grads.reshape(7, seq_size, width_block), 0, 1),
            in_rows(fcbias_full.reshape(seq_size, chunk)),
            in_rows(jnp.broadcast_to(vbias_local, (seq_size, hd))),
        ],
        axis=1,
    )
    small_rows = jnp.pad(
        small_rows,
        ((0, 0), (0, -small_rows.shape[1] % 8), (0, -width_block % 128)),
    )
    key_grad = dot_tn(normed, grad_keyval).astype(LOW)
    key_grad = key_grad.reshape(seq_size, tensor_size, -1, 2 * hd)
    key_grad = jnp.swapaxes(key_grad, 0, 1).reshape(1, tensor_size, -1, 2 * hd)
    query_sum, keyval_grad, input_rows, small_sum = last_stage(
        by_quarter(grad_normed.astype(LOW))[None],
        blocked(dot_tn(normed, grad_queries)),
        key_grad,
        small_rows,
        my_quarter(inputs),
        grad_middle,
        one_row(gain_one),
    )
    input_grad = by_batch(input_rows)
    small_sum = small_sum[:, :width_block]
    vec_grad = lax.dynamic_slice_in_dim(small_sum[:vec_rows], tensor_index * shard, shard, 1)
    fcbias_grad = lax.dynamic_slice_in_dim(
        small_sum[vec_rows : vec_rows + bias_rows].reshape(-1),
        tensor_index * bias_shard,
        bias_shard,
        0,
    )
    vbias_grad = small_sum[vec_rows + bias_rows :].reshape(-1)[:hd]
    return (
        result,
        input_grad,
        query_sum,
        keyval_grad,
        out_sum.T,
        fc_sum,
        proj_sum.T,
        vec_grad,
        fcbias_grad,
        vbias_grad,
        vec_grad[5],
    )


def solution(mesh):
    in_specs = (
        P(None, "seq", None),
        P(None, "seq"),
        P(None, "seq"),
        P("seq", "tensor"),
        P(("seq", "tensor"), None),
        P("tensor", "seq"),
        P("seq", "tensor"),
        P("tensor", "seq"),
        P(None, ("seq", "tensor")),
        P(("seq", "tensor")),
        P(),
        P(None, "seq", None),
    )
    out_specs = (
        P(None, "seq", None),
        P(None, "seq", None),
        P("seq", "tensor"),
        P(("seq", "tensor"), None),
        P("tensor", "seq"),
        P("seq", "tensor"),
        P("tensor", "seq"),
        P(None, ("seq", "tensor")),
        P(("seq", "tensor")),
        P(),
        P(("seq", "tensor")),
    )
    return jax.shard_map(local, mesh=mesh, in_specs=in_specs, out_specs=out_specs, check_vma=False)
```

```python
from functools import partial

import jax
import jax.numpy as jnp
from jax import lax
from jax.experimental import pallas as pl
from jax.experimental.pallas import tpu as pltpu
from jax.sharding import PartitionSpec as P

EPS = 1e-05
NEG = -1e30
LOG2E = 1.4426950408889634
LOW = jnp.bfloat16
F32 = jnp.float32


def bits_of(count):
    return count.bit_length() - 1


def swap(value, axis, bit):
    count = lax.axis_size(axis)
    return lax.ppermute(value, axis, [(i, i ^ (1 << bit)) for i in range(count)])


def after(value, *others):
    return lax.optimization_barrier((value,) + others)[0]


def dot(left, right):
    return jnp.dot(left, right, preferred_element_type=F32)


def dot_tn(left, right):
    return lax.dot_general(left, right, (((0,), (0,)), ((), ())), preferred_element_type=F32)


def dot_nt(left, right):
    return lax.dot_general(left, right, (((1,), (1,)), ((), ())), preferred_element_type=F32)


MESH = pl.DeviceIdType.MESH


def flip(index, mask):
    bit = 1
    out = index
    while bit <= mask:
        if mask & bit:
            out = out + bit * (1 - 2 * lax.rem(lax.div(index, bit), 2))
        bit *= 2
    return out


class Wire:
    def __init__(self, send_sem, recv_sem):
        self.send_sem, self.recv_sem = send_sem, recv_sem
        self.started = []
        self.landed = set()

    def copy(self, src, dst, peer):
        place = len(self.started)
        item = pltpu.make_async_remote_copy(
            src_ref=src,
            dst_ref=dst,
            send_sem=self.send_sem.at[place],
            recv_sem=self.recv_sem.at[place],
            device_id=peer,
            device_id_type=MESH,
        )
        item.start()
        self.started.append(item)
        return place

    def arrived(self, place):
        if place not in self.landed:
            self.landed.add(place)
            self.started[place].wait_recv()

    def finish(self):
        for place in range(len(self.started)):
            self.arrived(place)
        for item in self.started:
            item.wait_send()


def greet(peers):
    barrier = pltpu.get_barrier_semaphore()
    for peer in peers:
        pl.semaphore_signal(barrier, inc=1, device_id=peer, device_id_type=MESH)
    pl.semaphore_wait(barrier, len(peers))


def seq_peers(index, count):
    return [{"seq": flip(index, 2 * d)} for d in range(1, count // 2)] + [
        {"seq": flip(index, 1)}
    ]


def turns(lines):
    return list(range(lines // 2, lines)) + list(range(1, lines // 2))


def first_kernel(count, tensor, *refs):
    ins, outs = refs[:3], refs[3:6]
    send_sem, recv_sem, local_sem = refs[6:]
    index = lax.axis_index("seq")
    place = lax.axis_index("tensor")
    across = [{"tensor": flip(place, tensor >> (i + 1))} for i in range(bits_of(tensor))]
    along = seq_peers(index, count)
    far, near = along[:-1], along[-1]
    greet(across + along)
    wire = Wire(send_sem, recv_sem)
    own = []
    targets = [(lambda at, out=out: out.at[at, place]) for out in outs[:2]]
    targets.append(lambda at: outs[2].at[at])
    handles = []
    for source, target in zip(ins, targets):
        handles.append({d: wire.copy(source, target(index), far[d - 1]) for d in range(1, count // 2)})
        handles[-1][0] = wire.copy(source, target(index), near)
        item = pltpu.make_async_copy(source, target(index), local_sem.at[len(own)])
        item.start()
        own.append(item)
    relays = []
    for a, target in enumerate(targets):
        for d in range(1, count // 2):
            wire.arrived(handles[a][d])
            block = target(flip(index, 2 * d))
            relays.append(wire.copy(block, block, near))
        if a == 1:
            for handle in [handles[0][0], handles[1][0]] + relays:
                wire.arrived(handle)
            own[0].wait()
            own[1].wait()
            masks = [0]
            for i, peer in enumerate(across):
                step = tensor >> (i + 1)
                sent = [
                    wire.copy(out.at[:, flip(place, mask)], out.at[:, flip(place, mask)], peer)
                    for mask in masks
                    for out in outs[:2]
                ]
                masks = masks + [mask | step for mask in masks]
                if i + 1 < len(across):
                    for handle in sent:
                        wire.arrived(handle)
    own[2].wait()
    wire.finish()


def gather_first(small, keyval, query):
    count, tensor = lax.axis_size("seq"), lax.axis_size("tensor")
    arrays = (small, keyval, query)
    shapes = [
        (count, tensor) + small.shape,
        (count, tensor) + keyval.shape,
        (count,) + query.shape,
    ]
    copies = 3 * (count - 1) + 2 * (tensor - 1)
    return pl.pallas_call(
        partial(first_kernel, count, tensor),
        out_shape=[jax.ShapeDtypeStruct(shape, LOW) for shape in shapes],
        in_specs=[pl.BlockSpec(memory_space=pltpu.VMEM)] * 3,
        out_specs=[pl.BlockSpec(memory_space=pltpu.VMEM)] * 3,
        scratch_shapes=[
            pltpu.SemaphoreType.DMA((copies,)),
            pltpu.SemaphoreType.DMA((copies,)),
            pltpu.SemaphoreType.DMA((3,)),
        ],
        compiler_params=pltpu.CompilerParams(collective_id=0, has_side_effects=True),
        name="gather_first",
    )(*arrays)


def front_kernel(count, *refs):
    q_in, kv_in, mq_in, mk_in, x_in, vec_in, o_in, fc_in, pj_in, dy_in = refs[:10]
    mixed, lse, kv_all, out_t, middle, rows_two, fc_out, pj_out, dy_out = refs[10:19]
    (
        top,
        total,
        acc,
        core_keep,
        core_send,
        core_got,
        y_send,
        y_got,
        send_sem,
        recv_sem,
        local_sem,
    ) = refs[19:]
    index = lax.axis_index("seq")
    place = lax.axis_index("tensor")
    core = lax.rem(place, 2)
    side = lax.div(place, 2)
    half = lax.rem(lax.div(index, 2), 2)
    other_core = {"tensor": flip(place, 1)}
    other_side = {"tensor": flip(place, 2)}
    across = {"tensor": flip(place, 3)}
    along = seq_peers(index, count)
    far, near = along[:-1], along[-1]
    pair = far[0]
    lines = count // 2
    greet(along + [other_core, other_side, across])
    wire = Wire(send_sem, recv_sem)
    own = []

    def keep(src, dst):
        item = pltpu.make_async_copy(src, dst, local_sem.at[len(own)])
        item.start()
        own.append(item)

    order = range(1, lines)
    kv_far = {d: wire.copy(kv_in.at[core], kv_all.at[core, index], far[d - 1]) for d in order}
    kv_near = wire.copy(kv_in.at[core], kv_all.at[core, index], near)
    for batch in range(2):
        keep(kv_in.at[batch], kv_all.at[batch, index])
    o_far = {d: wire.copy(o_in, out_t.at[index], far[d - 1]) for d in order}
    o_near = [wire.copy(o_in, out_t.at[index], near)]
    keep(o_in, out_t.at[index])
    dy_pair = wire.copy(dy_in.at[place], dy_out.at[place], pair)

    def send_far(source, out):
        return {
            d: wire.copy(source.at[flip(half, d & 1)], out.at[index], far[d - 1]) for d in order
        }

    fc_far = send_far(fc_in, fc_out)
    kv_near = [(1, kv_near)]
    kv_core = []
    for d in order:
        wire.arrived(kv_far[d])
        block = kv_all.at[core, flip(index, 2 * d)]
        kv_near.append((2 * d + 1, wire.copy(block, block, near)))
        kv_core.append(wire.copy(block, block, other_core))
    wire.copy(fc_in.at[half], fc_out.at[index], near)
    wire.copy(pj_in.at[half], pj_out.at[index], near)
    keep(fc_in.at[half], fc_out.at[index])
    keep(pj_in.at[half], pj_out.at[index])
    for r, handle in kv_near:
        wire.arrived(handle)
        block = kv_all.at[core, flip(index, r)]
        kv_core.append(wire.copy(block, block, other_core))
    own[0].wait()
    own[1].wait()

    jobs = [(o_far, out_t, d) for d in order]
    jobs += [(fc_far, fc_out, d) for d in order]

    def tick(number):
        for _ in range(min(number, len(jobs))):
            handles, out, d = jobs.pop(0)
            wire.arrived(handles[d])
            block = out.at[flip(index, 2 * d)]
            handle = wire.copy(block, block, near)
            if out is out_t:
                o_near.append(handle)

    hd = kv_in.shape[-1] // 2
    heads = q_in.shape[-1] // hd
    scale = float(hd) ** (-0.5) * LOG2E

    def attend(batch, block):
        mask = visible(mq_in[batch], mk_in[batch, block])
        keys = kv_all[batch, block, :, :hd]
        values = kv_all[batch, block, :, hd:]
        for head in range(heads):
            cols = slice(head * hd, (head + 1) * hd)
            scores = jnp.where(mask, dot_nt(q_in[batch, :, cols], keys) * scale, NEG)
            before = top[head]
            now = jnp.maximum(before, jnp.max(scores, axis=-1, keepdims=True))
            shrink = jnp.exp2(before - now)
            probs = jnp.exp2(scores - now)
            total[head] = total[head] * shrink + jnp.sum(probs, axis=-1, keepdims=True)
            acc[:, cols] = acc[:, cols] * shrink + dot(probs.astype(LOW), values)
            top[head] = now

    def attend_batch(batch, ticks):
        top[...] = jnp.full_like(top, NEG)
        total[...] = jnp.zeros_like(total)
        acc[...] = jnp.zeros_like(acc)

        def block_body(block, carry):
            attend(batch, block)
            return carry

        parts = len(ticks)
        for i in range(parts):
            lax.fori_loop(i * count // parts, (i + 1) * count // parts, block_body, 0)
            tick(ticks[i])
        for head in range(heads):
            cols = slice(head * hd, (head + 1) * hd)
            mixed[batch, :, cols] = (acc[:, cols] / total[head]).astype(LOW)
            lse[batch, head] = top[head] + jnp.log2(total[head])

    spread = lines - 1
    attend_batch(core, [spread // 3, spread - spread // 3])
    for handle in kv_core:
        wire.arrived(handle)
    attend_batch(1 - core, [0, spread // 3])
    wire.arrived(dy_pair)
    for peer in (other_core, other_side, across):
        wire.copy(dy_out.at[place], dy_out.at[place], peer)

    quarter = x_in.shape[0] // 2
    for handle in o_near:
        wire.arrived(handle)
    own[2].wait()
    width = out_t.shape[1]
    group = max(1, 256 // width)
    for which, target in ((1 - core, core_send), (core, core_keep)):
        rows = [
            mixed[batch, pl.ds(pl.multiple_of((2 * s + which) * quarter, quarter), quarter), :]
            for s in range(2)
            for batch in range(2)
        ]
        rows = jnp.concatenate(rows, axis=0)

        def project(i, carry, rows=rows, target=target):
            cols = pl.ds(pl.multiple_of(i * group * width, group * width), group * width)
            block = out_t[pl.ds(i * group, group)].reshape(group * width, -1)
            target[:, cols] = dot_nt(rows, block).astype(target.dtype)
            return carry

        lax.fori_loop(0, count // group, project, 0)
        if target is core_send:
            core_handle = wire.copy(core_send, core_got, other_core)
    wire.arrived(core_handle)
    part = 2 * quarter
    step = 16

    def to_side(i, carry):
        at = pl.ds(pl.multiple_of((1 - side) * part + i * step, step), step)
        y_send[pl.ds(pl.multiple_of(i * step, step), step), :] = (
            core_keep[at, :] + core_got[at, :].astype(F32)
        ).astype(LOW)
        return carry

    lax.fori_loop(0, part // step, to_side, 0)
    y_handle = wire.copy(y_send, y_got, other_side)
    tick(spread - spread // 3 - 1)
    wire.arrived(y_handle)
    out_bias, gain_two, shift_two = vec_in[0:1, :], vec_in[1:2, :], vec_in[2:3, :]

    def norm(i, carry):
        at = pl.ds(pl.multiple_of(i * step, step), step)
        far_at = pl.ds(pl.multiple_of(side * part + i * step, step), step)
        value = core_keep[far_at, :] + core_got[far_at, :].astype(F32)
        value = value + y_got[at, :].astype(F32)
        value = x_in[at, :].astype(F32) + value + out_bias
        middle[at, :] = value
        centred, inverse = norm_parts(value)
        rows_two[0, place, at, :] = (centred * inverse * gain_two + shift_two).astype(LOW)
        return carry

    lax.fori_loop(0, part // step, norm, 0)
    mine = rows_two.at[0, place]
    pair_handle = wire.copy(mine, rows_two.at[1, place], pair)
    side_handle = wire.copy(mine, mine, other_side)
    wire.copy(mine, mine, other_core)
    pj_far = send_far(pj_in, pj_out)
    tick(len(jobs))
    jobs.extend((pj_far, pj_out, d) for d in order)
    wire.arrived(pair_handle)
    theirs = rows_two.at[1, place]
    side_two = wire.copy(theirs, theirs, other_side)
    wire.copy(theirs, theirs, other_core)
    wire.arrived(side_handle)
    block = rows_two.at[0, flip(place, 2)]
    wire.copy(block, block, other_core)
    wire.arrived(side_two)
    block = rows_two.at[1, flip(place, 2)]
    wire.copy(block, block, other_core)
    tick(len(jobs))
    for item in own[3:]:
        item.wait()
    wire.finish()


def front(queries, keyval, meta_q, meta_k, own_rows, vecs, out, fc, proj, grad_rows):
    count = lax.axis_size("seq")
    tensor = lax.axis_size("tensor")
    batches, rows, width = queries.shape
    two = keyval.shape[2]
    heads = 2 * width // two
    part, full = own_rows.shape
    shapes = [
        ((batches, rows, width), LOW),
        ((batches, heads, rows, 1), F32),
        ((batches, count, rows, two), LOW),
        ((count,) + out.shape, LOW),
        ((part, full), F32),
        ((2, tensor, part, full), LOW),
        ((count,) + fc.shape[1:], LOW),
        ((count,) + proj.shape[1:], LOW),
        ((tensor, part, full), LOW),
    ]
    copies = 2 * (count - 1) + 3 * (count - 1) + 4 + 2 + 7
    vmem, hbm = pl.BlockSpec(memory_space=pltpu.VMEM), pl.BlockSpec(memory_space=pl.ANY)
    return pl.pallas_call(
        partial(front_kernel, count),
        out_shape=[jax.ShapeDtypeStruct(shape, dtype) for shape, dtype in shapes],
        in_specs=[vmem] * 6 + [hbm] * 4,
        out_specs=[vmem] * 6 + [hbm] * 3,
        scratch_shapes=[
            pltpu.VMEM((heads, rows, 1), F32),
            pltpu.VMEM((heads, rows, 1), F32),
            pltpu.VMEM((rows, width), F32),
            pltpu.VMEM((2 * part, full), F32),
            pltpu.VMEM((2 * part, full), LOW),
            pltpu.VMEM((2 * part, full), LOW),
            pltpu.VMEM((part, full), LOW),
            pltpu.VMEM((part, full), LOW),
            pltpu.SemaphoreType.DMA((copies,)),
            pltpu.SemaphoreType.DMA((copies,)),
            pltpu.SemaphoreType.DMA((5,)),
        ],
        compiler_params=pltpu.CompilerParams(
            collective_id=1, has_side_effects=True, vmem_limit_bytes=56 << 20
        ),
        name="front",
    )(queries, keyval, meta_q, meta_k, own_rows, vecs, out, fc, proj, grad_rows)


def by_rows(rows, step, body):
    def run(i, carry):
        body(pl.ds(pl.multiple_of(i * step, step), step))
        return carry

    lax.fori_loop(0, rows // step, run, 0)


class SeqSum:
    def __init__(self, wire, index, peers, part, from_near, to_far, from_far, out, split):
        self.wire, self.index = wire, index
        self.far, self.near = peers[:-1], peers[-1]
        self.lines = len(peers)
        self.part, self.out, self.split = part, out, split
        self.from_near, self.to_far, self.from_far = from_near, to_far, from_far
        self.rows = part.shape[1]
        self.step = min(64, self.rows)
        self.near_handles, self.far_handles = {}, {}
        self.order = turns(self.lines)

    def start(self, order=None):
        for d in order or turns(self.lines) + [0]:
            block = self.part.at[flip(self.index, 2 * d + 1)]
            self.near_handles[d] = self.wire.copy(block, self.from_near.at[d], self.near)

    def relay(self, number):
        for _ in range(number):
            d = self.order.pop(0)
            self.wire.arrived(self.near_handles[d])

            def join(at, d=d):
                total = self.part[flip(self.index, 2 * d), at].astype(F32)
                total = total + self.from_near[d, at].astype(F32)
                self.to_far[d - 1, at] = total.astype(self.to_far.dtype)

            by_rows(self.rows, self.step, join)
            self.far_handles[d] = self.wire.copy(
                self.to_far.at[d - 1], self.from_far.at[d - 1], self.far[d - 1]
            )

    def close(self):
        self.wire.arrived(self.near_handles[0])
        for d in range(1, self.lines):
            self.wire.arrived(self.far_handles[d])
        width = self.part.shape[2]
        half = lax.rem(lax.div(self.index, 2), 2)

        def total(at):
            same = self.part[self.index, at].astype(F32) + self.from_near[0, at].astype(F32)
            other = None
            for d in range(1, self.lines):
                got = self.from_far[d - 1, at].astype(F32)
                if self.split and d % 2:
                    other = got if other is None else other + got
                else:
                    same = same + got
            if self.split:
                out = self.out
                out[at, pl.ds(pl.multiple_of(half * width, width), width)] = same
                out[at, pl.ds(pl.multiple_of((1 - half) * width, width), width)] = other
            else:
                self.out[at, :] = same

        by_rows(self.rows, self.step, total)


def seq_sum_scratch(part, dtype=LOW):
    lines = part.shape[0] // 2
    return [
        pltpu.VMEM((depth,) + part.shape[1:], dtype) for depth in (lines, lines - 1, lines - 1)
    ]


class RowSum:
    def __init__(self, wire, place, pair, part, core_got, y_send, y_got, pair_send, pair_got):
        self.wire, self.place, self.pair = wire, place, pair
        self.core, self.side = lax.rem(place, 2), lax.div(place, 2)
        self.part, self.core_got, self.y_send, self.y_got = part, core_got, y_send, y_got
        self.pair_send, self.pair_got = pair_send, pair_got
        self.sides = (1 - self.side, self.side)
        self.rows = part.shape[2]
        self.core_handles, self.y_handles = {}, {}

    def start(self):
        peer = {"tensor": flip(self.place, 1)}
        for which in range(2):
            for p in reversed(range(self.part.shape[0])):
                at = self.sides[which]
                block = self.part.at[p, 2 * at + 1 - self.core]
                self.core_handles[p, which] = self.wire.copy(block, self.core_got.at[p, at], peer)

    def both(self, p, which, at):
        side = self.sides[which]
        mine = self.part[p, 2 * side + self.core, at, :].astype(F32)
        return mine + self.core_got[p, side, at, :].astype(F32)

    def to_side(self, p):
        self.wire.arrived(self.core_handles[p, 0])

        def body(at):
            self.y_send[p, at, :] = self.both(p, 0, at).astype(LOW)

        by_rows(self.rows, 16, body)
        peer = {"tensor": flip(self.place, 2)}
        self.y_handles[p] = self.wire.copy(self.y_send.at[p], self.y_got.at[p], peer)

    def to_pair(self):
        self.wire.arrived(self.core_handles[1, 1])
        self.wire.arrived(self.y_handles[1])

        def body(at):
            total = self.both(1, 1, at) + self.y_got[1, at, :].astype(F32)
            self.pair_send[at, :] = total.astype(LOW)

        by_rows(self.rows, 16, body)
        self.pair_handle = self.wire.copy(self.pair_send, self.pair_got, self.pair)

    def ready(self):
        self.wire.arrived(self.core_handles[0, 1])
        self.wire.arrived(self.y_handles[0])
        if self.pair is not None:
            self.wire.arrived(self.pair_handle)

    def total(self, at):
        total = self.both(0, 1, at) + self.y_got[0, at, :].astype(F32)
        if self.pair is not None:
            total = total + self.pair_got[at, :].astype(F32)
        return total


def row_sum_scratch(part):
    pairs, _, rows, width = part.shape
    scratch = [pltpu.VMEM((pairs, 2, rows, width), LOW)]
    scratch += [pltpu.VMEM((pairs, rows, width), LOW)] * 2
    if pairs == 2:
        scratch += [pltpu.VMEM((rows, width), LOW)] * 2
    return scratch


class RowGather:
    def __init__(self, wire, place, rows):
        self.wire, self.place, self.rows = wire, place, rows

    def start(self):
        mine = self.rows.at[self.place]
        self.side_handle = self.wire.copy(mine, mine, {"tensor": flip(self.place, 2)})
        self.wire.copy(mine, mine, {"tensor": flip(self.place, 1)})

    def forward(self):
        self.wire.arrived(self.side_handle)
        block = self.rows.at[flip(self.place, 2)]
        self.wire.copy(block, block, {"tensor": flip(self.place, 1)})


def sem_scratch(copies):
    return [pltpu.SemaphoreType.DMA((copies,)), pltpu.SemaphoreType.DMA((copies,))]


def middle_kernel(count, *refs):
    back, proj, centre, dy, vec = refs[:5]
    proj_sum, grad, rows, sums = refs[5:9]
    row_refs, seq_refs, (send_sem, recv_sem) = refs[9:14], refs[14:17], refs[17:]
    index, place = lax.axis_index("seq"), lax.axis_index("tensor")
    along = seq_peers(index, count)
    greet(along + [{"tensor": flip(place, 1)}, {"tensor": flip(place, 2)}])
    wire = Wire(send_sem, recv_sem)
    reduce = RowSum(wire, place, along[0], back, *row_refs)
    bulk = SeqSum(wire, index, along, proj, *seq_refs, proj_sum, True)
    gather = RowGather(wire, place, rows)
    lines = count // 2
    reduce.start()
    bulk.start()
    reduce.to_side(1)
    reduce.to_side(0)
    bulk.relay(1)
    reduce.to_pair()
    bulk.relay((lines - 1) // 3)
    reduce.ready()
    sums[...] = jnp.zeros_like(sums)
    gain = vec[0:1, :]

    def body(at):
        over = reduce.total(at)
        inner, product = norm_back(centre[at, :], gain, over)
        value = dy[at, :].astype(F32) + inner
        grad[at, :] = value
        rows[place, at, :] = value.astype(LOW)
        sums[0] += product
        sums[1] += over
        sums[2] += value

    by_rows(centre.shape[0], 16, body)
    gather.start()
    bulk.relay(lines - 1 - 1 - (lines - 1) // 3)
    gather.forward()
    bulk.close()
    wire.finish()


def middle_stage(back, proj, centre, dy, vec):
    count = lax.axis_size("seq")
    tensor = lax.axis_size("tensor")
    part, full = centre.shape
    vmem = pl.BlockSpec(memory_space=pltpu.VMEM)
    copies = 2 * count + 12
    return pl.pallas_call(
        partial(middle_kernel, count),
        out_shape=[
            jax.ShapeDtypeStruct((proj.shape[1], 2 * proj.shape[2]), F32),
            jax.ShapeDtypeStruct((part, full), F32),
            jax.ShapeDtypeStruct((tensor, part, full), LOW),
            jax.ShapeDtypeStruct((3, 16, full), F32),
        ],
        in_specs=[vmem] * 5,
        out_specs=[vmem] * 4,
        scratch_shapes=row_sum_scratch(back) + seq_sum_scratch(proj) + sem_scratch(copies),
        compiler_params=pltpu.CompilerParams(
            collective_id=2, has_side_effects=True, vmem_limit_bytes=60 << 20
        ),
        name="middle",
    )(back, proj, centre, dy, vec)


def back_kernel(count, *refs):
    feed, fc, out, q_in, kv_in, mq_in, mk_in, mixed, lse, grad_o_in, centre, vec = refs[:12]
    fc_sum, out_sum, dq, dkv, result = refs[12:17]
    row_refs, seq_refs, out_refs, kv_refs = refs[17:22], refs[22:25], refs[25:28], refs[28:31]
    kv_send, kv_got, kv_part, kv_total, delta, acc, send_sem, recv_sem = refs[31:]
    index, place = lax.axis_index("seq"), lax.axis_index("tensor")
    core = lax.rem(place, 2)
    other_core = {"tensor": flip(place, 1)}
    along = seq_peers(index, count)
    lines = count // 2
    greet(along + [other_core, {"tensor": flip(place, 2)}])
    wire = Wire(send_sem, recv_sem)
    reduce = RowSum(wire, place, along[0], feed, *row_refs)
    bulk = SeqSum(wire, index, along, fc, *seq_refs, fc_sum, True)
    out_bulk = SeqSum(wire, index, along, out, *out_refs, out_sum, False)
    keys_sum = SeqSum(wire, index, along, kv_part, *kv_refs, kv_total, False)
    gather = RowGather(wire, place, result)
    hd = kv_in.shape[-1] // 2
    heads = q_in.shape[-1] // hd
    scale = float(hd) ** (-0.5)
    scale_two = scale * LOG2E
    near_x = 1 - lax.rem(index, 2)

    def open_batch(batch):
        acc[...] = jnp.zeros_like(acc)
        for head in range(heads):
            cols = slice(head * hd, (head + 1) * hd)
            product = grad_o_in[batch, :, cols].astype(F32) * mixed[batch, :, cols].astype(F32)
            delta[head] = jnp.sum(product, axis=-1, keepdims=True)

    def blocks_of(batch, which, target, extra):
        def body(line, carry):
            block = 2 * line + which
            mask = visible(mq_in[batch], mk_in[batch, block])
            keys = kv_in[batch, block, :, :hd]
            values = kv_in[batch, block, :, hd:]
            grad_k = jnp.zeros((keys.shape[0], hd), F32)
            grad_v = jnp.zeros((keys.shape[0], hd), F32)
            for head in range(heads):
                cols = slice(head * hd, (head + 1) * hd)
                query = q_in[batch, :, cols]
                grad_o = grad_o_in[batch, :, cols]
                scores = dot_nt(query, keys) * scale_two
                probs = jnp.where(mask, jnp.exp2(scores - lse[batch, head]), 0.0)
                grad_p = dot_nt(grad_o, values)
                grad_s = (probs * (grad_p - delta[head])).astype(LOW)
                acc[:, cols] += dot(grad_s, keys)
                grad_k = grad_k + dot_tn(grad_s, query)
                grad_v = grad_v + dot_tn(probs.astype(LOW), grad_o)
            grad_k = grad_k * scale
            if extra is not None:
                grad_k = grad_k + extra[block, :, :hd].astype(F32)
                grad_v = grad_v + extra[block, :, hd:].astype(F32)
            target[block, :, :hd] = grad_k.astype(LOW)
            target[block, :, hd:] = grad_v.astype(LOW)
            return carry

        lax.fori_loop(0, lines, body, 0)

    def close_batch(batch):
        dq[batch] = (acc[...] * scale).astype(LOW)

    def to_core(which):
        return [
            wire.copy(kv_send.at[2 * line + which], kv_got.at[2 * line + which], other_core)
            for line in range(lines)
        ]

    reduce.start()
    middle, edge = turns(lines)[: lines // 2], turns(lines)[lines // 2 :]
    bulk.start(middle)
    out_bulk.start(middle)
    bulk.start(edge)
    out_bulk.start(edge)
    open_batch(1 - core)
    blocks_of(1 - core, near_x, kv_send, None)
    near_handles = to_core(near_x)
    reduce.to_side(1)
    reduce.to_side(0)
    bulk.relay(lines // 4)
    blocks_of(1 - core, 1 - near_x, kv_send, None)
    own_handles = to_core(1 - near_x)
    close_batch(1 - core)
    bulk.relay(lines // 2 - lines // 4)
    for handle in near_handles:
        wire.arrived(handle)
    open_batch(core)
    blocks_of(core, near_x, kv_part, kv_got)
    keys_sum.start()
    bulk.start([0])
    out_bulk.start([0])
    reduce.to_pair()
    out_bulk.relay(lines // 2)
    for handle in own_handles:
        wire.arrived(handle)
    blocks_of(core, 1 - near_x, kv_part, kv_got)
    close_batch(core)
    bulk.relay(len(edge))
    out_bulk.relay(len(edge))
    reduce.ready()
    bias = vec[0:1, :]

    def body(at):
        total = centre[at, :] + reduce.total(at) + bias
        result[place, at, :] = total.astype(LOW)

    by_rows(centre.shape[0], 16, body)
    gather.start()
    keys_sum.relay(lines - 1)
    gather.forward()
    keys_sum.close()
    dkv[1 - core] = jnp.zeros(dkv.shape[1:], LOW)
    dkv[core] = kv_total[...].astype(LOW)
    bulk.close()
    out_bulk.close()
    wire.finish()


def back_stage(feed, fc, out, queries, keyval, meta_q, meta_k, mixed, lse, grad_mixed, centre, vec):
    count = lax.axis_size("seq")
    tensor = lax.axis_size("tensor")
    part, full = centre.shape
    batches, rows, width = queries.shape
    blocks, two = keyval.shape[1], keyval.shape[3]
    heads = 2 * width // two
    vmem = pl.BlockSpec(memory_space=pltpu.VMEM)
    kv_part = jax.ShapeDtypeStruct((blocks, rows, two), LOW)
    copies = 4 * count + 14
    return pl.pallas_call(
        partial(back_kernel, count),
        out_shape=[
            jax.ShapeDtypeStruct((fc.shape[1], 2 * fc.shape[2]), F32),
            jax.ShapeDtypeStruct(out.shape[1:], F32),
            jax.ShapeDtypeStruct((batches, rows, width), LOW),
            jax.ShapeDtypeStruct((batches, rows, two), LOW),
            jax.ShapeDtypeStruct((tensor, part, full), LOW),
        ],
        in_specs=[vmem] * 12,
        out_specs=[vmem] * 5,
        scratch_shapes=row_sum_scratch(feed)
        + seq_sum_scratch(fc)
        + seq_sum_scratch(out)
        + seq_sum_scratch(kv_part)
        + [pltpu.VMEM(kv_part.shape, LOW)] * 3
        + [
            pltpu.VMEM((rows, two), F32),
            pltpu.VMEM((heads, rows, 1), F32),
            pltpu.VMEM((rows, width), F32),
        ]
        + sem_scratch(copies),
        compiler_params=pltpu.CompilerParams(
            collective_id=3, has_side_effects=True, vmem_limit_bytes=60 << 20
        ),
        name="back",
    )(feed, fc, out, queries, keyval, meta_q, meta_k, mixed, lse, grad_mixed, centre, vec)


def last_kernel(count, *refs):
    back, query, keyval, small, own, dy, vec = refs[:7]
    query_sum, keyval_sum, rows, small_sum = refs[7:11]
    row_refs, key_row_refs = refs[11:14], refs[14:17]
    query_refs, key_refs, small_refs = refs[17:20], refs[20:23], refs[23:26]
    key_part, small_part, small_own, small_got, sums, send_sem, recv_sem = refs[26:]
    index, place = lax.axis_index("seq"), lax.axis_index("tensor")
    along = seq_peers(index, count)
    other_core, other_side = {"tensor": flip(place, 1)}, {"tensor": flip(place, 2)}
    greet(along + [other_core, other_side])
    wire = Wire(send_sem, recv_sem)
    reduce = RowSum(wire, place, None, back, *row_refs, None, None)
    key_reduce = RowSum(wire, place, None, keyval, *key_row_refs, None, None)
    query_bulk = SeqSum(wire, index, along, query, *query_refs, query_sum, False)
    key_bulk = SeqSum(wire, index, along, key_part, *key_refs, keyval_sum, False)
    small_bulk = SeqSum(wire, index, along, small_part, *small_refs, small_own.at[0], False)
    gather = RowGather(wire, place, rows)
    spread = count // 2 - 1
    reduce.start()
    query_bulk.start()
    key_reduce.start()
    reduce.to_side(0)
    key_reduce.to_side(0)
    query_bulk.relay(spread // 3)
    reduce.ready()
    sums[...] = jnp.zeros_like(sums)
    gain = vec[0:1, :]

    def body(at):
        over = reduce.total(at)
        inner, product = norm_back(own[at, :].astype(F32), gain, over)
        rows[place, at, :] = (dy[at, :] + inner).astype(LOW)
        sums[0] += product
        sums[1] += over

    by_rows(own.shape[0], 16, body)
    gather.start()
    small_part[...] = small[...]
    width = own.shape[1] // count
    for row in range(2):
        line = jnp.sum(sums[row], axis=0, keepdims=True)
        for block in range(count):
            part = line[:, block * width : (block + 1) * width]
            small_part[block, row : row + 1, 0:width] = part
    small_bulk.start()
    key_reduce.ready()
    step = key_part.shape[1]
    for block in range(count):
        key_part[block] = key_reduce.total(slice(block * step, (block + 1) * step)).astype(LOW)
    key_bulk.start()
    query_bulk.relay(spread // 3)
    gather.forward()
    small_bulk.relay(spread)
    query_bulk.relay(spread - 2 * (spread // 3))
    key_bulk.relay(spread)
    small_bulk.close()
    for turn, peer in enumerate((other_core, other_side)):
        handle = wire.copy(small_own.at[turn], small_got.at[turn], peer)
        wire.arrived(handle)
        total = small_own[turn] + small_got[turn]
        if turn:
            small_sum[...] = total
        else:
            small_own[1] = total
    query_bulk.close()
    key_bulk.close()
    wire.finish()


def last_stage(back, query, keyval, small, own, dy, vec):
    count = lax.axis_size("seq")
    tensor = lax.axis_size("tensor")
    part, full = own.shape
    vmem = pl.BlockSpec(memory_space=pltpu.VMEM)
    key_part = jax.ShapeDtypeStruct((count, keyval.shape[2] // count, keyval.shape[3]), LOW)
    copies = 3 * count + 12
    return pl.pallas_call(
        partial(last_kernel, count),
        out_shape=[
            jax.ShapeDtypeStruct(query.shape[1:], F32),
            jax.ShapeDtypeStruct(key_part.shape[1:], F32),
            jax.ShapeDtypeStruct((tensor, part, full), LOW),
            jax.ShapeDtypeStruct(small.shape[1:], F32),
        ],
        in_specs=[vmem] * 7,
        out_specs=[vmem] * 4,
        scratch_shapes=row_sum_scratch(back)
        + row_sum_scratch(keyval)
        + seq_sum_scratch(query)
        + seq_sum_scratch(key_part)
        + seq_sum_scratch(small, F32)
        + [
            pltpu.VMEM(key_part.shape, LOW),
            pltpu.VMEM(small.shape, F32),
            pltpu.VMEM((2,) + small.shape[1:], F32),
            pltpu.VMEM((2,) + small.shape[1:], F32),
            pltpu.VMEM((2, 16, full), F32),
        ]
        + sem_scratch(copies),
        compiler_params=pltpu.CompilerParams(
            collective_id=4, has_side_effects=True, vmem_limit_bytes=60 << 20
        ),
        name="last",
    )(back, query, keyval, small, own, dy, vec)


def visible(meta_q, meta_k):
    seg_q, pos_q = meta_q[:, 0:1], meta_q[:, 1:2]
    seg_k, pos_k = meta_k[0:1, :], meta_k[1:2, :]
    return ((seg_k == 0) | (seg_k == seg_q)) & (pos_k <= pos_q)


def norm_parts(values):
    average = jnp.mean(values, axis=-1, keepdims=True)
    centred = values - average
    spread = jnp.mean(centred * centred, axis=-1, keepdims=True)
    return centred, lax.rsqrt(spread + EPS)


def norm_back(values, gain, grad):
    centred, inverse = norm_parts(values)
    unit = centred * inverse
    scaled = grad * gain
    inner = (
        scaled
        - jnp.mean(scaled, axis=-1, keepdims=True)
        - unit * jnp.mean(scaled * unit, axis=-1, keepdims=True)
    )
    return inverse * inner, grad * unit


def gelu_pair(values):
    const = 0.7978845608028654
    square = values * values
    inner = jnp.tanh(const * (values + 0.044715 * (values * square)))
    half = 0.5 * (1.0 + inner)
    slope = half + 0.5 * values * (1.0 - inner * inner) * const * (1.0 + 3 * 0.044715 * square)
    return values * half, slope


def local(
    inputs,
    segment,
    position,
    w_query,
    w_keyval,
    w_out,
    w_fc,
    w_proj,
    vectors,
    fc_bias,
    value_bias,
    grad_out,
):
    seq_size, tensor_size = lax.axis_size("seq"), lax.axis_size("tensor")
    seq_index, tensor_index = lax.axis_index("seq"), lax.axis_index("tensor")
    batches, rows, full_width = inputs.shape
    width_block = w_query.shape[0]
    group_width = w_query.shape[1]
    hidden_width = w_fc.shape[1]
    unit_width = hidden_width // 2
    unit_half = (seq_index >> 1) & 1
    hd = value_bias.shape[0]
    quarter = rows // tensor_size
    shard = vectors.shape[1]
    bias_shard = fc_bias.shape[0]

    pieces = [
        vectors.reshape(-1).astype(LOW),
        fc_bias.astype(LOW),
        segment.reshape(-1).astype(LOW),
        (position // 128).reshape(-1).astype(LOW),
        (position % 128).reshape(-1).astype(LOW),
    ]
    cuts = [0]
    for piece in pieces:
        cuts.append(cuts[-1] + piece.shape[0])
    packed = jnp.concatenate(pieces)
    packed = jnp.pad(packed, (0, -packed.shape[0] % 2048)).reshape(-1, 128)

    def halves(array):
        return jnp.swapaxes(array.astype(LOW).reshape(width_block, 2, unit_width), 0, 1)

    small, kv_mat, q_mat = gather_first(packed, w_keyval.astype(LOW), w_query.astype(LOW))
    kv_mat = kv_mat.reshape(full_width, 2 * hd)
    q_mat = q_mat.reshape(full_width, group_width)

    small = small.reshape(seq_size, tensor_size, -1).astype(F32)
    vec_all = small[:, :, cuts[0] : cuts[1]].reshape(seq_size * tensor_size, 7, shard)
    vec_all = jnp.swapaxes(vec_all, 0, 1).reshape(7, full_width)
    fc_all = small[:, :, cuts[1] : cuts[2]].reshape(-1)
    seg_keys = small[:, 0, cuts[2] : cuts[3]].reshape(seq_size, batches, rows)
    pos_keys = 128.0 * small[:, 0, cuts[3] : cuts[4]] + small[:, 0, cuts[4] : cuts[5]]
    seg_keys = jnp.swapaxes(seg_keys, 0, 1).astype(jnp.int32)
    pos_keys = jnp.swapaxes(pos_keys.reshape(seq_size, batches, rows), 0, 1).astype(jnp.int32)
    meta_k = jnp.pad(jnp.stack([seg_keys, pos_keys], axis=2), ((0, 0), (0, 0), (0, 6), (0, 0)))
    meta_q = jnp.pad(jnp.stack([segment, position], axis=2), ((0, 0), (0, 0), (0, 126)))

    gain_one, shift_one, _, out_bias, gain_two, shift_two, proj_bias = [
        vec_all[i] for i in range(7)
    ]
    query_bias = lax.dynamic_slice_in_dim(vec_all[2], tensor_index * group_width, group_width, 0)
    fc_local = lax.dynamic_slice_in_dim(
        fc_all, tensor_index * hidden_width + unit_half * unit_width, unit_width, 0
    )
    bias_value = value_bias.astype(LOW).astype(F32)
    kv_bias = jnp.concatenate([jnp.zeros((hd,), F32), bias_value])

    residual = inputs.astype(F32)
    centred, inverse = norm_parts(residual)
    normed = (centred * inverse * gain_one + shift_one).astype(LOW).reshape(-1, full_width)
    keyval = (dot(normed, kv_mat) + kv_bias).astype(LOW).reshape(batches, rows, 2 * hd)
    queries = (dot(normed, q_mat) + query_bias).astype(LOW)
    queries = queries.reshape(batches, rows, group_width)

    def by_quarter(array):
        split = array.reshape(batches, tensor_size, quarter, array.shape[-1])
        return jnp.swapaxes(split, 0, 1).reshape(tensor_size, batches * quarter, -1)

    def by_batch(array):
        split = array.reshape(tensor_size, batches, quarter, array.shape[-1])
        return jnp.swapaxes(split, 0, 1).reshape(batches, rows, -1)

    def my_quarter(array):
        split = array.reshape(batches, tensor_size, quarter, full_width)
        own = lax.dynamic_index_in_dim(split, tensor_index, 1, keepdims=False)
        return own.reshape(batches * quarter, full_width)

    vecs = jnp.pad(jnp.stack([out_bias, gain_two, shift_two]), ((0, 5), (0, 0)))
    grad_split = by_quarter(grad_out)
    mixed, lse, kv_all, out_t, middle, rows_two, fc_mat, proj_t, grad_other = front(
        queries,
        keyval,
        meta_q,
        meta_k,
        my_quarter(inputs),
        vecs,
        w_out.T.astype(LOW),
        halves(w_fc),
        halves(w_proj.T),
        grad_split,
    )
    out_t = out_t.reshape(full_width, group_width)
    fc_mat = fc_mat.reshape(full_width, unit_width)
    proj_t = proj_t.reshape(full_width, unit_width)
    mixed_rows = by_quarter(mixed).reshape(-1, group_width)
    normed_two = rows_two.reshape(-1, full_width)
    hidden = dot(normed_two, fc_mat) + fc_local
    active_f, slope = gelu_pair(hidden)
    active = active_f.astype(LOW)

    grad_q_low = my_quarter(grad_out)
    grad_flat = jnp.concatenate([grad_split, grad_other]).reshape(-1, full_width)
    grad_hidden = (slope * dot(grad_flat, proj_t)).astype(LOW)
    fcbias_local = jnp.sum(grad_hidden.astype(F32), axis=0)
    back_part = dot_nt(grad_hidden, fc_mat).astype(LOW)
    back_part = back_part.reshape(2, tensor_size, batches * quarter, full_width)

    def blocked(array):
        return array.astype(LOW).reshape(seq_size, width_block, array.shape[-1])

    proj_sum, grad_middle, rows_middle, sums = middle_stage(
        back_part,
        blocked(dot_tn(grad_flat, active)),
        middle,
        grad_q_low,
        jnp.pad(gain_two[None], ((0, 7), (0, 0))),
    )
    grad_gain_two, grad_shift_two, grad_out_bias = jnp.sum(sums, axis=1)
    grad_proj_bias = jnp.sum(grad_q_low.astype(F32), axis=0)
    grad_middle_low = rows_middle.reshape(-1, full_width)
    def one_row(row):
        return jnp.pad(row[None], ((0, 7), (0, 0)))

    grad_mixed = by_batch(dot(grad_middle_low, out_t).astype(LOW))
    feed_part = dot_nt(active, proj_t).astype(LOW)
    fc_sum, out_sum, grad_queries, grad_keyval, result_rows = back_stage(
        feed_part.reshape(2, tensor_size, batches * quarter, full_width),
        blocked(dot_tn(normed_two, grad_hidden)),
        blocked(dot_tn(grad_middle_low, mixed_rows)),
        queries,
        kv_all,
        meta_q,
        meta_k,
        mixed,
        lse,
        grad_mixed,
        middle,
        one_row(proj_bias),
    )
    result = by_batch(result_rows)
    grad_keyval = grad_keyval.reshape(-1, 2 * hd)
    grad_queries = grad_queries.reshape(-1, group_width)
    grad_normed = dot_nt(grad_queries, q_mat) + dot_nt(grad_keyval, kv_mat)
    qbias_local = jnp.sum(grad_queries.astype(F32), axis=0)
    vbias_local = jnp.sum(grad_keyval[:, hd:].astype(F32), axis=0)

    qbias_full = lax.dynamic_update_slice_in_dim(
        jnp.zeros((full_width,), F32), qbias_local, tensor_index * group_width, 0
    )
    full_hidden = bias_shard * seq_size * tensor_size
    fcbias_full = lax.dynamic_update_slice_in_dim(
        jnp.zeros((full_hidden,), F32),
        fcbias_local,
        tensor_index * hidden_width + unit_half * unit_width,
        0,
    )
    chunk = full_hidden // seq_size
    blank = jnp.zeros((full_width,), F32)
    vec_grads = jnp.stack(
        [blank, blank, qbias_full, grad_out_bias, grad_gain_two, grad_shift_two, grad_proj_bias]
    )

    def in_rows(array):
        array = jnp.pad(array, ((0, 0), (0, -array.shape[1] % width_block)))
        return array.reshape(seq_size, -1, width_block)

    vec_rows = 7
    bias_rows = chunk // width_block
    small_rows = jnp.concatenate(
        [
            jnp.swapaxes(vec_grads.reshape(7, seq_size, width_block), 0, 1),
            in_rows(fcbias_full.reshape(seq_size, chunk)),
            in_rows(jnp.broadcast_to(vbias_local, (seq_size, hd))),
        ],
        axis=1,
    )
    small_rows = jnp.pad(
        small_rows,
        ((0, 0), (0, -small_rows.shape[1] % 8), (0, -width_block % 128)),
    )
    key_grad = dot_tn(normed, grad_keyval).astype(LOW)
    key_grad = key_grad.reshape(seq_size, tensor_size, -1, 2 * hd)
    key_grad = jnp.swapaxes(key_grad, 0, 1).reshape(1, tensor_size, -1, 2 * hd)
    query_sum, keyval_grad, input_rows, small_sum = last_stage(
        by_quarter(grad_normed.astype(LOW))[None],
        blocked(dot_tn(normed, grad_queries)),
        key_grad,
        small_rows,
        my_quarter(inputs),
        grad_middle,
        one_row(gain_one),
    )
    input_grad = by_batch(input_rows)
    small_sum = small_sum[:, :width_block]
    vec_grad = lax.dynamic_slice_in_dim(small_sum[:vec_rows], tensor_index * shard, shard, 1)
    fcbias_grad = lax.dynamic_slice_in_dim(
        small_sum[vec_rows : vec_rows + bias_rows].reshape(-1),
        tensor_index * bias_shard,
        bias_shard,
        0,
    )
    vbias_grad = small_sum[vec_rows + bias_rows :].reshape(-1)[:hd]
    return (
        result,
        input_grad,
        query_sum,
        keyval_grad,
        out_sum.T,
        fc_sum,
        proj_sum.T,
        vec_grad,
        fcbias_grad,
        vbias_grad,
        vec_grad[5],
    )


def solution(mesh):
    in_specs = (
        P(None, "seq", None),
        P(None, "seq"),
        P(None, "seq"),
        P("seq", "tensor"),
        P(("seq", "tensor"), None),
        P("tensor", "seq"),
        P("seq", "tensor"),
        P("tensor", "seq"),
        P(None, ("seq", "tensor")),
        P(("seq", "tensor")),
        P(),
        P(None, "seq", None),
    )
    out_specs = (
        P(None, "seq", None),
        P(None, "seq", None),
        P("seq", "tensor"),
        P(("seq", "tensor"), None),
        P("tensor", "seq"),
        P("seq", "tensor"),
        P("tensor", "seq"),
        P(None, ("seq", "tensor")),
        P(("seq", "tensor")),
        P(),
        P(("seq", "tensor")),
    )
    return jax.shard_map(local, mesh=mesh, in_specs=in_specs, out_specs=out_specs, check_vma=False)
```

```python
from functools import partial

import jax
import jax.numpy as jnp
from jax import lax
from jax.experimental import pallas as pl
from jax.experimental.pallas import tpu as pltpu
from jax.sharding import PartitionSpec as P

EPS = 1e-05
NEG = -1e30
LOG2E = 1.4426950408889634
LOW = jnp.bfloat16
F32 = jnp.float32


def bits_of(count):
    return count.bit_length() - 1


def swap(value, axis, bit):
    count = lax.axis_size(axis)
    return lax.ppermute(value, axis, [(i, i ^ (1 << bit)) for i in range(count)])


def after(value, *others):
    return lax.optimization_barrier((value,) + others)[0]


def dot(left, right):
    return jnp.dot(left, right, preferred_element_type=F32)


def dot_tn(left, right):
    return lax.dot_general(left, right, (((0,), (0,)), ((), ())), preferred_element_type=F32)


def dot_nt(left, right):
    return lax.dot_general(left, right, (((1,), (1,)), ((), ())), preferred_element_type=F32)


MESH = pl.DeviceIdType.MESH


def flip(index, mask):
    bit = 1
    out = index
    while bit <= mask:
        if mask & bit:
            out = out + bit * (1 - 2 * lax.rem(lax.div(index, bit), 2))
        bit *= 2
    return out


class Wire:
    def __init__(self, send_sem, recv_sem):
        self.send_sem, self.recv_sem = send_sem, recv_sem
        self.started = []
        self.landed = set()

    def copy(self, src, dst, peer):
        place = len(self.started)
        item = pltpu.make_async_remote_copy(
            src_ref=src,
            dst_ref=dst,
            send_sem=self.send_sem.at[place],
            recv_sem=self.recv_sem.at[place],
            device_id=peer,
            device_id_type=MESH,
        )
        item.start()
        self.started.append(item)
        return place

    def arrived(self, place):
        if place not in self.landed:
            self.landed.add(place)
            self.started[place].wait_recv()

    def finish(self):
        for place in range(len(self.started)):
            self.arrived(place)
        for item in self.started:
            item.wait_send()


def greet(peers):
    barrier = pltpu.get_barrier_semaphore()
    for peer in peers:
        pl.semaphore_signal(barrier, inc=1, device_id=peer, device_id_type=MESH)
    pl.semaphore_wait(barrier, len(peers))


def seq_peers(index, count):
    return [{"seq": flip(index, 2 * d)} for d in range(1, count // 2)] + [
        {"seq": flip(index, 1)}
    ]


def turns(lines):
    return list(range(lines // 2, lines)) + list(range(1, lines // 2))


def first_kernel(count, tensor, *refs):
    ins, outs = refs[:3], refs[3:6]
    send_sem, recv_sem, local_sem = refs[6:]
    index = lax.axis_index("seq")
    place = lax.axis_index("tensor")
    across = [{"tensor": flip(place, tensor >> (i + 1))} for i in range(bits_of(tensor))]
    along = seq_peers(index, count)
    far, near = along[:-1], along[-1]
    greet(across + along)
    wire = Wire(send_sem, recv_sem)
    own = []
    targets = [(lambda at, out=out: out.at[at, place]) for out in outs[:2]]
    targets.append(lambda at: outs[2].at[at])
    handles = []
    for source, target in zip(ins, targets):
        handles.append({d: wire.copy(source, target(index), far[d - 1]) for d in range(1, count // 2)})
        handles[-1][0] = wire.copy(source, target(index), near)
        item = pltpu.make_async_copy(source, target(index), local_sem.at[len(own)])
        item.start()
        own.append(item)
    relays = []
    for a, target in enumerate(targets):
        for d in range(1, count // 2):
            wire.arrived(handles[a][d])
            block = target(flip(index, 2 * d))
            relays.append(wire.copy(block, block, near))
        if a == 1:
            for handle in [handles[0][0], handles[1][0]] + relays:
                wire.arrived(handle)
            own[0].wait()
            own[1].wait()
            masks = [0]
            for i, peer in enumerate(across):
                step = tensor >> (i + 1)
                sent = [
                    wire.copy(out.at[:, flip(place, mask)], out.at[:, flip(place, mask)], peer)
                    for mask in masks
                    for out in outs[:2]
                ]
                masks = masks + [mask | step for mask in masks]
                if i + 1 < len(across):
                    for handle in sent:
                        wire.arrived(handle)
    own[2].wait()
    wire.finish()


def gather_first(small, keyval, query):
    count, tensor = lax.axis_size("seq"), lax.axis_size("tensor")
    arrays = (small, keyval, query)
    shapes = [
        (count, tensor) + small.shape,
        (count, tensor) + keyval.shape,
        (count,) + query.shape,
    ]
    copies = 3 * (count - 1) + 2 * (tensor - 1)
    return pl.pallas_call(
        partial(first_kernel, count, tensor),
        out_shape=[jax.ShapeDtypeStruct(shape, LOW) for shape in shapes],
        in_specs=[pl.BlockSpec(memory_space=pltpu.VMEM)] * 3,
        out_specs=[pl.BlockSpec(memory_space=pltpu.VMEM)] * 3,
        scratch_shapes=[
            pltpu.SemaphoreType.DMA((copies,)),
            pltpu.SemaphoreType.DMA((copies,)),
            pltpu.SemaphoreType.DMA((3,)),
        ],
        compiler_params=pltpu.CompilerParams(collective_id=0, has_side_effects=True),
        name="gather_first",
    )(*arrays)


def front_kernel(count, *refs):
    q_in, kv_in, mq_in, mk_in, x_in, vec_in, o_in, fc_in, pj_in, dy_in = refs[:10]
    mixed, lse, kv_all, out_t, middle, rows_two, fc_out, pj_out, dy_out = refs[10:19]
    (
        top,
        total,
        acc,
        core_keep,
        core_send,
        core_got,
        y_send,
        y_got,
        send_sem,
        recv_sem,
        local_sem,
    ) = refs[19:]
    index = lax.axis_index("seq")
    place = lax.axis_index("tensor")
    core = lax.rem(place, 2)
    side = lax.div(place, 2)
    half = lax.rem(lax.div(index, 2), 2)
    other_core = {"tensor": flip(place, 1)}
    other_side = {"tensor": flip(place, 2)}
    along = seq_peers(index, count)
    far, near = along[:-1], along[-1]
    pair = far[0]
    lines = count // 2
    greet(along + [other_core, other_side])
    wire = Wire(send_sem, recv_sem)
    own = []

    def keep(src, dst):
        item = pltpu.make_async_copy(src, dst, local_sem.at[len(own)])
        item.start()
        own.append(item)

    order = range(1, lines)
    kv_far = {d: wire.copy(kv_in.at[core], kv_all.at[core, index], far[d - 1]) for d in order}
    kv_near = wire.copy(kv_in.at[core], kv_all.at[core, index], near)
    for batch in range(2):
        keep(kv_in.at[batch], kv_all.at[batch, index])
    o_far = {d: wire.copy(o_in, out_t.at[index], far[d - 1]) for d in order}
    o_near = [wire.copy(o_in, out_t.at[index], near)]
    keep(o_in, out_t.at[index])
    dy_pair = wire.copy(dy_in.at[place], dy_out.at[place], pair)

    def send_far(source, out, which=order):
        return {
            d: wire.copy(source.at[flip(half, d & 1)], out.at[index], far[d - 1]) for d in which
        }

    fc_far = send_far(fc_in, fc_out)
    kv_near = [(1, kv_near)]
    kv_core = []
    for d in order:
        wire.arrived(kv_far[d])
        block = kv_all.at[core, flip(index, 2 * d)]
        kv_near.append((2 * d + 1, wire.copy(block, block, near)))
        kv_core.append(wire.copy(block, block, other_core))
    wire.copy(fc_in.at[half], fc_out.at[index], near)
    wire.copy(pj_in.at[half], pj_out.at[index], near)
    keep(fc_in.at[half], fc_out.at[index])
    keep(pj_in.at[half], pj_out.at[index])
    for r, handle in kv_near:
        wire.arrived(handle)
        block = kv_all.at[core, flip(index, r)]
        kv_core.append(wire.copy(block, block, other_core))
    own[0].wait()
    own[1].wait()

    jobs = [(o_far, out_t, d) for d in order]
    jobs += [(fc_far, fc_out, d) for d in order]

    def tick(number):
        for _ in range(min(number, len(jobs))):
            handles, out, d = jobs.pop(0)
            wire.arrived(handles[d])
            block = out.at[flip(index, 2 * d)]
            handle = wire.copy(block, block, near)
            if out is out_t:
                o_near.append(handle)

    hd = kv_in.shape[-1] // 2
    heads = q_in.shape[-1] // hd
    scale = float(hd) ** (-0.5) * LOG2E

    def attend(batch, block):
        mask = visible(mq_in[batch], mk_in[batch, block])
        keys = kv_all[batch, block, :, :hd]
        values = kv_all[batch, block, :, hd:]
        for head in range(heads):
            cols = slice(head * hd, (head + 1) * hd)
            scores = jnp.where(mask, dot_nt(q_in[batch, :, cols], keys) * scale, NEG)
            before = top[head]
            now = jnp.maximum(before, jnp.max(scores, axis=-1, keepdims=True))
            shrink = jnp.exp2(before - now)
            probs = jnp.exp2(scores - now)
            total[head] = total[head] * shrink + jnp.sum(probs, axis=-1, keepdims=True)
            acc[:, cols] = acc[:, cols] * shrink + dot(probs.astype(LOW), values)
            top[head] = now

    def attend_batch(batch, ticks):
        top[...] = jnp.full_like(top, NEG)
        total[...] = jnp.zeros_like(total)
        acc[...] = jnp.zeros_like(acc)

        def block_body(block, carry):
            attend(batch, block)
            return carry

        parts = len(ticks)
        for i in range(parts):
            lax.fori_loop(i * count // parts, (i + 1) * count // parts, block_body, 0)
            tick(ticks[i])
        for head in range(heads):
            cols = slice(head * hd, (head + 1) * hd)
            mixed[batch, :, cols] = (acc[:, cols] / total[head]).astype(LOW)
            lse[batch, head] = top[head] + jnp.log2(total[head])

    spread = lines - 1
    attend_batch(core, [spread])
    pj_far = send_far(pj_in, pj_out, order[:1])
    wire.arrived(dy_pair)
    dy_side = wire.copy(dy_out.at[place], dy_out.at[place], other_side)
    wire.copy(dy_out.at[place], dy_out.at[place], other_core)
    for handle in kv_core:
        wire.arrived(handle)
    attend_batch(1 - core, [spread // 3])
    wire.arrived(dy_side)
    block = dy_out.at[flip(place, 2)]
    wire.copy(block, block, other_core)

    quarter = x_in.shape[0] // 2
    for handle in o_near:
        wire.arrived(handle)
    own[2].wait()
    width = out_t.shape[1]
    group = max(1, 256 // width)
    for which, target in ((1 - core, core_send), (core, core_keep)):
        rows = [
            mixed[batch, pl.ds(pl.multiple_of((2 * s + which) * quarter, quarter), quarter), :]
            for s in range(2)
            for batch in range(2)
        ]
        rows = jnp.concatenate(rows, axis=0)

        def project(i, carry, rows=rows, target=target):
            cols = pl.ds(pl.multiple_of(i * group * width, group * width), group * width)
            block = out_t[pl.ds(i * group, group)].reshape(group * width, -1)
            target[:, cols] = dot_nt(rows, block).astype(target.dtype)
            return carry

        lax.fori_loop(0, count // group, project, 0)
        if target is core_send:
            core_handle = wire.copy(core_send, core_got, other_core)
    wire.arrived(core_handle)
    part = 2 * quarter
    step = 16

    def to_side(i, carry):
        at = pl.ds(pl.multiple_of((1 - side) * part + i * step, step), step)
        y_send[pl.ds(pl.multiple_of(i * step, step), step), :] = (
            core_keep[at, :] + core_got[at, :].astype(F32)
        ).astype(LOW)
        return carry

    lax.fori_loop(0, part // step, to_side, 0)
    y_handle = wire.copy(y_send, y_got, other_side)
    tick(spread - spread // 3 - 1)
    wire.arrived(y_handle)
    out_bias, gain_two, shift_two = vec_in[0:1, :], vec_in[1:2, :], vec_in[2:3, :]

    def norm(i, carry):
        at = pl.ds(pl.multiple_of(i * step, step), step)
        far_at = pl.ds(pl.multiple_of(side * part + i * step, step), step)
        value = core_keep[far_at, :] + core_got[far_at, :].astype(F32)
        value = value + y_got[at, :].astype(F32)
        value = x_in[at, :].astype(F32) + value + out_bias
        middle[at, :] = value
        centred, inverse = norm_parts(value)
        rows_two[0, place, at, :] = (centred * inverse * gain_two + shift_two).astype(LOW)
        return carry

    lax.fori_loop(0, part // step, norm, 0)
    mine = rows_two.at[0, place]
    pair_handle = wire.copy(mine, rows_two.at[1, place], pair)
    side_handle = wire.copy(mine, mine, other_side)
    wire.copy(mine, mine, other_core)
    pj_far.update(send_far(pj_in, pj_out, order[1:]))
    tick(len(jobs))
    jobs.extend((pj_far, pj_out, d) for d in order)
    wire.arrived(pair_handle)
    theirs = rows_two.at[1, place]
    side_two = wire.copy(theirs, theirs, other_side)
    wire.copy(theirs, theirs, other_core)
    wire.arrived(side_handle)
    block = rows_two.at[0, flip(place, 2)]
    wire.copy(block, block, other_core)
    wire.arrived(side_two)
    block = rows_two.at[1, flip(place, 2)]
    wire.copy(block, block, other_core)
    tick(len(jobs))
    for item in own[3:]:
        item.wait()
    wire.finish()


def front(queries, keyval, meta_q, meta_k, own_rows, vecs, out, fc, proj, grad_rows):
    count = lax.axis_size("seq")
    tensor = lax.axis_size("tensor")
    batches, rows, width = queries.shape
    two = keyval.shape[2]
    heads = 2 * width // two
    part, full = own_rows.shape
    shapes = [
        ((batches, rows, width), LOW),
        ((batches, heads, rows, 1), F32),
        ((batches, count, rows, two), LOW),
        ((count,) + out.shape, LOW),
        ((part, full), F32),
        ((2, tensor, part, full), LOW),
        ((count,) + fc.shape[1:], LOW),
        ((count,) + proj.shape[1:], LOW),
        ((tensor, part, full), LOW),
    ]
    copies = 2 * (count - 1) + 3 * (count - 1) + 4 + 2 + 7
    vmem, hbm = pl.BlockSpec(memory_space=pltpu.VMEM), pl.BlockSpec(memory_space=pl.ANY)
    return pl.pallas_call(
        partial(front_kernel, count),
        out_shape=[jax.ShapeDtypeStruct(shape, dtype) for shape, dtype in shapes],
        in_specs=[vmem] * 6 + [hbm] * 4,
        out_specs=[vmem] * 6 + [hbm] * 3,
        scratch_shapes=[
            pltpu.VMEM((heads, rows, 1), F32),
            pltpu.VMEM((heads, rows, 1), F32),
            pltpu.VMEM((rows, width), F32),
            pltpu.VMEM((2 * part, full), F32),
            pltpu.VMEM((2 * part, full), LOW),
            pltpu.VMEM((2 * part, full), LOW),
            pltpu.VMEM((part, full), LOW),
            pltpu.VMEM((part, full), LOW),
            pltpu.SemaphoreType.DMA((copies,)),
            pltpu.SemaphoreType.DMA((copies,)),
            pltpu.SemaphoreType.DMA((5,)),
        ],
        compiler_params=pltpu.CompilerParams(
            collective_id=1, has_side_effects=True, vmem_limit_bytes=56 << 20
        ),
        name="front",
    )(queries, keyval, meta_q, meta_k, own_rows, vecs, out, fc, proj, grad_rows)


def by_rows(rows, step, body):
    def run(i, carry):
        body(pl.ds(pl.multiple_of(i * step, step), step))
        return carry

    lax.fori_loop(0, rows // step, run, 0)


class SeqSum:
    def __init__(self, wire, index, peers, part, from_near, to_far, from_far, out, split):
        self.wire, self.index = wire, index
        self.far, self.near = peers[:-1], peers[-1]
        self.lines = len(peers)
        self.part, self.out, self.split = part, out, split
        self.from_near, self.to_far, self.from_far = from_near, to_far, from_far
        self.rows = part.shape[1]
        self.step = min(64, self.rows)
        self.near_handles, self.far_handles = {}, {}
        self.order = turns(self.lines)

    def start(self, order=None):
        for d in order or turns(self.lines) + [0]:
            block = self.part.at[flip(self.index, 2 * d + 1)]
            self.near_handles[d] = self.wire.copy(block, self.from_near.at[d], self.near)

    def relay(self, number):
        for _ in range(number):
            d = self.order.pop(0)
            self.wire.arrived(self.near_handles[d])

            def join(at, d=d):
                total = self.part[flip(self.index, 2 * d), at].astype(F32)
                total = total + self.from_near[d, at].astype(F32)
                self.to_far[d - 1, at] = total.astype(self.to_far.dtype)

            by_rows(self.rows, self.step, join)
            self.far_handles[d] = self.wire.copy(
                self.to_far.at[d - 1], self.from_far.at[d - 1], self.far[d - 1]
            )

    def close(self):
        self.wire.arrived(self.near_handles[0])
        for d in range(1, self.lines):
            self.wire.arrived(self.far_handles[d])
        width = self.part.shape[2]
        half = lax.rem(lax.div(self.index, 2), 2)

        def total(at):
            same = self.part[self.index, at].astype(F32) + self.from_near[0, at].astype(F32)
            other = None
            for d in range(1, self.lines):
                got = self.from_far[d - 1, at].astype(F32)
                if self.split and d % 2:
                    other = got if other is None else other + got
                else:
                    same = same + got
            if self.split:
                out = self.out
                out[at, pl.ds(pl.multiple_of(half * width, width), width)] = same
                out[at, pl.ds(pl.multiple_of((1 - half) * width, width), width)] = other
            else:
                self.out[at, :] = same

        by_rows(self.rows, self.step, total)


def seq_sum_scratch(part, dtype=LOW):
    lines = part.shape[0] // 2
    return [
        pltpu.VMEM((depth,) + part.shape[1:], dtype) for depth in (lines, lines - 1, lines - 1)
    ]


class RowSum:
    def __init__(self, wire, place, pair, part, core_got, y_send, y_got, pair_send, pair_got):
        self.wire, self.place, self.pair = wire, place, pair
        self.core, self.side = lax.rem(place, 2), lax.div(place, 2)
        self.part, self.core_got, self.y_send, self.y_got = part, core_got, y_send, y_got
        self.pair_send, self.pair_got = pair_send, pair_got
        self.sides = (1 - self.side, self.side)
        self.rows = part.shape[2]
        self.core_handles, self.y_handles = {}, {}

    def start(self):
        peer = {"tensor": flip(self.place, 1)}
        for which in range(2):
            for p in reversed(range(self.part.shape[0])):
                at = self.sides[which]
                block = self.part.at[p, 2 * at + 1 - self.core]
                self.core_handles[p, which] = self.wire.copy(block, self.core_got.at[p, at], peer)

    def both(self, p, which, at):
        side = self.sides[which]
        mine = self.part[p, 2 * side + self.core, at, :].astype(F32)
        return mine + self.core_got[p, side, at, :].astype(F32)

    def to_side(self, p):
        self.wire.arrived(self.core_handles[p, 0])

        def body(at):
            self.y_send[p, at, :] = self.both(p, 0, at).astype(LOW)

        by_rows(self.rows, 16, body)
        peer = {"tensor": flip(self.place, 2)}
        self.y_handles[p] = self.wire.copy(self.y_send.at[p], self.y_got.at[p], peer)

    def to_pair(self):
        self.wire.arrived(self.core_handles[1, 1])
        self.wire.arrived(self.y_handles[1])

        def body(at):
            total = self.both(1, 1, at) + self.y_got[1, at, :].astype(F32)
            self.pair_send[at, :] = total.astype(LOW)

        by_rows(self.rows, 16, body)
        self.pair_handle = self.wire.copy(self.pair_send, self.pair_got, self.pair)

    def ready(self):
        self.wire.arrived(self.core_handles[0, 1])
        self.wire.arrived(self.y_handles[0])
        if self.pair is not None:
            self.wire.arrived(self.pair_handle)

    def total(self, at):
        total = self.both(0, 1, at) + self.y_got[0, at, :].astype(F32)
        if self.pair is not None:
            total = total + self.pair_got[at, :].astype(F32)
        return total


def row_sum_scratch(part):
    pairs, _, rows, width = part.shape
    scratch = [pltpu.VMEM((pairs, 2, rows, width), LOW)]
    scratch += [pltpu.VMEM((pairs, rows, width), LOW)] * 2
    if pairs == 2:
        scratch += [pltpu.VMEM((rows, width), LOW)] * 2
    return scratch


class RowGather:
    def __init__(self, wire, place, rows):
        self.wire, self.place, self.rows = wire, place, rows

    def start(self):
        mine = self.rows.at[self.place]
        self.side_handle = self.wire.copy(mine, mine, {"tensor": flip(self.place, 2)})
        self.wire.copy(mine, mine, {"tensor": flip(self.place, 1)})

    def forward(self):
        self.wire.arrived(self.side_handle)
        block = self.rows.at[flip(self.place, 2)]
        self.wire.copy(block, block, {"tensor": flip(self.place, 1)})


def sem_scratch(copies):
    return [pltpu.SemaphoreType.DMA((copies,)), pltpu.SemaphoreType.DMA((copies,))]


def middle_kernel(count, *refs):
    back, proj, centre, dy, vec = refs[:5]
    sources, (feed_out, fc_out) = refs[5:9], refs[13:15]
    proj_sum, grad, rows, sums = refs[9:13]
    row_refs, seq_refs = refs[15:20], refs[20:23]
    local = refs[23:27]
    feed, fc_grad, send_sem, recv_sem, local_sem = refs[27:]
    loads = [
        pltpu.make_async_copy(source, target, local_sem.at[i])
        for i, (source, target) in enumerate(zip(sources, local))
    ]
    for item in loads:
        item.start()
    active, proj_t, unit, slope = local
    stores = [
        pltpu.make_async_copy(feed, feed_out, local_sem.at[4]),
        pltpu.make_async_copy(fc_grad, fc_out, local_sem.at[5]),
    ]
    tall, wide = active.shape[0] // 2, 256
    steps = proj_t.shape[0] // wide

    def feed_rows(which):
        at = slice(which * tall, (which + 1) * tall)

        def run(i, carry):
            cols = pl.ds(pl.multiple_of(i * wide, wide), wide)
            feed[at, cols] = dot_nt(active[at, :], proj_t[cols, :]).astype(LOW)
            return carry

        lax.fori_loop(0, steps, run, 0)

    def fc_rows(which):
        half_width = slope.shape[1] // 2
        out = slice(which * half_width, (which + 1) * half_width)

        def run(i, carry):
            cols = pl.ds(pl.multiple_of(i * wide, wide), wide)
            fc_grad[cols, out] = dot_tn(unit[:, cols], slope[:, out]).astype(LOW)
            return carry

        lax.fori_loop(0, steps, run, 0)

    index, place = lax.axis_index("seq"), lax.axis_index("tensor")
    along = seq_peers(index, count)
    greet(along + [{"tensor": flip(place, 1)}, {"tensor": flip(place, 2)}])
    wire = Wire(send_sem, recv_sem)
    reduce = RowSum(wire, place, along[0], back, *row_refs)
    bulk = SeqSum(wire, index, along, proj, *seq_refs, proj_sum, True)
    gather = RowGather(wire, place, rows)
    lines = count // 2
    reduce.start()
    bulk.start()
    reduce.to_side(1)
    reduce.to_side(0)
    loads[0].wait()
    loads[1].wait()
    feed_rows(0)
    bulk.relay(1)
    reduce.to_pair()
    feed_rows(1)
    stores[0].start()
    bulk.relay((lines - 1) // 3)
    reduce.ready()
    sums[...] = jnp.zeros_like(sums)
    gain = vec[0:1, :]

    def body(at):
        over = reduce.total(at)
        inner, product = norm_back(centre[at, :], gain, over)
        value = dy[at, :].astype(F32) + inner
        grad[at, :] = value
        rows[place, at, :] = value.astype(LOW)
        sums[0] += product
        sums[1] += over
        sums[2] += value

    by_rows(centre.shape[0], 16, body)
    gather.start()
    loads[2].wait()
    loads[3].wait()
    fc_rows(0)
    bulk.relay(lines - 1 - 1 - (lines - 1) // 3)
    gather.forward()
    fc_rows(1)
    stores[1].start()
    bulk.close()
    for item in stores:
        item.wait()
    wire.finish()


def middle_stage(back, proj, centre, dy, vec, active, proj_t, unit, slope):
    count = lax.axis_size("seq")
    tensor = lax.axis_size("tensor")
    part, full = centre.shape
    vmem = pl.BlockSpec(memory_space=pltpu.VMEM)
    hbm = pl.BlockSpec(memory_space=pl.ANY)
    feed = jax.ShapeDtypeStruct((active.shape[0], proj_t.shape[0]), LOW)
    fc_grad = jax.ShapeDtypeStruct((unit.shape[1], slope.shape[1]), LOW)
    copies = 2 * count + 12
    return pl.pallas_call(
        partial(middle_kernel, count),
        out_shape=[
            jax.ShapeDtypeStruct((proj.shape[1], 2 * proj.shape[2]), F32),
            jax.ShapeDtypeStruct((part, full), F32),
            jax.ShapeDtypeStruct((tensor, part, full), LOW),
            jax.ShapeDtypeStruct((3, 16, full), F32),
            feed,
            fc_grad,
        ],
        in_specs=[vmem] * 5 + [hbm] * 4,
        out_specs=[vmem] * 4 + [hbm] * 2,
        scratch_shapes=row_sum_scratch(back)
        + seq_sum_scratch(proj)
        + [pltpu.VMEM(array.shape, LOW) for array in (active, proj_t, unit, slope, feed, fc_grad)]
        + sem_scratch(copies)
        + [pltpu.SemaphoreType.DMA((6,))],
        compiler_params=pltpu.CompilerParams(
            collective_id=2, has_side_effects=True, vmem_limit_bytes=60 << 20
        ),
        name="middle",
    )(back, proj, centre, dy, vec, active, proj_t, unit, slope)


def back_kernel(count, *refs):
    feed, fc, out, q_in, kv_in, mq_in, mk_in, mixed, lse, grad_o_in, centre, vec = refs[:12]
    fc_sum, out_sum, dq, dkv, result = refs[12:17]
    row_refs, seq_refs, out_refs, kv_refs = refs[17:22], refs[22:25], refs[25:28], refs[28:31]
    kv_send, kv_got, kv_part, kv_total, kv_acc, delta, acc, send_sem, recv_sem = refs[31:]
    index, place = lax.axis_index("seq"), lax.axis_index("tensor")
    core = lax.rem(place, 2)
    other_core = {"tensor": flip(place, 1)}
    along = seq_peers(index, count)
    lines = count // 2
    greet(along + [other_core, {"tensor": flip(place, 2)}])
    wire = Wire(send_sem, recv_sem)
    reduce = RowSum(wire, place, along[0], feed, *row_refs)
    bulk = SeqSum(wire, index, along, fc, *seq_refs, fc_sum, True)
    out_bulk = SeqSum(wire, index, along, out, *out_refs, out_sum, False)
    keys_sum = SeqSum(wire, index, along, kv_part, *kv_refs, kv_total, False)
    gather = RowGather(wire, place, result)
    hd = kv_in.shape[-1] // 2
    heads = q_in.shape[-1] // hd
    scale = float(hd) ** (-0.5)
    scale_two = scale * LOG2E
    near_x = 1 - lax.rem(index, 2)

    def open_batch(batch):
        acc[...] = jnp.zeros_like(acc)
        for head in range(heads):
            cols = slice(head * hd, (head + 1) * hd)
            product = grad_o_in[batch, :, cols].astype(F32) * mixed[batch, :, cols].astype(F32)
            delta[head] = jnp.sum(product, axis=-1, keepdims=True)

    def blocks_of(batch, which, target, extra):
        def body(line, carry):
            block = 2 * line + which
            mask = visible(mq_in[batch], mk_in[batch, block])
            keys = kv_in[batch, block, :, :hd]
            values = kv_in[batch, block, :, hd:]
            kv_acc[...] = jnp.zeros_like(kv_acc)

            def one_head(head, inner):
                cols = pl.ds(pl.multiple_of(head * hd, hd), hd)
                query = q_in[batch, :, cols]
                grad_o = grad_o_in[batch, :, cols]
                scores = dot_nt(query, keys) * scale_two
                probs = jnp.where(mask, jnp.exp2(scores - lse[batch, head]), 0.0)
                grad_p = dot_nt(grad_o, values)
                grad_s = (probs * (grad_p - delta[head])).astype(LOW)
                acc[:, cols] += dot(grad_s, keys)
                kv_acc[:, :hd] += dot_tn(grad_s, query)
                kv_acc[:, hd:] += dot_tn(probs.astype(LOW), grad_o)
                return inner

            lax.fori_loop(0, heads, one_head, 0)
            grad_k = kv_acc[:, :hd] * scale
            grad_v = kv_acc[:, hd:]
            if extra is not None:
                grad_k = grad_k + extra[block, :, :hd].astype(F32)
                grad_v = grad_v + extra[block, :, hd:].astype(F32)
            target[block, :, :hd] = grad_k.astype(LOW)
            target[block, :, hd:] = grad_v.astype(LOW)
            return carry

        lax.fori_loop(0, lines, body, 0)

    def close_batch(batch):
        dq[batch] = (acc[...] * scale).astype(LOW)

    def to_core(which):
        return [
            wire.copy(kv_send.at[2 * line + which], kv_got.at[2 * line + which], other_core)
            for line in range(lines)
        ]

    reduce.start()
    middle, edge = turns(lines)[: lines // 2], turns(lines)[lines // 2 :]
    bulk.start(middle)
    out_bulk.start(middle)
    bulk.start(edge)
    out_bulk.start(edge)
    open_batch(1 - core)
    blocks_of(1 - core, near_x, kv_send, None)
    near_handles = to_core(near_x)
    reduce.to_side(1)
    reduce.to_side(0)
    bulk.relay(lines // 4)
    blocks_of(1 - core, 1 - near_x, kv_send, None)
    own_handles = to_core(1 - near_x)
    close_batch(1 - core)
    bulk.relay(lines // 2 - lines // 4)
    for handle in near_handles:
        wire.arrived(handle)
    open_batch(core)
    blocks_of(core, near_x, kv_part, kv_got)
    keys_sum.start()
    bulk.start([0])
    out_bulk.start([0])
    reduce.to_pair()
    out_bulk.relay(lines // 2)
    for handle in own_handles:
        wire.arrived(handle)
    blocks_of(core, 1 - near_x, kv_part, kv_got)
    close_batch(core)
    bulk.relay(len(edge))
    out_bulk.relay(len(edge))
    reduce.ready()
    bias = vec[0:1, :]

    def body(at):
        total = centre[at, :] + reduce.total(at) + bias
        result[place, at, :] = total.astype(LOW)

    by_rows(centre.shape[0], 16, body)
    gather.start()
    keys_sum.relay(lines - 1)
    gather.forward()
    keys_sum.close()
    dkv[1 - core] = jnp.zeros(dkv.shape[1:], LOW)
    dkv[core] = kv_total[...].astype(LOW)
    bulk.close()
    out_bulk.close()
    wire.finish()


def back_stage(feed, fc, out, queries, keyval, meta_q, meta_k, mixed, lse, grad_mixed, centre, vec):
    count = lax.axis_size("seq")
    tensor = lax.axis_size("tensor")
    part, full = centre.shape
    batches, rows, width = queries.shape
    blocks, two = keyval.shape[1], keyval.shape[3]
    heads = 2 * width // two
    vmem = pl.BlockSpec(memory_space=pltpu.VMEM)
    kv_part = jax.ShapeDtypeStruct((blocks, rows, two), LOW)
    copies = 4 * count + 14
    return pl.pallas_call(
        partial(back_kernel, count),
        out_shape=[
            jax.ShapeDtypeStruct((fc.shape[1], 2 * fc.shape[2]), F32),
            jax.ShapeDtypeStruct(out.shape[1:], F32),
            jax.ShapeDtypeStruct((batches, rows, width), LOW),
            jax.ShapeDtypeStruct((batches, rows, two), LOW),
            jax.ShapeDtypeStruct((tensor, part, full), LOW),
        ],
        in_specs=[vmem] * 12,
        out_specs=[vmem] * 5,
        scratch_shapes=row_sum_scratch(feed)
        + seq_sum_scratch(fc)
        + seq_sum_scratch(out)
        + seq_sum_scratch(kv_part)
        + [pltpu.VMEM(kv_part.shape, LOW)] * 3
        + [
            pltpu.VMEM((rows, two), F32),
            pltpu.VMEM((rows, two), F32),
            pltpu.VMEM((heads, rows, 1), F32),
            pltpu.VMEM((rows, width), F32),
        ]
        + sem_scratch(copies),
        compiler_params=pltpu.CompilerParams(
            collective_id=3, has_side_effects=True, vmem_limit_bytes=60 << 20
        ),
        name="back",
    )(feed, fc, out, queries, keyval, meta_q, meta_k, mixed, lse, grad_mixed, centre, vec)


def last_kernel(count, *refs):
    back, query, keyval, small, own, dy, vec = refs[:7]
    query_sum, keyval_sum, rows, small_sum = refs[7:11]
    row_refs, key_row_refs = refs[11:14], refs[14:17]
    query_refs, key_refs, small_refs = refs[17:20], refs[20:23], refs[23:26]
    key_part, small_part, small_own, small_got, sums, send_sem, recv_sem = refs[26:]
    index, place = lax.axis_index("seq"), lax.axis_index("tensor")
    along = seq_peers(index, count)
    other_core, other_side = {"tensor": flip(place, 1)}, {"tensor": flip(place, 2)}
    greet(along + [other_core, other_side])
    wire = Wire(send_sem, recv_sem)
    reduce = RowSum(wire, place, None, back, *row_refs, None, None)
    key_reduce = RowSum(wire, place, None, keyval, *key_row_refs, None, None)
    query_bulk = SeqSum(wire, index, along, query, *query_refs, query_sum, False)
    key_bulk = SeqSum(wire, index, along, key_part, *key_refs, keyval_sum, False)
    small_bulk = SeqSum(wire, index, along, small_part, *small_refs, small_own.at[0], False)
    gather = RowGather(wire, place, rows)
    spread = count // 2 - 1
    reduce.start()
    query_bulk.start()
    key_reduce.start()
    reduce.to_side(0)
    key_reduce.to_side(0)
    query_bulk.relay(spread // 3)
    reduce.ready()
    sums[...] = jnp.zeros_like(sums)
    gain = vec[0:1, :]

    def body(at):
        over = reduce.total(at)
        inner, product = norm_back(own[at, :].astype(F32), gain, over)
        rows[place, at, :] = (dy[at, :] + inner).astype(LOW)
        sums[0] += product
        sums[1] += over

    by_rows(own.shape[0], 16, body)
    gather.start()
    small_part[...] = small[...]
    width = own.shape[1] // count
    for row in range(2):
        line = jnp.sum(sums[row], axis=0, keepdims=True)
        for block in range(count):
            part = line[:, block * width : (block + 1) * width]
            small_part[block, row : row + 1, 0:width] = part
    small_bulk.start()
    key_reduce.ready()
    step = key_part.shape[1]
    for block in range(count):
        key_part[block] = key_reduce.total(slice(block * step, (block + 1) * step)).astype(LOW)
    key_bulk.start()
    query_bulk.relay(spread // 3)
    gather.forward()
    small_bulk.relay(spread)
    query_bulk.relay(spread - 2 * (spread // 3))
    key_bulk.relay(spread)
    small_bulk.close()
    for turn, peer in enumerate((other_core, other_side)):
        handle = wire.copy(small_own.at[turn], small_got.at[turn], peer)
        wire.arrived(handle)
        total = small_own[turn] + small_got[turn]
        if turn:
            small_sum[...] = total
        else:
            small_own[1] = total
    query_bulk.close()
    key_bulk.close()
    wire.finish()


def last_stage(back, query, keyval, small, own, dy, vec):
    count = lax.axis_size("seq")
    tensor = lax.axis_size("tensor")
    part, full = own.shape
    vmem = pl.BlockSpec(memory_space=pltpu.VMEM)
    key_part = jax.ShapeDtypeStruct((count, keyval.shape[2] // count, keyval.shape[3]), LOW)
    copies = 3 * count + 12
    return pl.pallas_call(
        partial(last_kernel, count),
        out_shape=[
            jax.ShapeDtypeStruct(query.shape[1:], F32),
            jax.ShapeDtypeStruct(key_part.shape[1:], F32),
            jax.ShapeDtypeStruct((tensor, part, full), LOW),
            jax.ShapeDtypeStruct(small.shape[1:], F32),
        ],
        in_specs=[vmem] * 7,
        out_specs=[vmem] * 4,
        scratch_shapes=row_sum_scratch(back)
        + row_sum_scratch(keyval)
        + seq_sum_scratch(query)
        + seq_sum_scratch(key_part)
        + seq_sum_scratch(small, F32)
        + [
            pltpu.VMEM(key_part.shape, LOW),
            pltpu.VMEM(small.shape, F32),
            pltpu.VMEM((2,) + small.shape[1:], F32),
            pltpu.VMEM((2,) + small.shape[1:], F32),
            pltpu.VMEM((2, 16, full), F32),
        ]
        + sem_scratch(copies),
        compiler_params=pltpu.CompilerParams(
            collective_id=4, has_side_effects=True, vmem_limit_bytes=60 << 20
        ),
        name="last",
    )(back, query, keyval, small, own, dy, vec)


def visible(meta_q, meta_k):
    seg_q, pos_q = meta_q[:, 0:1], meta_q[:, 1:2]
    seg_k, pos_k = meta_k[0:1, :], meta_k[1:2, :]
    return ((seg_k == 0) | (seg_k == seg_q)) & (pos_k <= pos_q)


def norm_parts(values):
    average = jnp.mean(values, axis=-1, keepdims=True)
    centred = values - average
    spread = jnp.mean(centred * centred, axis=-1, keepdims=True)
    return centred, lax.rsqrt(spread + EPS)


def norm_back(values, gain, grad):
    centred, inverse = norm_parts(values)
    unit = centred * inverse
    scaled = grad * gain
    inner = (
        scaled
        - jnp.mean(scaled, axis=-1, keepdims=True)
        - unit * jnp.mean(scaled * unit, axis=-1, keepdims=True)
    )
    return inverse * inner, grad * unit


def gelu_pair(values):
    const = 0.7978845608028654
    square = values * values
    inner = jnp.tanh(const * (values + 0.044715 * (values * square)))
    half = 0.5 * (1.0 + inner)
    slope = half + 0.5 * values * (1.0 - inner * inner) * const * (1.0 + 3 * 0.044715 * square)
    return values * half, slope


def local(
    inputs,
    segment,
    position,
    w_query,
    w_keyval,
    w_out,
    w_fc,
    w_proj,
    vectors,
    fc_bias,
    value_bias,
    grad_out,
):
    seq_size, tensor_size = lax.axis_size("seq"), lax.axis_size("tensor")
    seq_index, tensor_index = lax.axis_index("seq"), lax.axis_index("tensor")
    batches, rows, full_width = inputs.shape
    width_block = w_query.shape[0]
    group_width = w_query.shape[1]
    hidden_width = w_fc.shape[1]
    unit_width = hidden_width // 2
    unit_half = (seq_index >> 1) & 1
    hd = value_bias.shape[0]
    quarter = rows // tensor_size
    shard = vectors.shape[1]
    bias_shard = fc_bias.shape[0]

    pieces = [
        vectors.reshape(-1).astype(LOW),
        fc_bias.astype(LOW),
        segment.reshape(-1).astype(LOW),
        (position // 128).reshape(-1).astype(LOW),
        (position % 128).reshape(-1).astype(LOW),
    ]
    cuts = [0]
    for piece in pieces:
        cuts.append(cuts[-1] + piece.shape[0])
    packed = jnp.concatenate(pieces)
    packed = jnp.pad(packed, (0, -packed.shape[0] % 2048)).reshape(-1, 128)

    def halves(array):
        return jnp.swapaxes(array.astype(LOW).reshape(width_block, 2, unit_width), 0, 1)

    small, kv_mat, q_mat = gather_first(packed, w_keyval.astype(LOW), w_query.astype(LOW))
    kv_mat = kv_mat.reshape(full_width, 2 * hd)
    q_mat = q_mat.reshape(full_width, group_width)

    small = small.reshape(seq_size, tensor_size, -1).astype(F32)
    vec_all = small[:, :, cuts[0] : cuts[1]].reshape(seq_size * tensor_size, 7, shard)
    vec_all = jnp.swapaxes(vec_all, 0, 1).reshape(7, full_width)
    fc_all = small[:, :, cuts[1] : cuts[2]].reshape(-1)
    seg_keys = small[:, 0, cuts[2] : cuts[3]].reshape(seq_size, batches, rows)
    pos_keys = 128.0 * small[:, 0, cuts[3] : cuts[4]] + small[:, 0, cuts[4] : cuts[5]]
    seg_keys = jnp.swapaxes(seg_keys, 0, 1).astype(jnp.int32)
    pos_keys = jnp.swapaxes(pos_keys.reshape(seq_size, batches, rows), 0, 1).astype(jnp.int32)
    meta_k = jnp.pad(jnp.stack([seg_keys, pos_keys], axis=2), ((0, 0), (0, 0), (0, 6), (0, 0)))
    meta_q = jnp.pad(jnp.stack([segment, position], axis=2), ((0, 0), (0, 0), (0, 126)))

    gain_one, shift_one, _, out_bias, gain_two, shift_two, proj_bias = [
        vec_all[i] for i in range(7)
    ]
    query_bias = lax.dynamic_slice_in_dim(vec_all[2], tensor_index * group_width, group_width, 0)
    fc_local = lax.dynamic_slice_in_dim(
        fc_all, tensor_index * hidden_width + unit_half * unit_width, unit_width, 0
    )
    bias_value = value_bias.astype(LOW).astype(F32)
    kv_bias = jnp.concatenate([jnp.zeros((hd,), F32), bias_value])

    residual = inputs.astype(F32)
    centred, inverse = norm_parts(residual)
    normed = (centred * inverse * gain_one + shift_one).astype(LOW).reshape(-1, full_width)
    keyval = (dot(normed, kv_mat) + kv_bias).astype(LOW).reshape(batches, rows, 2 * hd)
    queries = (dot(normed, q_mat) + query_bias).astype(LOW)
    queries = queries.reshape(batches, rows, group_width)

    def by_quarter(array):
        split = array.reshape(batches, tensor_size, quarter, array.shape[-1])
        return jnp.swapaxes(split, 0, 1).reshape(tensor_size, batches * quarter, -1)

    def by_batch(array):
        split = array.reshape(tensor_size, batches, quarter, array.shape[-1])
        return jnp.swapaxes(split, 0, 1).reshape(batches, rows, -1)

    def my_quarter(array):
        split = array.reshape(batches, tensor_size, quarter, full_width)
        own = lax.dynamic_index_in_dim(split, tensor_index, 1, keepdims=False)
        return own.reshape(batches * quarter, full_width)

    vecs = jnp.pad(jnp.stack([out_bias, gain_two, shift_two]), ((0, 5), (0, 0)))
    grad_split = by_quarter(grad_out)
    mixed, lse, kv_all, out_t, middle, rows_two, fc_mat, proj_t, grad_other = front(
        queries,
        keyval,
        meta_q,
        meta_k,
        my_quarter(inputs),
        vecs,
        w_out.T.astype(LOW),
        halves(w_fc),
        halves(w_proj.T),
        grad_split,
    )
    out_t = out_t.reshape(full_width, group_width)
    fc_mat = fc_mat.reshape(full_width, unit_width)
    proj_t = proj_t.reshape(full_width, unit_width)
    mixed_rows = by_quarter(mixed).reshape(-1, group_width)
    normed_two = rows_two.reshape(-1, full_width)
    hidden = dot(normed_two, fc_mat) + fc_local
    active_f, slope = gelu_pair(hidden)
    active = active_f.astype(LOW)

    grad_q_low = my_quarter(grad_out)
    grad_flat = jnp.concatenate([grad_split, grad_other]).reshape(-1, full_width)
    grad_hidden = (slope * dot(grad_flat, proj_t)).astype(LOW)
    fcbias_local = jnp.sum(grad_hidden.astype(F32), axis=0)
    back_part = dot_nt(grad_hidden, fc_mat).astype(LOW)
    back_part = back_part.reshape(2, tensor_size, batches * quarter, full_width)

    def blocked(array):
        return array.astype(LOW).reshape(seq_size, width_block, array.shape[-1])

    proj_sum, grad_middle, rows_middle, sums, feed_part, fc_part = middle_stage(
        back_part,
        blocked(dot_tn(grad_flat, active)),
        middle,
        grad_q_low,
        jnp.pad(gain_two[None], ((0, 7), (0, 0))),
        active,
        proj_t,
        normed_two,
        grad_hidden,
    )
    grad_gain_two, grad_shift_two, grad_out_bias = jnp.sum(sums, axis=1)
    grad_proj_bias = jnp.sum(grad_q_low.astype(F32), axis=0)
    grad_middle_low = rows_middle.reshape(-1, full_width)
    def one_row(row):
        return jnp.pad(row[None], ((0, 7), (0, 0)))

    grad_mixed = by_batch(dot(grad_middle_low, out_t).astype(LOW))
    fc_sum, out_sum, grad_queries, grad_keyval, result_rows = back_stage(
        feed_part.reshape(2, tensor_size, batches * quarter, full_width),
        blocked(fc_part),
        blocked(dot_tn(grad_middle_low, mixed_rows)),
        queries,
        kv_all,
        meta_q,
        meta_k,
        mixed,
        lse,
        grad_mixed,
        middle,
        one_row(proj_bias),
    )
    result = by_batch(result_rows)
    grad_keyval = grad_keyval.reshape(-1, 2 * hd)
    grad_queries = grad_queries.reshape(-1, group_width)
    grad_normed = dot_nt(grad_queries, q_mat) + dot_nt(grad_keyval, kv_mat)
    qbias_local = jnp.sum(grad_queries.astype(F32), axis=0)
    vbias_local = jnp.sum(grad_keyval[:, hd:].astype(F32), axis=0)

    qbias_full = lax.dynamic_update_slice_in_dim(
        jnp.zeros((full_width,), F32), qbias_local, tensor_index * group_width, 0
    )
    full_hidden = bias_shard * seq_size * tensor_size
    fcbias_full = lax.dynamic_update_slice_in_dim(
        jnp.zeros((full_hidden,), F32),
        fcbias_local,
        tensor_index * hidden_width + unit_half * unit_width,
        0,
    )
    chunk = full_hidden // seq_size
    blank = jnp.zeros((full_width,), F32)
    vec_grads = jnp.stack(
        [blank, blank, qbias_full, grad_out_bias, grad_gain_two, grad_shift_two, grad_proj_bias]
    )

    def in_rows(array):
        array = jnp.pad(array, ((0, 0), (0, -array.shape[1] % width_block)))
        return array.reshape(seq_size, -1, width_block)

    vec_rows = 7
    bias_rows = chunk // width_block
    small_rows = jnp.concatenate(
        [
            jnp.swapaxes(vec_grads.reshape(7, seq_size, width_block), 0, 1),
            in_rows(fcbias_full.reshape(seq_size, chunk)),
            in_rows(jnp.broadcast_to(vbias_local, (seq_size, hd))),
        ],
        axis=1,
    )
    small_rows = jnp.pad(
        small_rows,
        ((0, 0), (0, -small_rows.shape[1] % 8), (0, -width_block % 128)),
    )
    key_grad = dot_tn(normed, grad_keyval).astype(LOW)
    key_grad = key_grad.reshape(seq_size, tensor_size, -1, 2 * hd)
    key_grad = jnp.swapaxes(key_grad, 0, 1).reshape(1, tensor_size, -1, 2 * hd)
    query_sum, keyval_grad, input_rows, small_sum = last_stage(
        by_quarter(grad_normed.astype(LOW))[None],
        blocked(dot_tn(normed, grad_queries)),
        key_grad,
        small_rows,
        my_quarter(inputs),
        grad_middle,
        one_row(gain_one),
    )
    input_grad = by_batch(input_rows)
    small_sum = small_sum[:, :width_block]
    vec_grad = lax.dynamic_slice_in_dim(small_sum[:vec_rows], tensor_index * shard, shard, 1)
    fcbias_grad = lax.dynamic_slice_in_dim(
        small_sum[vec_rows : vec_rows + bias_rows].reshape(-1),
        tensor_index * bias_shard,
        bias_shard,
        0,
    )
    vbias_grad = small_sum[vec_rows + bias_rows :].reshape(-1)[:hd]
    return (
        result,
        input_grad,
        query_sum,
        keyval_grad,
        out_sum.T,
        fc_sum,
        proj_sum.T,
        vec_grad,
        fcbias_grad,
        vbias_grad,
        vec_grad[5],
    )


def solution(mesh):
    in_specs = (
        P(None, "seq", None),
        P(None, "seq"),
        P(None, "seq"),
        P("seq", "tensor"),
        P(("seq", "tensor"), None),
        P("tensor", "seq"),
        P("seq", "tensor"),
        P("tensor", "seq"),
        P(None, ("seq", "tensor")),
        P(("seq", "tensor")),
        P(),
        P(None, "seq", None),
    )
    out_specs = (
        P(None, "seq", None),
        P(None, "seq", None),
        P("seq", "tensor"),
        P(("seq", "tensor"), None),
        P("tensor", "seq"),
        P("seq", "tensor"),
        P("tensor", "seq"),
        P(None, ("seq", "tensor")),
        P(("seq", "tensor")),
        P(),
        P(("seq", "tensor")),
    )
    return jax.shard_map(local, mesh=mesh, in_specs=in_specs, out_specs=out_specs, check_vma=False)
```

```python
from functools import partial

import jax
import jax.numpy as jnp
from jax import lax
from jax.experimental import pallas as pl
from jax.experimental.pallas import tpu as pltpu
from jax.sharding import PartitionSpec as P

EPS = 1e-05
NEG = -1e30
LOG2E = 1.4426950408889634
LOW = jnp.bfloat16
F32 = jnp.float32


def bits_of(count):
    return count.bit_length() - 1


def swap(value, axis, bit):
    count = lax.axis_size(axis)
    return lax.ppermute(value, axis, [(i, i ^ (1 << bit)) for i in range(count)])


def after(value, *others):
    return lax.optimization_barrier((value,) + others)[0]


def dot(left, right):
    return jnp.dot(left, right, preferred_element_type=F32)


def dot_tn(left, right):
    return lax.dot_general(left, right, (((0,), (0,)), ((), ())), preferred_element_type=F32)


def dot_nt(left, right):
    return lax.dot_general(left, right, (((1,), (1,)), ((), ())), preferred_element_type=F32)


MESH = pl.DeviceIdType.MESH


def flip(index, mask):
    bit = 1
    out = index
    while bit <= mask:
        if mask & bit:
            out = out + bit * (1 - 2 * lax.rem(lax.div(index, bit), 2))
        bit *= 2
    return out


class Wire:
    def __init__(self, send_sem, recv_sem, local_sem=None):
        self.send_sem, self.recv_sem, self.local_sem = send_sem, recv_sem, local_sem
        self.loads = []
        self.started = []
        self.landed = set()

    def copy(self, src, dst, peer):
        place = len(self.started)
        item = pltpu.make_async_remote_copy(
            src_ref=src,
            dst_ref=dst,
            send_sem=self.send_sem.at[place],
            recv_sem=self.recv_sem.at[place],
            device_id=peer,
            device_id_type=MESH,
        )
        item.start()
        self.started.append(item)
        return place

    def load(self, src, dst):
        item = pltpu.make_async_copy(src, dst, self.local_sem.at[len(self.loads)])
        item.start()
        self.loads.append(item)
        return item

    def arrived(self, place):
        if place not in self.landed:
            self.landed.add(place)
            self.started[place].wait_recv()

    def finish(self):
        for place in range(len(self.started)):
            self.arrived(place)
        for item in self.started:
            item.wait_send()


def greet(peers):
    barrier = pltpu.get_barrier_semaphore()
    for peer in peers:
        pl.semaphore_signal(barrier, inc=1, device_id=peer, device_id_type=MESH)
    pl.semaphore_wait(barrier, len(peers))


def seq_peers(index, count):
    return [{"seq": flip(index, 2 * d)} for d in range(1, count // 2)] + [
        {"seq": flip(index, 1)}
    ]


def turns(lines):
    return list(range(lines // 2, lines)) + list(range(1, lines // 2))


def first_kernel(count, tensor, *refs):
    ins, outs = refs[:3], refs[3:6]
    send_sem, recv_sem, local_sem = refs[6:]
    index = lax.axis_index("seq")
    place = lax.axis_index("tensor")
    across = [{"tensor": flip(place, tensor >> (i + 1))} for i in range(bits_of(tensor))]
    along = seq_peers(index, count)
    far, near = along[:-1], along[-1]
    greet(across + along)
    wire = Wire(send_sem, recv_sem)
    own = []
    targets = [(lambda at, out=out: out.at[at, place]) for out in outs[:2]]
    targets.append(lambda at: outs[2].at[at])
    handles = []
    for source, target in zip(ins, targets):
        handles.append({d: wire.copy(source, target(index), far[d - 1]) for d in range(1, count // 2)})
        handles[-1][0] = wire.copy(source, target(index), near)
        item = pltpu.make_async_copy(source, target(index), local_sem.at[len(own)])
        item.start()
        own.append(item)
    relays = [[], [], []]
    order = list(range(1, count // 2))

    def relay(a, d):
        wire.arrived(handles[a][d])
        block = targets[a](flip(index, 2 * d))
        relays[a].append(wire.copy(block, block, near))

    for d in order:
        relay(0, d)
        relay(1, d)
    cut = len(order) // 3
    for d in order[:cut]:
        relay(2, d)
    for handle in [handles[0][0], handles[1][0]] + relays[0] + relays[1]:
        wire.arrived(handle)
    own[0].wait()
    own[1].wait()
    masks = [0]
    for i, peer in enumerate(across):
        step = tensor >> (i + 1)
        sent = [
            wire.copy(out.at[:, flip(place, mask)], out.at[:, flip(place, mask)], peer)
            for mask in masks
            for out in outs[:2]
        ]
        masks = masks + [mask | step for mask in masks]
        for d in order[cut:] if i == 0 else []:
            relay(2, d)
        if i + 1 < len(across):
            for handle in sent:
                wire.arrived(handle)
    own[2].wait()
    wire.finish()


def gather_first(small, keyval, query):
    count, tensor = lax.axis_size("seq"), lax.axis_size("tensor")
    arrays = (small, keyval, query)
    shapes = [
        (count, tensor) + small.shape,
        (count, tensor) + keyval.shape,
        (count,) + query.shape,
    ]
    copies = 3 * (count - 1) + 2 * (tensor - 1)
    return pl.pallas_call(
        partial(first_kernel, count, tensor),
        out_shape=[jax.ShapeDtypeStruct(shape, LOW) for shape in shapes],
        in_specs=[pl.BlockSpec(memory_space=pltpu.VMEM)] * 3,
        out_specs=[pl.BlockSpec(memory_space=pltpu.VMEM)] * 3,
        scratch_shapes=[
            pltpu.SemaphoreType.DMA((copies,)),
            pltpu.SemaphoreType.DMA((copies,)),
            pltpu.SemaphoreType.DMA((3,)),
        ],
        compiler_params=pltpu.CompilerParams(collective_id=0, has_side_effects=True),
        name="gather_first",
    )(*arrays)


def front_kernel(count, *refs):
    q_in, kv_in, mq_in, mk_in, x_in, vec_in, o_in, fc_in, pj_in, dy_in = refs[:10]
    mixed, lse, kv_all, out_t, middle, rows_two, fc_out, pj_out, dy_out = refs[10:19]
    (
        top,
        total,
        acc,
        core_keep,
        core_send,
        core_got,
        y_send,
        y_got,
        send_sem,
        recv_sem,
        local_sem,
    ) = refs[19:]
    index = lax.axis_index("seq")
    place = lax.axis_index("tensor")
    core = lax.rem(place, 2)
    side = lax.div(place, 2)
    half = lax.rem(lax.div(index, 2), 2)
    other_core = {"tensor": flip(place, 1)}
    other_side = {"tensor": flip(place, 2)}
    along = seq_peers(index, count)
    far, near = along[:-1], along[-1]
    pair = far[0]
    lines = count // 2
    greet(along + [other_core, other_side])
    wire = Wire(send_sem, recv_sem)
    own = []

    def keep(src, dst):
        item = pltpu.make_async_copy(src, dst, local_sem.at[len(own)])
        item.start()
        own.append(item)

    order = range(1, lines)
    kv_far = {d: wire.copy(kv_in.at[core], kv_all.at[core, index], far[d - 1]) for d in order}
    kv_near = wire.copy(kv_in.at[core], kv_all.at[core, index], near)
    for batch in range(2):
        keep(kv_in.at[batch], kv_all.at[batch, index])
    o_far = {d: wire.copy(o_in, out_t.at[index], far[d - 1]) for d in order}
    o_near = [wire.copy(o_in, out_t.at[index], near)]
    keep(o_in, out_t.at[index])
    dy_pair = wire.copy(dy_in.at[place], dy_out.at[place], pair)

    def send_far(source, out, which=order):
        return {
            d: wire.copy(source.at[flip(half, d & 1)], out.at[index], far[d - 1]) for d in which
        }

    fc_far = send_far(fc_in, fc_out)
    kv_near = [(1, kv_near)]
    kv_core = []
    for d in order:
        wire.arrived(kv_far[d])
        block = kv_all.at[core, flip(index, 2 * d)]
        kv_near.append((2 * d + 1, wire.copy(block, block, near)))
        kv_core.append(wire.copy(block, block, other_core))
    wire.copy(fc_in.at[half], fc_out.at[index], near)
    wire.copy(pj_in.at[half], pj_out.at[index], near)
    keep(fc_in.at[half], fc_out.at[index])
    keep(pj_in.at[half], pj_out.at[index])
    for r, handle in kv_near:
        wire.arrived(handle)
        block = kv_all.at[core, flip(index, r)]
        kv_core.append(wire.copy(block, block, other_core))
    own[0].wait()
    own[1].wait()

    jobs = [(o_far, out_t, d) for d in order]
    jobs += [(fc_far, fc_out, d) for d in order]

    def tick(number):
        for _ in range(min(number, len(jobs))):
            handles, out, d = jobs.pop(0)
            wire.arrived(handles[d])
            block = out.at[flip(index, 2 * d)]
            handle = wire.copy(block, block, near)
            if out is out_t:
                o_near.append(handle)

    hd = kv_in.shape[-1] // 2
    heads = q_in.shape[-1] // hd
    scale = float(hd) ** (-0.5) * LOG2E

    def attend(batch, block):
        mask = visible(mq_in[batch], mk_in[batch, block])
        keys = kv_all[batch, block, :, :hd]
        values = kv_all[batch, block, :, hd:]
        for head in range(heads):
            cols = slice(head * hd, (head + 1) * hd)
            scores = jnp.where(mask, dot_nt(q_in[batch, :, cols], keys) * scale, NEG)
            before = top[head]
            now = jnp.maximum(before, jnp.max(scores, axis=-1, keepdims=True))
            shrink = jnp.exp2(before - now)
            probs = jnp.exp2(scores - now)
            total[head] = total[head] * shrink + jnp.sum(probs, axis=-1, keepdims=True)
            acc[:, cols] = acc[:, cols] * shrink + dot(probs.astype(LOW), values)
            top[head] = now

    def attend_batch(batch, ticks):
        top[...] = jnp.full_like(top, NEG)
        total[...] = jnp.zeros_like(total)
        acc[...] = jnp.zeros_like(acc)

        def block_body(block, carry):
            attend(batch, block)
            return carry

        parts = len(ticks)
        for i in range(parts):
            lax.fori_loop(i * count // parts, (i + 1) * count // parts, block_body, 0)
            tick(ticks[i])
        for head in range(heads):
            cols = slice(head * hd, (head + 1) * hd)
            mixed[batch, :, cols] = (acc[:, cols] / total[head]).astype(LOW)
            lse[batch, head] = top[head] + jnp.log2(total[head])

    spread = lines - 1
    attend_batch(core, [spread])
    pj_far = send_far(pj_in, pj_out, order[:1])
    wire.arrived(dy_pair)
    dy_side = wire.copy(dy_out.at[place], dy_out.at[place], other_side)
    wire.copy(dy_out.at[place], dy_out.at[place], other_core)
    for handle in kv_core:
        wire.arrived(handle)
    attend_batch(1 - core, [spread // 3])
    wire.arrived(dy_side)
    block = dy_out.at[flip(place, 2)]
    wire.copy(block, block, other_core)

    quarter = x_in.shape[0] // 2
    for handle in o_near:
        wire.arrived(handle)
    own[2].wait()
    width = out_t.shape[1]
    group = max(1, 256 // width)
    for which, target in ((1 - core, core_send), (core, core_keep)):
        rows = [
            mixed[batch, pl.ds(pl.multiple_of((2 * s + which) * quarter, quarter), quarter), :]
            for s in range(2)
            for batch in range(2)
        ]
        rows = jnp.concatenate(rows, axis=0)

        def project(i, carry, rows=rows, target=target):
            cols = pl.ds(pl.multiple_of(i * group * width, group * width), group * width)
            block = out_t[pl.ds(i * group, group)].reshape(group * width, -1)
            target[:, cols] = dot_nt(rows, block).astype(target.dtype)
            return carry

        lax.fori_loop(0, count // group, project, 0)
        if target is core_send:
            core_handle = wire.copy(core_send, core_got, other_core)
    wire.arrived(core_handle)
    part = 2 * quarter
    step = 16

    def to_side(i, carry):
        at = pl.ds(pl.multiple_of((1 - side) * part + i * step, step), step)
        y_send[pl.ds(pl.multiple_of(i * step, step), step), :] = (
            core_keep[at, :] + core_got[at, :].astype(F32)
        ).astype(LOW)
        return carry

    lax.fori_loop(0, part // step, to_side, 0)
    y_handle = wire.copy(y_send, y_got, other_side)
    tick(spread - spread // 3 - 1)
    wire.arrived(y_handle)
    out_bias, gain_two, shift_two = vec_in[0:1, :], vec_in[1:2, :], vec_in[2:3, :]

    def norm(i, carry):
        at = pl.ds(pl.multiple_of(i * step, step), step)
        far_at = pl.ds(pl.multiple_of(side * part + i * step, step), step)
        value = core_keep[far_at, :] + core_got[far_at, :].astype(F32)
        value = value + y_got[at, :].astype(F32)
        value = x_in[at, :].astype(F32) + value + out_bias
        middle[at, :] = value
        centred, inverse = norm_parts(value)
        rows_two[0, place, at, :] = (centred * inverse * gain_two + shift_two).astype(LOW)
        return carry

    lax.fori_loop(0, part // step, norm, 0)
    mine = rows_two.at[0, place]
    pair_handle = wire.copy(mine, rows_two.at[1, place], pair)
    side_handle = wire.copy(mine, mine, other_side)
    wire.copy(mine, mine, other_core)
    pj_far.update(send_far(pj_in, pj_out, order[1:]))
    tick(len(jobs))
    jobs.extend((pj_far, pj_out, d) for d in order)
    wire.arrived(pair_handle)
    theirs = rows_two.at[1, place]
    side_two = wire.copy(theirs, theirs, other_side)
    wire.copy(theirs, theirs, other_core)
    wire.arrived(side_handle)
    block = rows_two.at[0, flip(place, 2)]
    wire.copy(block, block, other_core)
    wire.arrived(side_two)
    block = rows_two.at[1, flip(place, 2)]
    wire.copy(block, block, other_core)
    tick(len(jobs))
    for item in own[3:]:
        item.wait()
    wire.finish()


def front(queries, keyval, meta_q, meta_k, own_rows, vecs, out, fc, proj, grad_rows):
    count = lax.axis_size("seq")
    tensor = lax.axis_size("tensor")
    batches, rows, width = queries.shape
    two = keyval.shape[2]
    heads = 2 * width // two
    part, full = own_rows.shape
    shapes = [
        ((batches, rows, width), LOW),
        ((batches, heads, rows, 1), F32),
        ((batches, count, rows, two), LOW),
        ((count,) + out.shape, LOW),
        ((part, full), F32),
        ((2, tensor, part, full), LOW),
        ((count,) + fc.shape[1:], LOW),
        ((count,) + proj.shape[1:], LOW),
        ((tensor, part, full), LOW),
    ]
    copies = 2 * (count - 1) + 3 * (count - 1) + 4 + 2 + 7
    vmem, hbm = pl.BlockSpec(memory_space=pltpu.VMEM), pl.BlockSpec(memory_space=pl.ANY)
    return pl.pallas_call(
        partial(front_kernel, count),
        out_shape=[jax.ShapeDtypeStruct(shape, dtype) for shape, dtype in shapes],
        in_specs=[vmem] * 6 + [hbm] * 4,
        out_specs=[vmem] * 6 + [hbm] * 3,
        scratch_shapes=[
            pltpu.VMEM((heads, rows, 1), F32),
            pltpu.VMEM((heads, rows, 1), F32),
            pltpu.VMEM((rows, width), F32),
            pltpu.VMEM((2 * part, full), F32),
            pltpu.VMEM((2 * part, full), LOW),
            pltpu.VMEM((2 * part, full), LOW),
            pltpu.VMEM((part, full), LOW),
            pltpu.VMEM((part, full), LOW),
            pltpu.SemaphoreType.DMA((copies,)),
            pltpu.SemaphoreType.DMA((copies,)),
            pltpu.SemaphoreType.DMA((5,)),
        ],
        compiler_params=pltpu.CompilerParams(
            collective_id=1, has_side_effects=True, vmem_limit_bytes=56 << 20
        ),
        name="front",
    )(queries, keyval, meta_q, meta_k, own_rows, vecs, out, fc, proj, grad_rows)


def by_rows(rows, step, body):
    def run(i, carry):
        body(pl.ds(pl.multiple_of(i * step, step), step))
        return carry

    lax.fori_loop(0, rows // step, run, 0)


class SeqSum:
    def __init__(self, wire, index, peers, part, from_near, to_far, from_far, held, out, split):
        self.wire, self.index = wire, index
        self.far, self.near = peers[:-1], peers[-1]
        self.lines = len(peers)
        self.part, self.out, self.split = part, out, split
        self.from_near, self.to_far, self.from_far = from_near, to_far, from_far
        self.rows = part.shape[1]
        self.step = min(64, self.rows)
        self.near_handles, self.far_handles = {}, {}
        self.order = turns(self.lines)
        self.held, self.loads = held, {}

    def load(self):
        for d in self.order + [0]:
            block = self.part.at[flip(self.index, 2 * d)]
            self.loads[d] = self.wire.load(block, self.held.at[d])

    def mine(self, d, at):
        if self.held is None:
            return self.part[flip(self.index, 2 * d), at].astype(F32)
        return self.held[d, at].astype(F32)

    def start(self, order=None):
        for d in order or turns(self.lines) + [0]:
            block = self.part.at[flip(self.index, 2 * d + 1)]
            self.near_handles[d] = self.wire.copy(block, self.from_near.at[d], self.near)

    def relay(self, number):
        for _ in range(number):
            d = self.order.pop(0)
            self.wire.arrived(self.near_handles[d])
            if self.held is not None:
                self.loads[d].wait()

            def join(at, d=d):
                total = self.mine(d, at)
                total = total + self.from_near[d, at].astype(F32)
                self.to_far[d - 1, at] = total.astype(self.to_far.dtype)

            by_rows(self.rows, self.step, join)
            self.far_handles[d] = self.wire.copy(
                self.to_far.at[d - 1], self.from_far.at[d - 1], self.far[d - 1]
            )

    def close(self):
        self.wire.arrived(self.near_handles[0])
        if self.held is not None:
            self.loads[0].wait()
        for d in range(1, self.lines):
            self.wire.arrived(self.far_handles[d])
        width = self.part.shape[2]
        half = lax.rem(lax.div(self.index, 2), 2)

        def total(at):
            same = self.mine(0, at) + self.from_near[0, at].astype(F32)
            other = None
            for d in range(1, self.lines):
                got = self.from_far[d - 1, at].astype(F32)
                if self.split and d % 2:
                    other = got if other is None else other + got
                else:
                    same = same + got
            if self.split:
                out = self.out
                out[at, pl.ds(pl.multiple_of(half * width, width), width)] = same
                out[at, pl.ds(pl.multiple_of((1 - half) * width, width), width)] = other
            else:
                self.out[at, :] = same

        by_rows(self.rows, self.step, total)


def seq_sum_scratch(part, dtype=LOW, held=False):
    lines = part.shape[0] // 2
    depths = [lines, lines - 1, lines - 1] + [lines] * held
    return [pltpu.VMEM((depth,) + part.shape[1:], dtype) for depth in depths]


class RowSum:
    def __init__(
        self, wire, place, pair, part, core_got, y_send, y_got, pair_send, pair_got, held
    ):
        self.wire, self.place, self.pair = wire, place, pair
        self.core, self.side = lax.rem(place, 2), lax.div(place, 2)
        self.part, self.core_got, self.y_send, self.y_got = part, core_got, y_send, y_got
        self.pair_send, self.pair_got = pair_send, pair_got
        self.sides = (1 - self.side, self.side)
        self.rows = part.shape[2]
        self.core_handles, self.y_handles = {}, {}
        self.held, self.loads = held, {}

    def start(self):
        peer = {"tensor": flip(self.place, 1)}
        for which in range(2):
            for p in reversed(range(self.part.shape[0])):
                at = self.sides[which]
                block = self.part.at[p, 2 * at + 1 - self.core]
                self.core_handles[p, which] = self.wire.copy(block, self.core_got.at[p, at], peer)
        for which in range(2):
            for p in reversed(range(self.part.shape[0])):
                at = self.sides[which]
                block = self.part.at[p, 2 * at + self.core]
                self.loads[p, which] = self.wire.load(block, self.held.at[p, at])

    def settle(self, p, which):
        self.wire.arrived(self.core_handles[p, which])
        self.loads[p, which].wait()

    def both(self, p, which, at):
        side = self.sides[which]
        mine = self.held[p, side, at, :].astype(F32)
        return mine + self.core_got[p, side, at, :].astype(F32)

    def to_side(self, p):
        self.settle(p, 0)

        def body(at):
            self.y_send[p, at, :] = self.both(p, 0, at).astype(LOW)

        by_rows(self.rows, 16, body)
        peer = {"tensor": flip(self.place, 2)}
        self.y_handles[p] = self.wire.copy(self.y_send.at[p], self.y_got.at[p], peer)

    def to_pair(self):
        self.settle(1, 1)
        self.wire.arrived(self.y_handles[1])

        def body(at):
            total = self.both(1, 1, at) + self.y_got[1, at, :].astype(F32)
            self.pair_send[at, :] = total.astype(LOW)

        by_rows(self.rows, 16, body)
        self.pair_handle = self.wire.copy(self.pair_send, self.pair_got, self.pair)

    def ready(self):
        self.settle(0, 1)
        self.wire.arrived(self.y_handles[0])
        if self.pair is not None:
            self.wire.arrived(self.pair_handle)

    def total(self, at):
        total = self.both(0, 1, at) + self.y_got[0, at, :].astype(F32)
        if self.pair is not None:
            total = total + self.pair_got[at, :].astype(F32)
        return total


def row_sum_scratch(part):
    pairs, _, rows, width = part.shape
    scratch = [pltpu.VMEM((pairs, 2, rows, width), LOW)]
    scratch += [pltpu.VMEM((pairs, rows, width), LOW)] * 2
    if pairs == 2:
        scratch += [pltpu.VMEM((rows, width), LOW)] * 2
    return scratch + [pltpu.VMEM((pairs, 2, rows, width), LOW)]


class RowGather:
    def __init__(self, wire, place, rows):
        self.wire, self.place, self.rows = wire, place, rows

    def start(self):
        mine = self.rows.at[self.place]
        self.side_handle = self.wire.copy(mine, mine, {"tensor": flip(self.place, 2)})
        self.wire.copy(mine, mine, {"tensor": flip(self.place, 1)})

    def forward(self):
        self.wire.arrived(self.side_handle)
        block = self.rows.at[flip(self.place, 2)]
        self.wire.copy(block, block, {"tensor": flip(self.place, 1)})


def sem_scratch(copies):
    return [pltpu.SemaphoreType.DMA((copies,)), pltpu.SemaphoreType.DMA((copies,))]


def middle_kernel(count, *refs):
    back, proj, centre, dy, vec = refs[:5]
    sources, (feed_out, fc_out) = refs[5:9], refs[13:15]
    proj_sum, grad, rows, sums = refs[9:13]
    row_refs, seq_refs = refs[15:21], refs[21:25]
    local = refs[25:29]
    feed, fc_grad, send_sem, recv_sem, local_sem, load_sem = refs[29:]
    loads = [
        pltpu.make_async_copy(source, target, local_sem.at[i])
        for i, (source, target) in enumerate(zip(sources, local))
    ]
    active, proj_t, unit, slope = local
    stores = [
        pltpu.make_async_copy(feed, feed_out, local_sem.at[4]),
        pltpu.make_async_copy(fc_grad, fc_out, local_sem.at[5]),
    ]
    tall, wide = active.shape[0] // 2, 256
    steps = proj_t.shape[0] // wide

    def feed_rows(which):
        at = slice(which * tall, (which + 1) * tall)

        def run(i, carry):
            cols = pl.ds(pl.multiple_of(i * wide, wide), wide)
            feed[at, cols] = dot_nt(active[at, :], proj_t[cols, :]).astype(LOW)
            return carry

        lax.fori_loop(0, steps, run, 0)

    def fc_rows(which):
        half_width = slope.shape[1] // 2
        out = slice(which * half_width, (which + 1) * half_width)

        def run(i, carry):
            cols = pl.ds(pl.multiple_of(i * wide, wide), wide)
            fc_grad[cols, out] = dot_tn(unit[:, cols], slope[:, out]).astype(LOW)
            return carry

        lax.fori_loop(0, steps, run, 0)

    index, place = lax.axis_index("seq"), lax.axis_index("tensor")
    along = seq_peers(index, count)
    greet(along + [{"tensor": flip(place, 1)}, {"tensor": flip(place, 2)}])
    wire = Wire(send_sem, recv_sem, load_sem)
    reduce = RowSum(wire, place, along[0], back, *row_refs)
    bulk = SeqSum(wire, index, along, proj, *seq_refs, proj_sum, True)
    gather = RowGather(wire, place, rows)
    lines = count // 2
    reduce.start()
    bulk.start()
    bulk.load()
    for item in loads:
        item.start()
    reduce.to_side(1)
    reduce.to_side(0)
    bulk.relay(lines // 4)
    reduce.to_pair()
    bulk.relay(lines // 2 - lines // 4)
    loads[0].wait()
    loads[1].wait()
    feed_rows(0)
    reduce.ready()
    sums[...] = jnp.zeros_like(sums)
    gain = vec[0:1, :]

    def body(at):
        over = reduce.total(at)
        inner, product = norm_back(centre[at, :], gain, over)
        value = dy[at, :].astype(F32) + inner
        grad[at, :] = value
        rows[place, at, :] = value.astype(LOW)
        sums[0] += product
        sums[1] += over
        sums[2] += value

    by_rows(centre.shape[0], 16, body)
    gather.start()
    bulk.relay(lines - 1 - lines // 2)
    feed_rows(1)
    stores[0].start()
    loads[2].wait()
    loads[3].wait()
    fc_rows(0)
    gather.forward()
    fc_rows(1)
    stores[1].start()
    bulk.close()
    for item in stores:
        item.wait()
    wire.finish()


def middle_stage(back, proj, centre, dy, vec, active, proj_t, unit, slope):
    count = lax.axis_size("seq")
    tensor = lax.axis_size("tensor")
    part, full = centre.shape
    vmem = pl.BlockSpec(memory_space=pltpu.VMEM)
    hbm = pl.BlockSpec(memory_space=pl.ANY)
    feed = jax.ShapeDtypeStruct((active.shape[0], proj_t.shape[0]), LOW)
    fc_grad = jax.ShapeDtypeStruct((unit.shape[1], slope.shape[1]), LOW)
    copies = 2 * count + 12
    return pl.pallas_call(
        partial(middle_kernel, count),
        out_shape=[
            jax.ShapeDtypeStruct((proj.shape[1], 2 * proj.shape[2]), F32),
            jax.ShapeDtypeStruct((part, full), F32),
            jax.ShapeDtypeStruct((tensor, part, full), LOW),
            jax.ShapeDtypeStruct((3, 16, full), F32),
            feed,
            fc_grad,
        ],
        in_specs=[hbm] * 2 + [vmem] * 3 + [hbm] * 4,
        out_specs=[vmem] * 4 + [hbm] * 2,
        scratch_shapes=row_sum_scratch(back)
        + seq_sum_scratch(proj, held=True)
        + [pltpu.VMEM(array.shape, LOW) for array in (active, proj_t, unit, slope, feed, fc_grad)]
        + sem_scratch(copies)
        + [pltpu.SemaphoreType.DMA((6,)), pltpu.SemaphoreType.DMA((4 + count // 2,))],
        compiler_params=pltpu.CompilerParams(
            collective_id=2, has_side_effects=True, vmem_limit_bytes=60 << 20
        ),
        name="middle",
    )(back, proj, centre, dy, vec, active, proj_t, unit, slope)


def back_kernel(count, *refs):
    feed, fc, out, q_in, kv_in, mq_in, mk_in, mixed, lse, grad_o_in, centre, vec = refs[:12]
    fc_sum, out_sum, dq, dkv, result = refs[12:17]
    row_refs, seq_refs, out_refs, kv_refs = refs[17:23], refs[23:27], refs[27:31], refs[31:34]
    kv_send, kv_got, kv_part, kv_total, kv_acc, delta, acc = refs[34:41]
    send_sem, recv_sem, load_sem = refs[41:]
    index, place = lax.axis_index("seq"), lax.axis_index("tensor")
    core = lax.rem(place, 2)
    other_core = {"tensor": flip(place, 1)}
    along = seq_peers(index, count)
    lines = count // 2
    greet(along + [other_core, {"tensor": flip(place, 2)}])
    wire = Wire(send_sem, recv_sem, load_sem)
    reduce = RowSum(wire, place, along[0], feed, *row_refs)
    bulk = SeqSum(wire, index, along, fc, *seq_refs, fc_sum, True)
    out_bulk = SeqSum(wire, index, along, out, *out_refs, out_sum, False)
    keys_sum = SeqSum(wire, index, along, kv_part, *kv_refs, None, kv_total, False)
    gather = RowGather(wire, place, result)
    hd = kv_in.shape[-1] // 2
    heads = q_in.shape[-1] // hd
    scale = float(hd) ** (-0.5)
    scale_two = scale * LOG2E
    near_x = 1 - lax.rem(index, 2)

    def open_batch(batch):
        acc[...] = jnp.zeros_like(acc)
        for head in range(heads):
            cols = slice(head * hd, (head + 1) * hd)
            product = grad_o_in[batch, :, cols].astype(F32) * mixed[batch, :, cols].astype(F32)
            delta[head] = jnp.sum(product, axis=-1, keepdims=True)

    def blocks_of(batch, which, target, extra):
        def body(line, carry):
            block = 2 * line + which
            mask = visible(mq_in[batch], mk_in[batch, block])
            keys = kv_in[batch, block, :, :hd]
            values = kv_in[batch, block, :, hd:]
            kv_acc[...] = jnp.zeros_like(kv_acc)

            def one_head(head, inner):
                cols = pl.ds(pl.multiple_of(head * hd, hd), hd)
                query = q_in[batch, :, cols]
                grad_o = grad_o_in[batch, :, cols]
                scores = dot_nt(query, keys) * scale_two
                probs = jnp.where(mask, jnp.exp2(scores - lse[batch, head]), 0.0)
                grad_p = dot_nt(grad_o, values)
                grad_s = (probs * (grad_p - delta[head])).astype(LOW)
                acc[:, cols] += dot(grad_s, keys)
                kv_acc[:, :hd] += dot_tn(grad_s, query)
                kv_acc[:, hd:] += dot_tn(probs.astype(LOW), grad_o)
                return inner

            lax.fori_loop(0, heads, one_head, 0)
            grad_k = kv_acc[:, :hd] * scale
            grad_v = kv_acc[:, hd:]
            if extra is not None:
                grad_k = grad_k + extra[block, :, :hd].astype(F32)
                grad_v = grad_v + extra[block, :, hd:].astype(F32)
            target[block, :, :hd] = grad_k.astype(LOW)
            target[block, :, hd:] = grad_v.astype(LOW)
            return carry

        lax.fori_loop(0, lines, body, 0)

    def close_batch(batch):
        dq[batch] = (acc[...] * scale).astype(LOW)

    def to_core(which):
        return [
            wire.copy(kv_send.at[2 * line + which], kv_got.at[2 * line + which], other_core)
            for line in range(lines)
        ]

    reduce.start()
    middle, edge = turns(lines)[: lines // 2], turns(lines)[lines // 2 :]
    bulk.start(middle)
    out_bulk.start(middle)
    bulk.start(edge)
    out_bulk.start(edge)
    bulk.load()
    out_bulk.load()
    reduce.to_side(1)
    reduce.to_side(0)
    bulk.relay(lines // 4)
    open_batch(1 - core)
    blocks_of(1 - core, near_x, kv_send, None)
    near_handles = to_core(near_x)
    bulk.relay(lines // 2 - lines // 4)
    blocks_of(1 - core, 1 - near_x, kv_send, None)
    own_handles = to_core(1 - near_x)
    close_batch(1 - core)
    reduce.to_pair()
    out_bulk.relay(lines // 4)
    for handle in near_handles:
        wire.arrived(handle)
    open_batch(core)
    blocks_of(core, near_x, kv_part, kv_got)
    keys_sum.start()
    bulk.start([0])
    out_bulk.start([0])
    out_bulk.relay(lines // 2 - lines // 4)
    bulk.relay(len(edge))
    out_bulk.relay(len(edge))
    reduce.ready()
    bias = vec[0:1, :]

    def body(at):
        total = centre[at, :] + reduce.total(at) + bias
        result[place, at, :] = total.astype(LOW)

    by_rows(centre.shape[0], 16, body)
    gather.start()
    for handle in own_handles:
        wire.arrived(handle)
    blocks_of(core, 1 - near_x, kv_part, kv_got)
    close_batch(core)
    keys_sum.relay(lines - 1)
    gather.forward()
    keys_sum.close()
    dkv[1 - core] = jnp.zeros(dkv.shape[1:], LOW)
    dkv[core] = kv_total[...].astype(LOW)
    bulk.close()
    out_bulk.close()
    wire.finish()


def back_stage(feed, fc, out, queries, keyval, meta_q, meta_k, mixed, lse, grad_mixed, centre, vec):
    count = lax.axis_size("seq")
    tensor = lax.axis_size("tensor")
    part, full = centre.shape
    batches, rows, width = queries.shape
    blocks, two = keyval.shape[1], keyval.shape[3]
    heads = 2 * width // two
    vmem, hbm = pl.BlockSpec(memory_space=pltpu.VMEM), pl.BlockSpec(memory_space=pl.ANY)
    kv_part = jax.ShapeDtypeStruct((blocks, rows, two), LOW)
    copies = 4 * count + 14
    return pl.pallas_call(
        partial(back_kernel, count),
        out_shape=[
            jax.ShapeDtypeStruct((fc.shape[1], 2 * fc.shape[2]), F32),
            jax.ShapeDtypeStruct(out.shape[1:], F32),
            jax.ShapeDtypeStruct((batches, rows, width), LOW),
            jax.ShapeDtypeStruct((batches, rows, two), LOW),
            jax.ShapeDtypeStruct((tensor, part, full), LOW),
        ],
        in_specs=[hbm] * 3 + [vmem] * 9,
        out_specs=[vmem] * 5,
        scratch_shapes=row_sum_scratch(feed)
        + seq_sum_scratch(fc, held=True)
        + seq_sum_scratch(out, held=True)
        + seq_sum_scratch(kv_part)
        + [pltpu.VMEM(kv_part.shape, LOW)] * 3
        + [
            pltpu.VMEM((rows, two), F32),
            pltpu.VMEM((rows, two), F32),
            pltpu.VMEM((heads, rows, 1), F32),
            pltpu.VMEM((rows, width), F32),
        ]
        + sem_scratch(copies)
        + [pltpu.SemaphoreType.DMA((4 + count,))],
        compiler_params=pltpu.CompilerParams(
            collective_id=3, has_side_effects=True, vmem_limit_bytes=60 << 20
        ),
        name="back",
    )(feed, fc, out, queries, keyval, meta_q, meta_k, mixed, lse, grad_mixed, centre, vec)


def last_kernel(count, *refs):
    back, query, keyval, small, own, dy, vec = refs[:7]
    query_sum, keyval_sum, rows, small_sum = refs[7:11]
    row_refs, key_row_refs = refs[11:15], refs[15:19]
    query_refs, key_refs, small_refs = refs[19:23], refs[23:26], refs[26:29]
    key_part, small_part, small_own, small_got, sums, send_sem, recv_sem, load_sem = refs[29:]
    index, place = lax.axis_index("seq"), lax.axis_index("tensor")
    along = seq_peers(index, count)
    other_core, other_side = {"tensor": flip(place, 1)}, {"tensor": flip(place, 2)}
    greet(along + [other_core, other_side])
    wire = Wire(send_sem, recv_sem, load_sem)
    reduce = RowSum(wire, place, None, back, *row_refs[:3], None, None, row_refs[3])
    key_reduce = RowSum(
        wire, place, None, keyval, *key_row_refs[:3], None, None, key_row_refs[3]
    )
    query_bulk = SeqSum(wire, index, along, query, *query_refs, query_sum, False)
    key_bulk = SeqSum(wire, index, along, key_part, *key_refs, None, keyval_sum, False)
    small_bulk = SeqSum(wire, index, along, small_part, *small_refs, None, small_own.at[0], False)
    gather = RowGather(wire, place, rows)
    spread = count // 2 - 1
    reduce.start()
    query_bulk.start()
    query_bulk.load()
    key_reduce.start()
    reduce.to_side(0)
    key_reduce.to_side(0)
    query_bulk.relay(spread // 3)
    reduce.ready()
    sums[...] = jnp.zeros_like(sums)
    gain = vec[0:1, :]

    def body(at):
        over = reduce.total(at)
        inner, product = norm_back(own[at, :].astype(F32), gain, over)
        rows[place, at, :] = (dy[at, :] + inner).astype(LOW)
        sums[0] += product
        sums[1] += over

    by_rows(own.shape[0], 16, body)
    gather.start()
    small_part[...] = small[...]
    width = own.shape[1] // count
    for row in range(2):
        line = jnp.sum(sums[row], axis=0, keepdims=True)
        for block in range(count):
            part = line[:, block * width : (block + 1) * width]
            small_part[block, row : row + 1, 0:width] = part
    small_bulk.start()
    key_reduce.ready()
    step = key_part.shape[1]
    for block in range(count):
        key_part[block] = key_reduce.total(slice(block * step, (block + 1) * step)).astype(LOW)
    key_bulk.start()
    query_bulk.relay(spread // 3)
    gather.forward()
    small_bulk.relay(spread)
    query_bulk.relay(spread - 2 * (spread // 3))
    key_bulk.relay(spread)
    small_bulk.close()
    for turn, peer in enumerate((other_core, other_side)):
        handle = wire.copy(small_own.at[turn], small_got.at[turn], peer)
        wire.arrived(handle)
        total = small_own[turn] + small_got[turn]
        if turn:
            small_sum[...] = total
        else:
            small_own[1] = total
    query_bulk.close()
    key_bulk.close()
    wire.finish()


def last_stage(back, query, keyval, small, own, dy, vec):
    count = lax.axis_size("seq")
    tensor = lax.axis_size("tensor")
    part, full = own.shape
    vmem, hbm = pl.BlockSpec(memory_space=pltpu.VMEM), pl.BlockSpec(memory_space=pl.ANY)
    key_part = jax.ShapeDtypeStruct((count, keyval.shape[2] // count, keyval.shape[3]), LOW)
    copies = 3 * count + 12
    return pl.pallas_call(
        partial(last_kernel, count),
        out_shape=[
            jax.ShapeDtypeStruct(query.shape[1:], F32),
            jax.ShapeDtypeStruct(key_part.shape[1:], F32),
            jax.ShapeDtypeStruct((tensor, part, full), LOW),
            jax.ShapeDtypeStruct(small.shape[1:], F32),
        ],
        in_specs=[hbm] * 3 + [vmem] * 4,
        out_specs=[vmem] * 4,
        scratch_shapes=row_sum_scratch(back)
        + row_sum_scratch(keyval)
        + seq_sum_scratch(query, held=True)
        + seq_sum_scratch(key_part)
        + seq_sum_scratch(small, F32)
        + [
            pltpu.VMEM(key_part.shape, LOW),
            pltpu.VMEM(small.shape, F32),
            pltpu.VMEM((2,) + small.shape[1:], F32),
            pltpu.VMEM((2,) + small.shape[1:], F32),
            pltpu.VMEM((2, 16, full), F32),
        ]
        + sem_scratch(copies)
        + [pltpu.SemaphoreType.DMA((4 + count // 2,))],
        compiler_params=pltpu.CompilerParams(
            collective_id=4, has_side_effects=True, vmem_limit_bytes=60 << 20
        ),
        name="last",
    )(back, query, keyval, small, own, dy, vec)


def visible(meta_q, meta_k):
    seg_q, pos_q = meta_q[:, 0:1], meta_q[:, 1:2]
    seg_k, pos_k = meta_k[0:1, :], meta_k[1:2, :]
    return ((seg_k == 0) | (seg_k == seg_q)) & (pos_k <= pos_q)


def norm_parts(values):
    average = jnp.mean(values, axis=-1, keepdims=True)
    centred = values - average
    spread = jnp.mean(centred * centred, axis=-1, keepdims=True)
    return centred, lax.rsqrt(spread + EPS)


def norm_back(values, gain, grad):
    centred, inverse = norm_parts(values)
    unit = centred * inverse
    scaled = grad * gain
    inner = (
        scaled
        - jnp.mean(scaled, axis=-1, keepdims=True)
        - unit * jnp.mean(scaled * unit, axis=-1, keepdims=True)
    )
    return inverse * inner, grad * unit


def gelu_pair(values):
    const = 0.7978845608028654
    square = values * values
    inner = jnp.tanh(const * (values + 0.044715 * (values * square)))
    half = 0.5 * (1.0 + inner)
    slope = half + 0.5 * values * (1.0 - inner * inner) * const * (1.0 + 3 * 0.044715 * square)
    return values * half, slope


def local(
    inputs,
    segment,
    position,
    w_query,
    w_keyval,
    w_out,
    w_fc,
    w_proj,
    vectors,
    fc_bias,
    value_bias,
    grad_out,
):
    seq_size, tensor_size = lax.axis_size("seq"), lax.axis_size("tensor")
    seq_index, tensor_index = lax.axis_index("seq"), lax.axis_index("tensor")
    batches, rows, full_width = inputs.shape
    width_block = w_query.shape[0]
    group_width = w_query.shape[1]
    hidden_width = w_fc.shape[1]
    unit_width = hidden_width // 2
    unit_half = (seq_index >> 1) & 1
    hd = value_bias.shape[0]
    quarter = rows // tensor_size
    shard = vectors.shape[1]
    bias_shard = fc_bias.shape[0]

    pieces = [
        vectors.reshape(-1).astype(LOW),
        fc_bias.astype(LOW),
        segment.reshape(-1).astype(LOW),
        (position // 128).reshape(-1).astype(LOW),
        (position % 128).reshape(-1).astype(LOW),
    ]
    cuts = [0]
    for piece in pieces:
        cuts.append(cuts[-1] + piece.shape[0])
    packed = jnp.concatenate(pieces)
    packed = jnp.pad(packed, (0, -packed.shape[0] % 2048)).reshape(-1, 128)

    def halves(array):
        return jnp.swapaxes(array.astype(LOW).reshape(width_block, 2, unit_width), 0, 1)

    small, kv_mat, q_mat = gather_first(packed, w_keyval.astype(LOW), w_query.astype(LOW))
    kv_mat = kv_mat.reshape(full_width, 2 * hd)
    q_mat = q_mat.reshape(full_width, group_width)

    small = small.reshape(seq_size, tensor_size, -1).astype(F32)
    vec_all = small[:, :, cuts[0] : cuts[1]].reshape(seq_size * tensor_size, 7, shard)
    vec_all = jnp.swapaxes(vec_all, 0, 1).reshape(7, full_width)
    fc_all = small[:, :, cuts[1] : cuts[2]].reshape(-1)
    seg_keys = small[:, 0, cuts[2] : cuts[3]].reshape(seq_size, batches, rows)
    pos_keys = 128.0 * small[:, 0, cuts[3] : cuts[4]] + small[:, 0, cuts[4] : cuts[5]]
    seg_keys = jnp.swapaxes(seg_keys, 0, 1).astype(jnp.int32)
    pos_keys = jnp.swapaxes(pos_keys.reshape(seq_size, batches, rows), 0, 1).astype(jnp.int32)
    meta_k = jnp.pad(jnp.stack([seg_keys, pos_keys], axis=2), ((0, 0), (0, 0), (0, 6), (0, 0)))
    meta_q = jnp.pad(jnp.stack([segment, position], axis=2), ((0, 0), (0, 0), (0, 126)))

    gain_one, shift_one, _, out_bias, gain_two, shift_two, proj_bias = [
        vec_all[i] for i in range(7)
    ]
    query_bias = lax.dynamic_slice_in_dim(vec_all[2], tensor_index * group_width, group_width, 0)
    fc_local = lax.dynamic_slice_in_dim(
        fc_all, tensor_index * hidden_width + unit_half * unit_width, unit_width, 0
    )
    bias_value = value_bias.astype(LOW).astype(F32)
    kv_bias = jnp.concatenate([jnp.zeros((hd,), F32), bias_value])

    residual = inputs.astype(F32)
    centred, inverse = norm_parts(residual)
    normed = (centred * inverse * gain_one + shift_one).astype(LOW).reshape(-1, full_width)
    keyval = (dot(normed, kv_mat) + kv_bias).astype(LOW).reshape(batches, rows, 2 * hd)
    queries = (dot(normed, q_mat) + query_bias).astype(LOW)
    queries = queries.reshape(batches, rows, group_width)

    def by_quarter(array):
        split = array.reshape(batches, tensor_size, quarter, array.shape[-1])
        return jnp.swapaxes(split, 0, 1).reshape(tensor_size, batches * quarter, -1)

    def by_batch(array):
        split = array.reshape(tensor_size, batches, quarter, array.shape[-1])
        return jnp.swapaxes(split, 0, 1).reshape(batches, rows, -1)

    def my_quarter(array):
        split = array.reshape(batches, tensor_size, quarter, full_width)
        own = lax.dynamic_index_in_dim(split, tensor_index, 1, keepdims=False)
        return own.reshape(batches * quarter, full_width)

    vecs = jnp.pad(jnp.stack([out_bias, gain_two, shift_two]), ((0, 5), (0, 0)))
    grad_split = by_quarter(grad_out)
    mixed, lse, kv_all, out_t, middle, rows_two, fc_mat, proj_t, grad_other = front(
        queries,
        keyval,
        meta_q,
        meta_k,
        my_quarter(inputs),
        vecs,
        w_out.T.astype(LOW),
        halves(w_fc),
        halves(w_proj.T),
        grad_split,
    )
    out_t = out_t.reshape(full_width, group_width)
    fc_mat = fc_mat.reshape(full_width, unit_width)
    proj_t = proj_t.reshape(full_width, unit_width)
    mixed_rows = by_quarter(mixed).reshape(-1, group_width)
    normed_two = rows_two.reshape(-1, full_width)
    hidden = dot(normed_two, fc_mat) + fc_local
    active_f, slope = gelu_pair(hidden)
    active = active_f.astype(LOW)

    grad_q_low = my_quarter(grad_out)
    grad_flat = jnp.concatenate([grad_split, grad_other]).reshape(-1, full_width)
    grad_hidden = (slope * dot(grad_flat, proj_t)).astype(LOW)
    fcbias_local = jnp.sum(grad_hidden.astype(F32), axis=0)
    back_part = dot_nt(grad_hidden, fc_mat).astype(LOW)
    back_part = back_part.reshape(2, tensor_size, batches * quarter, full_width)

    def blocked(array):
        return array.astype(LOW).reshape(seq_size, width_block, array.shape[-1])

    proj_sum, grad_middle, rows_middle, sums, feed_part, fc_part = middle_stage(
        back_part,
        blocked(dot_tn(grad_flat, active)),
        middle,
        grad_q_low,
        jnp.pad(gain_two[None], ((0, 7), (0, 0))),
        active,
        proj_t,
        normed_two,
        grad_hidden,
    )
    grad_gain_two, grad_shift_two, grad_out_bias = jnp.sum(sums, axis=1)
    grad_proj_bias = jnp.sum(grad_q_low.astype(F32), axis=0)
    grad_middle_low = rows_middle.reshape(-1, full_width)
    def one_row(row):
        return jnp.pad(row[None], ((0, 7), (0, 0)))

    grad_mixed = by_batch(dot(grad_middle_low, out_t).astype(LOW))
    fc_sum, out_sum, grad_queries, grad_keyval, result_rows = back_stage(
        feed_part.reshape(2, tensor_size, batches * quarter, full_width),
        blocked(fc_part),
        blocked(dot_tn(grad_middle_low, mixed_rows)),
        queries,
        kv_all,
        meta_q,
        meta_k,
        mixed,
        lse,
        grad_mixed,
        middle,
        one_row(proj_bias),
    )
    result = by_batch(result_rows)
    grad_keyval = grad_keyval.reshape(-1, 2 * hd)
    grad_queries = grad_queries.reshape(-1, group_width)
    grad_normed = dot_nt(grad_queries, q_mat) + dot_nt(grad_keyval, kv_mat)
    qbias_local = jnp.sum(grad_queries.astype(F32), axis=0)
    vbias_local = jnp.sum(grad_keyval[:, hd:].astype(F32), axis=0)

    qbias_full = lax.dynamic_update_slice_in_dim(
        jnp.zeros((full_width,), F32), qbias_local, tensor_index * group_width, 0
    )
    full_hidden = bias_shard * seq_size * tensor_size
    fcbias_full = lax.dynamic_update_slice_in_dim(
        jnp.zeros((full_hidden,), F32),
        fcbias_local,
        tensor_index * hidden_width + unit_half * unit_width,
        0,
    )
    chunk = full_hidden // seq_size
    blank = jnp.zeros((full_width,), F32)
    vec_grads = jnp.stack(
        [blank, blank, qbias_full, grad_out_bias, grad_gain_two, grad_shift_two, grad_proj_bias]
    )

    def in_rows(array):
        array = jnp.pad(array, ((0, 0), (0, -array.shape[1] % width_block)))
        return array.reshape(seq_size, -1, width_block)

    vec_rows = 7
    bias_rows = chunk // width_block
    small_rows = jnp.concatenate(
        [
            jnp.swapaxes(vec_grads.reshape(7, seq_size, width_block), 0, 1),
            in_rows(fcbias_full.reshape(seq_size, chunk)),
            in_rows(jnp.broadcast_to(vbias_local, (seq_size, hd))),
        ],
        axis=1,
    )
    small_rows = jnp.pad(
        small_rows,
        ((0, 0), (0, -small_rows.shape[1] % 8), (0, -width_block % 128)),
    )
    key_grad = dot_tn(normed, grad_keyval).astype(LOW)
    key_grad = key_grad.reshape(seq_size, tensor_size, -1, 2 * hd)
    key_grad = jnp.swapaxes(key_grad, 0, 1).reshape(1, tensor_size, -1, 2 * hd)
    query_sum, keyval_grad, input_rows, small_sum = last_stage(
        by_quarter(grad_normed.astype(LOW))[None],
        blocked(dot_tn(normed, grad_queries)),
        key_grad,
        small_rows,
        my_quarter(inputs),
        grad_middle,
        one_row(gain_one),
    )
    input_grad = by_batch(input_rows)
    small_sum = small_sum[:, :width_block]
    vec_grad = lax.dynamic_slice_in_dim(small_sum[:vec_rows], tensor_index * shard, shard, 1)
    fcbias_grad = lax.dynamic_slice_in_dim(
        small_sum[vec_rows : vec_rows + bias_rows].reshape(-1),
        tensor_index * bias_shard,
        bias_shard,
        0,
    )
    vbias_grad = small_sum[vec_rows + bias_rows :].reshape(-1)[:hd]
    return (
        result,
        input_grad,
        query_sum,
        keyval_grad,
        out_sum.T,
        fc_sum,
        proj_sum.T,
        vec_grad,
        fcbias_grad,
        vbias_grad,
        vec_grad[5],
    )


def solution(mesh):
    in_specs = (
        P(None, "seq", None),
        P(None, "seq"),
        P(None, "seq"),
        P("seq", "tensor"),
        P(("seq", "tensor"), None),
        P("tensor", "seq"),
        P("seq", "tensor"),
        P("tensor", "seq"),
        P(None, ("seq", "tensor")),
        P(("seq", "tensor")),
        P(),
        P(None, "seq", None),
    )
    out_specs = (
        P(None, "seq", None),
        P(None, "seq", None),
        P("seq", "tensor"),
        P(("seq", "tensor"), None),
        P("tensor", "seq"),
        P("seq", "tensor"),
        P("tensor", "seq"),
        P(None, ("seq", "tensor")),
        P(("seq", "tensor")),
        P(),
        P(("seq", "tensor")),
    )
    return jax.shard_map(local, mesh=mesh, in_specs=in_specs, out_specs=out_specs, check_vma=False)
```

```python
from functools import partial

import jax
import jax.numpy as jnp
from jax import lax
from jax.experimental import pallas as pl
from jax.experimental.pallas import tpu as pltpu
from jax.sharding import PartitionSpec as P

EPS = 1e-05
NEG = -1e30
LOG2E = 1.4426950408889634
LOW = jnp.bfloat16
F32 = jnp.float32


def bits_of(count):
    return count.bit_length() - 1


def swap(value, axis, bit):
    count = lax.axis_size(axis)
    return lax.ppermute(value, axis, [(i, i ^ (1 << bit)) for i in range(count)])


def after(value, *others):
    return lax.optimization_barrier((value,) + others)[0]


def dot(left, right):
    return jnp.dot(left, right, preferred_element_type=F32)


def dot_tn(left, right):
    return lax.dot_general(left, right, (((0,), (0,)), ((), ())), preferred_element_type=F32)


def dot_nt(left, right):
    return lax.dot_general(left, right, (((1,), (1,)), ((), ())), preferred_element_type=F32)


MESH = pl.DeviceIdType.MESH


def flip(index, mask):
    bit = 1
    out = index
    while bit <= mask:
        if mask & bit:
            out = out + bit * (1 - 2 * lax.rem(lax.div(index, bit), 2))
        bit *= 2
    return out


class Wire:
    def __init__(self, send_sem, recv_sem, local_sem=None):
        self.send_sem, self.recv_sem, self.local_sem = send_sem, recv_sem, local_sem
        self.loads = []
        self.started = []
        self.landed = set()

    def copy(self, src, dst, peer):
        place = len(self.started)
        item = pltpu.make_async_remote_copy(
            src_ref=src,
            dst_ref=dst,
            send_sem=self.send_sem.at[place],
            recv_sem=self.recv_sem.at[place],
            device_id=peer,
            device_id_type=MESH,
        )
        item.start()
        self.started.append(item)
        return place

    def load(self, src, dst):
        item = pltpu.make_async_copy(src, dst, self.local_sem.at[len(self.loads)])
        item.start()
        self.loads.append(item)
        return item

    def arrived(self, place):
        if place not in self.landed:
            self.landed.add(place)
            self.started[place].wait_recv()

    def finish(self):
        for place in range(len(self.started)):
            self.arrived(place)
        for item in self.started:
            item.wait_send()


def greet(peers):
    barrier = pltpu.get_barrier_semaphore()
    for peer in peers:
        pl.semaphore_signal(barrier, inc=1, device_id=peer, device_id_type=MESH)
    pl.semaphore_wait(barrier, len(peers))


def seq_peers(index, count):
    return [{"seq": flip(index, 2 * d)} for d in range(1, count // 2)] + [
        {"seq": flip(index, 1)}
    ]


def turns(lines):
    return list(range(lines // 2, lines)) + list(range(1, lines // 2))


def first_kernel(count, tensor, *refs):
    ins, outs = refs[:3], refs[3:6]
    send_sem, recv_sem, local_sem = refs[6:]
    index = lax.axis_index("seq")
    place = lax.axis_index("tensor")
    across = [{"tensor": flip(place, tensor >> (i + 1))} for i in range(bits_of(tensor))]
    along = seq_peers(index, count)
    far, near = along[:-1], along[-1]
    greet(across + along)
    wire = Wire(send_sem, recv_sem)
    own = []
    targets = [(lambda at, out=out: out.at[at, place]) for out in outs[:2]]
    targets.append(lambda at: outs[2].at[at])
    handles = []
    for source, target in zip(ins, targets):
        handles.append({d: wire.copy(source, target(index), far[d - 1]) for d in range(1, count // 2)})
        handles[-1][0] = wire.copy(source, target(index), near)
        item = pltpu.make_async_copy(source, target(index), local_sem.at[len(own)])
        item.start()
        own.append(item)
    relays = [[], [], []]
    order = list(range(1, count // 2))

    def relay(a, d):
        wire.arrived(handles[a][d])
        block = targets[a](flip(index, 2 * d))
        relays[a].append(wire.copy(block, block, near))

    for d in order:
        relay(0, d)
        relay(1, d)
    cut = len(order) // 3
    for d in order[:cut]:
        relay(2, d)
    for handle in [handles[0][0], handles[1][0]] + relays[0] + relays[1]:
        wire.arrived(handle)
    own[0].wait()
    own[1].wait()
    masks = [0]
    for i, peer in enumerate(across):
        step = tensor >> (i + 1)
        sent = [
            wire.copy(out.at[:, flip(place, mask)], out.at[:, flip(place, mask)], peer)
            for mask in masks
            for out in outs[:2]
        ]
        masks = masks + [mask | step for mask in masks]
        for d in order[cut:] if i == 0 else []:
            relay(2, d)
        if i + 1 < len(across):
            for handle in sent:
                wire.arrived(handle)
    own[2].wait()
    wire.finish()


def gather_first(small, keyval, query):
    count, tensor = lax.axis_size("seq"), lax.axis_size("tensor")
    arrays = (small, keyval, query)
    shapes = [
        (count, tensor) + small.shape,
        (count, tensor) + keyval.shape,
        (count,) + query.shape,
    ]
    copies = 3 * (count - 1) + 2 * (tensor - 1)
    return pl.pallas_call(
        partial(first_kernel, count, tensor),
        out_shape=[jax.ShapeDtypeStruct(shape, LOW) for shape in shapes],
        in_specs=[pl.BlockSpec(memory_space=pltpu.VMEM)] * 3,
        out_specs=[pl.BlockSpec(memory_space=pltpu.VMEM)] * 3,
        scratch_shapes=[
            pltpu.SemaphoreType.DMA((copies,)),
            pltpu.SemaphoreType.DMA((copies,)),
            pltpu.SemaphoreType.DMA((3,)),
        ],
        compiler_params=pltpu.CompilerParams(collective_id=0, has_side_effects=True),
        name="gather_first",
    )(*arrays)


def front_kernel(count, *refs):
    q_in, kv_in, mq_in, mk_in, x_in, vec_in, o_in, fc_in, pj_in, dy_in = refs[:10]
    mixed, lse, kv_all, out_t, middle, rows_two, fc_out, pj_out, dy_out = refs[10:19]
    (
        top,
        total,
        acc,
        core_keep,
        core_send,
        core_got,
        y_send,
        y_got,
        send_sem,
        recv_sem,
        local_sem,
    ) = refs[19:]
    index = lax.axis_index("seq")
    place = lax.axis_index("tensor")
    core = lax.rem(place, 2)
    side = lax.div(place, 2)
    half = lax.rem(lax.div(index, 2), 2)
    other_core = {"tensor": flip(place, 1)}
    other_side = {"tensor": flip(place, 2)}
    along = seq_peers(index, count)
    far, near = along[:-1], along[-1]
    pair = far[0]
    lines = count // 2
    greet(along + [other_core, other_side])
    wire = Wire(send_sem, recv_sem)
    own = []

    def keep(src, dst):
        item = pltpu.make_async_copy(src, dst, local_sem.at[len(own)])
        item.start()
        own.append(item)

    order = range(1, lines)
    kv_far = {d: wire.copy(kv_in.at[core], kv_all.at[core, index], far[d - 1]) for d in order}
    kv_near = wire.copy(kv_in.at[core], kv_all.at[core, index], near)
    for batch in range(2):
        keep(kv_in.at[batch], kv_all.at[batch, index])
    o_far = {d: wire.copy(o_in, out_t.at[index], far[d - 1]) for d in order}
    o_near = [wire.copy(o_in, out_t.at[index], near)]
    keep(o_in, out_t.at[index])
    dy_pair = wire.copy(dy_in.at[place], dy_out.at[place], pair)

    def send_far(source, out, which=order):
        return {
            d: wire.copy(source.at[flip(half, d & 1)], out.at[index], far[d - 1]) for d in which
        }

    fc_far = send_far(fc_in, fc_out)
    kv_near = [(1, kv_near)]
    kv_core = []
    for d in order:
        wire.arrived(kv_far[d])
        block = kv_all.at[core, flip(index, 2 * d)]
        kv_near.append((2 * d + 1, wire.copy(block, block, near)))
        kv_core.append(wire.copy(block, block, other_core))
    wire.copy(fc_in.at[half], fc_out.at[index], near)
    wire.copy(pj_in.at[half], pj_out.at[index], near)
    keep(fc_in.at[half], fc_out.at[index])
    keep(pj_in.at[half], pj_out.at[index])
    for r, handle in kv_near:
        wire.arrived(handle)
        block = kv_all.at[core, flip(index, r)]
        kv_core.append(wire.copy(block, block, other_core))
    own[0].wait()
    own[1].wait()

    jobs = [(o_far, out_t, d) for d in order]
    jobs += [(fc_far, fc_out, d) for d in order]

    def tick(number):
        for _ in range(min(number, len(jobs))):
            handles, out, d = jobs.pop(0)
            wire.arrived(handles[d])
            block = out.at[flip(index, 2 * d)]
            handle = wire.copy(block, block, near)
            if out is out_t:
                o_near.append(handle)

    hd = kv_in.shape[-1] // 2
    heads = q_in.shape[-1] // hd
    scale = float(hd) ** (-0.5) * LOG2E

    def attend(batch, block):
        mask = visible(mq_in[batch], mk_in[batch, block])
        keys = kv_all[batch, block, :, :hd]
        values = kv_all[batch, block, :, hd:]
        for head in range(heads):
            cols = slice(head * hd, (head + 1) * hd)
            scores = jnp.where(mask, dot_nt(q_in[batch, :, cols], keys) * scale, NEG)
            before = top[head]
            now = jnp.maximum(before, jnp.max(scores, axis=-1, keepdims=True))
            shrink = jnp.exp2(before - now)
            probs = jnp.exp2(scores - now)
            total[head] = total[head] * shrink + jnp.sum(probs, axis=-1, keepdims=True)
            acc[:, cols] = acc[:, cols] * shrink + dot(probs.astype(LOW), values)
            top[head] = now

    def attend_batch(batch, ticks):
        top[...] = jnp.full_like(top, NEG)
        total[...] = jnp.zeros_like(total)
        acc[...] = jnp.zeros_like(acc)

        def block_body(block, carry):
            attend(batch, block)
            return carry

        parts = len(ticks)
        for i in range(parts):
            lax.fori_loop(i * count // parts, (i + 1) * count // parts, block_body, 0)
            tick(ticks[i])
        for head in range(heads):
            cols = slice(head * hd, (head + 1) * hd)
            mixed[batch, :, cols] = (acc[:, cols] / total[head]).astype(LOW)
            lse[batch, head] = top[head] + jnp.log2(total[head])

    spread = lines - 1
    attend_batch(core, [spread])
    pj_far = send_far(pj_in, pj_out, order[:1])
    wire.arrived(dy_pair)
    dy_side = wire.copy(dy_out.at[place], dy_out.at[place], other_side)
    wire.copy(dy_out.at[place], dy_out.at[place], other_core)
    for handle in kv_core:
        wire.arrived(handle)
    attend_batch(1 - core, [spread // 3])
    pj_far.update(send_far(pj_in, pj_out, order[1 : lines // 2]))
    wire.arrived(dy_side)
    block = dy_out.at[flip(place, 2)]
    wire.copy(block, block, other_core)

    quarter = x_in.shape[0] // 2
    for handle in o_near:
        wire.arrived(handle)
    own[2].wait()
    width = out_t.shape[1]
    group = max(1, 256 // width)
    for which, target in ((1 - core, core_send), (core, core_keep)):
        rows = [
            mixed[batch, pl.ds(pl.multiple_of((2 * s + which) * quarter, quarter), quarter), :]
            for s in range(2)
            for batch in range(2)
        ]
        rows = jnp.concatenate(rows, axis=0)

        def project(i, carry, rows=rows, target=target):
            cols = pl.ds(pl.multiple_of(i * group * width, group * width), group * width)
            block = out_t[pl.ds(i * group, group)].reshape(group * width, -1)
            target[:, cols] = dot_nt(rows, block).astype(target.dtype)
            return carry

        lax.fori_loop(0, count // group, project, 0)
        if target is core_send:
            core_handle = wire.copy(core_send, core_got, other_core)
    wire.arrived(core_handle)
    part = 2 * quarter
    step = 16

    def to_side(i, carry):
        at = pl.ds(pl.multiple_of((1 - side) * part + i * step, step), step)
        y_send[pl.ds(pl.multiple_of(i * step, step), step), :] = (
            core_keep[at, :] + core_got[at, :].astype(F32)
        ).astype(LOW)
        return carry

    lax.fori_loop(0, part // step, to_side, 0)
    y_handle = wire.copy(y_send, y_got, other_side)
    tick(spread - spread // 3 - 1)
    wire.arrived(y_handle)
    out_bias, gain_two, shift_two = vec_in[0:1, :], vec_in[1:2, :], vec_in[2:3, :]

    def norm(i, carry):
        at = pl.ds(pl.multiple_of(i * step, step), step)
        far_at = pl.ds(pl.multiple_of(side * part + i * step, step), step)
        value = core_keep[far_at, :] + core_got[far_at, :].astype(F32)
        value = value + y_got[at, :].astype(F32)
        value = x_in[at, :].astype(F32) + value + out_bias
        middle[at, :] = value
        centred, inverse = norm_parts(value)
        rows_two[0, place, at, :] = (centred * inverse * gain_two + shift_two).astype(LOW)
        return carry

    lax.fori_loop(0, part // step, norm, 0)
    mine = rows_two.at[0, place]
    pair_handle = wire.copy(mine, rows_two.at[1, place], pair)
    side_handle = wire.copy(mine, mine, other_side)
    wire.copy(mine, mine, other_core)
    pj_far.update(send_far(pj_in, pj_out, order[lines // 2 :]))
    tick(len(jobs))
    jobs.extend((pj_far, pj_out, d) for d in order)
    tick(lines // 2)
    wire.arrived(pair_handle)
    theirs = rows_two.at[1, place]
    side_two = wire.copy(theirs, theirs, other_side)
    wire.copy(theirs, theirs, other_core)
    wire.arrived(side_handle)
    block = rows_two.at[0, flip(place, 2)]
    wire.copy(block, block, other_core)
    wire.arrived(side_two)
    block = rows_two.at[1, flip(place, 2)]
    wire.copy(block, block, other_core)
    tick(len(jobs))
    for item in own[3:]:
        item.wait()
    wire.finish()


def front(queries, keyval, meta_q, meta_k, own_rows, vecs, out, fc, proj, grad_rows):
    count = lax.axis_size("seq")
    tensor = lax.axis_size("tensor")
    batches, rows, width = queries.shape
    two = keyval.shape[2]
    heads = 2 * width // two
    part, full = own_rows.shape
    shapes = [
        ((batches, rows, width), LOW),
        ((batches, heads, rows, 1), F32),
        ((batches, count, rows, two), LOW),
        ((count,) + out.shape, LOW),
        ((part, full), F32),
        ((2, tensor, part, full), LOW),
        ((count,) + fc.shape[1:], LOW),
        ((count,) + proj.shape[1:], LOW),
        ((tensor, part, full), LOW),
    ]
    copies = 2 * (count - 1) + 3 * (count - 1) + 4 + 2 + 7
    vmem, hbm = pl.BlockSpec(memory_space=pltpu.VMEM), pl.BlockSpec(memory_space=pl.ANY)
    return pl.pallas_call(
        partial(front_kernel, count),
        out_shape=[jax.ShapeDtypeStruct(shape, dtype) for shape, dtype in shapes],
        in_specs=[vmem] * 6 + [hbm] * 4,
        out_specs=[vmem] * 6 + [hbm] * 3,
        scratch_shapes=[
            pltpu.VMEM((heads, rows, 1), F32),
            pltpu.VMEM((heads, rows, 1), F32),
            pltpu.VMEM((rows, width), F32),
            pltpu.VMEM((2 * part, full), F32),
            pltpu.VMEM((2 * part, full), LOW),
            pltpu.VMEM((2 * part, full), LOW),
            pltpu.VMEM((part, full), LOW),
            pltpu.VMEM((part, full), LOW),
            pltpu.SemaphoreType.DMA((copies,)),
            pltpu.SemaphoreType.DMA((copies,)),
            pltpu.SemaphoreType.DMA((5,)),
        ],
        compiler_params=pltpu.CompilerParams(
            collective_id=1, has_side_effects=True, vmem_limit_bytes=56 << 20
        ),
        name="front",
    )(queries, keyval, meta_q, meta_k, own_rows, vecs, out, fc, proj, grad_rows)


def by_rows(rows, step, body):
    def run(i, carry):
        body(pl.ds(pl.multiple_of(i * step, step), step))
        return carry

    lax.fori_loop(0, rows // step, run, 0)


class SeqSum:
    def __init__(self, wire, index, peers, part, from_near, to_far, from_far, held, out, split):
        self.wire, self.index = wire, index
        self.far, self.near = peers[:-1], peers[-1]
        self.lines = len(peers)
        self.part, self.out, self.split = part, out, split
        self.from_near, self.to_far, self.from_far = from_near, to_far, from_far
        self.rows = part.shape[1]
        self.step = min(64, self.rows)
        self.near_handles, self.far_handles = {}, {}
        self.order = turns(self.lines)
        self.held, self.loads = held, {}

    def load(self):
        for d in self.order + [0]:
            block = self.part.at[flip(self.index, 2 * d)]
            self.loads[d] = self.wire.load(block, self.held.at[d])

    def mine(self, d, at):
        if self.held is None:
            return self.part[flip(self.index, 2 * d), at].astype(F32)
        return self.held[d, at].astype(F32)

    def start(self, order=None):
        for d in order or turns(self.lines) + [0]:
            block = self.part.at[flip(self.index, 2 * d + 1)]
            self.near_handles[d] = self.wire.copy(block, self.from_near.at[d], self.near)

    def relay(self, number):
        for _ in range(number):
            d = self.order.pop(0)
            self.wire.arrived(self.near_handles[d])
            if self.held is not None:
                self.loads[d].wait()

            def join(at, d=d):
                total = self.mine(d, at)
                total = total + self.from_near[d, at].astype(F32)
                self.to_far[d - 1, at] = total.astype(self.to_far.dtype)

            by_rows(self.rows, self.step, join)
            self.far_handles[d] = self.wire.copy(
                self.to_far.at[d - 1], self.from_far.at[d - 1], self.far[d - 1]
            )

    def close(self):
        self.wire.arrived(self.near_handles[0])
        if self.held is not None:
            self.loads[0].wait()
        for d in range(1, self.lines):
            self.wire.arrived(self.far_handles[d])
        width = self.part.shape[2]
        half = lax.rem(lax.div(self.index, 2), 2)

        def total(at):
            same = self.mine(0, at) + self.from_near[0, at].astype(F32)
            other = None
            for d in range(1, self.lines):
                got = self.from_far[d - 1, at].astype(F32)
                if self.split and d % 2:
                    other = got if other is None else other + got
                else:
                    same = same + got
            if self.split:
                out = self.out
                out[at, pl.ds(pl.multiple_of(half * width, width), width)] = same
                out[at, pl.ds(pl.multiple_of((1 - half) * width, width), width)] = other
            else:
                self.out[at, :] = same

        by_rows(self.rows, self.step, total)


def seq_sum_scratch(part, dtype=LOW, held=False):
    lines = part.shape[0] // 2
    depths = [lines, lines - 1, lines - 1] + [lines] * held
    return [pltpu.VMEM((depth,) + part.shape[1:], dtype) for depth in depths]


class RowSum:
    def __init__(
        self, wire, place, pair, part, core_got, y_send, y_got, pair_send, pair_got, held
    ):
        self.wire, self.place, self.pair = wire, place, pair
        self.core, self.side = lax.rem(place, 2), lax.div(place, 2)
        self.part, self.core_got, self.y_send, self.y_got = part, core_got, y_send, y_got
        self.pair_send, self.pair_got = pair_send, pair_got
        self.sides = (1 - self.side, self.side)
        self.rows = part.shape[2]
        self.core_handles, self.y_handles = {}, {}
        self.held, self.loads = held, {}

    def start(self):
        peer = {"tensor": flip(self.place, 1)}
        for which in range(2):
            for p in reversed(range(self.part.shape[0])):
                at = self.sides[which]
                block = self.part.at[p, 2 * at + 1 - self.core]
                self.core_handles[p, which] = self.wire.copy(block, self.core_got.at[p, at], peer)
        for which in range(2):
            for p in reversed(range(self.part.shape[0])):
                at = self.sides[which]
                block = self.part.at[p, 2 * at + self.core]
                self.loads[p, which] = self.wire.load(block, self.held.at[p, at])

    def settle(self, p, which):
        self.wire.arrived(self.core_handles[p, which])
        self.loads[p, which].wait()

    def both(self, p, which, at):
        side = self.sides[which]
        mine = self.held[p, side, at, :].astype(F32)
        return mine + self.core_got[p, side, at, :].astype(F32)

    def to_side(self, p):
        self.settle(p, 0)

        def body(at):
            self.y_send[p, at, :] = self.both(p, 0, at).astype(LOW)

        by_rows(self.rows, 16, body)
        peer = {"tensor": flip(self.place, 2)}
        self.y_handles[p] = self.wire.copy(self.y_send.at[p], self.y_got.at[p], peer)

    def to_pair(self):
        self.settle(1, 1)
        self.wire.arrived(self.y_handles[1])

        def body(at):
            total = self.both(1, 1, at) + self.y_got[1, at, :].astype(F32)
            self.pair_send[at, :] = total.astype(LOW)

        by_rows(self.rows, 16, body)
        self.pair_handle = self.wire.copy(self.pair_send, self.pair_got, self.pair)

    def ready(self):
        self.settle(0, 1)
        self.wire.arrived(self.y_handles[0])
        if self.pair is not None:
            self.wire.arrived(self.pair_handle)

    def total(self, at):
        total = self.both(0, 1, at) + self.y_got[0, at, :].astype(F32)
        if self.pair is not None:
            total = total + self.pair_got[at, :].astype(F32)
        return total


def row_sum_scratch(part):
    pairs, _, rows, width = part.shape
    scratch = [pltpu.VMEM((pairs, 2, rows, width), LOW)]
    scratch += [pltpu.VMEM((pairs, rows, width), LOW)] * 2
    if pairs == 2:
        scratch += [pltpu.VMEM((rows, width), LOW)] * 2
    return scratch + [pltpu.VMEM((pairs, 2, rows, width), LOW)]


class RowGather:
    def __init__(self, wire, place, rows):
        self.wire, self.place, self.rows = wire, place, rows

    def start(self):
        mine = self.rows.at[self.place]
        self.side_handle = self.wire.copy(mine, mine, {"tensor": flip(self.place, 2)})
        self.wire.copy(mine, mine, {"tensor": flip(self.place, 1)})

    def forward(self):
        self.wire.arrived(self.side_handle)
        block = self.rows.at[flip(self.place, 2)]
        self.wire.copy(block, block, {"tensor": flip(self.place, 1)})


def sem_scratch(copies):
    return [pltpu.SemaphoreType.DMA((copies,)), pltpu.SemaphoreType.DMA((copies,))]


def middle_kernel(count, *refs):
    back, proj, centre, dy, vec = refs[:5]
    sources, (feed_out, fc_out) = refs[5:9], refs[13:15]
    proj_sum, grad, rows, sums = refs[9:13]
    row_refs, seq_refs = refs[15:21], refs[21:25]
    local = refs[25:29]
    feed, fc_grad, send_sem, recv_sem, local_sem, load_sem = refs[29:]
    loads = [
        pltpu.make_async_copy(source, target, local_sem.at[i])
        for i, (source, target) in enumerate(zip(sources, local))
    ]
    active, proj_t, unit, slope = local
    stores = [
        pltpu.make_async_copy(feed, feed_out, local_sem.at[4]),
        pltpu.make_async_copy(fc_grad, fc_out, local_sem.at[5]),
    ]
    tall, wide = active.shape[0] // 2, 256
    steps = proj_t.shape[0] // wide

    def feed_rows(which):
        at = slice(which * tall, (which + 1) * tall)

        def run(i, carry):
            cols = pl.ds(pl.multiple_of(i * wide, wide), wide)
            feed[at, cols] = dot_nt(active[at, :], proj_t[cols, :]).astype(LOW)
            return carry

        lax.fori_loop(0, steps, run, 0)

    def fc_rows(which):
        half_width = slope.shape[1] // 2
        out = slice(which * half_width, (which + 1) * half_width)

        def run(i, carry):
            cols = pl.ds(pl.multiple_of(i * wide, wide), wide)
            fc_grad[cols, out] = dot_tn(unit[:, cols], slope[:, out]).astype(LOW)
            return carry

        lax.fori_loop(0, steps, run, 0)

    index, place = lax.axis_index("seq"), lax.axis_index("tensor")
    along = seq_peers(index, count)
    greet(along + [{"tensor": flip(place, 1)}, {"tensor": flip(place, 2)}])
    wire = Wire(send_sem, recv_sem, load_sem)
    reduce = RowSum(wire, place, along[0], back, *row_refs)
    bulk = SeqSum(wire, index, along, proj, *seq_refs, proj_sum, True)
    gather = RowGather(wire, place, rows)
    lines = count // 2
    reduce.start()
    bulk.start()
    bulk.load()
    for item in loads:
        item.start()
    reduce.to_side(1)
    reduce.to_side(0)
    bulk.relay(lines // 4)
    reduce.to_pair()
    bulk.relay(lines // 2 - lines // 4)
    loads[0].wait()
    loads[1].wait()
    feed_rows(0)
    reduce.ready()
    sums[...] = jnp.zeros_like(sums)
    gain = vec[0:1, :]

    def body(at):
        over = reduce.total(at)
        inner, product = norm_back(centre[at, :], gain, over)
        value = dy[at, :].astype(F32) + inner
        grad[at, :] = value
        rows[place, at, :] = value.astype(LOW)
        sums[0] += product
        sums[1] += over
        sums[2] += value

    by_rows(centre.shape[0], 16, body)
    gather.start()
    bulk.relay(lines - 1 - lines // 2)
    feed_rows(1)
    stores[0].start()
    loads[2].wait()
    loads[3].wait()
    fc_rows(0)
    gather.forward()
    fc_rows(1)
    stores[1].start()
    bulk.close()
    for item in stores:
        item.wait()
    wire.finish()


def middle_stage(back, proj, centre, dy, vec, active, proj_t, unit, slope):
    count = lax.axis_size("seq")
    tensor = lax.axis_size("tensor")
    part, full = centre.shape
    vmem = pl.BlockSpec(memory_space=pltpu.VMEM)
    hbm = pl.BlockSpec(memory_space=pl.ANY)
    feed = jax.ShapeDtypeStruct((active.shape[0], proj_t.shape[0]), LOW)
    fc_grad = jax.ShapeDtypeStruct((unit.shape[1], slope.shape[1]), LOW)
    copies = 2 * count + 12
    return pl.pallas_call(
        partial(middle_kernel, count),
        out_shape=[
            jax.ShapeDtypeStruct((proj.shape[1], 2 * proj.shape[2]), F32),
            jax.ShapeDtypeStruct((part, full), F32),
            jax.ShapeDtypeStruct((tensor, part, full), LOW),
            jax.ShapeDtypeStruct((3, 16, full), F32),
            feed,
            fc_grad,
        ],
        in_specs=[hbm] * 2 + [vmem] * 3 + [hbm] * 4,
        out_specs=[vmem] * 4 + [hbm] * 2,
        scratch_shapes=row_sum_scratch(back)
        + seq_sum_scratch(proj, held=True)
        + [pltpu.VMEM(array.shape, LOW) for array in (active, proj_t, unit, slope, feed, fc_grad)]
        + sem_scratch(copies)
        + [pltpu.SemaphoreType.DMA((6,)), pltpu.SemaphoreType.DMA((4 + count // 2,))],
        compiler_params=pltpu.CompilerParams(
            collective_id=2, has_side_effects=True, vmem_limit_bytes=60 << 20
        ),
        name="middle",
    )(back, proj, centre, dy, vec, active, proj_t, unit, slope)


def back_kernel(count, *refs):
    feed, fc, out, q_in, kv_in, mq_in, mk_in, mixed, lse, grad_o_in, centre, vec = refs[:12]
    fc_sum, out_sum, dq, dkv, result = refs[12:17]
    row_refs, seq_refs, out_refs, kv_refs = refs[17:23], refs[23:27], refs[27:31], refs[31:34]
    kv_send, kv_got, kv_part, kv_total, kv_acc, delta, acc = refs[34:41]
    send_sem, recv_sem, load_sem = refs[41:]
    index, place = lax.axis_index("seq"), lax.axis_index("tensor")
    core = lax.rem(place, 2)
    other_core = {"tensor": flip(place, 1)}
    along = seq_peers(index, count)
    lines = count // 2
    greet(along + [other_core, {"tensor": flip(place, 2)}])
    wire = Wire(send_sem, recv_sem, load_sem)
    reduce = RowSum(wire, place, along[0], feed, *row_refs)
    bulk = SeqSum(wire, index, along, fc, *seq_refs, fc_sum, True)
    out_bulk = SeqSum(wire, index, along, out, *out_refs, out_sum, False)
    keys_sum = SeqSum(wire, index, along, kv_part, *kv_refs, None, kv_total, False)
    gather = RowGather(wire, place, result)
    hd = kv_in.shape[-1] // 2
    heads = q_in.shape[-1] // hd
    scale = float(hd) ** (-0.5)
    scale_two = scale * LOG2E
    near_x = 1 - lax.rem(index, 2)

    def open_batch(batch):
        acc[...] = jnp.zeros_like(acc)
        for head in range(heads):
            cols = slice(head * hd, (head + 1) * hd)
            product = grad_o_in[batch, :, cols].astype(F32) * mixed[batch, :, cols].astype(F32)
            delta[head] = jnp.sum(product, axis=-1, keepdims=True)

    def blocks_of(batch, which, target, extra):
        def body(line, carry):
            block = 2 * line + which
            mask = visible(mq_in[batch], mk_in[batch, block])
            keys = kv_in[batch, block, :, :hd]
            values = kv_in[batch, block, :, hd:]
            kv_acc[...] = jnp.zeros_like(kv_acc)

            def one_head(head, inner):
                cols = pl.ds(pl.multiple_of(head * hd, hd), hd)
                query = q_in[batch, :, cols]
                grad_o = grad_o_in[batch, :, cols]
                scores = dot_nt(query, keys) * scale_two
                probs = jnp.where(mask, jnp.exp2(scores - lse[batch, head]), 0.0)
                grad_p = dot_nt(grad_o, values)
                grad_s = (probs * (grad_p - delta[head])).astype(LOW)
                acc[:, cols] += dot(grad_s, keys)
                kv_acc[:, :hd] += dot_tn(grad_s, query)
                kv_acc[:, hd:] += dot_tn(probs.astype(LOW), grad_o)
                return inner

            lax.fori_loop(0, heads, one_head, 0)
            grad_k = kv_acc[:, :hd] * scale
            grad_v = kv_acc[:, hd:]
            if extra is not None:
                grad_k = grad_k + extra[block, :, :hd].astype(F32)
                grad_v = grad_v + extra[block, :, hd:].astype(F32)
            target[block, :, :hd] = grad_k.astype(LOW)
            target[block, :, hd:] = grad_v.astype(LOW)
            return carry

        lax.fori_loop(0, lines, body, 0)

    def close_batch(batch):
        dq[batch] = (acc[...] * scale).astype(LOW)

    def to_core(which):
        return [
            wire.copy(kv_send.at[2 * line + which], kv_got.at[2 * line + which], other_core)
            for line in range(lines)
        ]

    reduce.start()
    middle, edge = turns(lines)[: lines // 2], turns(lines)[lines // 2 :]
    bulk.start(middle)
    out_bulk.start(middle)
    bulk.start(edge)
    out_bulk.start(edge)
    bulk.load()
    out_bulk.load()
    reduce.to_side(1)
    reduce.to_side(0)
    bulk.relay(lines // 4)
    open_batch(1 - core)
    blocks_of(1 - core, near_x, kv_send, None)
    near_handles = to_core(near_x)
    bulk.relay(lines // 2 - lines // 4)
    blocks_of(1 - core, 1 - near_x, kv_send, None)
    own_handles = to_core(1 - near_x)
    close_batch(1 - core)
    reduce.to_pair()
    out_bulk.relay(lines // 4)
    for handle in near_handles:
        wire.arrived(handle)
    open_batch(core)
    blocks_of(core, near_x, kv_part, kv_got)
    keys_sum.start()
    bulk.start([0])
    out_bulk.start([0])
    out_bulk.relay(lines // 2 - lines // 4)
    bulk.relay(len(edge))
    out_bulk.relay(len(edge))
    reduce.ready()
    bias = vec[0:1, :]

    def body(at):
        total = centre[at, :] + reduce.total(at) + bias
        result[place, at, :] = total.astype(LOW)

    by_rows(centre.shape[0], 16, body)
    gather.start()
    for handle in own_handles:
        wire.arrived(handle)
    blocks_of(core, 1 - near_x, kv_part, kv_got)
    close_batch(core)
    keys_sum.relay(lines - 1)
    gather.forward()
    keys_sum.close()
    dkv[1 - core] = jnp.zeros(dkv.shape[1:], LOW)
    dkv[core] = kv_total[...].astype(LOW)
    bulk.close()
    out_bulk.close()
    wire.finish()


def back_stage(feed, fc, out, queries, keyval, meta_q, meta_k, mixed, lse, grad_mixed, centre, vec):
    count = lax.axis_size("seq")
    tensor = lax.axis_size("tensor")
    part, full = centre.shape
    batches, rows, width = queries.shape
    blocks, two = keyval.shape[1], keyval.shape[3]
    heads = 2 * width // two
    vmem, hbm = pl.BlockSpec(memory_space=pltpu.VMEM), pl.BlockSpec(memory_space=pl.ANY)
    kv_part = jax.ShapeDtypeStruct((blocks, rows, two), LOW)
    copies = 4 * count + 14
    return pl.pallas_call(
        partial(back_kernel, count),
        out_shape=[
            jax.ShapeDtypeStruct((fc.shape[1], 2 * fc.shape[2]), F32),
            jax.ShapeDtypeStruct(out.shape[1:], F32),
            jax.ShapeDtypeStruct((batches, rows, width), LOW),
            jax.ShapeDtypeStruct((batches, rows, two), LOW),
            jax.ShapeDtypeStruct((tensor, part, full), LOW),
        ],
        in_specs=[hbm] * 3 + [vmem] * 9,
        out_specs=[vmem] * 5,
        scratch_shapes=row_sum_scratch(feed)
        + seq_sum_scratch(fc, held=True)
        + seq_sum_scratch(out, held=True)
        + seq_sum_scratch(kv_part)
        + [pltpu.VMEM(kv_part.shape, LOW)] * 3
        + [
            pltpu.VMEM((rows, two), F32),
            pltpu.VMEM((rows, two), F32),
            pltpu.VMEM((heads, rows, 1), F32),
            pltpu.VMEM((rows, width), F32),
        ]
        + sem_scratch(copies)
        + [pltpu.SemaphoreType.DMA((4 + count,))],
        compiler_params=pltpu.CompilerParams(
            collective_id=3, has_side_effects=True, vmem_limit_bytes=60 << 20
        ),
        name="back",
    )(feed, fc, out, queries, keyval, meta_q, meta_k, mixed, lse, grad_mixed, centre, vec)


def last_kernel(count, *refs):
    back, query, keyval, small, own, dy, vec = refs[:7]
    query_sum, keyval_sum, rows, small_sum = refs[7:11]
    row_refs, key_row_refs = refs[11:15], refs[15:19]
    query_refs, key_refs, small_refs = refs[19:23], refs[23:26], refs[26:29]
    key_part, small_part, small_own, small_got, sums, send_sem, recv_sem, load_sem = refs[29:]
    index, place = lax.axis_index("seq"), lax.axis_index("tensor")
    along = seq_peers(index, count)
    other_core, other_side = {"tensor": flip(place, 1)}, {"tensor": flip(place, 2)}
    greet(along + [other_core, other_side])
    wire = Wire(send_sem, recv_sem, load_sem)
    reduce = RowSum(wire, place, None, back, *row_refs[:3], None, None, row_refs[3])
    key_reduce = RowSum(
        wire, place, None, keyval, *key_row_refs[:3], None, None, key_row_refs[3]
    )
    query_bulk = SeqSum(wire, index, along, query, *query_refs, query_sum, False)
    key_bulk = SeqSum(wire, index, along, key_part, *key_refs, None, keyval_sum, False)
    small_bulk = SeqSum(wire, index, along, small_part, *small_refs, None, small_own.at[0], False)
    gather = RowGather(wire, place, rows)
    spread = count // 2 - 1
    reduce.start()
    query_bulk.start()
    query_bulk.load()
    key_reduce.start()
    reduce.to_side(0)
    key_reduce.to_side(0)
    query_bulk.relay(spread // 3)
    reduce.ready()
    sums[...] = jnp.zeros_like(sums)
    gain = vec[0:1, :]

    def body(at):
        over = reduce.total(at)
        inner, product = norm_back(own[at, :].astype(F32), gain, over)
        rows[place, at, :] = (dy[at, :] + inner).astype(LOW)
        sums[0] += product
        sums[1] += over

    by_rows(own.shape[0], 16, body)
    gather.start()
    small_part[...] = small[...]
    width = own.shape[1] // count
    for row in range(2):
        line = jnp.sum(sums[row], axis=0, keepdims=True)
        for block in range(count):
            part = line[:, block * width : (block + 1) * width]
            small_part[block, row : row + 1, 0:width] = part
    small_bulk.start()
    key_reduce.ready()
    step = key_part.shape[1]
    for block in range(count):
        key_part[block] = key_reduce.total(slice(block * step, (block + 1) * step)).astype(LOW)
    key_bulk.start()
    query_bulk.relay(spread // 3)
    gather.forward()
    small_bulk.relay(spread)
    query_bulk.relay(spread - 2 * (spread // 3))
    key_bulk.relay(spread)
    small_bulk.close()
    for turn, peer in enumerate((other_core, other_side)):
        handle = wire.copy(small_own.at[turn], small_got.at[turn], peer)
        wire.arrived(handle)
        total = small_own[turn] + small_got[turn]
        if turn:
            small_sum[...] = total
        else:
            small_own[1] = total
    query_bulk.close()
    key_bulk.close()
    wire.finish()


def last_stage(back, query, keyval, small, own, dy, vec):
    count = lax.axis_size("seq")
    tensor = lax.axis_size("tensor")
    part, full = own.shape
    vmem, hbm = pl.BlockSpec(memory_space=pltpu.VMEM), pl.BlockSpec(memory_space=pl.ANY)
    key_part = jax.ShapeDtypeStruct((count, keyval.shape[2] // count, keyval.shape[3]), LOW)
    copies = 3 * count + 12
    return pl.pallas_call(
        partial(last_kernel, count),
        out_shape=[
            jax.ShapeDtypeStruct(query.shape[1:], F32),
            jax.ShapeDtypeStruct(key_part.shape[1:], F32),
            jax.ShapeDtypeStruct((tensor, part, full), LOW),
            jax.ShapeDtypeStruct(small.shape[1:], F32),
        ],
        in_specs=[hbm] * 3 + [vmem] * 4,
        out_specs=[vmem] * 4,
        scratch_shapes=row_sum_scratch(back)
        + row_sum_scratch(keyval)
        + seq_sum_scratch(query, held=True)
        + seq_sum_scratch(key_part)
        + seq_sum_scratch(small, F32)
        + [
            pltpu.VMEM(key_part.shape, LOW),
            pltpu.VMEM(small.shape, F32),
            pltpu.VMEM((2,) + small.shape[1:], F32),
            pltpu.VMEM((2,) + small.shape[1:], F32),
            pltpu.VMEM((2, 16, full), F32),
        ]
        + sem_scratch(copies)
        + [pltpu.SemaphoreType.DMA((4 + count // 2,))],
        compiler_params=pltpu.CompilerParams(
            collective_id=4, has_side_effects=True, vmem_limit_bytes=60 << 20
        ),
        name="last",
    )(back, query, keyval, small, own, dy, vec)


def visible(meta_q, meta_k):
    seg_q, pos_q = meta_q[:, 0:1], meta_q[:, 1:2]
    seg_k, pos_k = meta_k[0:1, :], meta_k[1:2, :]
    return ((seg_k == 0) | (seg_k == seg_q)) & (pos_k <= pos_q)


def norm_parts(values):
    average = jnp.mean(values, axis=-1, keepdims=True)
    centred = values - average
    spread = jnp.mean(centred * centred, axis=-1, keepdims=True)
    return centred, lax.rsqrt(spread + EPS)


def norm_back(values, gain, grad):
    centred, inverse = norm_parts(values)
    unit = centred * inverse
    scaled = grad * gain
    inner = (
        scaled
        - jnp.mean(scaled, axis=-1, keepdims=True)
        - unit * jnp.mean(scaled * unit, axis=-1, keepdims=True)
    )
    return inverse * inner, grad * unit


def gelu_pair(values):
    const = 0.7978845608028654
    square = values * values
    inner = jnp.tanh(const * (values + 0.044715 * (values * square)))
    half = 0.5 * (1.0 + inner)
    slope = half + 0.5 * values * (1.0 - inner * inner) * const * (1.0 + 3 * 0.044715 * square)
    return values * half, slope


def local(
    inputs,
    segment,
    position,
    w_query,
    w_keyval,
    w_out,
    w_fc,
    w_proj,
    vectors,
    fc_bias,
    value_bias,
    grad_out,
):
    seq_size, tensor_size = lax.axis_size("seq"), lax.axis_size("tensor")
    seq_index, tensor_index = lax.axis_index("seq"), lax.axis_index("tensor")
    batches, rows, full_width = inputs.shape
    width_block = w_query.shape[0]
    group_width = w_query.shape[1]
    hidden_width = w_fc.shape[1]
    unit_width = hidden_width // 2
    unit_half = (seq_index >> 1) & 1
    hd = value_bias.shape[0]
    quarter = rows // tensor_size
    shard = vectors.shape[1]
    bias_shard = fc_bias.shape[0]

    pieces = [
        vectors.reshape(-1).astype(LOW),
        fc_bias.astype(LOW),
        segment.reshape(-1).astype(LOW),
        (position // 128).reshape(-1).astype(LOW),
        (position % 128).reshape(-1).astype(LOW),
    ]
    cuts = [0]
    for piece in pieces:
        cuts.append(cuts[-1] + piece.shape[0])
    packed = jnp.concatenate(pieces)
    packed = jnp.pad(packed, (0, -packed.shape[0] % 2048)).reshape(-1, 128)

    def halves(array):
        return jnp.swapaxes(array.astype(LOW).reshape(width_block, 2, unit_width), 0, 1)

    small, kv_mat, q_mat = gather_first(packed, w_keyval.astype(LOW), w_query.astype(LOW))
    kv_mat = kv_mat.reshape(full_width, 2 * hd)
    q_mat = q_mat.reshape(full_width, group_width)

    small = small.reshape(seq_size, tensor_size, -1).astype(F32)
    vec_all = small[:, :, cuts[0] : cuts[1]].reshape(seq_size * tensor_size, 7, shard)
    vec_all = jnp.swapaxes(vec_all, 0, 1).reshape(7, full_width)
    fc_all = small[:, :, cuts[1] : cuts[2]].reshape(-1)
    seg_keys = small[:, 0, cuts[2] : cuts[3]].reshape(seq_size, batches, rows)
    pos_keys = 128.0 * small[:, 0, cuts[3] : cuts[4]] + small[:, 0, cuts[4] : cuts[5]]
    seg_keys = jnp.swapaxes(seg_keys, 0, 1).astype(jnp.int32)
    pos_keys = jnp.swapaxes(pos_keys.reshape(seq_size, batches, rows), 0, 1).astype(jnp.int32)
    meta_k = jnp.pad(jnp.stack([seg_keys, pos_keys], axis=2), ((0, 0), (0, 0), (0, 6), (0, 0)))
    meta_q = jnp.pad(jnp.stack([segment, position], axis=2), ((0, 0), (0, 0), (0, 126)))

    gain_one, shift_one, _, out_bias, gain_two, shift_two, proj_bias = [
        vec_all[i] for i in range(7)
    ]
    query_bias = lax.dynamic_slice_in_dim(vec_all[2], tensor_index * group_width, group_width, 0)
    fc_local = lax.dynamic_slice_in_dim(
        fc_all, tensor_index * hidden_width + unit_half * unit_width, unit_width, 0
    )
    bias_value = value_bias.astype(LOW).astype(F32)
    kv_bias = jnp.concatenate([jnp.zeros((hd,), F32), bias_value])

    residual = inputs.astype(F32)
    centred, inverse = norm_parts(residual)
    normed = (centred * inverse * gain_one + shift_one).astype(LOW).reshape(-1, full_width)
    keyval = (dot(normed, kv_mat) + kv_bias).astype(LOW).reshape(batches, rows, 2 * hd)
    queries = (dot(normed, q_mat) + query_bias).astype(LOW)
    queries = queries.reshape(batches, rows, group_width)

    def by_quarter(array):
        split = array.reshape(batches, tensor_size, quarter, array.shape[-1])
        return jnp.swapaxes(split, 0, 1).reshape(tensor_size, batches * quarter, -1)

    def by_batch(array):
        split = array.reshape(tensor_size, batches, quarter, array.shape[-1])
        return jnp.swapaxes(split, 0, 1).reshape(batches, rows, -1)

    def my_quarter(array):
        split = array.reshape(batches, tensor_size, quarter, full_width)
        own = lax.dynamic_index_in_dim(split, tensor_index, 1, keepdims=False)
        return own.reshape(batches * quarter, full_width)

    vecs = jnp.pad(jnp.stack([out_bias, gain_two, shift_two]), ((0, 5), (0, 0)))
    grad_split = by_quarter(grad_out)
    mixed, lse, kv_all, out_t, middle, rows_two, fc_mat, proj_t, grad_other = front(
        queries,
        keyval,
        meta_q,
        meta_k,
        my_quarter(inputs),
        vecs,
        w_out.T.astype(LOW),
        halves(w_fc),
        halves(w_proj.T),
        grad_split,
    )
    out_t = out_t.reshape(full_width, group_width)
    fc_mat = fc_mat.reshape(full_width, unit_width)
    proj_t = proj_t.reshape(full_width, unit_width)
    mixed_rows = by_quarter(mixed).reshape(-1, group_width)
    normed_two = rows_two.reshape(-1, full_width)
    hidden = dot(normed_two, fc_mat) + fc_local
    active_f, slope = gelu_pair(hidden)
    active = active_f.astype(LOW)

    grad_q_low = my_quarter(grad_out)
    grad_flat = jnp.concatenate([grad_split, grad_other]).reshape(-1, full_width)
    grad_hidden = (slope * dot(grad_flat, proj_t)).astype(LOW)
    fcbias_local = jnp.sum(grad_hidden.astype(F32), axis=0)
    back_part = dot_nt(grad_hidden, fc_mat).astype(LOW)
    back_part = back_part.reshape(2, tensor_size, batches * quarter, full_width)

    def blocked(array):
        return array.astype(LOW).reshape(seq_size, width_block, array.shape[-1])

    proj_sum, grad_middle, rows_middle, sums, feed_part, fc_part = middle_stage(
        back_part,
        blocked(dot_tn(grad_flat, active)),
        middle,
        grad_q_low,
        jnp.pad(gain_two[None], ((0, 7), (0, 0))),
        active,
        proj_t,
        normed_two,
        grad_hidden,
    )
    grad_gain_two, grad_shift_two, grad_out_bias = jnp.sum(sums, axis=1)
    grad_proj_bias = jnp.sum(grad_q_low.astype(F32), axis=0)
    grad_middle_low = rows_middle.reshape(-1, full_width)
    def one_row(row):
        return jnp.pad(row[None], ((0, 7), (0, 0)))

    grad_mixed = by_batch(dot(grad_middle_low, out_t).astype(LOW))
    fc_sum, out_sum, grad_queries, grad_keyval, result_rows = back_stage(
        feed_part.reshape(2, tensor_size, batches * quarter, full_width),
        blocked(fc_part),
        blocked(dot_tn(grad_middle_low, mixed_rows)),
        queries,
        kv_all,
        meta_q,
        meta_k,
        mixed,
        lse,
        grad_mixed,
        middle,
        one_row(proj_bias),
    )
    result = by_batch(result_rows)
    grad_keyval = grad_keyval.reshape(-1, 2 * hd)
    grad_queries = grad_queries.reshape(-1, group_width)
    grad_normed = dot_nt(grad_queries, q_mat) + dot_nt(grad_keyval, kv_mat)
    qbias_local = jnp.sum(grad_queries.astype(F32), axis=0)
    vbias_local = jnp.sum(grad_keyval[:, hd:].astype(F32), axis=0)

    qbias_full = lax.dynamic_update_slice_in_dim(
        jnp.zeros((full_width,), F32), qbias_local, tensor_index * group_width, 0
    )
    full_hidden = bias_shard * seq_size * tensor_size
    fcbias_full = lax.dynamic_update_slice_in_dim(
        jnp.zeros((full_hidden,), F32),
        fcbias_local,
        tensor_index * hidden_width + unit_half * unit_width,
        0,
    )
    chunk = full_hidden // seq_size
    blank = jnp.zeros((full_width,), F32)
    vec_grads = jnp.stack(
        [blank, blank, qbias_full, grad_out_bias, grad_gain_two, grad_shift_two, grad_proj_bias]
    )

    def in_rows(array):
        array = jnp.pad(array, ((0, 0), (0, -array.shape[1] % width_block)))
        return array.reshape(seq_size, -1, width_block)

    vec_rows = 7
    bias_rows = chunk // width_block
    small_rows = jnp.concatenate(
        [
            jnp.swapaxes(vec_grads.reshape(7, seq_size, width_block), 0, 1),
            in_rows(fcbias_full.reshape(seq_size, chunk)),
            in_rows(jnp.broadcast_to(vbias_local, (seq_size, hd))),
        ],
        axis=1,
    )
    small_rows = jnp.pad(
        small_rows,
        ((0, 0), (0, -small_rows.shape[1] % 8), (0, -width_block % 128)),
    )
    key_grad = dot_tn(normed, grad_keyval).astype(LOW)
    key_grad = key_grad.reshape(seq_size, tensor_size, -1, 2 * hd)
    key_grad = jnp.swapaxes(key_grad, 0, 1).reshape(1, tensor_size, -1, 2 * hd)
    query_sum, keyval_grad, input_rows, small_sum = last_stage(
        by_quarter(grad_normed.astype(LOW))[None],
        blocked(dot_tn(normed, grad_queries)),
        key_grad,
        small_rows,
        my_quarter(inputs),
        grad_middle,
        one_row(gain_one),
    )
    input_grad = by_batch(input_rows)
    small_sum = small_sum[:, :width_block]
    vec_grad = lax.dynamic_slice_in_dim(small_sum[:vec_rows], tensor_index * shard, shard, 1)
    fcbias_grad = lax.dynamic_slice_in_dim(
        small_sum[vec_rows : vec_rows + bias_rows].reshape(-1),
        tensor_index * bias_shard,
        bias_shard,
        0,
    )
    vbias_grad = small_sum[vec_rows + bias_rows :].reshape(-1)[:hd]
    return (
        result,
        input_grad,
        query_sum,
        keyval_grad,
        out_sum.T,
        fc_sum,
        proj_sum.T,
        vec_grad,
        fcbias_grad,
        vbias_grad,
        vec_grad[5],
    )


def solution(mesh):
    in_specs = (
        P(None, "seq", None),
        P(None, "seq"),
        P(None, "seq"),
        P("seq", "tensor"),
        P(("seq", "tensor"), None),
        P("tensor", "seq"),
        P("seq", "tensor"),
        P("tensor", "seq"),
        P(None, ("seq", "tensor")),
        P(("seq", "tensor")),
        P(),
        P(None, "seq", None),
    )
    out_specs = (
        P(None, "seq", None),
        P(None, "seq", None),
        P("seq", "tensor"),
        P(("seq", "tensor"), None),
        P("tensor", "seq"),
        P("seq", "tensor"),
        P("tensor", "seq"),
        P(None, ("seq", "tensor")),
        P(("seq", "tensor")),
        P(),
        P(("seq", "tensor")),
    )
    return jax.shard_map(local, mesh=mesh, in_specs=in_specs, out_specs=out_specs, check_vma=False)
```
